32 devices in a mesh: shard: 4 (over z), ctx: 2 (over x), tp: 4 (over y, core).
Axes of the slice: x: 2, y: 2, z: 4, core: 2. Of those that a mesh axis runs over, the one named last changes fastest.
Arguments:
- patches: bfloat16 [8, 2048, 1280], P('shard', 'ctx'), may hold values from -6 to 6
- cotangent: bfloat16 [8, 2048, 1280], P('shard', 'ctx'), may hold values from -6 to 6
- picture_ids: int32 [8, 2048], P('shard'), may hold values from -1 to 10, as said below
- positions: int32 [2, 8, 2048], P(None, 'shard', 'ctx'), may hold values from 0 to 63, as said below
- ln1_gain: float32 [1280], P('shard'), may hold values from 0.25 to 1.75
- ln1_bias: float32 [1280], P('shard'), may hold values from -1.25 to 1.25
- qkv_weight: float32 [1280, 3, 1280], P('shard', None, 'tp'), may hold values from -0.15625 to 0.15625
- qkv_bias: float32 [3, 16, 80], P(None, 'tp', 'shard'), may hold values from -0.625 to 0.625
- proj_weight: float32 [1280, 1280], P('tp', 'shard'), may hold values from -1.25 to 1.25
- proj_bias: float32 [1280], P('shard'), may hold values from -1.25 to 1.25
- ln2_gain: float32 [1280], P('shard'), may hold values from 0.25 to 1.75
- ln2_bias: float32 [1280], P('shard'), may hold values from -1.25 to 1.25
- fc1_weight: float32 [1280, 5120], P('shard', 'tp'), may hold values from -0.15625 to 0.15625
- fc1_bias: float32 [80, 64], P('tp', 'shard'), may hold values from -3 to 3
- fc2_weight: float32 [5120, 1280], P('tp', 'shard'), may hold values from -0.125 to 0.125
- fc2_bias: float32 [1280], P('shard'), may hold values from -1.25 to 1.25
Outputs:
- block_out: bfloat16 [8, 2048, 1280], P('shard', 'ctx')
- grad_patches: bfloat16 [8, 2048, 1280], P('shard', 'ctx')
- grad_ln1_gain: float32 [1280], P('shard')
- grad_ln1_bias: float32 [1280], P('shard')
- grad_qkv_weight: float32 [1280, 3, 1280], P('shard', None, 'tp')
- grad_qkv_bias: float32 [3, 16, 80], P(None, 'tp', 'shard')
- grad_proj_weight: float32 [1280, 1280], P('tp', 'shard')
- grad_proj_bias: float32 [1280], P('shard')
- grad_ln2_gain: float32 [1280], P('shard')
- grad_ln2_bias: float32 [1280], P('shard')
- grad_fc1_weight: float32 [1280, 5120], P('shard', 'tp')
- grad_fc1_bias: float32 [80, 64], P('tp', 'shard')
- grad_fc2_weight: float32 [5120, 1280], P('tp', 'shard')
- grad_fc2_bias: float32 [1280], P('shard')
The draws below stay inside these ranges and needn't reach their ends.
Inputs may be any that keep to these rules, and one draw needn't show every extreme that they name: `picture_ids`: in each packed row the pictures are numbered 0, 1, 2, ... in order and lie in runs of 100 to 1024 patches; one of the first two pictures of every row has exactly 1024 patches; -1 marks padding, which only follows a row's last picture. In every draw some row holds as many pictures as fit: all but its picture of 1024 patches have exactly 100. `positions`: each picture has a grid 16 to 32 patches wide, and its patches run row by row through it (row = index in the picture divided by the width, column = the remainder); a picture of 1024 patches is 16 wide; padding has row and column 0.
All inputs are finite; a program needn't handle non-finite values.
Results may differ from the reference program's by a relative error of at most 0.02.
Values may be sent and summed in bfloat16 or wider, within the bound.
No kernel may reach another device: no remote copies, remote signals or barrier semaphores. Data moves between devices by JAX's collectives and lax.ppermute only.
A program may use at most 512 MiB of HBM per device.

```python
import jax
import jax.numpy as jnp
from jax import lax

D = 1280
HEADS = 16
HEAD_DIM = 80
FF = 5120
ROW_LEN = 2048
PIC_MIN = 100
PIC_MAX = 1024
ROWS = 8


def picture_layout(key):
    picture_slots = ROW_LEN // PIC_MIN + 1

    def one_row(row_key, dense):
        len_key, pick_key, width_key = jax.random.split(row_key, 3)
        lengths = jax.random.randint(len_key, (picture_slots,), PIC_MIN, PIC_MAX + 1)
        lengths = jnp.where(dense, PIC_MIN, lengths)
        chosen = jax.random.randint(pick_key, (), 0, 2)
        lengths = jnp.where(jnp.arange(picture_slots) == chosen, PIC_MAX, lengths)
        end_points = jnp.cumsum(lengths)
        starts = end_points - lengths
        fitting = end_points <= ROW_LEN
        position_index = jnp.arange(ROW_LEN)[:, None]
        inside = ((position_index >= starts[None, :]) & (position_index < end_points[None, :]) & fitting[None, :]).astype(jnp.int32)
        present = jnp.sum(inside, axis=1)
        number = jnp.sum(inside * jnp.arange(picture_slots)[None, :], axis=1)
        picture = jnp.where(present > 0, number, -1)
        widths = jax.random.randint(width_key, (picture_slots,), 16, 33)
        widths = jnp.where(lengths == PIC_MAX, 16, widths)
        begin_at = jnp.sum(inside * starts[None, :], axis=1)
        across = jnp.maximum(jnp.sum(inside * widths[None, :], axis=1), 1)
        offset = jnp.arange(ROW_LEN) - begin_at
        grid_row = jnp.where(present > 0, offset // across, 0)
        grid_col = jnp.where(present > 0, offset % across, 0)
        return (picture.astype(jnp.int32), jnp.stack([grid_row, grid_col]).astype(jnp.int32))
    row_keys = jax.random.split(jax.random.fold_in(key, 17), ROWS)
    dense_row = jax.random.randint(jax.random.fold_in(key, 29), (), 0, ROWS)
    dense_flags = jnp.arange(ROWS) == dense_row
    pictures, places = jax.vmap(one_row)(row_keys, dense_flags)
    return (pictures, jnp.moveaxis(places, 1, 0))


def draw_picture_ids(key, part):
    return picture_layout(key)[0]


def draw_positions(key, part):
    return picture_layout(key)[1]


def shard_levels(key, shape, pieces, smallest, high):
    level, own = 1.0, jax.random.fold_in(key, 6)
    for dim, parts in pieces:
        steps = jnp.exp(jax.random.uniform(jax.random.fold_in(own, dim), (parts,), jnp.float32, smallest / len(pieces), high / len(pieces)))
        level = level * jnp.repeat(steps, shape[dim] // parts).reshape([-1 if axis == dim else 1 for axis in range(len(shape))])
    return level


def scatter_about(key, extent, spread, most, cuts=(), kind=jnp.bfloat16):
    values = spread * jax.random.normal(key, extent, jnp.float32)
    if cuts:
        values = values * shard_levels(key, extent, cuts, -0.22, 0.18)
    return jnp.clip(values, -most, most).astype(kind)


def setup_inputs(seed: int = 0) -> dict:
    key_of = jax.random.split(jax.random.key(seed), 17)
    patches = scatter_about(key_of[0], (ROWS, ROW_LEN, D), 1.0, 6.0, ((0, 4), (1, 2)))
    cotangent = scatter_about(key_of[1], (ROWS, ROW_LEN, D), 1.0, 6.0, ((0, 4), (1, 2)))
    picture_ids = draw_picture_ids(jax.random.fold_in(key_of[16], 71), 0)
    positions = draw_positions(jax.random.fold_in(key_of[16], 71), 0)
    ln1_gain = jnp.clip(1.0 + 0.15 * jax.random.normal(key_of[4], (D,), jnp.float32), 0.25, 1.75)
    ln1_bias = scatter_about(key_of[5], (D,), 0.2, 1.25, ((0, 4),), jnp.float32)
    qkv_weight = scatter_about(key_of[6], (D, 3, D), D ** -0.5, 0.15625, ((0, 4), (2, 4)), jnp.float32)
    qkv_bias = scatter_about(key_of[7], (3, HEADS, HEAD_DIM), 0.1, 0.625, ((1, 4), (2, 4)), jnp.float32)
    proj_weight = scatter_about(key_of[8], (D, D), (D // 64) ** -0.5, 1.25, ((0, 4), (1, 4)), jnp.float32)
    proj_bias = scatter_about(key_of[9], (D,), 0.2, 1.25, ((0, 4),), jnp.float32)
    ln2_gain = jnp.clip(1.0 + 0.15 * jax.random.normal(key_of[10], (D,), jnp.float32), 0.25, 1.75)
    ln2_bias = scatter_about(key_of[11], (D,), 0.2, 1.25, ((0, 4),), jnp.float32)
    fc1_weight = scatter_about(key_of[12], (D, FF), D ** -0.5, 0.15625, ((0, 4), (1, 4)), jnp.float32)
    fc1_bias = scatter_about(key_of[13], (FF // 64, 64), 0.5, 3.0, ((0, 4), (1, 4)), jnp.float32)
    fc2_weight = scatter_about(key_of[14], (FF, D), (FF // 2) ** -0.5, 0.125, ((0, 4), (1, 4)), jnp.float32)
    fc2_bias = scatter_about(key_of[15], (D,), 0.2, 1.25, ((0, 4),), jnp.float32)
    return dict(patches=patches, cotangent=cotangent, picture_ids=picture_ids, positions=positions, ln1_gain=ln1_gain, ln1_bias=ln1_bias, qkv_weight=qkv_weight, qkv_bias=qkv_bias, proj_weight=proj_weight, proj_bias=proj_bias, ln2_gain=ln2_gain, ln2_bias=ln2_bias, fc1_weight=fc1_weight, fc1_bias=fc1_bias, fc2_weight=fc2_weight, fc2_bias=fc2_bias)


@jax.custom_vjp
def low(v):
    return lax.optimization_barrier(v.astype(jnp.bfloat16)).astype(jnp.float32)

@jax.custom_vjp
def low_back(v):
    return v

def low_keep(v):
    return (low(v), None)

def low_pass(kept, grad):
    return (grad,)

def back_keep(v):
    return (v, None)

def back_low(kept, grad):
    return (low(grad),)
low.defvjp(low_keep, low_pass)
low_back.defvjp(back_keep, back_low)
norm_eps = 1e-06
masked_score = -1e+30
highest = lax.Precision.HIGHEST

def layer_norm(rows_in, norm_gain, norm_bias):
    center = rows_in - lax.optimization_barrier(jnp.mean(rows_in, axis=-1, keepdims=True))
    inverse = lax.rsqrt(lax.optimization_barrier(jnp.mean(center * center, axis=-1, keepdims=True)) + norm_eps)
    return center * inverse * norm_gain + norm_bias

def rotary_tables(grid_pos):
    quarter = HEAD_DIM // 4
    frequency = jnp.power(10000.0, -4.0 * jnp.arange(quarter, dtype=jnp.float32) / HEAD_DIM)
    rows_angle = grid_pos[0].astype(jnp.float32)[..., None] * frequency
    cols_angle = grid_pos[1].astype(jnp.float32)[..., None] * frequency
    angles = jnp.concatenate([rows_angle, cols_angle, rows_angle, cols_angle], axis=-1)
    return (jnp.cos(angles), jnp.sin(angles))

def rotate(vectors, cos_table, sin_table):
    half_dim = vectors.shape[-1] // 2
    turned = jnp.concatenate([-vectors[..., half_dim:], vectors[..., :half_dim]], axis=-1)
    return vectors * cos_table[..., None, :] + turned * sin_table[..., None, :]

def attend_row(query_rows, key_rows, value_rows, row_ids):
    raw_scores = jnp.einsum('qhd,khd->hqk', query_rows, key_rows, precision=highest)
    scores = low_back(raw_scores) * HEAD_DIM ** (-0.5)
    live_rows = row_ids >= 0
    allowed = (row_ids[:, None] == row_ids[None, :]) & live_rows[:, None]
    row_max = lax.optimization_barrier(jnp.max(jnp.where(allowed[None], scores, masked_score), axis=-1, keepdims=True))
    row_max = jnp.where(live_rows[None, :, None], row_max, 0.0)
    exponentials = jnp.where(allowed[None], jnp.exp(scores - row_max), 0.0)
    totals = lax.optimization_barrier(jnp.sum(exponentials, axis=-1, keepdims=True)) + jnp.where(live_rows, 0.0, 1.0)[None, :, None]
    probabilities = low(exponentials / totals)
    return jnp.einsum('hqk,khd->qhd', probabilities, value_rows, precision=highest)

def row_pass(params, row_x, row_ids, row_pos):
    ln1_gain, ln1_bias, qkv_weight, qkv_bias, proj_weight, proj_bias, ln2_gain, ln2_bias, fc1_weight, fc1_bias, fc2_weight, fc2_bias = params
    normed = low(layer_norm(row_x, ln1_gain, ln1_bias))
    projected = jnp.dot(normed, qkv_weight.reshape(D, 3 * D), precision=highest, preferred_element_type=jnp.float32) + qkv_bias.reshape(3 * D)
    projected = low_back(projected).reshape(ROW_LEN, 3, HEADS, HEAD_DIM)
    cos_table, sin_table = rotary_tables(row_pos)
    query_rows = low(rotate(projected[:, 0], cos_table, sin_table))
    key_rows = low(rotate(projected[:, 1], cos_table, sin_table))
    value_rows = low(projected[:, 2])
    attended = attend_row(query_rows, key_rows, value_rows, row_ids).reshape(ROW_LEN, D)
    attended = low(low_back(attended))
    branch = low_back(jnp.dot(attended, proj_weight, precision=highest, preferred_element_type=jnp.float32) + proj_bias)
    hidden = row_x + branch
    mixed = low(layer_norm(hidden, ln2_gain, ln2_bias))
    inner = low_back(jnp.dot(mixed, fc1_weight, precision=highest, preferred_element_type=jnp.float32) + fc1_bias.reshape(FF))
    activated = low(inner * jax.nn.sigmoid(1.702 * inner))
    feed = low_back(jnp.dot(activated, fc2_weight, precision=highest, preferred_element_type=jnp.float32) + fc2_bias)
    return (hidden + feed) * (row_ids >= 0).astype(jnp.float32)[:, None]

def row_step(params, row_item):
    return row_pass(params, row_item[0], row_item[1], row_item[2])

def reference(patches, cotangent, picture_ids, positions, ln1_gain, ln1_bias, qkv_weight, qkv_bias, proj_weight, proj_bias, ln2_gain, ln2_bias, fc1_weight, fc1_bias, fc2_weight, fc2_bias):
    masters = (ln1_gain, ln1_bias, qkv_weight, qkv_bias, proj_weight, proj_bias, ln2_gain, ln2_bias, fc1_weight, fc1_bias, fc2_weight, fc2_bias)
    row_items = (picture_ids, jnp.moveaxis(positions, 0, 1))

    def whole(inputs, params):
        rounded = tuple((low(master) for master in params))
        checked = jax.checkpoint(row_step)
        return lax.map(lambda row_item: checked(rounded, (row_item[0], row_item[1], row_item[2])), (inputs, row_items[0], row_items[1]))
    block_out, pull_back = jax.vjp(whole, patches.astype(jnp.float32), masters)
    grad_inputs, grads = pull_back(cotangent.astype(jnp.float32))
    return (block_out.astype(jnp.bfloat16), grad_inputs.astype(jnp.bfloat16), grads[0], grads[1], grads[2], grads[3], grads[4], grads[5], grads[6], grads[7], grads[8], grads[9], grads[10], grads[11])
```

```python
import functools
import math

import jax
import jax.numpy as jnp
from jax import lax
from jax.experimental import pallas as pl
from jax.experimental.pallas import tpu as pltpu
from jax.sharding import PartitionSpec as P

HEAD_DIM = 80
LANES = 128
norm_eps = 1e-06
hide = 1e30
floor_max = -1e29
log2e = math.log2(math.e)
bf16 = jnp.bfloat16
f32 = jnp.float32
NT = (((1,), (1,)), ((), ()))
NN = (((1,), (0,)), ((), ()))
TN = (((0,), (0,)), ((), ()))


def mm(a, b, dims=NN):
    return lax.dot_general(a, b, dims, preferred_element_type=f32)


def lane_index(rows):
    return lax.broadcasted_iota(jnp.int32, (rows, LANES), 1)


def swap_halves(w, lane):
    half = HEAD_DIM // 2
    up = pltpu.roll(w, LANES - half, 1)
    down = pltpu.roll(w, half, 1)
    return jnp.where(lane < half, up, down)


def widen(piece):
    rows = piece.shape[0]
    tail = jnp.zeros((rows, LANES - piece.shape[1]), piece.dtype)
    return jnp.concatenate([piece, tail], axis=1)


def split_three(column):
    high = column.astype(bf16).astype(f32)
    rest = column - high
    mid = rest.astype(bf16).astype(f32)
    return high, mid, rest - mid


def place_three(base, column, lane):
    high, mid, low = split_three(column)
    base = jnp.where(lane == 96, high, base)
    base = jnp.where(lane == 97, mid, base)
    return jnp.where(lane == 98, low, base)


def qkv_kernel(heads, x_ref, w_ref, ln_ref, b_ref, cos_ref, sin_ref, feat_ref, a_ref, q_ref, kv_ref):
    width = heads * HEAD_DIM
    x = x_ref[...].astype(f32)
    rows = x.shape[0]
    center = x - jnp.mean(x, axis=1, keepdims=True)
    inverse = lax.rsqrt(jnp.mean(center * center, axis=1, keepdims=True) + norm_eps)
    a = (center * inverse * ln_ref[0:1, :] + ln_ref[1:2, :]).astype(bf16)
    a_ref[...] = a
    y = mm(a, w_ref[...]) + b_ref[0:1, :]
    cos, sin = cos_ref[...], sin_ref[...]
    lane = lane_index(rows)
    kv = []
    for h in range(heads):
        w = widen(y[:, h * HEAD_DIM : (h + 1) * HEAD_DIM])
        q = (w * cos + swap_halves(w, lane) * sin) * (HEAD_DIM**-0.5 * log2e)
        q_ref[h] = jnp.where(lane < HEAD_DIM, q.astype(bf16), feat_ref[...])
    for h in range(heads):
        begin = width + h * HEAD_DIM
        w = widen(y[:, begin : begin + HEAD_DIM])
        kv.append((w * cos + swap_halves(w, lane) * sin)[:, :HEAD_DIM].astype(bf16))
    kv.append(y[:, 2 * width : 3 * width].astype(bf16))
    kv_ref[...] = jnp.concatenate(kv, axis=1)


def project_row(x, w, ln, bias, cos, sin, feat, heads):
    rows, width = x.shape
    block = min(256, rows)
    wide = w.shape[1]
    local = heads * HEAD_DIM
    by_rows = lambda n: pl.BlockSpec((block, n), lambda i: (i, 0))
    whole = lambda a: pl.BlockSpec(a.shape, lambda i: (0,) * a.ndim)
    return pl.pallas_call(
        functools.partial(qkv_kernel, heads),
        grid=(rows // block,),
        in_specs=[
            by_rows(width),
            whole(w),
            whole(ln),
            whole(bias),
            by_rows(LANES),
            by_rows(LANES),
            by_rows(LANES),
        ],
        out_specs=[
            by_rows(width),
            pl.BlockSpec((heads, block, LANES), lambda i: (0, i, 0)),
            by_rows(2 * local),
        ],
        out_shape=[
            jax.ShapeDtypeStruct((rows, width), bf16),
            jax.ShapeDtypeStruct((heads, rows, LANES), bf16),
            jax.ShapeDtypeStruct((rows, 2 * local), bf16),
        ],
        cost_estimate=pl.CostEstimate(
            flops=2 * rows * width * wide, bytes_accessed=rows * width * 4 + width * wide * 2, transcendentals=0
        ),
        name="project_row",
    )(x, w, ln, bias, cos, sin, feat)


def forward_kernel(heads, segments, block, flag_ref, q_ref, *refs):
    kv_refs = refs[:segments]
    feat_refs = refs[segments : 2 * segments]
    o_ref, q_out, k_aug, v_aug, m_scr, acc_scr = refs[2 * segments :]
    width = heads * HEAD_DIM
    step = pl.program_id(0)
    keys = k_aug.shape[1]
    count = keys // block
    rows = q_ref.shape[1]

    @pl.when(step == 0)
    def build():
        offset = 0
        for s in range(segments):
            length = kv_refs[s].shape[0]
            piece = min(length, 256)
            for t in range(length // piece):
                at = pl.ds(t * piece, piece)
                to = pl.ds(offset + t * piece, piece)
                kv = kv_refs[s][at, :]
                feat = feat_refs[s][at, :]
                lane = lane_index(piece)
                tail = jnp.where(lane == HEAD_DIM, 1.0, jnp.where((lane >= 96) & (lane < 99), -1.0, 0.0)).astype(bf16)
                for h in range(heads):
                    k = kv[:, h * HEAD_DIM : (h + 1) * HEAD_DIM]
                    v = kv[:, width + h * HEAD_DIM : width + (h + 1) * HEAD_DIM]
                    k_aug[h, to, :] = jnp.concatenate([k, feat[:, HEAD_DIM:]], axis=1)
                    v_aug[h, to, :] = jnp.concatenate([v, tail[:, HEAD_DIM:]], axis=1)
            offset += length

    m_scr[...] = jnp.full(m_scr.shape, floor_max, f32)
    acc_scr[...] = jnp.zeros(acc_scr.shape, f32)

    def visit(j, carry):
        @pl.when(flag_ref[step * count + j] > 0)
        def go():
            at = pl.ds(pl.multiple_of(j * block, block), block)
            for h in range(heads):
                s = mm(q_ref[h], k_aug[h, at, :], NT)
                old = m_scr[h]
                new = jnp.maximum(old, jnp.max(s, axis=1, keepdims=True))
                p = jnp.exp2(s - new[:, 0:1])
                m_scr[h] = new
                acc_scr[h] = acc_scr[h] * jnp.exp2(old - new) + mm(p.astype(bf16), v_aug[h, at, :])

        return carry

    lax.fori_loop(0, count, visit, 0)
    lane = lane_index(rows)
    outs = []
    for h in range(heads):
        acc = acc_scr[h]
        total = acc[:, HEAD_DIM : HEAD_DIM + 1]
        alive = total > 0.0
        safe = jnp.where(alive, total, 1.0)
        outs.append((acc / safe)[:, :HEAD_DIM].astype(bf16))
        level = jnp.where(alive, m_scr[h][:, 0:1] + jnp.log2(safe), 0.0)
        q_out[h] = place_three(q_ref[h].astype(f32), level, lane).astype(bf16)
    o_ref[...] = jnp.concatenate(outs, axis=1)


def attend_forward(flags, q_aug, kvs, feats, heads, block):
    rows = q_aug.shape[1]
    tall = min(256, rows)
    keys = sum(kv.shape[0] for kv in kvs)
    segments = len(kvs)
    whole = lambda a: pl.BlockSpec(a.shape, lambda i, f: (0,) * a.ndim)
    q_spec = pl.BlockSpec((heads, tall, LANES), lambda i, f: (0, i, 0))
    k_spec = pl.BlockSpec((heads, keys, LANES), lambda i, f: (0, 0, 0))
    local = heads * HEAD_DIM
    return pl.pallas_call(
        functools.partial(forward_kernel, heads, segments, block),
        grid_spec=pltpu.PrefetchScalarGridSpec(
            num_scalar_prefetch=1,
            grid=(rows // tall,),
            in_specs=[q_spec] + [whole(kv) for kv in kvs] + [whole(f) for f in feats],
            out_specs=[pl.BlockSpec((tall, local), lambda i, f: (i, 0)), q_spec, k_spec, k_spec],
            scratch_shapes=[
                pltpu.VMEM((heads, tall, LANES), f32),
                pltpu.VMEM((heads, tall, LANES), f32),
            ],
        ),
        out_shape=[
            jax.ShapeDtypeStruct((rows, local), bf16),
            jax.ShapeDtypeStruct((heads, rows, LANES), bf16),
            jax.ShapeDtypeStruct((heads, keys, LANES), bf16),
            jax.ShapeDtypeStruct((heads, keys, LANES), bf16),
        ],
        cost_estimate=pl.CostEstimate(
            flops=2 * rows * keys * heads * LANES, bytes_accessed=8 * keys * local, transcendentals=rows * keys * heads // 2
        ),
        name="attend_forward",
    )(flags, q_aug, *kvs, *feats)


def backward_kernel(
    heads, segments, block, flag_ref, q_ref, go_ref, o_ref, k_aug, v_aug, cosq_ref, sinq_ref, *refs
):
    cosk_refs = refs[:segments]
    sink_refs = refs[segments : 2 * segments]
    dq_ref = refs[2 * segments]
    dkv_refs = refs[2 * segments + 1 : 3 * segments + 1]
    k_turn, dk_acc, dv_acc, dq_acc, go_scr = refs[3 * segments + 1 :]
    step = pl.program_id(0)
    keys = k_aug.shape[1]
    count = keys // block
    rows = q_ref.shape[1]
    scale = HEAD_DIM**-0.5

    @pl.when(step == 0)
    def build():
        dk_acc[...] = jnp.zeros(dk_acc.shape, f32)
        dv_acc[...] = jnp.zeros(dv_acc.shape, f32)
        for h in range(heads):
            for t in range(count):
                at = pl.ds(t * block, block)
                k_turn[h, :, at] = k_aug[h, at, :].T

    lane = lane_index(rows)
    for h in range(heads):
        cut = slice(h * HEAD_DIM, (h + 1) * HEAD_DIM)
        go = go_ref[:, cut].astype(f32)
        delta = jnp.sum(go * o_ref[:, cut].astype(f32), axis=1, keepdims=True)
        go_scr[h] = place_three(widen(go), delta, lane).astype(bf16)
    dq_acc[...] = jnp.zeros(dq_acc.shape, f32)

    def visit(j, carry):
        @pl.when(flag_ref[step * count + j] > 0)
        def run():
            at = pl.ds(pl.multiple_of(j * block, block), block)
            for h in range(heads):
                q, go = q_ref[h], go_scr[h]
                p = jnp.exp2(mm(k_aug[h, at, :], q, NT))
                ds = (p * mm(v_aug[h, at, :], go, NT)).astype(bf16)
                dv_acc[h, at, :] += mm(p.astype(bf16), go)
                dk_acc[h, at, :] += mm(ds, q)
                dq_acc[h] += mm(k_turn[h, :, at], ds)

        return carry

    lax.fori_loop(0, count, visit, 0)

    def turn_back(w, cos, sin, index):
        return w * cos - swap_halves(w, index) * sin

    outs = []
    for h in range(heads):
        w = dq_acc[h].T
        back = turn_back(w, cosq_ref[...], sinq_ref[...], lane) * scale
        outs.append(back[:, :HEAD_DIM].astype(bf16))
    dq_ref[...] = jnp.concatenate(outs, axis=1)

    @pl.when(step == pl.num_programs(0) - 1)
    def finish():
        offset = 0
        for s in range(segments):
            length = dkv_refs[s].shape[0]
            piece = min(length, 256)
            index = lane_index(piece)
            for t in range(length // piece):
                at = pl.ds(t * piece, piece)
                of = pl.ds(offset + t * piece, piece)
                parts = []
                for h in range(heads):
                    w = dk_acc[h, of, :]
                    back = turn_back(w, cosk_refs[s][at, :], sink_refs[s][at, :], index) * (1.0 / log2e)
                    parts.append(back[:, :HEAD_DIM].astype(bf16))
                for h in range(heads):
                    parts.append(dv_acc[h, of, :][:, :HEAD_DIM].astype(bf16))
                dkv_refs[s][at, :] = jnp.concatenate(parts, axis=1)
            offset += length


def attend_backward(flags, q_aug, go, o, k_aug, v_aug, cos_q, sin_q, cos_k, sin_k, heads, block):
    rows = q_aug.shape[1]
    tall = min(256, rows)
    keys = k_aug.shape[1]
    segments = len(cos_k)
    local = heads * HEAD_DIM
    whole = lambda a: pl.BlockSpec(a.shape, lambda i, f: (0,) * a.ndim)
    by_rows = lambda n: pl.BlockSpec((tall, n), lambda i, f: (i, 0))
    q_spec = pl.BlockSpec((heads, tall, LANES), lambda i, f: (0, i, 0))
    return pl.pallas_call(
        functools.partial(backward_kernel, heads, segments, block),
        grid_spec=pltpu.PrefetchScalarGridSpec(
            num_scalar_prefetch=1,
            grid=(rows // tall,),
            in_specs=[q_spec, by_rows(local), by_rows(local), whole(k_aug), whole(v_aug), by_rows(LANES), by_rows(LANES)]
            + [whole(t) for t in cos_k]
            + [whole(t) for t in sin_k],
            out_specs=[by_rows(local)]
            + [pl.BlockSpec((t.shape[0], 2 * local), lambda i, f: (0, 0)) for t in cos_k],
            scratch_shapes=[
                pltpu.VMEM((heads, LANES, keys), bf16),
                pltpu.VMEM((heads, keys, LANES), f32),
                pltpu.VMEM((heads, keys, LANES), f32),
                pltpu.VMEM((heads, LANES, tall), f32),
                pltpu.VMEM((heads, tall, LANES), bf16),
            ],
        ),
        out_shape=[jax.ShapeDtypeStruct((rows, local), bf16)]
        + [jax.ShapeDtypeStruct((t.shape[0], 2 * local), bf16) for t in cos_k],
        cost_estimate=pl.CostEstimate(
            flops=5 * rows * keys * heads * LANES, bytes_accessed=16 * keys * local, transcendentals=rows * keys * heads // 2
        ),
        name="attend_backward",
    )(flags, q_aug, go, o, k_aug, v_aug, cos_q, sin_q, *cos_k, *sin_k)


def norm_stats(rows_in):
    center = rows_in - jnp.mean(rows_in, axis=1, keepdims=True)
    inverse = lax.rsqrt(jnp.mean(center * center, axis=1, keepdims=True) + norm_eps)
    return center * inverse, inverse


def norm_backward(grad_rows, unit_rows, inverse, gain):
    scaled = grad_rows * gain
    grad_in = inverse * (
        scaled
        - jnp.mean(scaled, axis=1, keepdims=True)
        - unit_rows * jnp.mean(scaled * unit_rows, axis=1, keepdims=True)
    )
    return (grad_in, jnp.sum(grad_rows * unit_rows, axis=0), jnp.sum(grad_rows, axis=0))


def tables(grid_pos):
    lane = jnp.arange(LANES)
    quarter = HEAD_DIM // 4
    frequency = jnp.power(10000.0, -4.0 * (lane % quarter).astype(f32) / HEAD_DIM)
    place = jnp.where((lane // quarter) % 2 == 0, grid_pos[0][:, None], grid_pos[1][:, None])
    angle = jnp.where(lane < HEAD_DIM, place.astype(f32) * frequency, 0.0)
    return jnp.cos(angle), jnp.where(lane < HEAD_DIM // 2, -1.0, 1.0) * jnp.sin(angle)


def query_features(ids):
    lane = jnp.arange(LANES)
    return (lane == HEAD_DIM + 1 + ids[:, None]).astype(bf16)


def key_features(ids):
    lane = jnp.arange(LANES)
    slot = lane - HEAD_DIM
    same = (slot >= 1) & (slot == ids[:, None] + 1)
    wall = jnp.where((slot >= 0) & (slot < 16) & ~same, -hide, 0.0)
    return jnp.where((lane >= 96) & (lane < 99), -1.0, wall).astype(bf16)


def visit_flags(query_ids, key_ids, tall, block):
    q = query_ids.reshape(-1, tall)
    k = key_ids.reshape(-1, block)
    q_top, k_top = jnp.max(q, axis=1), jnp.max(k, axis=1)
    q_low = jnp.min(jnp.where(q >= 0, q, 1 << 20), axis=1)
    k_low = jnp.min(jnp.where(k >= 0, k, 1 << 20), axis=1)
    meet = (q_low[:, None] <= k_top[None, :]) & (k_low[None, :] <= q_top[:, None])
    return meet.astype(jnp.int32).reshape(-1)


def on_device(
    patches,
    cotangent,
    picture_ids,
    positions,
    ln1_gain,
    ln1_bias,
    qkv_weight,
    qkv_bias,
    proj_weight,
    proj_bias,
    ln2_gain,
    ln2_bias,
    fc1_weight,
    fc1_bias,
    fc2_weight,
    fc2_bias,
):
    row_count, row_share, width = patches.shape
    owners = lax.axis_size("shard")
    contexts = lax.axis_size("ctx")
    ways = lax.axis_size("tp")
    part = qkv_weight.shape[0]
    local = qkv_weight.shape[2]
    heads = local // HEAD_DIM
    half = row_share // 2
    side = lax.axis_index("tp") % 2
    context = lax.axis_index("ctx")
    pairs_near = [(i, i ^ 1) for i in range(ways)]
    pairs_far = [(i, i ^ 2) for i in range(ways)]
    pad = -3 * local % 256
    wide = 3 * local + pad

    def near(v):
        return lax.ppermute(v, "tp", pairs_near)

    def far(v):
        return lax.ppermute(v, "tp", pairs_far)

    def over_ctx(v):
        return lax.ppermute(v, "ctx", [(0, 1), (1, 0)])

    def mine_first(v, axis=0):
        return jnp.where(side == 0, v, jnp.roll(v, half, axis=axis))

    def column(v):
        flat = v.reshape(-1)
        return jnp.pad(flat, (0, part - flat.shape[0]))

    vectors = [ln1_gain, ln1_bias, ln2_gain, ln2_bias, proj_bias, fc2_bias, qkv_bias, fc1_bias]
    tail = jnp.stack([column(v) for v in vectors], axis=1)
    tail = jnp.pad(tail, ((0, 0), (0, pad - len(vectors))))
    qkv_piece = jnp.concatenate([qkv_weight.reshape(part, 3 * local), tail], axis=1).astype(bf16)
    gather = lambda v: lax.all_gather(v, "shard", axis=0, tiled=True)
    w_qkv = gather(qkv_piece)
    w_proj = gather(proj_weight.T.astype(bf16))
    w_up = gather(fc1_weight.astype(bf16))
    w_down = gather(fc2_weight.T.astype(bf16))
    packed = w_qkv[:, 3 * local : 3 * local + len(vectors)].T.astype(f32)
    gain_one, bias_one, gain_two, bias_two, proj_shift, down_shift = [packed[i] for i in range(6)]
    qb_size = qkv_bias.size
    qkv_shift = packed[6].reshape(owners, part)[:, :qb_size].reshape((owners,) + qkv_bias.shape)
    qkv_shift = jnp.transpose(qkv_shift, (1, 2, 0, 3)).reshape(-1)
    qkv_shift = jnp.pad(qkv_shift, (0, pad)).reshape(1, wide)
    up_shift = packed[7].reshape(owners, part)[:, : fc1_bias.size].reshape((owners,) + fc1_bias.shape)
    up_shift = jnp.transpose(up_shift, (1, 0, 2)).reshape(-1)
    ln_one = packed[0:2]

    ids_by_ctx = mine_first(picture_ids.reshape(row_count, contexts, row_share), axis=2)
    places = mine_first(positions, axis=2)
    block = min(256, row_share)
    key_block = 256
    rows = []
    for r in range(row_count):
        x = mine_first(patches[r])
        g = mine_first(cotangent[r])
        ids = lax.dynamic_index_in_dim(ids_by_ctx[r], context, 0, keepdims=False)
        if contexts == 2:
            other = lax.dynamic_index_in_dim(ids_by_ctx[r], 1 - context, 0, keepdims=False)
            key_ids = [ids, other]
            spots = [places[:, r], over_ctx(places[:, r])]
        else:
            key_ids = [ids_by_ctx[r].reshape(-1)]
            spots = [lax.all_gather(places[:, r], "ctx", axis=1, tiled=True)]
        live = (ids >= 0).astype(f32)[:, None]
        turns = [tables(spot) for spot in spots]
        own_turn = turns[0] if contexts == 2 else tables(places[:, r])
        rows.append(
            dict(
                x=x,
                g=(g.astype(f32) * live).astype(bf16),
                live=live,
                ids=ids,
                cos=own_turn[0],
                sin=own_turn[1],
                cos_k=[t[0] for t in turns],
                sin_k=[t[1] for t in turns],
                q_feat=query_features(ids),
                k_feat=[key_features(k) for k in key_ids],
                flags=visit_flags(ids, jnp.concatenate(key_ids), block, key_block),
            )
        )

    for row in rows:
        row["a"], row["q"], row["kv"] = project_row(
            row["x"], w_qkv, ln_one, qkv_shift, row["cos"], row["sin"], row["q_feat"], heads
        )
        if contexts == 2:
            row["kvs"] = [row["kv"], over_ctx(row["kv"])]
        else:
            row["kvs"] = [lax.all_gather(row["kv"], "ctx", axis=0, tiled=True)]

    def sum_half(partial):
        got = near(partial[half:])
        mine = (partial[:half].astype(f32) + got.astype(f32)).astype(bf16)
        return mine.astype(f32) + far(mine).astype(f32)

    def both_halves(mine):
        return jnp.concatenate([mine, near(mine)], axis=0)

    for row in rows:
        row["o"], row["q"], row["k_aug"], row["v_aug"] = attend_forward(
            row["flags"], row["q"], row["kvs"], row["k_feat"], heads, key_block
        )
        branch = sum_half(mm(row["o"], w_proj, NT).astype(bf16))
        row["h"] = row["x"][:half].astype(f32) + branch + proj_shift
        row["unit"], row["inv"] = norm_stats(row["h"])
        row["c"] = both_halves((row["unit"] * gain_two + bias_two).astype(bf16))

    for row in rows:
        inner = mm(row["c"], w_up) + up_shift
        sg = jax.nn.sigmoid(1.702 * inner)
        row["z"] = (inner * sg).astype(bf16)
        slope = sg + 1.702 * inner * sg * (1.0 - sg)
        row["gu"] = (mm(row["g"], w_down) * slope).astype(bf16)
        row["gc"] = sum_half(mm(row["gu"], w_up, NT).astype(bf16))
        row["feed"] = sum_half(mm(row["z"], w_down, NT).astype(bf16))

    join = lambda key: jnp.concatenate([row[key] for row in rows], axis=0)
    c_all, gu_all, z_all, g_all = join("c"), join("gu"), join("z"), join("g")
    scatter = lambda v: lax.psum_scatter(v, "shard", scatter_dimension=0, tiled=True)
    if contexts == 2:
        finish = lambda v: v.astype(f32) + over_ctx(v).astype(f32)
    else:
        finish = lambda v: lax.psum(v, "ctx").astype(f32)
    grad_up = finish(scatter(mm(c_all, gu_all, TN).astype(bf16)))
    grad_down = finish(scatter(mm(g_all, z_all, TN).astype(bf16)))

    pair_sums = []
    for row in rows:
        g_half = row["g"][:half].astype(f32)
        grad_in, d_gain, d_bias = norm_backward(row["gc"], row["unit"], row["inv"], gain_two)
        row["gh"] = g_half + grad_in
        ga = row["gh"].astype(bf16)
        pair_sums.append(jnp.stack([d_gain, d_bias, jnp.sum(ga.astype(f32), axis=0)]))
        row["ga"] = both_halves(ga)
        go = mm(row["ga"], w_proj).astype(bf16)
        out = attend_backward(
            row["flags"],
            row["q"],
            go,
            row["o"],
            row["k_aug"],
            row["v_aug"],
            row["cos"],
            row["sin"],
            row["cos_k"],
            row["sin_k"],
            heads,
            key_block,
        )
        if contexts == 2:
            dkv = (out[1].astype(f32) + over_ctx(out[2]).astype(f32)).astype(bf16)
        else:
            dkv = lax.psum_scatter(out[1], "ctx", scatter_dimension=0, tiled=True)
        empty = jnp.zeros((row_share, pad), bf16)
        row["gqkv"] = jnp.concatenate([out[0], dkv, empty], axis=1)
        row["ga1"] = sum_half(mm(row["gqkv"], w_qkv, NT).astype(bf16))

    ga_all, o_all, a_all, gqkv_all = join("ga"), join("o"), join("a"), join("gqkv")
    grad_proj = finish(scatter(mm(ga_all, o_all, TN).astype(bf16)))
    pair = sum(pair_sums)
    pair = pair + near(pair)
    d_qb = jnp.sum(gqkv_all[:, : 3 * local].astype(f32), axis=0).reshape(3, heads, owners, -1)
    d_qb = jnp.transpose(d_qb, (2, 0, 1, 3)).reshape(owners, -1)
    d_qb = jnp.pad(d_qb, ((0, 0), (0, part - d_qb.shape[1]))).reshape(-1)
    d_ub = jnp.sum(gu_all.astype(f32), axis=0).reshape(fc1_bias.shape[0], owners, fc1_bias.shape[1])
    d_ub = jnp.transpose(d_ub, (1, 0, 2)).reshape(owners, -1)
    d_ub = jnp.pad(d_ub, ((0, 0), (0, part - d_ub.shape[1]))).reshape(-1)
    d_db = jnp.sum(g_all.astype(f32), axis=0)
    sides = jnp.stack([pair[0], pair[1], pair[2], d_db, d_qb, d_ub], axis=1)
    sides = jnp.pad(sides, ((0, 0), (3 * local, pad - sides.shape[1])))
    grad_qkv = finish(scatter((mm(a_all, gqkv_all, TN) + sides).astype(bf16)))

    ends = []
    outs, ins = [], []
    for row in rows:
        mine = ((row["h"] + row["feed"] + down_shift) * row["live"][:half]).astype(bf16)
        outs.append(mine_first(both_halves(mine)))
        x_half = row["x"][:half].astype(f32)
        unit, inverse = norm_stats(x_half)
        grad_in, d_gain, d_bias = norm_backward(row["ga1"], unit, inverse, gain_one)
        ends.append(jnp.stack([d_gain, d_bias]))
        ins.append(mine_first(both_halves((row["gh"] + grad_in).astype(bf16))))
    end = sum(ends)
    end = end + near(end)
    end = lax.psum(end, ("shard", "ctx"))
    end = lax.dynamic_slice_in_dim(end, lax.axis_index("shard") * part, part, axis=1)
    base = 3 * local
    return (
        jnp.stack(outs),
        jnp.stack(ins),
        end[0],
        end[1],
        grad_qkv[:, :base].reshape(qkv_weight.shape),
        grad_qkv[:qb_size, base + 4].reshape(qkv_bias.shape),
        grad_proj.T,
        grad_qkv[:, base + 2],
        grad_qkv[:, base + 0],
        grad_qkv[:, base + 1],
        grad_up,
        grad_qkv[: fc1_bias.size, base + 5].reshape(fc1_bias.shape),
        grad_down.T,
        grad_qkv[:, base + 3],
    )


def solution(mesh):
    in_specs = (
        P("shard", "ctx", None),
        P("shard", "ctx", None),
        P("shard", None),
        P(None, "shard", "ctx"),
        P("shard"),
        P("shard"),
        P("shard", None, "tp"),
        P(None, "tp", "shard"),
        P("tp", "shard"),
        P("shard"),
        P("shard"),
        P("shard"),
        P("shard", "tp"),
        P("tp", "shard"),
        P("tp", "shard"),
        P("shard"),
    )
    out_specs = (
        P("shard", "ctx", None),
        P("shard", "ctx", None),
        P("shard"),
        P("shard"),
        P("shard", None, "tp"),
        P(None, "tp", "shard"),
        P("tp", "shard"),
        P("shard"),
        P("shard"),
        P("shard"),
        P("shard", "tp"),
        P("tp", "shard"),
        P("tp", "shard"),
        P("shard"),
    )
    return jax.shard_map(
        on_device, mesh=mesh, in_specs=in_specs, out_specs=out_specs, check_vma=False
    )
```

```python
import functools
import math

import jax
import jax.numpy as jnp
from jax import lax
from jax.experimental import pallas as pl
from jax.experimental.pallas import tpu as pltpu
from jax.sharding import PartitionSpec as P

HEAD_DIM = 80
LANES = 128
norm_eps = 1e-06
hide = 1e30
floor_max = -1e29
log2e = math.log2(math.e)
bf16 = jnp.bfloat16
f32 = jnp.float32
NT = (((1,), (1,)), ((), ()))
NN = (((1,), (0,)), ((), ()))
TN = (((0,), (0,)), ((), ()))


def mm(a, b, dims=NN):
    return lax.dot_general(a, b, dims, preferred_element_type=f32)


def tie(value, *others):
    return lax.optimization_barrier((value,) + others)[0]


def first_blocks(steps):
    return lambda i, *_: (jnp.minimum(i, steps // 2 - 1), 0)


def last_blocks(steps):
    return lambda i, *_: (jnp.maximum(i - steps // 2, 0), 0)


def store_halves(first_ref, last_ref, value):
    step, split = pl.program_id(0), pl.num_programs(0) // 2

    @pl.when(step < split)
    def first():
        first_ref[...] = value

    @pl.when(step >= split)
    def last():
        last_ref[...] = value


def lane_index(rows):
    return lax.broadcasted_iota(jnp.int32, (rows, LANES), 1)


def swap_halves(w, lane):
    half = HEAD_DIM // 2
    up = pltpu.roll(w, LANES - half, 1)
    down = pltpu.roll(w, half, 1)
    return jnp.where(lane < half, up, down)


def widen(piece):
    rows = piece.shape[0]
    tail = jnp.zeros((rows, LANES - piece.shape[1]), piece.dtype)
    return jnp.concatenate([piece, tail], axis=1)


def split_three(column):
    high = column.astype(bf16).astype(f32)
    rest = column - high
    mid = rest.astype(bf16).astype(f32)
    return high, mid, rest - mid


def place_three(base, column, lane):
    high, mid, low = split_three(column)
    base = jnp.where(lane == 96, high, base)
    base = jnp.where(lane == 97, mid, base)
    return jnp.where(lane == 98, low, base)


def qkv_kernel(heads, x_ref, w_ref, ln_ref, b_ref, cos_ref, sin_ref, feat_ref, a_ref, q_ref, kv_ref):
    width = heads * HEAD_DIM
    x = x_ref[...].astype(f32)
    rows = x.shape[0]
    center = x - jnp.mean(x, axis=1, keepdims=True)
    inverse = lax.rsqrt(jnp.mean(center * center, axis=1, keepdims=True) + norm_eps)
    a = (center * inverse * ln_ref[0:1, :] + ln_ref[1:2, :]).astype(bf16)
    a_ref[...] = a
    y = mm(a, w_ref[...]) + b_ref[0:1, :]
    cos, sin = cos_ref[...], sin_ref[...]
    lane = lane_index(rows)
    kv = []
    for h in range(heads):
        w = widen(y[:, h * HEAD_DIM : (h + 1) * HEAD_DIM])
        q = (w * cos + swap_halves(w, lane) * sin) * (HEAD_DIM**-0.5 * log2e)
        q_ref[h] = jnp.where(lane < HEAD_DIM, q.astype(bf16), feat_ref[...])
    for h in range(heads):
        begin = width + h * HEAD_DIM
        w = widen(y[:, begin : begin + HEAD_DIM])
        kv.append((w * cos + swap_halves(w, lane) * sin)[:, :HEAD_DIM].astype(bf16))
    kv.append(y[:, 2 * width : 3 * width].astype(bf16))
    kv_ref[...] = jnp.concatenate(kv, axis=1)


def project_row(x, w, ln, bias, cos, sin, feat, heads):
    rows, width = x.shape
    block = min(256, rows)
    wide = w.shape[1]
    local = heads * HEAD_DIM
    by_rows = lambda n: pl.BlockSpec((block, n), lambda i: (i, 0))
    whole = lambda a: pl.BlockSpec(a.shape, lambda i: (0,) * a.ndim)
    return pl.pallas_call(
        functools.partial(qkv_kernel, heads),
        grid=(rows // block,),
        in_specs=[
            by_rows(width),
            whole(w),
            whole(ln),
            whole(bias),
            by_rows(LANES),
            by_rows(LANES),
            by_rows(LANES),
        ],
        out_specs=[
            by_rows(width),
            pl.BlockSpec((heads, block, LANES), lambda i: (0, i, 0)),
            by_rows(2 * local),
        ],
        out_shape=[
            jax.ShapeDtypeStruct((rows, width), bf16),
            jax.ShapeDtypeStruct((heads, rows, LANES), bf16),
            jax.ShapeDtypeStruct((rows, 2 * local), bf16),
        ],
        cost_estimate=pl.CostEstimate(
            flops=2 * rows * width * wide, bytes_accessed=rows * width * 4 + width * wide * 2, transcendentals=0
        ),
        name="project_row",
    )(x, w, ln, bias, cos, sin, feat)


def forward_kernel(heads, segments, block, flag_ref, q_ref, w_ref, *refs):
    kv_refs = refs[:segments]
    feat_refs = refs[segments : 2 * segments]
    o_ref, q_out, k_aug, v_aug, p_first, p_last, m_scr, acc_scr = refs[2 * segments :]
    width = heads * HEAD_DIM
    step = pl.program_id(0)
    keys = k_aug.shape[1]
    count = keys // block
    rows = q_ref.shape[1]

    @pl.when(step == 0)
    def build():
        offset = 0
        for s in range(segments):
            length = kv_refs[s].shape[0]
            piece = min(length, 256)
            for t in range(length // piece):
                at = pl.ds(t * piece, piece)
                to = pl.ds(offset + t * piece, piece)
                kv = kv_refs[s][at, :]
                feat = feat_refs[s][at, :]
                lane = lane_index(piece)
                tail = jnp.where(lane == HEAD_DIM, 1.0, jnp.where((lane >= 96) & (lane < 99), -1.0, 0.0)).astype(bf16)
                for h in range(heads):
                    k = kv[:, h * HEAD_DIM : (h + 1) * HEAD_DIM]
                    v = kv[:, width + h * HEAD_DIM : width + (h + 1) * HEAD_DIM]
                    k_aug[h, to, :] = jnp.concatenate([k, feat[:, HEAD_DIM:]], axis=1)
                    v_aug[h, to, :] = jnp.concatenate([v, tail[:, HEAD_DIM:]], axis=1)
            offset += length

    m_scr[...] = jnp.full(m_scr.shape, floor_max, f32)
    acc_scr[...] = jnp.zeros(acc_scr.shape, f32)

    def visit(j, carry):
        @pl.when(flag_ref[step * count + j] > 0)
        def go():
            at = pl.ds(pl.multiple_of(j * block, block), block)
            for h in range(heads):
                s = mm(q_ref[h], k_aug[h, at, :], NT)
                old = m_scr[h]
                new = jnp.maximum(old, jnp.max(s, axis=1, keepdims=True))
                p = jnp.exp2(s - new[:, 0:1])
                m_scr[h] = new
                acc_scr[h] = acc_scr[h] * jnp.exp2(old - new) + mm(p.astype(bf16), v_aug[h, at, :])

        return carry

    lax.fori_loop(0, count, visit, 0)
    lane = lane_index(rows)
    outs = []
    for h in range(heads):
        acc = acc_scr[h]
        total = acc[:, HEAD_DIM : HEAD_DIM + 1]
        alive = total > 0.0
        safe = jnp.where(alive, total, 1.0)
        outs.append((acc / safe)[:, :HEAD_DIM].astype(bf16))
        level = jnp.where(alive, m_scr[h][:, 0:1] + jnp.log2(safe), 0.0)
        q_out[h] = place_three(q_ref[h].astype(f32), level, lane).astype(bf16)
    o = jnp.concatenate(outs, axis=1)
    o_ref[...] = o
    store_halves(p_first, p_last, mm(o, w_ref[...], NT).astype(bf16))


def attend_forward(flags, q_aug, w, kvs, feats, heads, block):
    rows = q_aug.shape[1]
    tall = min(256, rows // 2)
    steps = rows // tall
    width = w.shape[0]
    keys = sum(kv.shape[0] for kv in kvs)
    segments = len(kvs)
    whole = lambda a: pl.BlockSpec(a.shape, lambda i, f: (0,) * a.ndim)
    q_spec = pl.BlockSpec((heads, tall, LANES), lambda i, f: (0, i, 0))
    k_spec = pl.BlockSpec((heads, keys, LANES), lambda i, f: (0, 0, 0))
    local = heads * HEAD_DIM
    return pl.pallas_call(
        functools.partial(forward_kernel, heads, segments, block),
        grid_spec=pltpu.PrefetchScalarGridSpec(
            num_scalar_prefetch=1,
            grid=(rows // tall,),
            in_specs=[q_spec, whole(w)] + [whole(kv) for kv in kvs] + [whole(f) for f in feats],
            out_specs=[
                pl.BlockSpec((tall, local), lambda i, f: (i, 0)),
                q_spec,
                k_spec,
                k_spec,
                pl.BlockSpec((tall, width), first_blocks(steps)),
                pl.BlockSpec((tall, width), last_blocks(steps)),
            ],
            scratch_shapes=[
                pltpu.VMEM((heads, tall, LANES), f32),
                pltpu.VMEM((heads, tall, LANES), f32),
            ],
        ),
        out_shape=[
            jax.ShapeDtypeStruct((rows, local), bf16),
            jax.ShapeDtypeStruct((heads, rows, LANES), bf16),
            jax.ShapeDtypeStruct((heads, keys, LANES), bf16),
            jax.ShapeDtypeStruct((heads, keys, LANES), bf16),
            jax.ShapeDtypeStruct((rows // 2, width), bf16),
            jax.ShapeDtypeStruct((rows // 2, width), bf16),
        ],
        cost_estimate=pl.CostEstimate(
            flops=2 * rows * keys * heads * LANES, bytes_accessed=8 * keys * local, transcendentals=rows * keys * heads // 2
        ),
        name="attend_forward",
    )(flags, q_aug, w, *kvs, *feats)


def backward_kernel(
    heads, segments, block, flag_ref, q_ref, ga_first, ga_last, w_ref, o_ref, k_aug, v_aug, cosq_ref, sinq_ref, *refs
):
    cosk_refs = refs[:segments]
    sink_refs = refs[segments : 2 * segments]
    dq_ref = refs[2 * segments]
    dkv_refs = refs[2 * segments + 1 : 3 * segments + 1]
    k_turn, dk_acc, dv_acc, dq_acc, go_scr = refs[3 * segments + 1 :]
    step = pl.program_id(0)
    keys = k_aug.shape[1]
    count = keys // block
    rows = q_ref.shape[1]
    scale = HEAD_DIM**-0.5

    @pl.when(step == 0)
    def build():
        dk_acc[...] = jnp.zeros(dk_acc.shape, f32)
        dv_acc[...] = jnp.zeros(dv_acc.shape, f32)
        for h in range(heads):
            for t in range(count):
                at = pl.ds(t * block, block)
                k_turn[h, :, at] = k_aug[h, at, :].T

    lane = lane_index(rows)
    ga = jnp.where(step < pl.num_programs(0) // 2, ga_first[...], ga_last[...])
    go_all = mm(ga, w_ref[...]).astype(bf16).astype(f32)
    for h in range(heads):
        cut = slice(h * HEAD_DIM, (h + 1) * HEAD_DIM)
        go = go_all[:, cut]
        delta = jnp.sum(go * o_ref[:, cut].astype(f32), axis=1, keepdims=True)
        go_scr[h] = place_three(widen(go), delta, lane).astype(bf16)
    dq_acc[...] = jnp.zeros(dq_acc.shape, f32)

    def visit(j, carry):
        @pl.when(flag_ref[step * count + j] > 0)
        def run():
            at = pl.ds(pl.multiple_of(j * block, block), block)
            for h in range(heads):
                q, go = q_ref[h], go_scr[h]
                p = jnp.exp2(mm(k_aug[h, at, :], q, NT))
                ds = (p * mm(v_aug[h, at, :], go, NT)).astype(bf16)
                dv_acc[h, at, :] += mm(p.astype(bf16), go)
                dk_acc[h, at, :] += mm(ds, q)
                dq_acc[h] += mm(k_turn[h, :, at], ds)

        return carry

    lax.fori_loop(0, count, visit, 0)

    def turn_back(w, cos, sin, index):
        return w * cos - swap_halves(w, index) * sin

    outs = []
    for h in range(heads):
        w = dq_acc[h].T
        back = turn_back(w, cosq_ref[...], sinq_ref[...], lane) * scale
        outs.append(back[:, :HEAD_DIM].astype(bf16))
    dq_ref[...] = jnp.concatenate(outs, axis=1)

    @pl.when(step == pl.num_programs(0) - 1)
    def finish():
        offset = 0
        for s in range(segments):
            length = dkv_refs[s].shape[0]
            piece = min(length, 256)
            index = lane_index(piece)
            for t in range(length // piece):
                at = pl.ds(t * piece, piece)
                of = pl.ds(offset + t * piece, piece)
                parts = []
                for h in range(heads):
                    w = dk_acc[h, of, :]
                    back = turn_back(w, cosk_refs[s][at, :], sink_refs[s][at, :], index) * (1.0 / log2e)
                    parts.append(back[:, :HEAD_DIM].astype(bf16))
                for h in range(heads):
                    parts.append(dv_acc[h, of, :][:, :HEAD_DIM].astype(bf16))
                dkv_refs[s][at, :] = jnp.concatenate(parts, axis=1)
            offset += length


def attend_backward(flags, q_aug, ga, w, o, k_aug, v_aug, cos_q, sin_q, cos_k, sin_k, heads, block):
    rows = q_aug.shape[1]
    tall = min(256, rows // 2)
    steps = rows // tall
    width = w.shape[0]
    keys = k_aug.shape[1]
    segments = len(cos_k)
    local = heads * HEAD_DIM
    whole = lambda a: pl.BlockSpec(a.shape, lambda i, f: (0,) * a.ndim)
    by_rows = lambda n: pl.BlockSpec((tall, n), lambda i, f: (i, 0))
    q_spec = pl.BlockSpec((heads, tall, LANES), lambda i, f: (0, i, 0))
    return pl.pallas_call(
        functools.partial(backward_kernel, heads, segments, block),
        grid_spec=pltpu.PrefetchScalarGridSpec(
            num_scalar_prefetch=1,
            grid=(rows // tall,),
            in_specs=[
                q_spec,
                pl.BlockSpec((tall, width), first_blocks(steps)),
                pl.BlockSpec((tall, width), last_blocks(steps)),
                whole(w),
                by_rows(local),
                whole(k_aug),
                whole(v_aug),
                by_rows(LANES),
                by_rows(LANES),
            ]
            + [whole(t) for t in cos_k]
            + [whole(t) for t in sin_k],
            out_specs=[by_rows(local)]
            + [pl.BlockSpec((t.shape[0], 2 * local), lambda i, f: (0, 0)) for t in cos_k],
            scratch_shapes=[
                pltpu.VMEM((heads, LANES, keys), bf16),
                pltpu.VMEM((heads, keys, LANES), f32),
                pltpu.VMEM((heads, keys, LANES), f32),
                pltpu.VMEM((heads, LANES, tall), f32),
                pltpu.VMEM((heads, tall, LANES), bf16),
            ],
        ),
        out_shape=[jax.ShapeDtypeStruct((rows, local), bf16)]
        + [jax.ShapeDtypeStruct((t.shape[0], 2 * local), bf16) for t in cos_k],
        cost_estimate=pl.CostEstimate(
            flops=5 * rows * keys * heads * LANES, bytes_accessed=16 * keys * local, transcendentals=rows * keys * heads // 2
        ),
        name="attend_backward",
    )(flags, q_aug, *ga, w, o, k_aug, v_aug, cos_q, sin_q, *cos_k, *sin_k)


def feed_kernel(chunk, c_first, c_last, g_ref, up_ref, down_ref, shift_ref, z_ref, gu_ref, gc_first, gc_last, feed_first, feed_last, sum_ref):
    step = pl.program_id(0)
    c = jnp.where(step < pl.num_programs(0) // 2, c_first[...], c_last[...])
    g = g_ref[...]
    gc, feed, sums = 0.0, 0.0, []
    for begin in range(0, up_ref.shape[1], chunk):
        cut = slice(begin, begin + chunk)
        u = mm(c, up_ref[:, cut]) + shift_ref[0:1, cut]
        sg = 0.5 + 0.5 * jnp.tanh(0.851 * u)
        z = (u * sg).astype(bf16)
        gu = (mm(g, down_ref[:, cut]) * (sg + 1.702 * u * sg * (1.0 - sg))).astype(bf16)
        z_ref[:, cut] = z
        gu_ref[:, cut] = gu
        gc = gc + mm(gu, up_ref[:, cut], NT)
        feed = feed + mm(z, down_ref[:, cut], NT)
        sums.append(jnp.sum(gu.astype(f32), axis=0, keepdims=True))
    store_halves(gc_first, gc_last, gc.astype(bf16))
    store_halves(feed_first, feed_last, feed.astype(bf16))

    @pl.when(step == 0)
    def clear():
        sum_ref[...] = jnp.zeros(sum_ref.shape, f32)

    sum_ref[0:1, :] += jnp.concatenate(sums, axis=1)
    sum_ref[1:2, : g.shape[1]] += jnp.sum(g.astype(f32), axis=0, keepdims=True)


def feed_forward(c, g, w_up, w_down, shift):
    rows, width = g.shape
    hidden = w_up.shape[1]
    tall = min(256, rows // 2)
    steps = rows // tall
    chunk = 256 if hidden % 256 == 0 else hidden
    by_rows = lambda n: pl.BlockSpec((tall, n), lambda i: (i, 0))
    whole = lambda a: pl.BlockSpec(a.shape, lambda i: (0,) * a.ndim)
    first = pl.BlockSpec((tall, width), first_blocks(steps))
    last = pl.BlockSpec((tall, width), last_blocks(steps))
    part = jax.ShapeDtypeStruct((rows // 2, width), bf16)
    longest = max(width, hidden)
    return pl.pallas_call(
        functools.partial(feed_kernel, chunk),
        grid=(steps,),
        in_specs=[first, last, by_rows(width), whole(w_up), whole(w_down), whole(shift)],
        out_specs=[by_rows(hidden), by_rows(hidden), first, last, first, last, pl.BlockSpec((8, longest), lambda i: (0, 0))],
        out_shape=[
            jax.ShapeDtypeStruct((rows, hidden), bf16),
            jax.ShapeDtypeStruct((rows, hidden), bf16),
            part,
            part,
            part,
            part,
            jax.ShapeDtypeStruct((8, longest), f32),
        ],
        cost_estimate=pl.CostEstimate(
            flops=8 * rows * width * hidden, bytes_accessed=4 * width * hidden + 12 * rows * width, transcendentals=rows * hidden
        ),
        name="feed_forward",
    )(*c, g, w_up, w_down, shift)


def back_kernel(pieces, x_ref, wq_ref, wkv_ref, gq_ref, *refs):
    kv_refs = refs[:pieces]
    p_first, p_last, dkv_ref, sum_ref = refs[pieces:]
    gq = gq_ref[...]
    if pieces == 1:
        dkv = kv_refs[0][...]
    else:
        dkv = (kv_refs[0][...].astype(f32) + kv_refs[1][...].astype(f32)).astype(bf16)
    dkv_ref[...] = dkv
    e = mm(gq, wq_ref[...], NT) + mm(dkv, wkv_ref[...], NT)
    store_halves(p_first, p_last, e.astype(bf16))
    x = x_ref[...].astype(f32)
    center = x - jnp.mean(x, axis=1, keepdims=True)
    unit = center * lax.rsqrt(jnp.mean(center * center, axis=1, keepdims=True) + norm_eps)

    @pl.when(pl.program_id(0) == 0)
    def clear():
        sum_ref[...] = jnp.zeros(sum_ref.shape, f32)

    local = gq.shape[1]
    sum_ref[0:1, :] += jnp.sum(e * unit, axis=0, keepdims=True)
    sum_ref[1:2, :] += jnp.sum(e, axis=0, keepdims=True)
    sum_ref[2:3, :local] += jnp.sum(gq.astype(f32), axis=0, keepdims=True)
    sum_ref[3:4, : 2 * local] += jnp.sum(dkv.astype(f32), axis=0, keepdims=True)


def project_back(x, w_q, w_kv, gq, dkvs):
    rows, width = x.shape
    local = gq.shape[1]
    tall = min(256, rows // 2)
    steps = rows // tall
    by_rows = lambda n: pl.BlockSpec((tall, n), lambda i: (i, 0))
    whole = lambda a: pl.BlockSpec(a.shape, lambda i: (0,) * a.ndim)
    part = jax.ShapeDtypeStruct((rows // 2, width), bf16)
    return pl.pallas_call(
        functools.partial(back_kernel, len(dkvs)),
        grid=(steps,),
        in_specs=[by_rows(width), whole(w_q), whole(w_kv), by_rows(local)] + [by_rows(2 * local)] * len(dkvs),
        out_specs=[
            pl.BlockSpec((tall, width), first_blocks(steps)),
            pl.BlockSpec((tall, width), last_blocks(steps)),
            by_rows(2 * local),
            pl.BlockSpec((8, width), lambda i: (0, 0)),
        ],
        out_shape=[part, part, jax.ShapeDtypeStruct((rows, 2 * local), bf16), jax.ShapeDtypeStruct((8, width), f32)],
        cost_estimate=pl.CostEstimate(
            flops=6 * rows * width * local, bytes_accessed=6 * width * local + 6 * rows * width, transcendentals=rows
        ),
        name="project_back",
    )(x, w_q, w_kv, gq, *dkvs)


def norm_stats(rows_in):
    center = rows_in - jnp.mean(rows_in, axis=1, keepdims=True)
    inverse = lax.rsqrt(jnp.mean(center * center, axis=1, keepdims=True) + norm_eps)
    return center * inverse, inverse


def norm_backward(grad_rows, unit_rows, inverse, gain):
    scaled = grad_rows * gain
    grad_in = inverse * (
        scaled
        - jnp.mean(scaled, axis=1, keepdims=True)
        - unit_rows * jnp.mean(scaled * unit_rows, axis=1, keepdims=True)
    )
    return (grad_in, jnp.sum(grad_rows * unit_rows, axis=0), jnp.sum(grad_rows, axis=0))


def tables(grid_pos):
    lane = jnp.arange(LANES)
    quarter = HEAD_DIM // 4
    frequency = jnp.power(10000.0, -4.0 * (lane % quarter).astype(f32) / HEAD_DIM)
    place = jnp.where((lane // quarter) % 2 == 0, grid_pos[0][:, None], grid_pos[1][:, None])
    angle = jnp.where(lane < HEAD_DIM, place.astype(f32) * frequency, 0.0)
    return jnp.cos(angle), jnp.where(lane < HEAD_DIM // 2, -1.0, 1.0) * jnp.sin(angle)


def query_features(ids):
    lane = jnp.arange(LANES)
    return (lane == HEAD_DIM + 1 + ids[:, None]).astype(bf16)


def key_features(ids):
    lane = jnp.arange(LANES)
    slot = lane - HEAD_DIM
    same = (slot >= 1) & (slot == ids[:, None] + 1)
    wall = jnp.where((slot >= 0) & (slot < 16) & ~same, -hide, 0.0)
    return jnp.where((lane >= 96) & (lane < 99), -1.0, wall).astype(bf16)


def visit_flags(query_ids, key_ids, tall, block):
    q = query_ids.reshape(-1, tall)
    k = key_ids.reshape(-1, block)
    q_top, k_top = jnp.max(q, axis=1), jnp.max(k, axis=1)
    q_low = jnp.min(jnp.where(q >= 0, q, 1 << 20), axis=1)
    k_low = jnp.min(jnp.where(k >= 0, k, 1 << 20), axis=1)
    meet = (q_low[:, None] <= k_top[None, :]) & (k_low[None, :] <= q_top[:, None])
    return meet.astype(jnp.int32).reshape(-1)


def on_device(
    patches,
    cotangent,
    picture_ids,
    positions,
    ln1_gain,
    ln1_bias,
    qkv_weight,
    qkv_bias,
    proj_weight,
    proj_bias,
    ln2_gain,
    ln2_bias,
    fc1_weight,
    fc1_bias,
    fc2_weight,
    fc2_bias,
):
    row_count, row_share, width = patches.shape
    owners = lax.axis_size("shard")
    contexts = lax.axis_size("ctx")
    ways = lax.axis_size("tp")
    part = qkv_weight.shape[0]
    local = qkv_weight.shape[2]
    heads = local // HEAD_DIM
    half = row_share // 2
    side = lax.axis_index("tp") % 2
    context = lax.axis_index("ctx")
    pairs_near = [(i, i ^ 1) for i in range(ways)]
    pairs_far = [(i, i ^ 2) for i in range(ways)]
    pad = -3 * local % 256
    wide = 3 * local + pad

    def near(v):
        return lax.ppermute(v, "tp", pairs_near)

    def far(v):
        return lax.ppermute(v, "tp", pairs_far)

    def over_ctx(v):
        return lax.ppermute(v, "ctx", [(0, 1), (1, 0)])

    def mine_first(v, axis=0):
        return jnp.where(side == 0, v, jnp.roll(v, half, axis=axis))

    def column(v):
        flat = v.reshape(-1)
        return jnp.pad(flat, (0, part - flat.shape[0]))

    vectors = [ln1_gain, ln1_bias, ln2_gain, ln2_bias, proj_bias, fc2_bias, qkv_bias, fc1_bias]
    tail = jnp.stack([column(v) for v in vectors], axis=1)
    tail = jnp.pad(tail, ((0, 0), (0, pad - len(vectors))))
    qkv_piece = jnp.concatenate([qkv_weight.reshape(part, 3 * local), tail], axis=1).astype(bf16)
    gather = lambda v: lax.all_gather(v, "shard", axis=0, tiled=True)
    up_piece = fc1_weight.astype(bf16)
    down_piece = fc2_weight.T.astype(bf16)
    proj_piece = proj_weight.T.astype(bf16)
    place = lax.axis_index("shard")
    context_first = context == 0

    slots = jnp.zeros((3 * owners - 2,) + qkv_piece.shape, bf16)
    slots = lax.dynamic_update_index_in_dim(slots, qkv_piece, place + owners - 1, 0)
    up_line = [(i, i + 1) for i in range(owners - 1)]
    down_line = [(i + 1, i) for i in range(owners - 1)]
    rising = falling = qkv_piece
    for step in range(1, owners):
        rising = lax.ppermute(rising, "shard", up_line)
        falling = lax.ppermute(falling, "shard", down_line)
        slots = lax.dynamic_update_index_in_dim(slots, rising, place - step + owners - 1, 0)
        slots = lax.dynamic_update_index_in_dim(slots, falling, place + step + owners - 1, 0)
    w_qkv = slots[owners - 1 : 2 * owners - 1].reshape(owners * part, wide)

    proj_piece, down_piece, up_piece = lax.optimization_barrier((proj_piece, down_piece, up_piece, w_qkv))[:3]
    if contexts == 2:
        down_cut = down_piece.reshape(2, part // 2, -1)
        down_near = gather(lax.dynamic_index_in_dim(down_cut, context, 0, keepdims=False))
        down_near = down_near.reshape(owners, part // 2, -1)
        down_far = over_ctx(down_near)
    else:
        w_down = gather(down_piece)
    w_up = gather(up_piece)
    w_proj = jnp.zeros((owners,) + proj_piece.shape, bf16)
    w_proj = lax.dynamic_update_index_in_dim(w_proj, proj_piece, place, 0)
    for step in range(1, owners):
        got = lax.ppermute(proj_piece, "shard", [(i, (i + step) % owners) for i in range(owners)])
        w_proj = lax.dynamic_update_index_in_dim(w_proj, got, (place - step) % owners, 0)
    w_proj = w_proj.reshape(owners * part, local)
    w_q, w_kv = w_qkv[:, :local], w_qkv[:, local : 3 * local]
    packed = w_qkv[:, 3 * local : 3 * local + len(vectors)].T.astype(f32)
    gain_one, bias_one, gain_two, bias_two, proj_shift, down_shift = [packed[i] for i in range(6)]
    qb_size = qkv_bias.size
    qkv_shift = packed[6].reshape(owners, part)[:, :qb_size].reshape((owners,) + qkv_bias.shape)
    qkv_shift = jnp.transpose(qkv_shift, (1, 2, 0, 3)).reshape(-1)
    qkv_shift = jnp.pad(qkv_shift, (0, pad)).reshape(1, wide)
    up_shift = packed[7].reshape(owners, part)[:, : fc1_bias.size].reshape((owners,) + fc1_bias.shape)
    up_shift = jnp.transpose(up_shift, (1, 0, 2)).reshape(1, -1)
    ln_one = tie(packed[0:2], up_piece, down_piece)

    ids_by_ctx = mine_first(picture_ids.reshape(row_count, contexts, row_share), axis=2)
    places = mine_first(positions, axis=2)
    block = min(256, half)
    key_block = 256
    rows = []
    for r in range(row_count):
        x = mine_first(patches[r])
        g = mine_first(cotangent[r])
        ids = lax.dynamic_index_in_dim(ids_by_ctx[r], context, 0, keepdims=False)
        if contexts == 2:
            other = lax.dynamic_index_in_dim(ids_by_ctx[r], 1 - context, 0, keepdims=False)
            key_ids = [ids, other]
            spots = [places[:, r], over_ctx(places[:, r])]
        else:
            key_ids = [ids_by_ctx[r].reshape(-1)]
            spots = [lax.all_gather(places[:, r], "ctx", axis=1, tiled=True)]
        live = (ids >= 0).astype(f32)[:, None]
        turns = [tables(spot) for spot in spots]
        own_turn = turns[0] if contexts == 2 else tables(places[:, r])
        rows.append(
            dict(
                x=x,
                g=(g.astype(f32) * live).astype(bf16),
                live=live,
                ids=ids,
                cos=own_turn[0],
                sin=own_turn[1],
                cos_k=[t[0] for t in turns],
                sin_k=[t[1] for t in turns],
                q_feat=query_features(ids),
                k_feat=[key_features(k) for k in key_ids],
                flags=visit_flags(ids, jnp.concatenate(key_ids), block, key_block),
            )
        )

    for row in rows:
        row["a"], row["q"], row["kv"] = project_row(
            row["x"], w_qkv, ln_one, qkv_shift, row["cos"], row["sin"], row["q_feat"], heads
        )
        if contexts == 2:
            row["kvs"] = [row["kv"], over_ctx(row["kv"])]
        else:
            row["kvs"] = [lax.all_gather(row["kv"], "ctx", axis=0, tiled=True)]

    def sum_near(first, last):
        return (first.astype(f32) + near(last).astype(f32)).astype(bf16)

    def both_halves(mine):
        return jnp.concatenate([mine, near(mine)], axis=0)

    def norm_two(row, shift):
        row["h"] = row["x"][:half].astype(f32) + (row["branch"].astype(f32) + row["branch_far"].astype(f32)) + shift
        row["unit"], row["inv"] = norm_stats(row["h"])
        mine = (row["unit"] * gain_two + bias_two).astype(bf16)
        row["c"] = (mine, near(mine))

    hold = lax.optimization_barrier
    before = rows[-1]["kv"]
    for index, row in enumerate(rows):
        row["o"], row["q"], row["k_aug"], row["v_aug"], first, last = attend_forward(
            tie(row["flags"], before), row["q"], w_proj, row["kvs"], row["k_feat"], heads, key_block
        )
        if index:
            prior = rows[index - 1]
            first, last, prior["branch_far"] = hold((first, last, prior["branch_far"]))
        if index + 1 < row_count:
            follow = rows[index + 1]
            first, last, follow["kvs"] = hold((first, last, follow["kvs"]))
        elif contexts == 2:
            first, last, down_far = hold((first, last, down_far))
        before = row["branch"] = sum_near(first, last)
        row["branch_far"] = far(before)
    if contexts == 2:
        low = jnp.where(context_first, down_near, down_far)
        high = jnp.where(context_first, down_far, down_near)
        w_down = jnp.concatenate([low, high], axis=1).reshape(owners * part, -1)

    norm_two(rows[0], tie(proj_shift, before))
    for index, row in enumerate(rows):
        shift = tie(up_shift, before)
        row["z"], row["gu"], gc_first, gc_last, feed_first, feed_last, row["feed_sums"] = feed_forward(
            row["c"], row["g"], w_up, w_down, shift
        )
        other, key = (rows[-1], "branch_far") if index == 0 else (rows[index - 1], "gc_far")
        gc_first, gc_last, other[key] = hold((gc_first, gc_last, other[key]))
        before = row["gc"] = sum_near(gc_first, gc_last)
        row["gc_far"] = far(before)
        row["feed"] = (feed_first, feed_last)
        if index + 1 < row_count:
            norm_two(rows[index + 1], proj_shift)
    for row in rows:
        row["feed"] = sum_near(*row["feed"])

    join = lambda key: jnp.concatenate([row[key] for row in rows], axis=0)
    join_two = lambda key: jnp.concatenate([piece for row in rows for piece in row[key]], axis=0)
    scatter = lambda v: lax.psum_scatter(v, "shard", scatter_dimension=0, tiled=True)
    if contexts == 2:
        finish = lambda v: v.astype(f32) + over_ctx(v).astype(f32)
    else:
        finish = lambda v: lax.psum(v, "ctx").astype(f32)
    last_row = rows[-1]
    last_row["gu"], last_row["z"] = hold((last_row["gu"], last_row["z"], before))[:2]
    grad_up = mm(join_two("c"), join("gu"), TN).astype(bf16)
    grad_down = mm(join("g"), join("z"), TN).astype(bf16)
    grad_up, grad_down, last_row["gc_far"] = hold((grad_up, grad_down, last_row["gc_far"]))
    before = (grad_up, grad_down)
    y_free = last_row["gc_far"]
    grad_up = finish(scatter(grad_up))
    grad_down = finish(scatter(grad_down))

    pair = 0.0
    for row in rows:
        gc = row["gc"].astype(f32) + row["gc_far"].astype(f32)
        grad_in, d_gain, d_bias = norm_backward(gc, row["unit"], row["inv"], gain_two)
        row["gh"] = row["g"][:half].astype(f32) + grad_in
        ga = row["gh"].astype(bf16)
        pair = pair + jnp.stack([d_gain, d_bias, jnp.sum(ga.astype(f32), axis=0)])
        row["ga"] = (ga, near(ga))
    for index, row in enumerate(rows):
        feed_far = far(tie(row["feed"], y_free))
        out = attend_backward(
            tie(row["flags"], *before),
            row["q"],
            row["ga"],
            w_proj,
            row["o"],
            row["k_aug"],
            row["v_aug"],
            row["cos"],
            row["sin"],
            row["cos_k"],
            row["sin_k"],
            heads,
            key_block,
        )
        if index:
            prior = rows[index - 1]
            *out, feed_far, prior["dkvs"] = hold((*out, feed_far, prior["dkvs"]))
        else:
            *out, feed_far = hold((*out, feed_far))
        y_free = feed_far
        before = (out[0],)
        row["gq"] = out[0]
        row["feed"] = row["feed"].astype(f32) + feed_far.astype(f32)
        if contexts == 2:
            row["dkvs"] = [out[1], over_ctx(out[2])]
        else:
            row["dkvs"] = [lax.psum_scatter(out[1], "ctx", scatter_dimension=0, tiled=True)]

    outs = []
    sums = 0.0
    for index, row in enumerate(rows):
        first, last, row["dkv"], back_sums = project_back(row["x"], w_q, w_kv, tie(row["gq"], *before), row["dkvs"])
        sums = sums + back_sums
        mine = sum_near(first, last)
        row["ga1"] = mine.astype(f32) + far(mine).astype(f32)
        before = (mine,)
        if index == 0:
            grad_q = mm(join("a"), join("gq"), TN).astype(bf16)
            grad_proj = mm(join_two("ga"), join("o"), TN).astype(bf16)
            before = before + (grad_q, grad_proj)
            for done in rows:
                ready = ((done["h"] + done["feed"] + down_shift) * done["live"][:half]).astype(bf16)
                outs.append(mine_first(both_halves(ready)))
    grad_kv = finish(scatter(mm(join("a"), join("dkv"), TN).astype(bf16)))
    grad_q = finish(scatter(grad_q))
    grad_proj = finish(scatter(grad_proj))

    def sum_over(v, axis):
        size, step = lax.axis_size(axis), 1
        while step < size:
            v = v + lax.ppermute(v, axis, [(i, i ^ step) for i in range(size)])
            step *= 2
        return v

    def owned(v):
        v = v.reshape(owners, -1)
        return jnp.pad(v, ((0, 0), (0, part - v.shape[1]))).reshape(-1)

    feed_sums = sum(row["feed_sums"] for row in rows)
    d_qb = jnp.concatenate([sums[2, :local], sums[3, : 2 * local]]).reshape(3, heads, owners, -1)
    d_qb = owned(jnp.transpose(d_qb, (2, 0, 1, 3)))
    d_ub = feed_sums[0, : fc1_bias.size * owners].reshape(fc1_bias.shape[0], owners, fc1_bias.shape[1])
    d_ub = owned(jnp.transpose(d_ub, (1, 0, 2)))
    vector = jnp.concatenate(
        [pair + near(pair), feed_sums[1:2, :width], d_qb[None], d_ub[None], sum_over(sums[0:2], "tp")], axis=0
    )
    vector = sum_over(sum_over(vector, "ctx"), "shard")
    vector = lax.dynamic_slice_in_dim(vector, place * part, part, axis=1)

    ins = []
    for row in rows:
        x_half = row["x"][:half].astype(f32)
        unit, inverse = norm_stats(x_half)
        grad_in = norm_backward(row["ga1"], unit, inverse, gain_one)[0]
        ins.append(mine_first(both_halves((row["gh"] + grad_in).astype(bf16))))
    return (
        jnp.stack(outs),
        jnp.stack(ins),
        vector[6],
        vector[7],
        jnp.concatenate([grad_q, grad_kv], axis=1).reshape(qkv_weight.shape),
        vector[4, :qb_size].reshape(qkv_bias.shape),
        grad_proj.T,
        vector[2],
        vector[0],
        vector[1],
        grad_up,
        vector[5, : fc1_bias.size].reshape(fc1_bias.shape),
        grad_down.T,
        vector[3],
    )


def solution(mesh):
    in_specs = (
        P("shard", "ctx", None),
        P("shard", "ctx", None),
        P("shard", None),
        P(None, "shard", "ctx"),
        P("shard"),
        P("shard"),
        P("shard", None, "tp"),
        P(None, "tp", "shard"),
        P("tp", "shard"),
        P("shard"),
        P("shard"),
        P("shard"),
        P("shard", "tp"),
        P("tp", "shard"),
        P("tp", "shard"),
        P("shard"),
    )
    out_specs = (
        P("shard", "ctx", None),
        P("shard", "ctx", None),
        P("shard"),
        P("shard"),
        P("shard", None, "tp"),
        P(None, "tp", "shard"),
        P("tp", "shard"),
        P("shard"),
        P("shard"),
        P("shard"),
        P("shard", "tp"),
        P("tp", "shard"),
        P("tp", "shard"),
        P("shard"),
    )
    return jax.shard_map(
        on_device, mesh=mesh, in_specs=in_specs, out_specs=out_specs, check_vma=False
    )
```

```python
import functools
import math

import jax
import jax.numpy as jnp
from jax import lax
from jax.experimental import pallas as pl
from jax.experimental.pallas import tpu as pltpu
from jax.sharding import PartitionSpec as P

HEAD_DIM = 80
LANES = 128
norm_eps = 1e-06
hide = 1e30
floor_max = -1e29
log2e = math.log2(math.e)
bf16 = jnp.bfloat16
f32 = jnp.float32
NT = (((1,), (1,)), ((), ()))
NN = (((1,), (0,)), ((), ()))
TN = (((0,), (0,)), ((), ()))


def mm(a, b, dims=NN):
    return lax.dot_general(a, b, dims, preferred_element_type=f32)


def tie(value, *others):
    return lax.optimization_barrier((value,) + others)[0]


def first_blocks(steps):
    return lambda i, *_: (jnp.minimum(i, steps // 2 - 1), 0)


def last_blocks(steps):
    return lambda i, *_: (jnp.maximum(i - steps // 2, 0), 0)


def store_halves(first_ref, last_ref, value):
    step, split = pl.program_id(0), pl.num_programs(0) // 2

    @pl.when(step < split)
    def first():
        first_ref[...] = value

    @pl.when(step >= split)
    def last():
        last_ref[...] = value


def lane_index(rows):
    return lax.broadcasted_iota(jnp.int32, (rows, LANES), 1)


def swap_halves(w, lane):
    half = HEAD_DIM // 2
    up = pltpu.roll(w, LANES - half, 1)
    down = pltpu.roll(w, half, 1)
    return jnp.where(lane < half, up, down)


def widen(piece):
    rows = piece.shape[0]
    tail = jnp.zeros((rows, LANES - piece.shape[1]), piece.dtype)
    return jnp.concatenate([piece, tail], axis=1)


def split_three(column):
    high = column.astype(bf16).astype(f32)
    rest = column - high
    mid = rest.astype(bf16).astype(f32)
    return high, mid, rest - mid


def place_three(base, column, lane):
    high, mid, low = split_three(column)
    base = jnp.where(lane == 96, high, base)
    base = jnp.where(lane == 97, mid, base)
    return jnp.where(lane == 98, low, base)


def qkv_kernel(heads, x_ref, w_ref, ln_ref, b_ref, cos_ref, sin_ref, feat_ref, a_ref, q_ref, kv_ref):
    width = heads * HEAD_DIM
    x = x_ref[...].astype(f32)
    rows = x.shape[0]
    center = x - jnp.mean(x, axis=1, keepdims=True)
    inverse = lax.rsqrt(jnp.mean(center * center, axis=1, keepdims=True) + norm_eps)
    a = (center * inverse * ln_ref[0:1, :] + ln_ref[1:2, :]).astype(bf16)
    a_ref[...] = a
    y = mm(a, w_ref[...]) + b_ref[0:1, :]
    cos, sin = cos_ref[...], sin_ref[...]
    lane = lane_index(rows)
    kv = []
    for h in range(heads):
        w = widen(y[:, h * HEAD_DIM : (h + 1) * HEAD_DIM])
        q = (w * cos + swap_halves(w, lane) * sin) * (HEAD_DIM**-0.5 * log2e)
        q_ref[h] = jnp.where(lane < HEAD_DIM, q.astype(bf16), feat_ref[...])
    for h in range(heads):
        begin = width + h * HEAD_DIM
        w = widen(y[:, begin : begin + HEAD_DIM])
        kv.append((w * cos + swap_halves(w, lane) * sin)[:, :HEAD_DIM].astype(bf16))
    kv.append(y[:, 2 * width : 3 * width].astype(bf16))
    kv_ref[...] = jnp.concatenate(kv, axis=1)


def project_row(x, w, ln, bias, cos, sin, feat, heads):
    rows, width = x.shape
    block = min(256, rows)
    wide = w.shape[1]
    local = heads * HEAD_DIM
    by_rows = lambda n: pl.BlockSpec((block, n), lambda i: (i, 0))
    whole = lambda a: pl.BlockSpec(a.shape, lambda i: (0,) * a.ndim)
    return pl.pallas_call(
        functools.partial(qkv_kernel, heads),
        grid=(rows // block,),
        in_specs=[
            by_rows(width),
            whole(w),
            whole(ln),
            whole(bias),
            by_rows(LANES),
            by_rows(LANES),
            by_rows(LANES),
        ],
        out_specs=[
            by_rows(width),
            pl.BlockSpec((heads, block, LANES), lambda i: (0, i, 0)),
            by_rows(2 * local),
        ],
        out_shape=[
            jax.ShapeDtypeStruct((rows, width), bf16),
            jax.ShapeDtypeStruct((heads, rows, LANES), bf16),
            jax.ShapeDtypeStruct((rows, 2 * local), bf16),
        ],
        cost_estimate=pl.CostEstimate(
            flops=2 * rows * width * wide, bytes_accessed=rows * width * 4 + width * wide * 2, transcendentals=0
        ),
        name="project_row",
    )(x, w, ln, bias, cos, sin, feat)


def forward_kernel(heads, segments, block, flag_ref, q_ref, w_ref, *refs):
    kv_refs = refs[:segments]
    feat_refs = refs[segments : 2 * segments]
    o_ref, q_out, k_aug, v_aug, p_first, p_last, m_scr, acc_scr = refs[2 * segments :]
    width = heads * HEAD_DIM
    step = pl.program_id(0)
    keys = k_aug.shape[1]
    count = keys // block
    rows = q_ref.shape[1]

    @pl.when(step == 0)
    def build():
        offset = 0
        for s in range(segments):
            length = kv_refs[s].shape[0]
            piece = min(length, 256)
            for t in range(length // piece):
                at = pl.ds(t * piece, piece)
                to = pl.ds(offset + t * piece, piece)
                kv = kv_refs[s][at, :]
                feat = feat_refs[s][at, :]
                lane = lane_index(piece)
                tail = jnp.where(lane == HEAD_DIM, 1.0, jnp.where((lane >= 96) & (lane < 99), -1.0, 0.0)).astype(bf16)
                for h in range(heads):
                    k = kv[:, h * HEAD_DIM : (h + 1) * HEAD_DIM]
                    v = kv[:, width + h * HEAD_DIM : width + (h + 1) * HEAD_DIM]
                    k_aug[h, to, :] = jnp.concatenate([k, feat[:, HEAD_DIM:]], axis=1)
                    v_aug[h, to, :] = jnp.concatenate([v, tail[:, HEAD_DIM:]], axis=1)
            offset += length

    m_scr[...] = jnp.full(m_scr.shape, floor_max, f32)
    acc_scr[...] = jnp.zeros(acc_scr.shape, f32)

    def visit(j, carry):
        @pl.when(flag_ref[step * count + j] > 0)
        def go():
            at = pl.ds(pl.multiple_of(j * block, block), block)
            for h in range(heads):
                s = mm(q_ref[h], k_aug[h, at, :], NT)
                old = m_scr[h]
                new = jnp.maximum(old, jnp.max(s, axis=1, keepdims=True))
                p = jnp.exp2(s - new[:, 0:1])
                m_scr[h] = new
                acc_scr[h] = acc_scr[h] * jnp.exp2(old - new) + mm(p.astype(bf16), v_aug[h, at, :])

        return carry

    lax.fori_loop(0, count, visit, 0)
    lane = lane_index(rows)
    outs = []
    for h in range(heads):
        acc = acc_scr[h]
        total = acc[:, HEAD_DIM : HEAD_DIM + 1]
        alive = total > 0.0
        safe = jnp.where(alive, total, 1.0)
        outs.append((acc / safe)[:, :HEAD_DIM].astype(bf16))
        level = jnp.where(alive, m_scr[h][:, 0:1] + jnp.log2(safe), 0.0)
        q_out[h] = place_three(q_ref[h].astype(f32), level, lane).astype(bf16)
    o = jnp.concatenate(outs, axis=1)
    o_ref[...] = o
    store_halves(p_first, p_last, mm(o, w_ref[...], NT).astype(bf16))


def attend_forward(flags, q_aug, w, kvs, feats, heads, block):
    rows = q_aug.shape[1]
    tall = min(256, rows // 2)
    steps = rows // tall
    width = w.shape[0]
    keys = sum(kv.shape[0] for kv in kvs)
    segments = len(kvs)
    whole = lambda a: pl.BlockSpec(a.shape, lambda i, f: (0,) * a.ndim)
    q_spec = pl.BlockSpec((heads, tall, LANES), lambda i, f: (0, i, 0))
    k_spec = pl.BlockSpec((heads, keys, LANES), lambda i, f: (0, 0, 0))
    local = heads * HEAD_DIM
    return pl.pallas_call(
        functools.partial(forward_kernel, heads, segments, block),
        grid_spec=pltpu.PrefetchScalarGridSpec(
            num_scalar_prefetch=1,
            grid=(rows // tall,),
            in_specs=[q_spec, whole(w)] + [whole(kv) for kv in kvs] + [whole(f) for f in feats],
            out_specs=[
                pl.BlockSpec((tall, local), lambda i, f: (i, 0)),
                q_spec,
                k_spec,
                k_spec,
                pl.BlockSpec((tall, width), first_blocks(steps)),
                pl.BlockSpec((tall, width), last_blocks(steps)),
            ],
            scratch_shapes=[
                pltpu.VMEM((heads, tall, LANES), f32),
                pltpu.VMEM((heads, tall, LANES), f32),
            ],
        ),
        out_shape=[
            jax.ShapeDtypeStruct((rows, local), bf16),
            jax.ShapeDtypeStruct((heads, rows, LANES), bf16),
            jax.ShapeDtypeStruct((heads, keys, LANES), bf16),
            jax.ShapeDtypeStruct((heads, keys, LANES), bf16),
            jax.ShapeDtypeStruct((rows // 2, width), bf16),
            jax.ShapeDtypeStruct((rows // 2, width), bf16),
        ],
        cost_estimate=pl.CostEstimate(
            flops=2 * rows * keys * heads * LANES, bytes_accessed=8 * keys * local, transcendentals=rows * keys * heads // 2
        ),
        name="attend_forward",
    )(flags, q_aug, w, *kvs, *feats)


def backward_kernel(
    heads, segments, block, flag_ref, q_ref, ga_first, ga_last, w_ref, o_ref, k_aug, v_aug, cosq_ref, sinq_ref, *refs
):
    cosk_refs = refs[:segments]
    sink_refs = refs[segments : 2 * segments]
    dq_ref = refs[2 * segments]
    dkv_refs = refs[2 * segments + 1 : 3 * segments + 1]
    k_turn, dk_acc, dv_acc, dq_acc, go_scr = refs[3 * segments + 1 :]
    step = pl.program_id(0)
    keys = k_aug.shape[1]
    count = keys // block
    rows = q_ref.shape[1]
    scale = HEAD_DIM**-0.5

    @pl.when(step == 0)
    def build():
        dk_acc[...] = jnp.zeros(dk_acc.shape, f32)
        dv_acc[...] = jnp.zeros(dv_acc.shape, f32)
        for h in range(heads):
            for t in range(count):
                at = pl.ds(t * block, block)
                k_turn[h, :, at] = k_aug[h, at, :].T

    lane = lane_index(rows)
    ga = jnp.where(step < pl.num_programs(0) // 2, ga_first[...], ga_last[...])
    go_all = mm(ga, w_ref[...]).astype(bf16).astype(f32)
    for h in range(heads):
        cut = slice(h * HEAD_DIM, (h + 1) * HEAD_DIM)
        go = go_all[:, cut]
        delta = jnp.sum(go * o_ref[:, cut].astype(f32), axis=1, keepdims=True)
        go_scr[h] = place_three(widen(go), delta, lane).astype(bf16)
    dq_acc[...] = jnp.zeros(dq_acc.shape, f32)

    def visit(j, carry):
        @pl.when(flag_ref[step * count + j] > 0)
        def run():
            at = pl.ds(pl.multiple_of(j * block, block), block)
            for h in range(heads):
                q, go = q_ref[h], go_scr[h]
                p = jnp.exp2(mm(k_aug[h, at, :], q, NT))
                ds = (p * mm(v_aug[h, at, :], go, NT)).astype(bf16)
                dv_acc[h, at, :] += mm(p.astype(bf16), go)
                dk_acc[h, at, :] += mm(ds, q)
                dq_acc[h] += mm(k_turn[h, :, at], ds)

        return carry

    lax.fori_loop(0, count, visit, 0)

    def turn_back(w, cos, sin, index):
        return w * cos - swap_halves(w, index) * sin

    outs = []
    for h in range(heads):
        w = dq_acc[h].T
        back = turn_back(w, cosq_ref[...], sinq_ref[...], lane) * scale
        outs.append(back[:, :HEAD_DIM].astype(bf16))
    dq_ref[...] = jnp.concatenate(outs, axis=1)

    @pl.when(step == pl.num_programs(0) - 1)
    def finish():
        offset = 0
        for s in range(segments):
            length = dkv_refs[s].shape[0]
            piece = min(length, 256)
            index = lane_index(piece)
            for t in range(length // piece):
                at = pl.ds(t * piece, piece)
                of = pl.ds(offset + t * piece, piece)
                parts = []
                for h in range(heads):
                    w = dk_acc[h, of, :]
                    back = turn_back(w, cosk_refs[s][at, :], sink_refs[s][at, :], index) * (1.0 / log2e)
                    parts.append(back[:, :HEAD_DIM].astype(bf16))
                for h in range(heads):
                    parts.append(dv_acc[h, of, :][:, :HEAD_DIM].astype(bf16))
                dkv_refs[s][at, :] = jnp.concatenate(parts, axis=1)
            offset += length


def attend_backward(flags, q_aug, ga, w, o, k_aug, v_aug, cos_q, sin_q, cos_k, sin_k, heads, block):
    rows = q_aug.shape[1]
    tall = min(256, rows // 2)
    steps = rows // tall
    width = w.shape[0]
    keys = k_aug.shape[1]
    segments = len(cos_k)
    local = heads * HEAD_DIM
    whole = lambda a: pl.BlockSpec(a.shape, lambda i, f: (0,) * a.ndim)
    by_rows = lambda n: pl.BlockSpec((tall, n), lambda i, f: (i, 0))
    q_spec = pl.BlockSpec((heads, tall, LANES), lambda i, f: (0, i, 0))
    return pl.pallas_call(
        functools.partial(backward_kernel, heads, segments, block),
        grid_spec=pltpu.PrefetchScalarGridSpec(
            num_scalar_prefetch=1,
            grid=(rows // tall,),
            in_specs=[
                q_spec,
                pl.BlockSpec((tall, width), first_blocks(steps)),
                pl.BlockSpec((tall, width), last_blocks(steps)),
                whole(w),
                by_rows(local),
                whole(k_aug),
                whole(v_aug),
                by_rows(LANES),
                by_rows(LANES),
            ]
            + [whole(t) for t in cos_k]
            + [whole(t) for t in sin_k],
            out_specs=[by_rows(local)]
            + [pl.BlockSpec((t.shape[0], 2 * local), lambda i, f: (0, 0)) for t in cos_k],
            scratch_shapes=[
                pltpu.VMEM((heads, LANES, keys), bf16),
                pltpu.VMEM((heads, keys, LANES), f32),
                pltpu.VMEM((heads, keys, LANES), f32),
                pltpu.VMEM((heads, LANES, tall), f32),
                pltpu.VMEM((heads, tall, LANES), bf16),
            ],
        ),
        out_shape=[jax.ShapeDtypeStruct((rows, local), bf16)]
        + [jax.ShapeDtypeStruct((t.shape[0], 2 * local), bf16) for t in cos_k],
        cost_estimate=pl.CostEstimate(
            flops=5 * rows * keys * heads * LANES, bytes_accessed=16 * keys * local, transcendentals=rows * keys * heads // 2
        ),
        name="attend_backward",
    )(flags, q_aug, *ga, w, o, k_aug, v_aug, cos_q, sin_q, *cos_k, *sin_k)


def feed_kernel(chunk, c_first, c_last, g_ref, up_ref, down_ref, shift_ref, z_ref, gu_ref, gc_first, gc_last, feed_first, feed_last, sum_ref):
    step = pl.program_id(0)
    c = jnp.where(step < pl.num_programs(0) // 2, c_first[...], c_last[...])
    g = g_ref[...]
    gc, feed, sums = 0.0, 0.0, []
    for begin in range(0, up_ref.shape[1], chunk):
        cut = slice(begin, begin + chunk)
        u = mm(c, up_ref[:, cut]) + shift_ref[0:1, cut]
        sg = 0.5 + 0.5 * jnp.tanh(0.851 * u)
        z = (u * sg).astype(bf16)
        gu = (mm(g, down_ref[:, cut]) * (sg + 1.702 * u * sg * (1.0 - sg))).astype(bf16)
        z_ref[:, cut] = z
        gu_ref[:, cut] = gu
        gc = gc + mm(gu, up_ref[:, cut], NT)
        feed = feed + mm(z, down_ref[:, cut], NT)
        sums.append(jnp.sum(gu.astype(f32), axis=0, keepdims=True))
    store_halves(gc_first, gc_last, gc.astype(bf16))
    store_halves(feed_first, feed_last, feed.astype(bf16))

    @pl.when(step == 0)
    def clear():
        sum_ref[...] = jnp.zeros(sum_ref.shape, f32)

    sum_ref[0:1, :] += jnp.concatenate(sums, axis=1)
    sum_ref[1:2, : g.shape[1]] += jnp.sum(g.astype(f32), axis=0, keepdims=True)


def feed_forward(c, g, w_up, w_down, shift):
    rows, width = g.shape
    hidden = w_up.shape[1]
    tall = min(512, rows // 2)
    steps = rows // tall
    chunk = 256 if hidden % 256 == 0 else hidden
    by_rows = lambda n: pl.BlockSpec((tall, n), lambda i: (i, 0))
    whole = lambda a: pl.BlockSpec(a.shape, lambda i: (0,) * a.ndim)
    first = pl.BlockSpec((tall, width), first_blocks(steps))
    last = pl.BlockSpec((tall, width), last_blocks(steps))
    part = jax.ShapeDtypeStruct((rows // 2, width), bf16)
    longest = max(width, hidden)
    return pl.pallas_call(
        functools.partial(feed_kernel, chunk),
        grid=(steps,),
        in_specs=[first, last, by_rows(width), whole(w_up), whole(w_down), whole(shift)],
        out_specs=[by_rows(hidden), by_rows(hidden), first, last, first, last, pl.BlockSpec((8, longest), lambda i: (0, 0))],
        out_shape=[
            jax.ShapeDtypeStruct((rows, hidden), bf16),
            jax.ShapeDtypeStruct((rows, hidden), bf16),
            part,
            part,
            part,
            part,
            jax.ShapeDtypeStruct((8, longest), f32),
        ],
        cost_estimate=pl.CostEstimate(
            flops=8 * rows * width * hidden, bytes_accessed=4 * width * hidden + 12 * rows * width, transcendentals=rows * hidden
        ),
        name="feed_forward",
    )(*c, g, w_up, w_down, shift)


def back_kernel(pieces, x_ref, w_ref, gq_ref, *refs):
    kv_refs = refs[:pieces]
    p_first, p_last, dkv_ref, sum_ref = refs[pieces:]
    gq = gq_ref[...]
    if pieces == 1:
        dkv = kv_refs[0][...]
    else:
        dkv = (kv_refs[0][...].astype(f32) + kv_refs[1][...].astype(f32)).astype(bf16)
    dkv_ref[...] = dkv
    tail = jnp.zeros((gq.shape[0], w_ref.shape[1] - gq.shape[1] - dkv.shape[1]), bf16)
    e = mm(jnp.concatenate([gq, dkv, tail], axis=1), w_ref[...], NT)
    store_halves(p_first, p_last, e.astype(bf16))
    x = x_ref[...].astype(f32)
    center = x - jnp.mean(x, axis=1, keepdims=True)
    unit = center * lax.rsqrt(jnp.mean(center * center, axis=1, keepdims=True) + norm_eps)

    @pl.when(pl.program_id(0) == 0)
    def clear():
        sum_ref[...] = jnp.zeros(sum_ref.shape, f32)

    local = gq.shape[1]
    sum_ref[0:1, :] += jnp.sum(e * unit, axis=0, keepdims=True)
    sum_ref[1:2, :] += jnp.sum(e, axis=0, keepdims=True)
    sum_ref[2:3, :local] += jnp.sum(gq.astype(f32), axis=0, keepdims=True)
    sum_ref[3:4, : 2 * local] += jnp.sum(dkv.astype(f32), axis=0, keepdims=True)


def project_back(x, w, gq, dkvs):
    rows, width = x.shape
    local = gq.shape[1]
    tall = min(512, rows // 2)
    steps = rows // tall
    by_rows = lambda n: pl.BlockSpec((tall, n), lambda i: (i, 0))
    whole = lambda a: pl.BlockSpec(a.shape, lambda i: (0,) * a.ndim)
    part = jax.ShapeDtypeStruct((rows // 2, width), bf16)
    return pl.pallas_call(
        functools.partial(back_kernel, len(dkvs)),
        grid=(steps,),
        in_specs=[by_rows(width), whole(w), by_rows(local)] + [by_rows(2 * local)] * len(dkvs),
        out_specs=[
            pl.BlockSpec((tall, width), first_blocks(steps)),
            pl.BlockSpec((tall, width), last_blocks(steps)),
            by_rows(2 * local),
            pl.BlockSpec((8, width), lambda i: (0, 0)),
        ],
        out_shape=[part, part, jax.ShapeDtypeStruct((rows, 2 * local), bf16), jax.ShapeDtypeStruct((8, width), f32)],
        cost_estimate=pl.CostEstimate(
            flops=6 * rows * width * local, bytes_accessed=6 * width * local + 6 * rows * width, transcendentals=rows
        ),
        name="project_back",
    )(x, w, gq, *dkvs)


def norm_stats(rows_in):
    center = rows_in - jnp.mean(rows_in, axis=1, keepdims=True)
    inverse = lax.rsqrt(jnp.mean(center * center, axis=1, keepdims=True) + norm_eps)
    return center * inverse, inverse


def norm_backward(grad_rows, unit_rows, inverse, gain):
    scaled = grad_rows * gain
    grad_in = inverse * (
        scaled
        - jnp.mean(scaled, axis=1, keepdims=True)
        - unit_rows * jnp.mean(scaled * unit_rows, axis=1, keepdims=True)
    )
    return (grad_in, jnp.sum(grad_rows * unit_rows, axis=0), jnp.sum(grad_rows, axis=0))


def tables(grid_pos):
    lane = jnp.arange(LANES)
    quarter = HEAD_DIM // 4
    frequency = jnp.power(10000.0, -4.0 * (lane % quarter).astype(f32) / HEAD_DIM)
    place = jnp.where((lane // quarter) % 2 == 0, grid_pos[0][:, None], grid_pos[1][:, None])
    angle = jnp.where(lane < HEAD_DIM, place.astype(f32) * frequency, 0.0)
    return jnp.cos(angle), jnp.where(lane < HEAD_DIM // 2, -1.0, 1.0) * jnp.sin(angle)


def query_features(ids):
    lane = jnp.arange(LANES)
    return (lane == HEAD_DIM + 1 + ids[:, None]).astype(bf16)


def key_features(ids):
    lane = jnp.arange(LANES)
    slot = lane - HEAD_DIM
    same = (slot >= 1) & (slot == ids[:, None] + 1)
    wall = jnp.where((slot >= 0) & (slot < 16) & ~same, -hide, 0.0)
    return jnp.where((lane >= 96) & (lane < 99), -1.0, wall).astype(bf16)


def visit_flags(query_ids, key_ids, tall, block):
    q = query_ids.reshape(-1, tall)
    k = key_ids.reshape(-1, block)
    q_top, k_top = jnp.max(q, axis=1), jnp.max(k, axis=1)
    q_low = jnp.min(jnp.where(q >= 0, q, 1 << 20), axis=1)
    k_low = jnp.min(jnp.where(k >= 0, k, 1 << 20), axis=1)
    meet = (q_low[:, None] <= k_top[None, :]) & (k_low[None, :] <= q_top[:, None])
    return meet.astype(jnp.int32).reshape(-1)


def on_device(
    patches,
    cotangent,
    picture_ids,
    positions,
    ln1_gain,
    ln1_bias,
    qkv_weight,
    qkv_bias,
    proj_weight,
    proj_bias,
    ln2_gain,
    ln2_bias,
    fc1_weight,
    fc1_bias,
    fc2_weight,
    fc2_bias,
):
    row_count, row_share, width = patches.shape
    owners = lax.axis_size("shard")
    contexts = lax.axis_size("ctx")
    ways = lax.axis_size("tp")
    part = qkv_weight.shape[0]
    local = qkv_weight.shape[2]
    heads = local // HEAD_DIM
    half = row_share // 2
    side = lax.axis_index("tp") % 2
    context = lax.axis_index("ctx")
    pairs_near = [(i, i ^ 1) for i in range(ways)]
    pairs_far = [(i, i ^ 2) for i in range(ways)]
    pad = -3 * local % 256
    wide = 3 * local + pad

    def near(v):
        return lax.ppermute(v, "tp", pairs_near)

    def far(v):
        return lax.ppermute(v, "tp", pairs_far)

    def over_ctx(v):
        return lax.ppermute(v, "ctx", [(0, 1), (1, 0)])

    def mine_first(v, axis=0):
        return jnp.where(side == 0, v, jnp.roll(v, half, axis=axis))

    def column(v):
        flat = v.reshape(-1)
        return jnp.pad(flat, (0, part - flat.shape[0]))

    vectors = [ln1_gain, ln1_bias, ln2_gain, ln2_bias, proj_bias, fc2_bias, qkv_bias, fc1_bias]
    tail = jnp.stack([column(v) for v in vectors], axis=1)
    tail = jnp.pad(tail, ((0, 0), (0, pad - len(vectors))))
    qkv_piece = jnp.concatenate([qkv_weight.reshape(part, 3 * local), tail], axis=1).astype(bf16)
    gather = lambda v: lax.all_gather(v, "shard", axis=0, tiled=True)
    up_piece = fc1_weight.astype(bf16)
    down_piece = fc2_weight.T.astype(bf16)
    proj_piece = proj_weight.T.astype(bf16)
    place = lax.axis_index("shard")
    context_first = context == 0

    w_qkv = gather(qkv_piece)
    proj_piece = tie(proj_piece, w_qkv)
    w_proj = jnp.zeros((owners,) + proj_piece.shape, bf16)
    w_proj = lax.dynamic_update_index_in_dim(w_proj, proj_piece, place, 0)
    for step in range(1, owners):
        got = lax.ppermute(proj_piece, "shard", [(i, (i + step) % owners) for i in range(owners)])
        w_proj = lax.dynamic_update_index_in_dim(w_proj, got, (place - step) % owners, 0)
    w_proj = w_proj.reshape(owners * part, local)
    packed = w_qkv[:, 3 * local : 3 * local + len(vectors)].T.astype(f32)
    gain_one, bias_one, gain_two, bias_two, proj_shift, down_shift = [packed[i] for i in range(6)]
    qb_size = qkv_bias.size
    qkv_shift = packed[6].reshape(owners, part)[:, :qb_size].reshape((owners,) + qkv_bias.shape)
    qkv_shift = jnp.transpose(qkv_shift, (1, 2, 0, 3)).reshape(-1)
    qkv_shift = jnp.pad(qkv_shift, (0, pad)).reshape(1, wide)
    up_shift = packed[7].reshape(owners, part)[:, : fc1_bias.size].reshape((owners,) + fc1_bias.shape)
    up_shift = jnp.transpose(up_shift, (1, 0, 2)).reshape(1, -1)
    ln_one = tie(packed[0:2], up_piece, down_piece)

    ids_by_ctx = mine_first(picture_ids.reshape(row_count, contexts, row_share), axis=2)
    places = mine_first(positions, axis=2)
    block = min(256, half)
    key_block = 256
    rows = []
    for r in range(row_count):
        x = mine_first(patches[r])
        g = mine_first(cotangent[r])
        ids = lax.dynamic_index_in_dim(ids_by_ctx[r], context, 0, keepdims=False)
        if contexts == 2:
            other = lax.dynamic_index_in_dim(ids_by_ctx[r], 1 - context, 0, keepdims=False)
            key_ids = [ids, other]
            spots = [places[:, r], over_ctx(places[:, r])]
        else:
            key_ids = [ids_by_ctx[r].reshape(-1)]
            spots = [lax.all_gather(places[:, r], "ctx", axis=1, tiled=True)]
        live = (ids >= 0).astype(f32)[:, None]
        turns = [tables(spot) for spot in spots]
        own_turn = turns[0] if contexts == 2 else tables(places[:, r])
        rows.append(
            dict(
                x=x,
                g=(g.astype(f32) * live).astype(bf16),
                live=live,
                ids=ids,
                cos=own_turn[0],
                sin=own_turn[1],
                cos_k=[t[0] for t in turns],
                sin_k=[t[1] for t in turns],
                q_feat=query_features(ids),
                k_feat=[key_features(k) for k in key_ids],
                flags=visit_flags(ids, jnp.concatenate(key_ids), block, key_block),
            )
        )

    for row in rows:
        row["a"], row["q"], row["kv"] = project_row(
            row["x"], w_qkv, ln_one, qkv_shift, row["cos"], row["sin"], row["q_feat"], heads
        )
        if row is rows[0]:
            row["kv"], w_proj = lax.optimization_barrier((row["kv"], w_proj))
        if contexts == 2:
            row["kvs"] = [row["kv"], over_ctx(row["kv"])]
        else:
            row["kvs"] = [lax.all_gather(row["kv"], "ctx", axis=0, tiled=True)]

    down_piece, up_piece = lax.optimization_barrier((down_piece, up_piece, w_proj))[:2]
    if contexts == 2:
        down_cut = down_piece.reshape(2, part // 2, -1)
        down_near = gather(lax.dynamic_index_in_dim(down_cut, context, 0, keepdims=False))
        down_near = down_near.reshape(owners, part // 2, -1)
    else:
        w_down = gather(down_piece)
    w_up = gather(up_piece)

    def sum_near(first, last):
        return (first.astype(f32) + near(last).astype(f32)).astype(bf16)

    def norm_two(row, shift):
        row["h"] = row["x"][:half].astype(f32) + (row["branch"].astype(f32) + row["branch_far"].astype(f32)) + shift
        row["unit"], row["inv"] = norm_stats(row["h"])
        mine = (row["unit"] * gain_two + bias_two).astype(bf16)
        row["c"] = (mine, near(mine))

    hold = lax.optimization_barrier
    before = rows[-1]["kv"]
    for index, row in enumerate(rows):
        row["o"], row["q"], row["k_aug"], row["v_aug"], first, last = attend_forward(
            tie(row["flags"], before), row["q"], w_proj, row["kvs"], row["k_feat"], heads, key_block
        )
        if index:
            prior = rows[index - 1]
            first, last, prior["branch_far"] = hold((first, last, prior["branch_far"]))
        if index + 1 < row_count:
            follow = rows[index + 1]
            first, last, follow["kvs"] = hold((first, last, follow["kvs"]))
            if contexts == 2:
                first, last, down_near = hold((first, last, down_near))
                down_far = over_ctx(down_near)
        elif contexts == 2:
            first, last, down_far, w_up = hold((first, last, down_far, w_up))
        before = row["branch"] = sum_near(first, last)
        row["branch_far"] = far(before)
    if contexts == 2:
        low = jnp.where(context_first, down_near, down_far)
        high = jnp.where(context_first, down_far, down_near)
        w_down = jnp.concatenate([low, high], axis=1).reshape(owners * part, -1)

    norm_two(rows[0], tie(proj_shift, before))
    for index, row in enumerate(rows):
        shift = tie(up_shift, before)
        row["z"], row["gu"], gc_first, gc_last, feed_first, feed_last, row["feed_sums"] = feed_forward(
            row["c"], row["g"], w_up, w_down, shift
        )
        other, key = (rows[-1], "branch_far") if index == 0 else (rows[index - 1], "gc_far")
        gc_first, gc_last, other[key] = hold((gc_first, gc_last, other[key]))
        before = row["gc"] = sum_near(gc_first, gc_last)
        row["gc_far"] = far(before)
        row["feed"] = (feed_first, feed_last)
        if index + 1 < row_count:
            norm_two(rows[index + 1], proj_shift)
    for row in rows:
        row["feed"] = sum_near(*row["feed"])

    join = lambda key: jnp.concatenate([row[key] for row in rows], axis=0)
    join_two = lambda key: jnp.concatenate([piece for row in rows for piece in row[key]], axis=0)
    scatter = lambda v: lax.psum_scatter(v, "shard", scatter_dimension=0, tiled=True)
    if contexts == 2:
        finish = lambda v: v.astype(f32) + over_ctx(v).astype(f32)
    else:
        finish = lambda v: lax.psum(v, "ctx").astype(f32)
    last_row = rows[-1]
    last_row["gu"], last_row["z"] = hold((last_row["gu"], last_row["z"], before))[:2]
    grad_up = mm(join_two("c"), join("gu"), TN).astype(bf16)
    grad_down = mm(join("g"), join("z"), TN).astype(bf16)
    grad_up, grad_down, last_row["gc_far"] = hold((grad_up, grad_down, last_row["gc_far"]))
    before = (grad_up, grad_down)
    y_free = last_row["gc_far"]
    grad_up = scatter(grad_up)
    grad_down = scatter(grad_down)

    pair = 0.0
    for row in rows:
        gc = row["gc"].astype(f32) + row["gc_far"].astype(f32)
        grad_in, d_gain, d_bias = norm_backward(gc, row["unit"], row["inv"], gain_two)
        row["gh"] = row["g"][:half].astype(f32) + grad_in
        ga = row["gh"].astype(bf16)
        pair = pair + jnp.stack([d_gain, d_bias, jnp.sum(ga.astype(f32), axis=0)])
        row["ga"] = (ga, near(ga))
    for index, row in enumerate(rows):
        feed_far = far(tie(row["feed"], y_free))
        out = attend_backward(
            tie(row["flags"], *before),
            row["q"],
            row["ga"],
            w_proj,
            row["o"],
            row["k_aug"],
            row["v_aug"],
            row["cos"],
            row["sin"],
            row["cos_k"],
            row["sin_k"],
            heads,
            key_block,
        )
        if index:
            prior = rows[index - 1]
            *out, feed_far, prior["dkvs"], grad_up = hold((*out, feed_far, prior["dkvs"], grad_up))
        else:
            *out, feed_far = hold((*out, feed_far))
        y_free = feed_far
        before = (out[0],)
        row["gq"] = out[0]
        row["feed"] = row["feed"].astype(f32) + feed_far.astype(f32)
        if contexts == 2:
            row["dkvs"] = [out[1], over_ctx(out[2])]
        else:
            row["dkvs"] = [lax.psum_scatter(out[1], "ctx", scatter_dimension=0, tiled=True)]

    def whole_row(mine):
        other = near(mine)
        return [jnp.where(side == 0, mine, other), jnp.where(side == 0, other, mine)]

    def whole_rows(pieces):
        return jnp.concatenate(pieces, axis=0).reshape(row_count, row_share, width)

    outs, ins = [], []
    sums = 0.0
    for index, row in enumerate(rows):
        first, last, row["dkv"], back_sums = project_back(row["x"], w_qkv, tie(row["gq"], *before), row["dkvs"])
        sums = sums + back_sums
        before = (row["dkv"],)
        if index == 0:
            last_row["gq"] = tie(last_row["gq"], *before)
            grad_q = mm(join("a"), join("gq"), TN).astype(bf16)
            grad_proj = mm(join_two("ga"), join("o"), TN).astype(bf16)
            grad_q, grad_proj, grad_down, last_row["dkvs"] = hold((grad_q, grad_proj, grad_down, last_row["dkvs"]))
            grad_q, grad_proj = scatter(grad_q), scatter(grad_proj)
            before = before + (last_row["dkvs"][0],)
        mine = sum_near(first, last)
        row["ga1"] = mine.astype(f32) + far(mine).astype(f32)
    grad_kv = mm(join("a"), join("dkv"), TN).astype(bf16)
    grad_kv, grad_q, grad_proj = hold((grad_kv, grad_q, grad_proj))
    grad_kv = scatter(grad_kv)
    grad_up, grad_down, grad_q, grad_proj = [finish(v) for v in (grad_up, grad_down, grad_q, grad_proj)]

    def sum_over(v, axis):
        size, step = lax.axis_size(axis), 1
        while step < size:
            v = v + lax.ppermute(v, axis, [(i, i ^ step) for i in range(size)])
            step *= 2
        return v

    def owned(v):
        v = v.reshape(owners, -1)
        return jnp.pad(v, ((0, 0), (0, part - v.shape[1]))).reshape(-1)

    feed_sums = sum(row["feed_sums"] for row in rows)
    d_qb = jnp.concatenate([sums[2, :local], sums[3, : 2 * local]]).reshape(3, heads, owners, -1)
    d_qb = owned(jnp.transpose(d_qb, (2, 0, 1, 3)))
    d_ub = feed_sums[0, : fc1_bias.size * owners].reshape(fc1_bias.shape[0], owners, fc1_bias.shape[1])
    d_ub = owned(jnp.transpose(d_ub, (1, 0, 2)))
    vector = jnp.concatenate(
        [pair + near(pair), feed_sums[1:2, :width], d_qb[None], d_ub[None], sum_over(sums[0:2], "tp")], axis=0
    )
    vector = sum_over(sum_over(vector, "ctx"), "shard")
    vector = lax.dynamic_slice_in_dim(vector, place * part, part, axis=1)

    for row in rows:
        outs += whole_row(((row["h"] + row["feed"] + down_shift) * row["live"][:half]).astype(bf16))
        unit, inverse = norm_stats(row["x"][:half].astype(f32))
        grad_in = norm_backward(row["ga1"], unit, inverse, gain_one)[0]
        ins += whole_row((row["gh"] + grad_in).astype(bf16))
    outs, ins = whole_rows(outs), whole_rows(ins)
    grad_kv = finish(tie(grad_kv, outs, ins, grad_up, grad_down, grad_q, grad_proj, vector))
    return (
        outs,
        ins,
        vector[6],
        vector[7],
        jnp.concatenate([grad_q, grad_kv], axis=1).reshape(qkv_weight.shape),
        vector[4, :qb_size].reshape(qkv_bias.shape),
        grad_proj.T,
        vector[2],
        vector[0],
        vector[1],
        grad_up,
        vector[5, : fc1_bias.size].reshape(fc1_bias.shape),
        grad_down.T,
        vector[3],
    )


def solution(mesh):
    in_specs = (
        P("shard", "ctx", None),
        P("shard", "ctx", None),
        P("shard", None),
        P(None, "shard", "ctx"),
        P("shard"),
        P("shard"),
        P("shard", None, "tp"),
        P(None, "tp", "shard"),
        P("tp", "shard"),
        P("shard"),
        P("shard"),
        P("shard"),
        P("shard", "tp"),
        P("tp", "shard"),
        P("tp", "shard"),
        P("shard"),
    )
    out_specs = (
        P("shard", "ctx", None),
        P("shard", "ctx", None),
        P("shard"),
        P("shard"),
        P("shard", None, "tp"),
        P(None, "tp", "shard"),
        P("tp", "shard"),
        P("shard"),
        P("shard"),
        P("shard"),
        P("shard", "tp"),
        P("tp", "shard"),
        P("tp", "shard"),
        P("shard"),
    )
    return jax.shard_map(
        on_device, mesh=mesh, in_specs=in_specs, out_specs=out_specs, check_vma=False
    )
```

```python
import functools
import math

import jax
import jax.numpy as jnp
from jax import lax
from jax.experimental import pallas as pl
from jax.experimental.pallas import tpu as pltpu
from jax.sharding import PartitionSpec as P

HEAD_DIM = 80
LANES = 128
norm_eps = 1e-06
hide = 1e30
floor_max = -1e29
log2e = math.log2(math.e)
bf16 = jnp.bfloat16
f32 = jnp.float32
NT = (((1,), (1,)), ((), ()))
NN = (((1,), (0,)), ((), ()))
TN = (((0,), (0,)), ((), ()))


def mm(a, b, dims=NN):
    return lax.dot_general(a, b, dims, preferred_element_type=f32)


def tie(value, *others):
    return lax.optimization_barrier((value,) + others)[0]


def first_blocks(steps):
    return lambda i, *_: (jnp.minimum(i, steps // 2 - 1), 0)


def last_blocks(steps):
    return lambda i, *_: (jnp.maximum(i - steps // 2, 0), 0)


def store_halves(first_ref, last_ref, value):
    step, split = pl.program_id(0), pl.num_programs(0) // 2

    @pl.when(step < split)
    def first():
        first_ref[...] = value

    @pl.when(step >= split)
    def last():
        last_ref[...] = value


def lane_index(rows):
    return lax.broadcasted_iota(jnp.int32, (rows, LANES), 1)


def swap_halves(w, lane):
    half = HEAD_DIM // 2
    up = pltpu.roll(w, LANES - half, 1)
    down = pltpu.roll(w, half, 1)
    return jnp.where(lane < half, up, down)


def widen(piece):
    rows = piece.shape[0]
    tail = jnp.zeros((rows, LANES - piece.shape[1]), piece.dtype)
    return jnp.concatenate([piece, tail], axis=1)


def split_three(column):
    high = column.astype(bf16).astype(f32)
    rest = column - high
    mid = rest.astype(bf16).astype(f32)
    return high, mid, rest - mid


def place_three(base, column, lane):
    high, mid, low = split_three(column)
    base = jnp.where(lane == 96, high, base)
    base = jnp.where(lane == 97, mid, base)
    return jnp.where(lane == 98, low, base)


def qkv_kernel(heads, x_ref, w_ref, ln_ref, b_ref, cos_ref, sin_ref, feat_ref, a_ref, q_ref, kv_ref):
    width = heads * HEAD_DIM
    x = x_ref[...].astype(f32)
    rows = x.shape[0]
    center = x - jnp.mean(x, axis=1, keepdims=True)
    inverse = lax.rsqrt(jnp.mean(center * center, axis=1, keepdims=True) + norm_eps)
    a = (center * inverse * ln_ref[0:1, :] + ln_ref[1:2, :]).astype(bf16)
    a_ref[...] = a
    y = mm(a, w_ref[...]) + b_ref[0:1, :]
    cos, sin = cos_ref[...], sin_ref[...]
    lane = lane_index(rows)
    kv = []
    for h in range(heads):
        w = widen(y[:, h * HEAD_DIM : (h + 1) * HEAD_DIM])
        q = (w * cos + swap_halves(w, lane) * sin) * (HEAD_DIM**-0.5 * log2e)
        q_ref[h] = jnp.where(lane < HEAD_DIM, q.astype(bf16), feat_ref[...])
    for h in range(heads):
        begin = width + h * HEAD_DIM
        w = widen(y[:, begin : begin + HEAD_DIM])
        kv.append((w * cos + swap_halves(w, lane) * sin)[:, :HEAD_DIM].astype(bf16))
    kv.append(y[:, 2 * width : 3 * width].astype(bf16))
    kv_ref[...] = jnp.concatenate(kv, axis=1)


def project_row(x, w, ln, bias, cos, sin, feat, heads):
    rows, width = x.shape
    block = min(256, rows)
    wide = w.shape[1]
    local = heads * HEAD_DIM
    by_rows = lambda n: pl.BlockSpec((block, n), lambda i: (i, 0))
    whole = lambda a: pl.BlockSpec(a.shape, lambda i: (0,) * a.ndim)
    return pl.pallas_call(
        functools.partial(qkv_kernel, heads),
        grid=(rows // block,),
        in_specs=[
            by_rows(width),
            whole(w),
            whole(ln),
            whole(bias),
            by_rows(LANES),
            by_rows(LANES),
            by_rows(LANES),
        ],
        out_specs=[
            by_rows(width),
            pl.BlockSpec((heads, block, LANES), lambda i: (0, i, 0)),
            by_rows(2 * local),
        ],
        out_shape=[
            jax.ShapeDtypeStruct((rows, width), bf16),
            jax.ShapeDtypeStruct((heads, rows, LANES), bf16),
            jax.ShapeDtypeStruct((rows, 2 * local), bf16),
        ],
        cost_estimate=pl.CostEstimate(
            flops=2 * rows * width * wide, bytes_accessed=rows * width * 4 + width * wide * 2, transcendentals=0
        ),
        name="project_row",
    )(x, w, ln, bias, cos, sin, feat)


def forward_kernel(heads, segments, block, flag_ref, q_ref, w_ref, *refs):
    kv_refs = refs[:segments]
    feat_refs = refs[segments : 2 * segments]
    o_ref, q_out, k_aug, v_aug, p_first, p_last, m_scr, acc_scr = refs[2 * segments :]
    width = heads * HEAD_DIM
    step = pl.program_id(0)
    keys = k_aug.shape[1]
    count = keys // block
    rows = q_ref.shape[1]

    @pl.when(step == 0)
    def build():
        offset = 0
        for s in range(segments):
            length = kv_refs[s].shape[0]
            piece = min(length, 256)
            for t in range(length // piece):
                at = pl.ds(t * piece, piece)
                to = pl.ds(offset + t * piece, piece)
                kv = kv_refs[s][at, :]
                feat = feat_refs[s][at, :]
                lane = lane_index(piece)
                tail = jnp.where(lane == HEAD_DIM, 1.0, jnp.where((lane >= 96) & (lane < 99), -1.0, 0.0)).astype(bf16)
                for h in range(heads):
                    k = kv[:, h * HEAD_DIM : (h + 1) * HEAD_DIM]
                    v = kv[:, width + h * HEAD_DIM : width + (h + 1) * HEAD_DIM]
                    k_aug[h, to, :] = jnp.concatenate([k, feat[:, HEAD_DIM:]], axis=1)
                    v_aug[h, to, :] = jnp.concatenate([v, tail[:, HEAD_DIM:]], axis=1)
            offset += length

    m_scr[...] = jnp.full(m_scr.shape, floor_max, f32)
    acc_scr[...] = jnp.zeros(acc_scr.shape, f32)

    def visit(j, carry):
        @pl.when(flag_ref[step * count + j] > 0)
        def go():
            at = pl.ds(pl.multiple_of(j * block, block), block)
            for h in range(heads):
                s = mm(q_ref[h], k_aug[h, at, :], NT)
                old = m_scr[h]
                new = jnp.maximum(old, jnp.max(s, axis=1, keepdims=True))
                p = jnp.exp2(s - new[:, 0:1])
                m_scr[h] = new
                acc_scr[h] = acc_scr[h] * jnp.exp2(old - new) + mm(p.astype(bf16), v_aug[h, at, :])

        return carry

    lax.fori_loop(0, count, visit, 0)
    lane = lane_index(rows)
    outs = []
    for h in range(heads):
        acc = acc_scr[h]
        total = acc[:, HEAD_DIM : HEAD_DIM + 1]
        alive = total > 0.0
        safe = jnp.where(alive, total, 1.0)
        outs.append((acc / safe)[:, :HEAD_DIM].astype(bf16))
        level = jnp.where(alive, m_scr[h][:, 0:1] + jnp.log2(safe), 0.0)
        q_out[h] = place_three(q_ref[h].astype(f32), level, lane).astype(bf16)
    o = jnp.concatenate(outs, axis=1)
    o_ref[...] = o
    store_halves(p_first, p_last, mm(o, w_ref[...], NT).astype(bf16))


def attend_forward(flags, q_aug, w, kvs, feats, heads, block):
    rows = q_aug.shape[1]
    tall = min(256, rows // 2)
    steps = rows // tall
    width = w.shape[0]
    keys = sum(kv.shape[0] for kv in kvs)
    segments = len(kvs)
    whole = lambda a: pl.BlockSpec(a.shape, lambda i, f: (0,) * a.ndim)
    q_spec = pl.BlockSpec((heads, tall, LANES), lambda i, f: (0, i, 0))
    k_spec = pl.BlockSpec((heads, keys, LANES), lambda i, f: (0, 0, 0))
    local = heads * HEAD_DIM
    return pl.pallas_call(
        functools.partial(forward_kernel, heads, segments, block),
        grid_spec=pltpu.PrefetchScalarGridSpec(
            num_scalar_prefetch=1,
            grid=(rows // tall,),
            in_specs=[q_spec, whole(w)] + [whole(kv) for kv in kvs] + [whole(f) for f in feats],
            out_specs=[
                pl.BlockSpec((tall, local), lambda i, f: (i, 0)),
                q_spec,
                k_spec,
                k_spec,
                pl.BlockSpec((tall, width), first_blocks(steps)),
                pl.BlockSpec((tall, width), last_blocks(steps)),
            ],
            scratch_shapes=[
                pltpu.VMEM((heads, tall, LANES), f32),
                pltpu.VMEM((heads, tall, LANES), f32),
            ],
        ),
        out_shape=[
            jax.ShapeDtypeStruct((rows, local), bf16),
            jax.ShapeDtypeStruct((heads, rows, LANES), bf16),
            jax.ShapeDtypeStruct((heads, keys, LANES), bf16),
            jax.ShapeDtypeStruct((heads, keys, LANES), bf16),
            jax.ShapeDtypeStruct((rows // 2, width), bf16),
            jax.ShapeDtypeStruct((rows // 2, width), bf16),
        ],
        cost_estimate=pl.CostEstimate(
            flops=2 * rows * keys * heads * LANES, bytes_accessed=8 * keys * local, transcendentals=rows * keys * heads // 2
        ),
        name="attend_forward",
    )(flags, q_aug, w, *kvs, *feats)


def backward_kernel(
    heads, segments, block, flag_ref, q_ref, ga_first, ga_last, w_ref, o_ref, k_aug, v_aug, cosq_ref, sinq_ref, *refs
):
    cosk_refs = refs[:segments]
    sink_refs = refs[segments : 2 * segments]
    dq_ref = refs[2 * segments]
    dkv_refs = refs[2 * segments + 1 : 3 * segments + 1]
    k_turn, dk_acc, dv_acc, dq_acc, go_scr = refs[3 * segments + 1 :]
    step = pl.program_id(0)
    keys = k_aug.shape[1]
    count = keys // block
    rows = q_ref.shape[1]
    scale = HEAD_DIM**-0.5

    @pl.when(step == 0)
    def build():
        dk_acc[...] = jnp.zeros(dk_acc.shape, f32)
        dv_acc[...] = jnp.zeros(dv_acc.shape, f32)
        for h in range(heads):
            for t in range(count):
                at = pl.ds(t * block, block)
                k_turn[h, :, at] = k_aug[h, at, :].T

    lane = lane_index(rows)
    ga = jnp.where(step < pl.num_programs(0) // 2, ga_first[...], ga_last[...])
    go_all = mm(ga, w_ref[...]).astype(bf16).astype(f32)
    for h in range(heads):
        cut = slice(h * HEAD_DIM, (h + 1) * HEAD_DIM)
        go = go_all[:, cut]
        delta = jnp.sum(go * o_ref[:, cut].astype(f32), axis=1, keepdims=True)
        go_scr[h] = place_three(widen(go), delta, lane).astype(bf16)
    dq_acc[...] = jnp.zeros(dq_acc.shape, f32)

    def visit(j, carry):
        @pl.when(flag_ref[step * count + j] > 0)
        def run():
            at = pl.ds(pl.multiple_of(j * block, block), block)
            for h in range(heads):
                q, go = q_ref[h], go_scr[h]
                p = jnp.exp2(mm(k_aug[h, at, :], q, NT))
                ds = (p * mm(v_aug[h, at, :], go, NT)).astype(bf16)
                dv_acc[h, at, :] += mm(p.astype(bf16), go)
                dk_acc[h, at, :] += mm(ds, q)
                dq_acc[h] += mm(k_turn[h, :, at], ds)

        return carry

    lax.fori_loop(0, count, visit, 0)

    def turn_back(w, cos, sin, index):
        return w * cos - swap_halves(w, index) * sin

    outs = []
    for h in range(heads):
        w = dq_acc[h].T
        back = turn_back(w, cosq_ref[...], sinq_ref[...], lane) * scale
        outs.append(back[:, :HEAD_DIM].astype(bf16))
    dq_ref[...] = jnp.concatenate(outs, axis=1)

    @pl.when(step == pl.num_programs(0) - 1)
    def finish():
        offset = 0
        for s in range(segments):
            length = dkv_refs[s].shape[0]
            piece = min(length, 256)
            index = lane_index(piece)
            for t in range(length // piece):
                at = pl.ds(t * piece, piece)
                of = pl.ds(offset + t * piece, piece)
                parts = []
                for h in range(heads):
                    w = dk_acc[h, of, :]
                    back = turn_back(w, cosk_refs[s][at, :], sink_refs[s][at, :], index) * (1.0 / log2e)
                    parts.append(back[:, :HEAD_DIM].astype(bf16))
                for h in range(heads):
                    parts.append(dv_acc[h, of, :][:, :HEAD_DIM].astype(bf16))
                dkv_refs[s][at, :] = jnp.concatenate(parts, axis=1)
            offset += length


def attend_backward(flags, q_aug, ga, w, o, k_aug, v_aug, cos_q, sin_q, cos_k, sin_k, heads, block):
    rows = q_aug.shape[1]
    tall = min(256, rows // 2)
    steps = rows // tall
    width = w.shape[0]
    keys = k_aug.shape[1]
    segments = len(cos_k)
    local = heads * HEAD_DIM
    whole = lambda a: pl.BlockSpec(a.shape, lambda i, f: (0,) * a.ndim)
    by_rows = lambda n: pl.BlockSpec((tall, n), lambda i, f: (i, 0))
    q_spec = pl.BlockSpec((heads, tall, LANES), lambda i, f: (0, i, 0))
    return pl.pallas_call(
        functools.partial(backward_kernel, heads, segments, block),
        grid_spec=pltpu.PrefetchScalarGridSpec(
            num_scalar_prefetch=1,
            grid=(rows // tall,),
            in_specs=[
                q_spec,
                pl.BlockSpec((tall, width), first_blocks(steps)),
                pl.BlockSpec((tall, width), last_blocks(steps)),
                whole(w),
                by_rows(local),
                whole(k_aug),
                whole(v_aug),
                by_rows(LANES),
                by_rows(LANES),
            ]
            + [whole(t) for t in cos_k]
            + [whole(t) for t in sin_k],
            out_specs=[by_rows(local)]
            + [pl.BlockSpec((t.shape[0], 2 * local), lambda i, f: (0, 0)) for t in cos_k],
            scratch_shapes=[
                pltpu.VMEM((heads, LANES, keys), bf16),
                pltpu.VMEM((heads, keys, LANES), f32),
                pltpu.VMEM((heads, keys, LANES), f32),
                pltpu.VMEM((heads, LANES, tall), f32),
                pltpu.VMEM((heads, tall, LANES), bf16),
            ],
        ),
        out_shape=[jax.ShapeDtypeStruct((rows, local), bf16)]
        + [jax.ShapeDtypeStruct((t.shape[0], 2 * local), bf16) for t in cos_k],
        cost_estimate=pl.CostEstimate(
            flops=5 * rows * keys * heads * LANES, bytes_accessed=16 * keys * local, transcendentals=rows * keys * heads // 2
        ),
        name="attend_backward",
    )(flags, q_aug, *ga, w, o, k_aug, v_aug, cos_q, sin_q, *cos_k, *sin_k)


def feed_kernel(chunk, c_first, c_last, g_ref, up_ref, down_ref, shift_ref, z_ref, gu_ref, gc_first, gc_last, feed_first, feed_last, sum_ref):
    step = pl.program_id(0)
    c = jnp.where(step < pl.num_programs(0) // 2, c_first[...], c_last[...])
    g = g_ref[...]
    gc, feed, sums = 0.0, 0.0, []
    for begin in range(0, up_ref.shape[1], chunk):
        cut = slice(begin, begin + chunk)
        u = mm(c, up_ref[:, cut]) + shift_ref[0:1, cut]
        sg = 0.5 + 0.5 * jnp.tanh(0.851 * u)
        z = (u * sg).astype(bf16)
        gu = (mm(g, down_ref[:, cut]) * (sg + 1.702 * u * sg * (1.0 - sg))).astype(bf16)
        z_ref[:, cut] = z
        gu_ref[:, cut] = gu
        gc = gc + mm(gu, up_ref[:, cut], NT)
        feed = feed + mm(z, down_ref[:, cut], NT)
        sums.append(jnp.sum(gu.astype(f32), axis=0, keepdims=True))
    store_halves(gc_first, gc_last, gc.astype(bf16))
    store_halves(feed_first, feed_last, feed.astype(bf16))

    @pl.when(step == 0)
    def clear():
        sum_ref[...] = jnp.zeros(sum_ref.shape, f32)

    sum_ref[0:1, :] += jnp.concatenate(sums, axis=1)
    sum_ref[1:2, : g.shape[1]] += jnp.sum(g.astype(f32), axis=0, keepdims=True)


def feed_forward(c, g, w_up, w_down, shift):
    rows, width = g.shape
    hidden = w_up.shape[1]
    tall = min(512, rows // 2)
    steps = rows // tall
    chunk = 256 if hidden % 256 == 0 else hidden
    by_rows = lambda n: pl.BlockSpec((tall, n), lambda i: (i, 0))
    whole = lambda a: pl.BlockSpec(a.shape, lambda i: (0,) * a.ndim)
    first = pl.BlockSpec((tall, width), first_blocks(steps))
    last = pl.BlockSpec((tall, width), last_blocks(steps))
    part = jax.ShapeDtypeStruct((rows // 2, width), bf16)
    longest = max(width, hidden)
    return pl.pallas_call(
        functools.partial(feed_kernel, chunk),
        grid=(steps,),
        in_specs=[first, last, by_rows(width), whole(w_up), whole(w_down), whole(shift)],
        out_specs=[by_rows(hidden), by_rows(hidden), first, last, first, last, pl.BlockSpec((8, longest), lambda i: (0, 0))],
        out_shape=[
            jax.ShapeDtypeStruct((rows, hidden), bf16),
            jax.ShapeDtypeStruct((rows, hidden), bf16),
            part,
            part,
            part,
            part,
            jax.ShapeDtypeStruct((8, longest), f32),
        ],
        cost_estimate=pl.CostEstimate(
            flops=8 * rows * width * hidden, bytes_accessed=4 * width * hidden + 12 * rows * width, transcendentals=rows * hidden
        ),
        name="feed_forward",
    )(*c, g, w_up, w_down, shift)


def back_kernel(pieces, x_ref, w_ref, gq_ref, *refs):
    kv_refs = refs[:pieces]
    p_first, p_last, dkv_ref, sum_ref = refs[pieces:]
    gq = gq_ref[...]
    if pieces == 1:
        dkv = kv_refs[0][...]
    else:
        other = jnp.where(pl.program_id(0) < pl.num_programs(0) // 2, kv_refs[1][...], kv_refs[2][...])
        dkv = (kv_refs[0][...].astype(f32) + other.astype(f32)).astype(bf16)
    dkv_ref[...] = dkv
    tail = jnp.zeros((gq.shape[0], w_ref.shape[1] - gq.shape[1] - dkv.shape[1]), bf16)
    e = mm(jnp.concatenate([gq, dkv, tail], axis=1), w_ref[...], NT)
    store_halves(p_first, p_last, e.astype(bf16))
    x = x_ref[...].astype(f32)
    center = x - jnp.mean(x, axis=1, keepdims=True)
    unit = center * lax.rsqrt(jnp.mean(center * center, axis=1, keepdims=True) + norm_eps)

    @pl.when(pl.program_id(0) == 0)
    def clear():
        sum_ref[...] = jnp.zeros(sum_ref.shape, f32)

    local = gq.shape[1]
    sum_ref[0:1, :] += jnp.sum(e * unit, axis=0, keepdims=True)
    sum_ref[1:2, :] += jnp.sum(e, axis=0, keepdims=True)
    sum_ref[2:3, :local] += jnp.sum(gq.astype(f32), axis=0, keepdims=True)
    sum_ref[3:4, : 2 * local] += jnp.sum(dkv.astype(f32), axis=0, keepdims=True)


def project_back(x, w, gq, dkvs):
    rows, width = x.shape
    local = gq.shape[1]
    tall = min(512, rows // 2)
    steps = rows // tall
    by_rows = lambda n: pl.BlockSpec((tall, n), lambda i: (i, 0))
    whole = lambda a: pl.BlockSpec(a.shape, lambda i: (0,) * a.ndim)
    part = jax.ShapeDtypeStruct((rows // 2, width), bf16)
    kv_specs = [
        by_rows(2 * local),
        pl.BlockSpec((tall, 2 * local), first_blocks(steps)),
        pl.BlockSpec((tall, 2 * local), last_blocks(steps)),
    ]
    return pl.pallas_call(
        functools.partial(back_kernel, len(dkvs)),
        grid=(steps,),
        in_specs=[by_rows(width), whole(w), by_rows(local)] + kv_specs[: len(dkvs)],
        out_specs=[
            pl.BlockSpec((tall, width), first_blocks(steps)),
            pl.BlockSpec((tall, width), last_blocks(steps)),
            by_rows(2 * local),
            pl.BlockSpec((8, width), lambda i: (0, 0)),
        ],
        out_shape=[part, part, jax.ShapeDtypeStruct((rows, 2 * local), bf16), jax.ShapeDtypeStruct((8, width), f32)],
        cost_estimate=pl.CostEstimate(
            flops=6 * rows * width * local, bytes_accessed=6 * width * local + 6 * rows * width, transcendentals=rows
        ),
        name="project_back",
    )(x, w, gq, *dkvs)


def norm_stats(rows_in):
    center = rows_in - jnp.mean(rows_in, axis=1, keepdims=True)
    inverse = lax.rsqrt(jnp.mean(center * center, axis=1, keepdims=True) + norm_eps)
    return center * inverse, inverse


def norm_backward(grad_rows, unit_rows, inverse, gain):
    scaled = grad_rows * gain
    return inverse * (
        scaled
        - jnp.mean(scaled, axis=1, keepdims=True)
        - unit_rows * jnp.mean(scaled * unit_rows, axis=1, keepdims=True)
    )


def norm_two_kernel(x_ref, near_ref, far_ref, vec_ref, h_ref, c_ref):
    h = x_ref[...].astype(f32) + (near_ref[...].astype(f32) + far_ref[...].astype(f32)) + vec_ref[0:1, :]
    h_ref[...] = h
    c_ref[...] = (norm_stats(h)[0] * vec_ref[1:2, :] + vec_ref[2:3, :]).astype(bf16)


def norm_two_back_kernel(h_ref, near_ref, far_ref, g_ref, vec_ref, gh_ref, ga_ref, sum_ref):
    unit, inverse = norm_stats(h_ref[...])
    gc = near_ref[...].astype(f32) + far_ref[...].astype(f32)
    gh = g_ref[...].astype(f32) + norm_backward(gc, unit, inverse, vec_ref[1:2, :])
    ga = gh.astype(bf16)
    gh_ref[...] = gh
    ga_ref[...] = ga

    @pl.when(pl.program_id(0) == 0)
    def clear():
        sum_ref[...] = jnp.zeros(sum_ref.shape, f32)

    sum_ref[0:1, :] += jnp.sum(gc * unit, axis=0, keepdims=True)
    sum_ref[1:2, :] += jnp.sum(gc, axis=0, keepdims=True)
    sum_ref[2:3, :] += jnp.sum(ga.astype(f32), axis=0, keepdims=True)


def norm_one_back_kernel(x_ref, near_ref, far_ref, gh_ref, vec_ref, out_ref):
    unit, inverse = norm_stats(x_ref[...].astype(f32))
    ga1 = near_ref[...].astype(f32) + far_ref[...].astype(f32)
    out_ref[...] = (gh_ref[...] + norm_backward(ga1, unit, inverse, vec_ref[0:1, :])).astype(bf16)


def close_kernel(h_ref, near_ref, far_ref, live_ref, vec_ref, out_ref):
    feed = near_ref[...].astype(f32) + far_ref[...].astype(f32)
    out_ref[...] = ((h_ref[...] + feed + vec_ref[0:1, :]) * live_ref[...]).astype(bf16)


def by_tokens(body, arrays, vectors, kinds, name, sums=False):
    count, width = arrays[1].shape
    tall = min(256, count)
    in_specs = [pl.BlockSpec((tall, a.shape[1]), lambda i: (i, 0)) for a in arrays]
    out_specs = [pl.BlockSpec((tall, width), lambda i: (i, 0)) for _ in kinds]
    out_shape = [jax.ShapeDtypeStruct((count, width), kind) for kind in kinds]
    if sums:
        out_specs.append(pl.BlockSpec((8, width), lambda i: (0, 0)))
        out_shape.append(jax.ShapeDtypeStruct((8, width), f32))
    return pl.pallas_call(
        body,
        grid=(count // tall,),
        in_specs=in_specs + [pl.BlockSpec(vectors.shape, lambda i: (0, 0))],
        out_specs=out_specs,
        out_shape=out_shape,
        cost_estimate=pl.CostEstimate(flops=20 * count * width, bytes_accessed=14 * count * width, transcendentals=count),
        name=name,
    )(*arrays, vectors)


def gather_rows_kernel(side_ref, *refs):
    step = pl.program_id(0)
    for index, piece in enumerate(refs[:-1]):

        @pl.when(step == index)
        def copy(piece=piece):
            refs[-1][0] = piece[...]


def gather_rows(side, pieces):
    half, width = pieces[0].shape
    count = len(pieces)
    return pl.pallas_call(
        gather_rows_kernel,
        grid_spec=pltpu.PrefetchScalarGridSpec(
            num_scalar_prefetch=1,
            grid=(count,),
            in_specs=[pl.BlockSpec((half, width), lambda t, s: (0, 0)) for _ in pieces],
            out_specs=pl.BlockSpec((1, half, width), lambda t, s: (t // 2, jnp.where(t % 2 == 0, s[0], 1 - s[0]), 0)),
        ),
        out_shape=jax.ShapeDtypeStruct((count // 2, 2 * half, width), bf16),
        cost_estimate=pl.CostEstimate(flops=0, bytes_accessed=4 * count * half * width, transcendentals=0),
        name="gather_rows",
    )(side, *pieces)


def tables(grid_pos):
    lane = jnp.arange(LANES)
    quarter = HEAD_DIM // 4
    frequency = jnp.power(10000.0, -4.0 * (lane % quarter).astype(f32) / HEAD_DIM)
    place = jnp.where((lane // quarter) % 2 == 0, grid_pos[0][:, None], grid_pos[1][:, None])
    angle = jnp.where(lane < HEAD_DIM, place.astype(f32) * frequency, 0.0)
    return jnp.cos(angle), jnp.where(lane < HEAD_DIM // 2, -1.0, 1.0) * jnp.sin(angle)


def query_features(ids):
    lane = jnp.arange(LANES)
    return (lane == HEAD_DIM + 1 + ids[:, None]).astype(bf16)


def key_features(ids):
    lane = jnp.arange(LANES)
    slot = lane - HEAD_DIM
    same = (slot >= 1) & (slot == ids[:, None] + 1)
    wall = jnp.where((slot >= 0) & (slot < 16) & ~same, -hide, 0.0)
    return jnp.where((lane >= 96) & (lane < 99), -1.0, wall).astype(bf16)


def visit_flags(query_ids, key_ids, tall, block):
    q = query_ids.reshape(-1, tall)
    k = key_ids.reshape(-1, block)
    q_top, k_top = jnp.max(q, axis=1), jnp.max(k, axis=1)
    q_low = jnp.min(jnp.where(q >= 0, q, 1 << 20), axis=1)
    k_low = jnp.min(jnp.where(k >= 0, k, 1 << 20), axis=1)
    meet = (q_low[:, None] <= k_top[None, :]) & (k_low[None, :] <= q_top[:, None])
    return meet.astype(jnp.int32).reshape(-1)


def on_device(
    patches,
    cotangent,
    picture_ids,
    positions,
    ln1_gain,
    ln1_bias,
    qkv_weight,
    qkv_bias,
    proj_weight,
    proj_bias,
    ln2_gain,
    ln2_bias,
    fc1_weight,
    fc1_bias,
    fc2_weight,
    fc2_bias,
):
    row_count, row_share, width = patches.shape
    owners = lax.axis_size("shard")
    contexts = lax.axis_size("ctx")
    ways = lax.axis_size("tp")
    part = qkv_weight.shape[0]
    local = qkv_weight.shape[2]
    heads = local // HEAD_DIM
    half = row_share // 2
    side = lax.axis_index("tp") % 2
    context = lax.axis_index("ctx")
    pairs_near = [(i, i ^ 1) for i in range(ways)]
    pairs_far = [(i, i ^ 2) for i in range(ways)]
    pad = -3 * local % 256
    wide = 3 * local + pad

    def near(v):
        return lax.ppermute(v, "tp", pairs_near)

    def far(v):
        return lax.ppermute(v, "tp", pairs_far)

    def over_ctx(v):
        return lax.ppermute(v, "ctx", [(0, 1), (1, 0)])

    def mine_first(v, axis=0):
        return jnp.where(side == 0, v, jnp.roll(v, half, axis=axis))

    def column(v):
        flat = v.reshape(-1)
        return jnp.pad(flat, (0, part - flat.shape[0]))

    vectors = [ln1_gain, ln1_bias, ln2_gain, ln2_bias, proj_bias, fc2_bias, qkv_bias, fc1_bias]
    tail = jnp.stack([column(v) for v in vectors], axis=1)
    tail = jnp.pad(tail, ((0, 0), (0, pad - len(vectors))))
    qkv_piece = jnp.concatenate([qkv_weight.reshape(part, 3 * local), tail], axis=1).astype(bf16)
    gather = lambda v: lax.all_gather(v, "shard", axis=0, tiled=True)
    up_piece = fc1_weight.astype(bf16)
    down_piece = fc2_weight.T.astype(bf16)
    proj_piece = proj_weight.T.astype(bf16)
    place = lax.axis_index("shard")
    context_first = context == 0

    w_qkv = gather(qkv_piece)
    proj_piece = tie(proj_piece, w_qkv)
    w_proj = jnp.zeros((owners,) + proj_piece.shape, bf16)
    w_proj = lax.dynamic_update_index_in_dim(w_proj, proj_piece, place, 0)
    for step in range(1, owners):
        got = lax.ppermute(proj_piece, "shard", [(i, (i + step) % owners) for i in range(owners)])
        w_proj = lax.dynamic_update_index_in_dim(w_proj, got, (place - step) % owners, 0)
    w_proj = w_proj.reshape(owners * part, local)
    packed = w_qkv[:, 3 * local : 3 * local + len(vectors)].T.astype(f32)
    gain_one, bias_one, gain_two, bias_two, proj_shift, down_shift = [packed[i] for i in range(6)]
    qb_size = qkv_bias.size
    qkv_shift = packed[6].reshape(owners, part)[:, :qb_size].reshape((owners,) + qkv_bias.shape)
    qkv_shift = jnp.transpose(qkv_shift, (1, 2, 0, 3)).reshape(-1)
    qkv_shift = jnp.pad(qkv_shift, (0, pad)).reshape(1, wide)
    up_shift = packed[7].reshape(owners, part)[:, : fc1_bias.size].reshape((owners,) + fc1_bias.shape)
    up_shift = jnp.transpose(up_shift, (1, 0, 2)).reshape(1, -1)
    ln_one = tie(packed[0:2], up_piece, down_piece)

    ids_by_ctx = mine_first(picture_ids.reshape(row_count, contexts, row_share), axis=2)
    places = mine_first(positions, axis=2)
    block = min(256, half)

    def cut_last(spots):
        return [spots[0], spots[1][:half], spots[1][half:]] if contexts == 2 else spots

    key_block = 256
    rows = []
    for r in range(row_count):
        x = mine_first(patches[r])
        g = mine_first(cotangent[r])
        ids = lax.dynamic_index_in_dim(ids_by_ctx[r], context, 0, keepdims=False)
        if contexts == 2:
            other = lax.dynamic_index_in_dim(ids_by_ctx[r], 1 - context, 0, keepdims=False)
            key_ids = [ids, other]
            spots = [places[:, r], over_ctx(places[:, r])]
        else:
            key_ids = [ids_by_ctx[r].reshape(-1)]
            spots = [lax.all_gather(places[:, r], "ctx", axis=1, tiled=True)]
        live = (ids >= 0).astype(f32)[:, None]
        turns = [tables(spot) for spot in spots]
        own_turn = turns[0] if contexts == 2 else tables(places[:, r])
        rows.append(
            dict(
                x=x,
                g=(g.astype(f32) * live).astype(bf16),
                live=live,
                ids=ids,
                cos=own_turn[0],
                sin=own_turn[1],
                cos_k=cut_last([t[0] for t in turns]),
                sin_k=cut_last([t[1] for t in turns]),
                q_feat=query_features(ids),
                k_feat=[key_features(k) for k in key_ids],
                flags=visit_flags(ids, jnp.concatenate(key_ids), block, key_block),
            )
        )

    for row in rows:
        row["a"], row["q"], row["kv"] = project_row(
            row["x"], w_qkv, ln_one, qkv_shift, row["cos"], row["sin"], row["q_feat"], heads
        )
        if row is rows[0]:
            row["kv"], w_proj = lax.optimization_barrier((row["kv"], w_proj))
        if contexts == 2:
            row["kvs"] = [row["kv"], over_ctx(row["kv"])]
        else:
            row["kvs"] = [lax.all_gather(row["kv"], "ctx", axis=0, tiled=True)]

    down_piece, up_piece = lax.optimization_barrier((down_piece, up_piece, w_proj))[:2]
    if contexts == 2:
        down_cut = down_piece.reshape(2, part // 2, -1)
        down_near = gather(lax.dynamic_index_in_dim(down_cut, context, 0, keepdims=False))
        down_near = down_near.reshape(owners, part // 2, -1)
    else:
        w_down = gather(down_piece)
    w_up = gather(up_piece)

    def sum_near(first, last):
        return (first.astype(f32) + near(last).astype(f32)).astype(bf16)

    norm_vectors = jnp.pad(jnp.stack([proj_shift, gain_two, bias_two]), ((0, 5), (0, 0)))

    def norm_two(row, vectors):
        row["h"], mine = by_tokens(
            norm_two_kernel, [row["x"], row["branch"], row["branch_far"]], vectors, [f32, bf16], "norm_two"
        )
        row["c"] = (mine, near(mine))

    hold = lax.optimization_barrier
    before = rows[-1]["kv"]
    for index, row in enumerate(rows):
        row["o"], row["q"], row["k_aug"], row["v_aug"], first, last = attend_forward(
            tie(row["flags"], before), row["q"], w_proj, row["kvs"], row["k_feat"], heads, key_block
        )
        if index:
            prior = rows[index - 1]
            first, last, prior["branch_far"] = hold((first, last, prior["branch_far"]))
        if index + 1 < row_count:
            follow = rows[index + 1]
            first, last, follow["kvs"] = hold((first, last, follow["kvs"]))
            if contexts == 2:
                first, last, down_near = hold((first, last, down_near))
                down_far = over_ctx(down_near)
        elif contexts == 2:
            first, last, down_far, w_up = hold((first, last, down_far, w_up))
        before = row["branch"] = sum_near(first, last)
        row["branch_far"] = far(before)
    if contexts == 2:
        low = jnp.where(context_first, down_near, down_far)
        high = jnp.where(context_first, down_far, down_near)
        w_down = jnp.concatenate([low, high], axis=1).reshape(owners * part, -1)

    norm_two(rows[0], tie(norm_vectors, before))
    for index, row in enumerate(rows):
        shift = tie(up_shift, before)
        row["z"], row["gu"], gc_first, gc_last, feed_first, feed_last, row["feed_sums"] = feed_forward(
            row["c"], row["g"], w_up, w_down, shift
        )
        other, key = (rows[-1], "branch_far") if index == 0 else (rows[index - 1], "gc_far")
        gc_first, gc_last, other[key] = hold((gc_first, gc_last, other[key]))
        before = row["gc"] = sum_near(gc_first, gc_last)
        row["gc_far"] = far(before)
        row["feed"] = (feed_first, feed_last)
        if index + 1 < row_count:
            norm_two(rows[index + 1], norm_vectors)
    for row in rows:
        row["feed"] = sum_near(*row["feed"])

    join = lambda key: jnp.concatenate([row[key] for row in rows], axis=0)
    join_two = lambda key: jnp.concatenate([piece for row in rows for piece in row[key]], axis=0)
    scatter = lambda v: lax.psum_scatter(v, "shard", scatter_dimension=0, tiled=True)
    if contexts == 2:
        finish = lambda v: v.astype(f32) + over_ctx(v).astype(f32)
    else:
        finish = lambda v: lax.psum(v, "ctx").astype(f32)
    last_row = rows[-1]
    last_row["gu"], last_row["z"] = hold((last_row["gu"], last_row["z"], before))[:2]
    grad_up = mm(join_two("c"), join("gu"), TN).astype(bf16)
    grad_down = mm(join("g"), join("z"), TN).astype(bf16)
    grad_up, grad_down, last_row["gc_far"] = hold((grad_up, grad_down, last_row["gc_far"]))
    before = (grad_up, grad_down)
    y_free = last_row["gc_far"]
    grad_up = scatter(grad_up)
    grad_down = scatter(grad_down)

    pair = 0.0
    for row in rows:
        row["gh"], ga, norm_sums = by_tokens(
            norm_two_back_kernel,
            [row["h"], row["gc"], row["gc_far"], row["g"]],
            norm_vectors,
            [f32, bf16],
            "norm_two_back",
            sums=True,
        )
        pair = pair + norm_sums[0:3]
        row["ga"] = (ga, near(ga))
    grad_proj = mm(join_two("ga"), join("o"), TN).astype(bf16)
    for index, row in enumerate(rows):
        feed_far = far(tie(row["feed"], y_free))
        out = attend_backward(
            tie(row["flags"], *before),
            row["q"],
            row["ga"],
            w_proj,
            row["o"],
            row["k_aug"],
            row["v_aug"],
            row["cos"],
            row["sin"],
            row["cos_k"],
            row["sin_k"],
            heads,
            key_block,
        )
        if index:
            prior = rows[index - 1]
            *out, feed_far, prior["dkvs"], grad_up = hold((*out, feed_far, prior["dkvs"], grad_up))
        else:
            *out, feed_far = hold((*out, feed_far))
        y_free = feed_far
        before = (out[0], grad_proj)
        row["gq"] = out[0]
        row["feed_far"] = feed_far
        if contexts == 2:
            row["dkvs"] = [out[1], over_ctx(out[2]), over_ctx(out[3])]
        else:
            row["dkvs"] = [lax.psum_scatter(out[1], "ctx", scatter_dimension=0, tiled=True)]

    grad_proj = scatter(grad_proj)
    sums = 0.0
    for index, row in enumerate(rows):
        first, last, row["dkv"], back_sums = project_back(row["x"], w_qkv, tie(row["gq"], *before), row["dkvs"])
        sums = sums + back_sums
        before = (row["dkv"],)
        if index == 0:
            kvs = last_row["dkvs"]
            first, last, row["dkv"], kvs[:-1] = hold((first, last, row["dkv"], kvs[:-1]))
            last_row["gq"] = tie(last_row["gq"], row["dkv"])
            grad_q = mm(join("a"), join("gq"), TN).astype(bf16)
            grad_q, grad_down, kvs[-1] = hold((grad_q, grad_down, kvs[-1]))
            grad_q = scatter(grad_q)
            before = (row["dkv"], kvs[-1])
        else:
            prior = rows[index - 1]
            first, last, prior["ga1_far"], grad_proj = hold((first, last, prior["ga1_far"], grad_proj))
        row["ga1"] = sum_near(first, last)
        row["ga1_far"] = far(row["ga1"])
    grad_kv = mm(join("a"), join("dkv"), TN).astype(bf16)
    grad_kv, grad_q = hold((grad_kv, grad_q))
    grad_kv = scatter(grad_kv)
    grad_up, grad_down, grad_q, grad_proj = [finish(v) for v in (grad_up, grad_down, grad_q, grad_proj)]

    def sum_over(v, axis):
        size, step = lax.axis_size(axis), 1
        while step < size:
            v = v + lax.ppermute(v, axis, [(i, i ^ step) for i in range(size)])
            step *= 2
        return v

    def owned(v):
        v = v.reshape(owners, -1)
        return jnp.pad(v, ((0, 0), (0, part - v.shape[1]))).reshape(-1)

    feed_sums = sum(row["feed_sums"] for row in rows)
    d_qb = jnp.concatenate([sums[2, :local], sums[3, : 2 * local]]).reshape(3, heads, owners, -1)
    d_qb = owned(jnp.transpose(d_qb, (2, 0, 1, 3)))
    d_ub = feed_sums[0, : fc1_bias.size * owners].reshape(fc1_bias.shape[0], owners, fc1_bias.shape[1])
    d_ub = owned(jnp.transpose(d_ub, (1, 0, 2)))
    vector = jnp.concatenate(
        [pair + near(pair), feed_sums[1:2, :width], d_qb[None], d_ub[None], sum_over(sums[0:2], "tp")], axis=0
    )
    vector = sum_over(sum_over(vector, "ctx"), "shard")
    vector = lax.dynamic_slice_in_dim(vector, place * part, part, axis=1)

    side_list = side.reshape(1).astype(jnp.int32)
    outs, ins = [], []
    for row in rows:
        mine = by_tokens(
            close_kernel,
            [row["h"], row["feed"], row["feed_far"], row["live"]],
            jnp.broadcast_to(down_shift, (8, width)),
            [bf16],
            "close",
        )[0]
        outs += [mine, near(mine)]
    outs = gather_rows(side_list, outs)
    for row in rows:
        mine = by_tokens(
            norm_one_back_kernel,
            [row["x"], row["ga1"], row["ga1_far"], row["gh"]],
            jnp.broadcast_to(gain_one, (8, width)),
            [bf16],
            "norm_one_back",
        )[0]
        ins += [mine, near(mine)]
    ins = gather_rows(side_list, ins)
    grad_kv = finish(tie(grad_kv, outs, ins, grad_up, grad_down, grad_q, grad_proj, vector))
    return (
        outs,
        ins,
        vector[6],
        vector[7],
        jnp.concatenate([grad_q, grad_kv], axis=1).reshape(qkv_weight.shape),
        vector[4, :qb_size].reshape(qkv_bias.shape),
        grad_proj.T,
        vector[2],
        vector[0],
        vector[1],
        grad_up,
        vector[5, : fc1_bias.size].reshape(fc1_bias.shape),
        grad_down.T,
        vector[3],
    )


def solution(mesh):
    in_specs = (
        P("shard", "ctx", None),
        P("shard", "ctx", None),
        P("shard", None),
        P(None, "shard", "ctx"),
        P("shard"),
        P("shard"),
        P("shard", None, "tp"),
        P(None, "tp", "shard"),
        P("tp", "shard"),
        P("shard"),
        P("shard"),
        P("shard"),
        P("shard", "tp"),
        P("tp", "shard"),
        P("tp", "shard"),
        P("shard"),
    )
    out_specs = (
        P("shard", "ctx", None),
        P("shard", "ctx", None),
        P("shard"),
        P("shard"),
        P("shard", None, "tp"),
        P(None, "tp", "shard"),
        P("tp", "shard"),
        P("shard"),
        P("shard"),
        P("shard"),
        P("shard", "tp"),
        P("tp", "shard"),
        P("tp", "shard"),
        P("shard"),
    )
    return jax.shard_map(
        on_device, mesh=mesh, in_specs=in_specs, out_specs=out_specs, check_vma=False
    )
```

```python
import functools
import math

import jax
import jax.numpy as jnp
from jax import lax
from jax.experimental import pallas as pl
from jax.experimental.pallas import tpu as pltpu
from jax.sharding import PartitionSpec as P

HEAD_DIM = 80
LANES = 128
norm_eps = 1e-06
hide = 1e30
floor_max = -1e29
log2e = math.log2(math.e)
bf16 = jnp.bfloat16
f32 = jnp.float32
NT = (((1,), (1,)), ((), ()))
NN = (((1,), (0,)), ((), ()))
TN = (((0,), (0,)), ((), ()))


def mm(a, b, dims=NN):
    return lax.dot_general(a, b, dims, preferred_element_type=f32)


def tie(value, *others):
    return lax.optimization_barrier((value,) + others)[0]


def first_blocks(steps):
    return lambda i, *_: (jnp.minimum(i, steps // 2 - 1), 0)


def last_blocks(steps):
    return lambda i, *_: (jnp.maximum(i - steps // 2, 0), 0)


def store_halves(first_ref, last_ref, value):
    step, split = pl.program_id(0), pl.num_programs(0) // 2

    @pl.when(step < split)
    def first():
        first_ref[...] = value

    @pl.when(step >= split)
    def last():
        last_ref[...] = value


def lane_index(rows):
    return lax.broadcasted_iota(jnp.int32, (rows, LANES), 1)


def swap_halves(w, lane):
    half = HEAD_DIM // 2
    up = pltpu.roll(w, LANES - half, 1)
    down = pltpu.roll(w, half, 1)
    return jnp.where(lane < half, up, down)


def widen(piece):
    rows = piece.shape[0]
    tail = jnp.zeros((rows, LANES - piece.shape[1]), piece.dtype)
    return jnp.concatenate([piece, tail], axis=1)


def split_three(column):
    high = column.astype(bf16).astype(f32)
    rest = column - high
    mid = rest.astype(bf16).astype(f32)
    return high, mid, rest - mid


def place_three(base, column, lane):
    high, mid, low = split_three(column)
    base = jnp.where(lane == 96, high, base)
    base = jnp.where(lane == 97, mid, base)
    return jnp.where(lane == 98, low, base)


def qkv_kernel(heads, x_ref, w_ref, ln_ref, b_ref, cos_ref, sin_ref, feat_ref, a_ref, q_ref, kv_ref):
    width = heads * HEAD_DIM
    x = x_ref[...].astype(f32)
    rows = x.shape[0]
    center = x - jnp.mean(x, axis=1, keepdims=True)
    inverse = lax.rsqrt(jnp.mean(center * center, axis=1, keepdims=True) + norm_eps)
    a = (center * inverse * ln_ref[0:1, :] + ln_ref[1:2, :]).astype(bf16)
    a_ref[...] = a
    y = mm(a, w_ref[...]) + b_ref[0:1, :]
    cos, sin = cos_ref[...], sin_ref[...]
    lane = lane_index(rows)
    kv = []
    for h in range(heads):
        w = widen(y[:, h * HEAD_DIM : (h + 1) * HEAD_DIM])
        q = (w * cos + swap_halves(w, lane) * sin) * (HEAD_DIM**-0.5 * log2e)
        q_ref[h] = jnp.where(lane < HEAD_DIM, q.astype(bf16), feat_ref[...])
    for h in range(heads):
        begin = width + h * HEAD_DIM
        w = widen(y[:, begin : begin + HEAD_DIM])
        kv.append((w * cos + swap_halves(w, lane) * sin)[:, :HEAD_DIM].astype(bf16))
    kv.append(y[:, 2 * width : 3 * width].astype(bf16))
    kv_ref[...] = jnp.concatenate(kv, axis=1)


def project_row(x, w, ln, bias, cos, sin, feat, heads):
    rows, width = x.shape
    block = min(256, rows)
    wide = w.shape[1]
    local = heads * HEAD_DIM
    by_rows = lambda n: pl.BlockSpec((block, n), lambda i: (i, 0))
    whole = lambda a: pl.BlockSpec(a.shape, lambda i: (0,) * a.ndim)
    return pl.pallas_call(
        functools.partial(qkv_kernel, heads),
        grid=(rows // block,),
        in_specs=[
            by_rows(width),
            whole(w),
            whole(ln),
            whole(bias),
            by_rows(LANES),
            by_rows(LANES),
            by_rows(LANES),
        ],
        out_specs=[
            by_rows(width),
            pl.BlockSpec((heads, block, LANES), lambda i: (0, i, 0)),
            by_rows(2 * local),
        ],
        out_shape=[
            jax.ShapeDtypeStruct((rows, width), bf16),
            jax.ShapeDtypeStruct((heads, rows, LANES), bf16),
            jax.ShapeDtypeStruct((rows, 2 * local), bf16),
        ],
        cost_estimate=pl.CostEstimate(
            flops=2 * rows * width * wide, bytes_accessed=rows * width * 4 + width * wide * 2, transcendentals=0
        ),
        name="project_row",
    )(x, w, ln, bias, cos, sin, feat)


def forward_kernel(heads, segments, block, flag_ref, q_ref, w_ref, *refs):
    kv_refs = refs[:segments]
    feat_refs = refs[segments : 2 * segments]
    o_ref, q_out, k_aug, v_aug, p_first, p_last, m_scr, acc_scr = refs[2 * segments :]
    width = heads * HEAD_DIM
    step = pl.program_id(0)
    keys = k_aug.shape[1]
    count = keys // block
    rows = q_ref.shape[1]

    @pl.when(step == 0)
    def build():
        offset = 0
        for s in range(segments):
            length = kv_refs[s].shape[0]
            piece = min(length, 256)
            for t in range(length // piece):
                at = pl.ds(t * piece, piece)
                to = pl.ds(offset + t * piece, piece)
                kv = kv_refs[s][at, :]
                feat = feat_refs[s][at, :]
                lane = lane_index(piece)
                tail = jnp.where(lane == HEAD_DIM, 1.0, jnp.where((lane >= 96) & (lane < 99), -1.0, 0.0)).astype(bf16)
                for h in range(heads):
                    k = kv[:, h * HEAD_DIM : (h + 1) * HEAD_DIM]
                    v = kv[:, width + h * HEAD_DIM : width + (h + 1) * HEAD_DIM]
                    k_aug[h, to, :] = jnp.concatenate([k, feat[:, HEAD_DIM:]], axis=1)
                    v_aug[h, to, :] = jnp.concatenate([v, tail[:, HEAD_DIM:]], axis=1)
            offset += length

    m_scr[...] = jnp.full(m_scr.shape, floor_max, f32)
    acc_scr[...] = jnp.zeros(acc_scr.shape, f32)

    def visit(j, carry):
        @pl.when(flag_ref[step * count + j] > 0)
        def go():
            at = pl.ds(pl.multiple_of(j * block, block), block)
            for h in range(heads):
                s = mm(q_ref[h], k_aug[h, at, :], NT)
                old = m_scr[h]
                new = jnp.maximum(old, jnp.max(s, axis=1, keepdims=True))
                p = jnp.exp2(s - new[:, 0:1])
                m_scr[h] = new
                acc_scr[h] = acc_scr[h] * jnp.exp2(old - new) + mm(p.astype(bf16), v_aug[h, at, :])

        return carry

    lax.fori_loop(0, count, visit, 0)
    lane = lane_index(rows)
    outs = []
    for h in range(heads):
        acc = acc_scr[h]
        total = acc[:, HEAD_DIM : HEAD_DIM + 1]
        alive = total > 0.0
        safe = jnp.where(alive, total, 1.0)
        outs.append((acc / safe)[:, :HEAD_DIM].astype(bf16))
        level = jnp.where(alive, m_scr[h][:, 0:1] + jnp.log2(safe), 0.0)
        q_out[h] = place_three(q_ref[h].astype(f32), level, lane).astype(bf16)
    o = jnp.concatenate(outs, axis=1)
    o_ref[...] = o
    store_halves(p_first, p_last, mm(o, w_ref[...], NT).astype(bf16))


def attend_forward(flags, q_aug, w, kvs, feats, heads, block):
    rows = q_aug.shape[1]
    tall = min(256, rows // 2)
    steps = rows // tall
    width = w.shape[0]
    keys = sum(kv.shape[0] for kv in kvs)
    segments = len(kvs)
    whole = lambda a: pl.BlockSpec(a.shape, lambda i, f: (0,) * a.ndim)
    q_spec = pl.BlockSpec((heads, tall, LANES), lambda i, f: (0, i, 0))
    k_spec = pl.BlockSpec((heads, keys, LANES), lambda i, f: (0, 0, 0))
    local = heads * HEAD_DIM
    return pl.pallas_call(
        functools.partial(forward_kernel, heads, segments, block),
        grid_spec=pltpu.PrefetchScalarGridSpec(
            num_scalar_prefetch=1,
            grid=(rows // tall,),
            in_specs=[q_spec, whole(w)] + [whole(kv) for kv in kvs] + [whole(f) for f in feats],
            out_specs=[
                pl.BlockSpec((tall, local), lambda i, f: (i, 0)),
                q_spec,
                k_spec,
                k_spec,
                pl.BlockSpec((tall, width), first_blocks(steps)),
                pl.BlockSpec((tall, width), last_blocks(steps)),
            ],
            scratch_shapes=[
                pltpu.VMEM((heads, tall, LANES), f32),
                pltpu.VMEM((heads, tall, LANES), f32),
            ],
        ),
        out_shape=[
            jax.ShapeDtypeStruct((rows, local), bf16),
            jax.ShapeDtypeStruct((heads, rows, LANES), bf16),
            jax.ShapeDtypeStruct((heads, keys, LANES), bf16),
            jax.ShapeDtypeStruct((heads, keys, LANES), bf16),
            jax.ShapeDtypeStruct((rows // 2, width), bf16),
            jax.ShapeDtypeStruct((rows // 2, width), bf16),
        ],
        cost_estimate=pl.CostEstimate(
            flops=2 * rows * keys * heads * LANES, bytes_accessed=8 * keys * local, transcendentals=rows * keys * heads // 2
        ),
        name="attend_forward",
    )(flags, q_aug, w, *kvs, *feats)


def backward_kernel(
    heads, segments, block, flag_ref, q_ref, ga_first, ga_last, w_ref, o_ref, k_aug, v_aug, cosq_ref, sinq_ref, *refs
):
    cosk_refs = refs[:segments]
    sink_refs = refs[segments : 2 * segments]
    dq_ref = refs[2 * segments]
    dkv_refs = refs[2 * segments + 1 : 3 * segments + 1]
    k_turn, dk_acc, dv_acc, dq_acc, go_scr = refs[3 * segments + 1 :]
    step = pl.program_id(0)
    keys = k_aug.shape[1]
    count = keys // block
    rows = q_ref.shape[1]
    scale = HEAD_DIM**-0.5

    @pl.when(step == 0)
    def build():
        dk_acc[...] = jnp.zeros(dk_acc.shape, f32)
        dv_acc[...] = jnp.zeros(dv_acc.shape, f32)
        for h in range(heads):
            for t in range(count):
                at = pl.ds(t * block, block)
                k_turn[h, :, at] = k_aug[h, at, :].T

    lane = lane_index(rows)
    ga = jnp.where(step < pl.num_programs(0) // 2, ga_first[...], ga_last[...])
    go_all = mm(ga, w_ref[...]).astype(bf16).astype(f32)
    for h in range(heads):
        cut = slice(h * HEAD_DIM, (h + 1) * HEAD_DIM)
        go = go_all[:, cut]
        delta = jnp.sum(go * o_ref[:, cut].astype(f32), axis=1, keepdims=True)
        go_scr[h] = place_three(widen(go), delta, lane).astype(bf16)
    dq_acc[...] = jnp.zeros(dq_acc.shape, f32)

    def visit(j, carry):
        @pl.when(flag_ref[step * count + j] > 0)
        def run():
            at = pl.ds(pl.multiple_of(j * block, block), block)
            for h in range(heads):
                q, go = q_ref[h], go_scr[h]
                p = jnp.exp2(mm(k_aug[h, at, :], q, NT))
                ds = (p * mm(v_aug[h, at, :], go, NT)).astype(bf16)
                dv_acc[h, at, :] += mm(p.astype(bf16), go)
                dk_acc[h, at, :] += mm(ds, q)
                dq_acc[h] += mm(k_turn[h, :, at], ds)

        return carry

    lax.fori_loop(0, count, visit, 0)

    def turn_back(w, cos, sin, index):
        return w * cos - swap_halves(w, index) * sin

    outs = []
    for h in range(heads):
        w = dq_acc[h].T
        back = turn_back(w, cosq_ref[...], sinq_ref[...], lane) * scale
        outs.append(back[:, :HEAD_DIM].astype(bf16))
    dq_ref[...] = jnp.concatenate(outs, axis=1)

    @pl.when(step == pl.num_programs(0) - 1)
    def finish():
        offset = 0
        for s in range(segments):
            length = dkv_refs[s].shape[0]
            piece = min(length, 256)
            index = lane_index(piece)
            for t in range(length // piece):
                at = pl.ds(t * piece, piece)
                of = pl.ds(offset + t * piece, piece)
                parts = []
                for h in range(heads):
                    w = dk_acc[h, of, :]
                    back = turn_back(w, cosk_refs[s][at, :], sink_refs[s][at, :], index) * (1.0 / log2e)
                    parts.append(back[:, :HEAD_DIM].astype(bf16))
                for h in range(heads):
                    parts.append(dv_acc[h, of, :][:, :HEAD_DIM].astype(bf16))
                dkv_refs[s][at, :] = jnp.concatenate(parts, axis=1)
            offset += length


def attend_backward(flags, q_aug, ga, w, o, k_aug, v_aug, cos_q, sin_q, cos_k, sin_k, heads, block):
    rows = q_aug.shape[1]
    tall = min(256, rows // 2)
    steps = rows // tall
    width = w.shape[0]
    keys = k_aug.shape[1]
    segments = len(cos_k)
    local = heads * HEAD_DIM
    whole = lambda a: pl.BlockSpec(a.shape, lambda i, f: (0,) * a.ndim)
    by_rows = lambda n: pl.BlockSpec((tall, n), lambda i, f: (i, 0))
    q_spec = pl.BlockSpec((heads, tall, LANES), lambda i, f: (0, i, 0))
    return pl.pallas_call(
        functools.partial(backward_kernel, heads, segments, block),
        grid_spec=pltpu.PrefetchScalarGridSpec(
            num_scalar_prefetch=1,
            grid=(rows // tall,),
            in_specs=[
                q_spec,
                pl.BlockSpec((tall, width), first_blocks(steps)),
                pl.BlockSpec((tall, width), last_blocks(steps)),
                whole(w),
                by_rows(local),
                whole(k_aug),
                whole(v_aug),
                by_rows(LANES),
                by_rows(LANES),
            ]
            + [whole(t) for t in cos_k]
            + [whole(t) for t in sin_k],
            out_specs=[by_rows(local)]
            + [pl.BlockSpec((t.shape[0], 2 * local), lambda i, f: (0, 0)) for t in cos_k],
            scratch_shapes=[
                pltpu.VMEM((heads, LANES, keys), bf16),
                pltpu.VMEM((heads, keys, LANES), f32),
                pltpu.VMEM((heads, keys, LANES), f32),
                pltpu.VMEM((heads, LANES, tall), f32),
                pltpu.VMEM((heads, tall, LANES), bf16),
            ],
        ),
        out_shape=[jax.ShapeDtypeStruct((rows, local), bf16)]
        + [jax.ShapeDtypeStruct((t.shape[0], 2 * local), bf16) for t in cos_k],
        cost_estimate=pl.CostEstimate(
            flops=5 * rows * keys * heads * LANES, bytes_accessed=16 * keys * local, transcendentals=rows * keys * heads // 2
        ),
        name="attend_backward",
    )(flags, q_aug, *ga, w, o, k_aug, v_aug, cos_q, sin_q, *cos_k, *sin_k)


def feed_kernel(chunk, c_first, c_last, g_ref, up_ref, down_ref, shift_ref, z_ref, gu_ref, gc_first, gc_last, feed_first, feed_last, sum_ref):
    step = pl.program_id(0)
    c = jnp.where(step < pl.num_programs(0) // 2, c_first[...], c_last[...])
    g = g_ref[...]
    gc, feed, sums = 0.0, 0.0, []
    for begin in range(0, up_ref.shape[1], chunk):
        cut = slice(begin, begin + chunk)
        u = mm(c, up_ref[:, cut]) + shift_ref[0:1, cut]
        sg = 0.5 + 0.5 * jnp.tanh(0.851 * u)
        z = (u * sg).astype(bf16)
        gu = (mm(g, down_ref[:, cut]) * (sg + 1.702 * u * sg * (1.0 - sg))).astype(bf16)
        z_ref[:, cut] = z
        gu_ref[:, cut] = gu
        gc = gc + mm(gu, up_ref[:, cut], NT)
        feed = feed + mm(z, down_ref[:, cut], NT)
        sums.append(jnp.sum(gu.astype(f32), axis=0, keepdims=True))
    store_halves(gc_first, gc_last, gc.astype(bf16))
    store_halves(feed_first, feed_last, feed.astype(bf16))

    @pl.when(step == 0)
    def clear():
        sum_ref[...] = jnp.zeros(sum_ref.shape, f32)

    sum_ref[0:1, :] += jnp.concatenate(sums, axis=1)
    sum_ref[1:2, : g.shape[1]] += jnp.sum(g.astype(f32), axis=0, keepdims=True)


def feed_forward(c, g, w_up, w_down, shift):
    rows, width = g.shape
    hidden = w_up.shape[1]
    tall = min(512, rows // 2)
    steps = rows // tall
    chunk = 256 if hidden % 256 == 0 else hidden
    by_rows = lambda n: pl.BlockSpec((tall, n), lambda i: (i, 0))
    whole = lambda a: pl.BlockSpec(a.shape, lambda i: (0,) * a.ndim)
    first = pl.BlockSpec((tall, width), first_blocks(steps))
    last = pl.BlockSpec((tall, width), last_blocks(steps))
    part = jax.ShapeDtypeStruct((rows // 2, width), bf16)
    longest = max(width, hidden)
    return pl.pallas_call(
        functools.partial(feed_kernel, chunk),
        grid=(steps,),
        in_specs=[first, last, by_rows(width), whole(w_up), whole(w_down), whole(shift)],
        out_specs=[by_rows(hidden), by_rows(hidden), first, last, first, last, pl.BlockSpec((8, longest), lambda i: (0, 0))],
        out_shape=[
            jax.ShapeDtypeStruct((rows, hidden), bf16),
            jax.ShapeDtypeStruct((rows, hidden), bf16),
            part,
            part,
            part,
            part,
            jax.ShapeDtypeStruct((8, longest), f32),
        ],
        cost_estimate=pl.CostEstimate(
            flops=8 * rows * width * hidden, bytes_accessed=4 * width * hidden + 12 * rows * width, transcendentals=rows * hidden
        ),
        name="feed_forward",
    )(*c, g, w_up, w_down, shift)


def back_kernel(pieces, x_ref, w_ref, gq_ref, *refs):
    kv_refs = refs[:pieces]
    p_first, p_last, dkv_ref, sum_ref = refs[pieces:]
    gq = gq_ref[...]
    if pieces == 1:
        dkv = kv_refs[0][...]
    else:
        other = jnp.where(pl.program_id(0) < pl.num_programs(0) // 2, kv_refs[1][...], kv_refs[2][...])
        dkv = (kv_refs[0][...].astype(f32) + other.astype(f32)).astype(bf16)
    dkv_ref[...] = dkv
    tail = jnp.zeros((gq.shape[0], w_ref.shape[1] - gq.shape[1] - dkv.shape[1]), bf16)
    e = mm(jnp.concatenate([gq, dkv, tail], axis=1), w_ref[...], NT)
    store_halves(p_first, p_last, e.astype(bf16))
    x = x_ref[...].astype(f32)
    center = x - jnp.mean(x, axis=1, keepdims=True)
    unit = center * lax.rsqrt(jnp.mean(center * center, axis=1, keepdims=True) + norm_eps)

    @pl.when(pl.program_id(0) == 0)
    def clear():
        sum_ref[...] = jnp.zeros(sum_ref.shape, f32)

    local = gq.shape[1]
    sum_ref[0:1, :] += jnp.sum(e * unit, axis=0, keepdims=True)
    sum_ref[1:2, :] += jnp.sum(e, axis=0, keepdims=True)
    sum_ref[2:3, :local] += jnp.sum(gq.astype(f32), axis=0, keepdims=True)
    sum_ref[3:4, : 2 * local] += jnp.sum(dkv.astype(f32), axis=0, keepdims=True)


def project_back(x, w, gq, dkvs):
    rows, width = x.shape
    local = gq.shape[1]
    tall = min(512, rows // 2)
    steps = rows // tall
    by_rows = lambda n: pl.BlockSpec((tall, n), lambda i: (i, 0))
    whole = lambda a: pl.BlockSpec(a.shape, lambda i: (0,) * a.ndim)
    part = jax.ShapeDtypeStruct((rows // 2, width), bf16)
    kv_specs = [
        by_rows(2 * local),
        pl.BlockSpec((tall, 2 * local), first_blocks(steps)),
        pl.BlockSpec((tall, 2 * local), last_blocks(steps)),
    ]
    return pl.pallas_call(
        functools.partial(back_kernel, len(dkvs)),
        grid=(steps,),
        in_specs=[by_rows(width), whole(w), by_rows(local)] + kv_specs[: len(dkvs)],
        out_specs=[
            pl.BlockSpec((tall, width), first_blocks(steps)),
            pl.BlockSpec((tall, width), last_blocks(steps)),
            by_rows(2 * local),
            pl.BlockSpec((8, width), lambda i: (0, 0)),
        ],
        out_shape=[part, part, jax.ShapeDtypeStruct((rows, 2 * local), bf16), jax.ShapeDtypeStruct((8, width), f32)],
        cost_estimate=pl.CostEstimate(
            flops=6 * rows * width * local, bytes_accessed=6 * width * local + 6 * rows * width, transcendentals=rows
        ),
        name="project_back",
    )(x, w, gq, *dkvs)


def norm_stats(rows_in):
    center = rows_in - jnp.mean(rows_in, axis=1, keepdims=True)
    inverse = lax.rsqrt(jnp.mean(center * center, axis=1, keepdims=True) + norm_eps)
    return center * inverse, inverse


def norm_backward(grad_rows, unit_rows, inverse, gain):
    scaled = grad_rows * gain
    return inverse * (
        scaled
        - jnp.mean(scaled, axis=1, keepdims=True)
        - unit_rows * jnp.mean(scaled * unit_rows, axis=1, keepdims=True)
    )


def norm_two_kernel(x_ref, near_ref, far_ref, vec_ref, h_ref, c_ref):
    h = x_ref[...].astype(f32) + (near_ref[...].astype(f32) + far_ref[...].astype(f32)) + vec_ref[0:1, :]
    h_ref[...] = h
    c_ref[...] = (norm_stats(h)[0] * vec_ref[1:2, :] + vec_ref[2:3, :]).astype(bf16)


def norm_two_back_kernel(h_ref, near_ref, far_ref, g_ref, vec_ref, gh_ref, ga_ref, sum_ref):
    unit, inverse = norm_stats(h_ref[...])
    gc = near_ref[...].astype(f32) + far_ref[...].astype(f32)
    gh = g_ref[...].astype(f32) + norm_backward(gc, unit, inverse, vec_ref[1:2, :])
    ga = gh.astype(bf16)
    gh_ref[...] = gh
    ga_ref[...] = ga

    @pl.when(pl.program_id(0) == 0)
    def clear():
        sum_ref[...] = jnp.zeros(sum_ref.shape, f32)

    sum_ref[0:1, :] += jnp.sum(gc * unit, axis=0, keepdims=True)
    sum_ref[1:2, :] += jnp.sum(gc, axis=0, keepdims=True)
    sum_ref[2:3, :] += jnp.sum(ga.astype(f32), axis=0, keepdims=True)


def norm_one_back_kernel(x_ref, near_ref, far_ref, gh_ref, vec_ref, out_ref):
    unit, inverse = norm_stats(x_ref[...].astype(f32))
    ga1 = near_ref[...].astype(f32) + far_ref[...].astype(f32)
    out_ref[...] = (gh_ref[...] + norm_backward(ga1, unit, inverse, vec_ref[0:1, :])).astype(bf16)


def close_kernel(h_ref, near_ref, far_ref, live_ref, vec_ref, out_ref):
    feed = near_ref[...].astype(f32) + far_ref[...].astype(f32)
    out_ref[...] = ((h_ref[...] + feed + vec_ref[0:1, :]) * live_ref[...]).astype(bf16)


def by_tokens(body, arrays, vectors, kinds, name, sums=False):
    count, width = arrays[1].shape
    tall = min(256, count)
    in_specs = [pl.BlockSpec((tall, a.shape[1]), lambda i: (i, 0)) for a in arrays]
    out_specs = [pl.BlockSpec((tall, width), lambda i: (i, 0)) for _ in kinds]
    out_shape = [jax.ShapeDtypeStruct((count, width), kind) for kind in kinds]
    if sums:
        out_specs.append(pl.BlockSpec((8, width), lambda i: (0, 0)))
        out_shape.append(jax.ShapeDtypeStruct((8, width), f32))
    return pl.pallas_call(
        body,
        grid=(count // tall,),
        in_specs=in_specs + [pl.BlockSpec(vectors.shape, lambda i: (0, 0))],
        out_specs=out_specs,
        out_shape=out_shape,
        cost_estimate=pl.CostEstimate(flops=20 * count * width, bytes_accessed=14 * count * width, transcendentals=count),
        name=name,
    )(*arrays, vectors)


def gather_rows_kernel(side_ref, *refs):
    step = pl.program_id(0)
    for index, piece in enumerate(refs[:-1]):

        @pl.when(step == index)
        def copy(piece=piece):
            refs[-1][0] = piece[...]


def gather_rows(side, pieces):
    half, width = pieces[0].shape
    count = len(pieces)
    return pl.pallas_call(
        gather_rows_kernel,
        grid_spec=pltpu.PrefetchScalarGridSpec(
            num_scalar_prefetch=1,
            grid=(count,),
            in_specs=[pl.BlockSpec((half, width), lambda t, s: (0, 0)) for _ in pieces],
            out_specs=pl.BlockSpec((1, half, width), lambda t, s: (t // 2, jnp.where(t % 2 == 0, s[0], 1 - s[0]), 0)),
        ),
        out_shape=jax.ShapeDtypeStruct((count // 2, 2 * half, width), bf16),
        cost_estimate=pl.CostEstimate(flops=0, bytes_accessed=4 * count * half * width, transcendentals=0),
        name="gather_rows",
    )(side, *pieces)


def tables(grid_pos):
    lane = jnp.arange(LANES)
    quarter = HEAD_DIM // 4
    frequency = jnp.power(10000.0, -4.0 * (lane % quarter).astype(f32) / HEAD_DIM)
    place = jnp.where((lane // quarter) % 2 == 0, grid_pos[0][:, None], grid_pos[1][:, None])
    angle = jnp.where(lane < HEAD_DIM, place.astype(f32) * frequency, 0.0)
    return jnp.cos(angle), jnp.where(lane < HEAD_DIM // 2, -1.0, 1.0) * jnp.sin(angle)


def query_features(ids):
    lane = jnp.arange(LANES)
    return (lane == HEAD_DIM + 1 + ids[:, None]).astype(bf16)


def key_features(ids):
    lane = jnp.arange(LANES)
    slot = lane - HEAD_DIM
    same = (slot >= 1) & (slot == ids[:, None] + 1)
    wall = jnp.where((slot >= 0) & (slot < 16) & ~same, -hide, 0.0)
    return jnp.where((lane >= 96) & (lane < 99), -1.0, wall).astype(bf16)


def visit_flags(query_ids, key_ids, tall, block):
    q = query_ids.reshape(-1, tall)
    k = key_ids.reshape(-1, block)
    q_top, k_top = jnp.max(q, axis=1), jnp.max(k, axis=1)
    q_low = jnp.min(jnp.where(q >= 0, q, 1 << 20), axis=1)
    k_low = jnp.min(jnp.where(k >= 0, k, 1 << 20), axis=1)
    meet = (q_low[:, None] <= k_top[None, :]) & (k_low[None, :] <= q_top[:, None])
    return meet.astype(jnp.int32).reshape(-1)


def on_device(
    patches,
    cotangent,
    picture_ids,
    positions,
    ln1_gain,
    ln1_bias,
    qkv_weight,
    qkv_bias,
    proj_weight,
    proj_bias,
    ln2_gain,
    ln2_bias,
    fc1_weight,
    fc1_bias,
    fc2_weight,
    fc2_bias,
):
    row_count, row_share, width = patches.shape
    owners = lax.axis_size("shard")
    contexts = lax.axis_size("ctx")
    ways = lax.axis_size("tp")
    part = qkv_weight.shape[0]
    local = qkv_weight.shape[2]
    heads = local // HEAD_DIM
    half = row_share // 2
    side = lax.axis_index("tp") % 2
    context = lax.axis_index("ctx")
    pairs_near = [(i, i ^ 1) for i in range(ways)]
    pairs_far = [(i, i ^ 2) for i in range(ways)]
    pad = -3 * local % 256
    wide = 3 * local + pad

    def near(v):
        return lax.ppermute(v, "tp", pairs_near)

    def far(v):
        return lax.ppermute(v, "tp", pairs_far)

    def over_ctx(v):
        return lax.ppermute(v, "ctx", [(0, 1), (1, 0)])

    def mine_first(v, axis=0):
        return jnp.where(side == 0, v, jnp.roll(v, half, axis=axis))

    def column(v):
        flat = v.reshape(-1)
        return jnp.pad(flat, (0, part - flat.shape[0]))

    vectors = [ln1_gain, ln1_bias, ln2_gain, ln2_bias, proj_bias, fc2_bias, qkv_bias, fc1_bias]
    place = lax.axis_index("shard")
    context_first = context == 0

    def rotate_gather(piece):
        whole = lax.dynamic_update_index_in_dim(jnp.zeros((owners,) + piece.shape, piece.dtype), piece, place, 0)
        for step in range(1, owners):
            got = lax.ppermute(piece, "shard", [(i, (i + step) % owners) for i in range(owners)])
            whole = lax.dynamic_update_index_in_dim(whole, got, (place - step) % owners, 0)
        return whole

    tail = rotate_gather(jnp.stack([column(v) for v in vectors]).astype(bf16))
    packed = jnp.transpose(tail, (1, 0, 2)).reshape(len(vectors), width).astype(f32)
    qkv_piece = jnp.pad(qkv_weight.reshape(part, 3 * local), ((0, 0), (0, pad))).astype(bf16)
    gather = lambda v: lax.all_gather(v, "shard", axis=0, tiled=True)
    up_piece = fc1_weight.astype(bf16)
    down_piece = fc2_weight.T.astype(bf16)
    w_qkv = gather(qkv_piece)
    w_proj = rotate_gather(tie(proj_weight.T.astype(bf16), w_qkv)).reshape(owners * part, local)
    gain_one, bias_one, gain_two, bias_two, proj_shift, down_shift = [packed[i] for i in range(6)]
    qb_size = qkv_bias.size
    qkv_shift = packed[6].reshape(owners, part)[:, :qb_size].reshape((owners,) + qkv_bias.shape)
    qkv_shift = jnp.transpose(qkv_shift, (1, 2, 0, 3)).reshape(-1)
    qkv_shift = jnp.pad(qkv_shift, (0, pad)).reshape(1, wide)
    up_shift = packed[7].reshape(owners, part)[:, : fc1_bias.size].reshape((owners,) + fc1_bias.shape)
    up_shift = jnp.transpose(up_shift, (1, 0, 2)).reshape(1, -1)
    ln_one = tie(packed[0:2], up_piece, down_piece)

    ids_by_ctx = mine_first(picture_ids.reshape(row_count, contexts, row_share), axis=2)
    places = mine_first(positions, axis=2)
    block = min(256, half)

    def cut_last(spots):
        return [spots[0], spots[1][:half], spots[1][half:]] if contexts == 2 else spots

    key_block = 256
    rows = []
    for r in range(row_count):
        x = mine_first(patches[r])
        g = mine_first(cotangent[r])
        ids = lax.dynamic_index_in_dim(ids_by_ctx[r], context, 0, keepdims=False)
        if contexts == 2:
            other = lax.dynamic_index_in_dim(ids_by_ctx[r], 1 - context, 0, keepdims=False)
            key_ids = [ids, other]
            spots = [places[:, r], over_ctx(places[:, r])]
        else:
            key_ids = [ids_by_ctx[r].reshape(-1)]
            spots = [lax.all_gather(places[:, r], "ctx", axis=1, tiled=True)]
        live = (ids >= 0).astype(f32)[:, None]
        turns = [tables(spot) for spot in spots]
        own_turn = turns[0] if contexts == 2 else tables(places[:, r])
        rows.append(
            dict(
                x=x,
                g=(g.astype(f32) * live).astype(bf16),
                live=live,
                ids=ids,
                cos=own_turn[0],
                sin=own_turn[1],
                cos_k=cut_last([t[0] for t in turns]),
                sin_k=cut_last([t[1] for t in turns]),
                q_feat=query_features(ids),
                k_feat=[key_features(k) for k in key_ids],
                flags=visit_flags(ids, jnp.concatenate(key_ids), block, key_block),
            )
        )

    ln_one = tie(ln_one, qkv_shift, up_shift, *[row["g"] for row in rows])

    for row in rows:
        row["a"], row["q"], row["kv"] = project_row(
            row["x"], w_qkv, ln_one, qkv_shift, row["cos"], row["sin"], row["q_feat"], heads
        )
        if row is rows[0]:
            row["kv"], w_proj = lax.optimization_barrier((row["kv"], w_proj))
        if contexts == 2:
            row["kvs"] = [row["kv"], over_ctx(row["kv"])]
        else:
            row["kvs"] = [lax.all_gather(row["kv"], "ctx", axis=0, tiled=True)]

    down_piece, up_piece = lax.optimization_barrier((down_piece, up_piece, w_proj))[:2]
    if contexts == 2:
        down_cut = down_piece.reshape(2, part // 2, -1)
        down_near = gather(lax.dynamic_index_in_dim(down_cut, context, 0, keepdims=False))
        down_near = down_near.reshape(owners, part // 2, -1)
    else:
        w_down = gather(down_piece)
    w_up = gather(up_piece)

    def sum_near(first, last):
        return (first.astype(f32) + near(last).astype(f32)).astype(bf16)

    norm_vectors = jnp.pad(jnp.stack([proj_shift, gain_two, bias_two]), ((0, 5), (0, 0)))

    def norm_two(row, vectors):
        row["h"], mine = by_tokens(
            norm_two_kernel, [row["x"], row["branch"], row["branch_far"]], vectors, [f32, bf16], "norm_two"
        )
        row["c"] = (mine, near(mine))

    hold = lax.optimization_barrier
    before = rows[-1]["kv"]
    for index, row in enumerate(rows):
        row["o"], row["q"], row["k_aug"], row["v_aug"], first, last = attend_forward(
            tie(row["flags"], before), row["q"], w_proj, row["kvs"], row["k_feat"], heads, key_block
        )
        if index:
            prior = rows[index - 1]
            first, last, prior["branch_far"] = hold((first, last, prior["branch_far"]))
        if index + 1 < row_count:
            follow = rows[index + 1]
            first, last, follow["kvs"] = hold((first, last, follow["kvs"]))
            if contexts == 2:
                first, last, down_near = hold((first, last, down_near))
                down_far = over_ctx(down_near)
        elif contexts == 2:
            first, last, down_far, w_up = hold((first, last, down_far, w_up))
        before = row["branch"] = sum_near(first, last)
        row["branch_far"] = far(before)
    if contexts == 2:
        low = jnp.where(context_first, down_near, down_far)
        high = jnp.where(context_first, down_far, down_near)
        w_down = jnp.concatenate([low, high], axis=1).reshape(owners * part, -1)

    norm_two(rows[0], tie(norm_vectors, before))
    for index, row in enumerate(rows):
        shift = tie(up_shift, before)
        row["z"], row["gu"], gc_first, gc_last, feed_first, feed_last, row["feed_sums"] = feed_forward(
            row["c"], row["g"], w_up, w_down, shift
        )
        other, key = (rows[-1], "branch_far") if index == 0 else (rows[index - 1], "gc_far")
        gc_first, gc_last, other[key] = hold((gc_first, gc_last, other[key]))
        before = row["gc"] = sum_near(gc_first, gc_last)
        row["gc_far"] = far(before)
        row["feed"] = (feed_first, feed_last)
        if index + 1 < row_count:
            norm_two(rows[index + 1], norm_vectors)
    for row in rows:
        row["feed"] = sum_near(*row["feed"])

    join = lambda key: jnp.concatenate([row[key] for row in rows], axis=0)
    join_two = lambda key: jnp.concatenate([piece for row in rows for piece in row[key]], axis=0)
    scatter = lambda v: lax.psum_scatter(v, "shard", scatter_dimension=0, tiled=True)
    if contexts == 2:
        finish = lambda v: v.astype(f32) + over_ctx(v).astype(f32)
    else:
        finish = lambda v: lax.psum(v, "ctx").astype(f32)
    last_row = rows[-1]
    last_row["gu"], last_row["z"] = hold((last_row["gu"], last_row["z"], before))[:2]
    grad_up = mm(join_two("c"), join("gu"), TN).astype(bf16)
    grad_down = mm(join("g"), join("z"), TN).astype(bf16)
    grad_up, grad_down, last_row["gc_far"] = hold((grad_up, grad_down, last_row["gc_far"]))
    before = (grad_up, grad_down)
    y_free = last_row["gc_far"]
    grad_up = scatter(grad_up)
    if contexts == 2:
        cut = grad_down.reshape(owners, 2, part // 2, -1)
        keep = lax.dynamic_index_in_dim(cut, context, 1, keepdims=False)
        came = over_ctx(lax.dynamic_index_in_dim(cut, 1 - context, 1, keepdims=False))
    else:
        grad_down = scatter(grad_down)

    pair = 0.0
    for row in rows:
        row["gh"], ga, norm_sums = by_tokens(
            norm_two_back_kernel,
            [row["h"], row["gc"], row["gc_far"], row["g"]],
            norm_vectors,
            [f32, bf16],
            "norm_two_back",
            sums=True,
        )
        pair = pair + norm_sums[0:3]
        row["ga"] = (ga, near(ga))
    grad_proj = mm(join_two("ga"), join("o"), TN).astype(bf16)
    for index, row in enumerate(rows):
        feed_far = far(tie(row["feed"], y_free))
        out = attend_backward(
            tie(row["flags"], *before),
            row["q"],
            row["ga"],
            w_proj,
            row["o"],
            row["k_aug"],
            row["v_aug"],
            row["cos"],
            row["sin"],
            row["cos_k"],
            row["sin_k"],
            heads,
            key_block,
        )
        if index:
            prior = rows[index - 1]
            *out, feed_far, prior["dkvs"], grad_up = hold((*out, feed_far, prior["dkvs"], grad_up))
            if contexts == 2:
                *out, grad_down = hold((*out, grad_down))
        elif contexts == 2:
            *out, feed_far, came = hold((*out, feed_far, came))
            grad_down = scatter((keep.astype(f32) + came.astype(f32)).astype(bf16).reshape(owners * part // 2, -1))
        else:
            *out, feed_far = hold((*out, feed_far))
        y_free = feed_far
        before = (out[0], grad_proj)
        row["gq"] = out[0]
        row["feed_far"] = feed_far
        if contexts == 2:
            row["dkvs"] = [out[1], over_ctx(out[2]), over_ctx(out[3])]
        else:
            row["dkvs"] = [lax.psum_scatter(out[1], "ctx", scatter_dimension=0, tiled=True)]

    side_list = side.reshape(1).astype(jnp.int32)
    grad_proj = scatter(grad_proj)
    sums = 0.0
    for index, row in enumerate(rows):
        first, last, row["dkv"], back_sums = project_back(row["x"], w_qkv, tie(row["gq"], *before), row["dkvs"])
        sums = sums + back_sums
        if index == 0:
            kvs = last_row["dkvs"]
            first, last, row["dkv"], kvs[:-1] = hold((first, last, row["dkv"], kvs[:-1]))
            last_row["gq"] = tie(last_row["gq"], row["dkv"])
            grad_q = mm(join("a"), join("gq"), TN).astype(bf16)
            grad_q, kvs[-1] = hold((grad_q, kvs[-1]))
            grad_q = scatter(grad_q)
            outs = []
            for done in rows:
                mine = by_tokens(
                    close_kernel,
                    [done["h"], done["feed"], done["feed_far"], done["live"]],
                    tie(jnp.broadcast_to(down_shift, (8, width)), row["dkv"]),
                    [bf16],
                    "close",
                )[0]
                outs += [mine, near(mine)]
            outs = gather_rows(side_list, outs)
            before = (row["dkv"], kvs[-1], outs)
        else:
            prior = rows[index - 1]
            first, last, prior["ga1_far"] = hold((first, last, prior["ga1_far"]))
            before = (row["dkv"],)
        row["ga1"] = sum_near(first, last)
        row["ga1_far"] = far(row["ga1"])
    grad_kv = mm(join("a"), join("dkv"), TN).astype(bf16)
    up_came = over_ctx(grad_up) if contexts == 2 else grad_up
    down_came = over_ctx(grad_down) if contexts == 2 else grad_down
    last_row["ga1_far"], up_came, down_came = hold((last_row["ga1_far"], up_came, down_came))
    grad_kv, grad_q, grad_proj = hold((grad_kv, grad_q, grad_proj))
    grad_kv = scatter(grad_kv)
    if contexts == 2:
        grad_up = grad_up.astype(f32) + up_came.astype(f32)
        low = jnp.where(context_first, grad_down, down_came)
        high = jnp.where(context_first, down_came, grad_down)
        grad_down = jnp.concatenate([low, high], axis=0).astype(f32)
    else:
        grad_up, grad_down = finish(up_came), finish(down_came)
    grad_q, grad_proj = finish(grad_q), finish(grad_proj)

    ins = []
    for row in rows:
        mine = by_tokens(
            norm_one_back_kernel,
            [row["x"], row["ga1"], row["ga1_far"], row["gh"]],
            jnp.broadcast_to(gain_one, (8, width)),
            [bf16],
            "norm_one_back",
        )[0]
        ins += [mine, near(mine)]

    def sum_over(v, axis):
        size, step = lax.axis_size(axis), 1
        while step < size:
            v = v + lax.ppermute(v, axis, [(i, i ^ step) for i in range(size)])
            step *= 2
        return v

    def owned(v):
        v = v.reshape(owners, -1)
        return jnp.pad(v, ((0, 0), (0, part - v.shape[1]))).reshape(-1)

    feed_sums = sum(row["feed_sums"] for row in rows)
    d_qb = jnp.concatenate([sums[2, :local], sums[3, : 2 * local]]).reshape(3, heads, owners, -1)
    d_qb = owned(jnp.transpose(d_qb, (2, 0, 1, 3)))
    d_ub = feed_sums[0, : fc1_bias.size * owners].reshape(fc1_bias.shape[0], owners, fc1_bias.shape[1])
    d_ub = owned(jnp.transpose(d_ub, (1, 0, 2)))
    vector = jnp.concatenate([pair, feed_sums[1:2, :width], d_qb[None], d_ub[None], sums[0:2]], axis=0)
    vector = sum_over(sum_over(tie(vector, ins[0]), "ctx"), "shard")
    vector = lax.dynamic_slice_in_dim(vector, place * part, part, axis=1)
    both = vector + near(vector)
    norm_one = both[6:8] + far(both[6:8])

    ins = gather_rows(side_list, ins)
    grad_kv = finish(tie(grad_kv, ins, grad_q, grad_proj))
    return (
        outs,
        ins,
        norm_one[0],
        norm_one[1],
        jnp.concatenate([grad_q, grad_kv], axis=1).reshape(qkv_weight.shape),
        vector[4, :qb_size].reshape(qkv_bias.shape),
        grad_proj.T,
        both[2],
        both[0],
        both[1],
        grad_up,
        vector[5, : fc1_bias.size].reshape(fc1_bias.shape),
        grad_down.T,
        vector[3],
    )


def solution(mesh):
    in_specs = (
        P("shard", "ctx", None),
        P("shard", "ctx", None),
        P("shard", None),
        P(None, "shard", "ctx"),
        P("shard"),
        P("shard"),
        P("shard", None, "tp"),
        P(None, "tp", "shard"),
        P("tp", "shard"),
        P("shard"),
        P("shard"),
        P("shard"),
        P("shard", "tp"),
        P("tp", "shard"),
        P("tp", "shard"),
        P("shard"),
    )
    out_specs = (
        P("shard", "ctx", None),
        P("shard", "ctx", None),
        P("shard"),
        P("shard"),
        P("shard", None, "tp"),
        P(None, "tp", "shard"),
        P("tp", "shard"),
        P("shard"),
        P("shard"),
        P("shard"),
        P("shard", "tp"),
        P("tp", "shard"),
        P("tp", "shard"),
        P("shard"),
    )
    return jax.shard_map(
        on_device, mesh=mesh, in_specs=in_specs, out_specs=out_specs, check_vma=False
    )
```

```python
import functools
import math

import jax
import jax.numpy as jnp
from jax import lax
from jax.experimental import pallas as pl
from jax.experimental.pallas import tpu as pltpu
from jax.sharding import PartitionSpec as P

HEAD_DIM = 80
LANES = 128
norm_eps = 1e-06
hide = 1e30
floor_max = -1e29
log2e = math.log2(math.e)
bf16 = jnp.bfloat16
f32 = jnp.float32
NT = (((1,), (1,)), ((), ()))
NN = (((1,), (0,)), ((), ()))
TN = (((0,), (0,)), ((), ()))


def mm(a, b, dims=NN):
    return lax.dot_general(a, b, dims, preferred_element_type=f32)


def tie(value, *others):
    return lax.optimization_barrier((value,) + others)[0]


def first_blocks(steps):
    return lambda i, *_: (jnp.minimum(i, steps // 2 - 1), 0)


def last_blocks(steps):
    return lambda i, *_: (jnp.maximum(i - steps // 2, 0), 0)


def store_halves(first_ref, last_ref, value):
    step, split = pl.program_id(0), pl.num_programs(0) // 2

    @pl.when(step < split)
    def first():
        first_ref[...] = value

    @pl.when(step >= split)
    def last():
        last_ref[...] = value


def lane_index(rows):
    return lax.broadcasted_iota(jnp.int32, (rows, LANES), 1)


def swap_halves(w, lane):
    half = HEAD_DIM // 2
    up = pltpu.roll(w, LANES - half, 1)
    down = pltpu.roll(w, half, 1)
    return jnp.where(lane < half, up, down)


def widen(piece):
    rows = piece.shape[0]
    tail = jnp.zeros((rows, LANES - piece.shape[1]), piece.dtype)
    return jnp.concatenate([piece, tail], axis=1)


def split_three(column):
    high = column.astype(bf16).astype(f32)
    rest = column - high
    mid = rest.astype(bf16).astype(f32)
    return high, mid, rest - mid


def place_three(base, column, lane):
    high, mid, low = split_three(column)
    base = jnp.where(lane == 96, high, base)
    base = jnp.where(lane == 97, mid, base)
    return jnp.where(lane == 98, low, base)


def qkv_kernel(heads, x_ref, w_ref, ln_ref, b_ref, cos_ref, sin_ref, feat_ref, a_ref, q_ref, kv_ref):
    width = heads * HEAD_DIM
    x = x_ref[...].astype(f32)
    rows = x.shape[0]
    center = x - jnp.mean(x, axis=1, keepdims=True)
    inverse = lax.rsqrt(jnp.mean(center * center, axis=1, keepdims=True) + norm_eps)
    a = (center * inverse * ln_ref[0:1, :] + ln_ref[1:2, :]).astype(bf16)
    a_ref[...] = a
    y = mm(a, w_ref[...]) + b_ref[0:1, :]
    cos, sin = cos_ref[...], sin_ref[...]
    lane = lane_index(rows)
    kv = []
    for h in range(heads):
        w = widen(y[:, h * HEAD_DIM : (h + 1) * HEAD_DIM])
        q = (w * cos + swap_halves(w, lane) * sin) * (HEAD_DIM**-0.5 * log2e)
        q_ref[h] = jnp.where(lane < HEAD_DIM, q.astype(bf16), feat_ref[...])
    for h in range(heads):
        begin = width + h * HEAD_DIM
        w = widen(y[:, begin : begin + HEAD_DIM])
        kv.append((w * cos + swap_halves(w, lane) * sin)[:, :HEAD_DIM].astype(bf16))
    kv.append(y[:, 2 * width : 3 * width].astype(bf16))
    kv_ref[...] = jnp.concatenate(kv, axis=1)


def project_row(x, w, ln, bias, cos, sin, feat, heads):
    rows, width = x.shape
    block = min(256, rows)
    wide = w.shape[1]
    local = heads * HEAD_DIM
    by_rows = lambda n: pl.BlockSpec((block, n), lambda i: (i, 0))
    whole = lambda a: pl.BlockSpec(a.shape, lambda i: (0,) * a.ndim)
    return pl.pallas_call(
        functools.partial(qkv_kernel, heads),
        grid=(rows // block,),
        in_specs=[
            by_rows(width),
            whole(w),
            whole(ln),
            whole(bias),
            by_rows(LANES),
            by_rows(LANES),
            by_rows(LANES),
        ],
        out_specs=[
            by_rows(width),
            pl.BlockSpec((heads, block, LANES), lambda i: (0, i, 0)),
            by_rows(2 * local),
        ],
        out_shape=[
            jax.ShapeDtypeStruct((rows, width), bf16),
            jax.ShapeDtypeStruct((heads, rows, LANES), bf16),
            jax.ShapeDtypeStruct((rows, 2 * local), bf16),
        ],
        cost_estimate=pl.CostEstimate(
            flops=2 * rows * width * wide, bytes_accessed=rows * width * 4 + width * wide * 2, transcendentals=0
        ),
        name="project_row",
    )(x, w, ln, bias, cos, sin, feat)


def forward_kernel(heads, segments, block, flag_ref, q_ref, w_ref, *refs):
    kv_refs = refs[:segments]
    feat_refs = refs[segments : 2 * segments]
    o_ref, q_out, k_aug, v_aug, p_first, p_last, m_scr, acc_scr = refs[2 * segments :]
    width = heads * HEAD_DIM
    step = pl.program_id(0)
    keys = k_aug.shape[1]
    count = keys // block
    rows = q_ref.shape[1]

    @pl.when(step == 0)
    def build():
        offset = 0
        for s in range(segments):
            length = kv_refs[s].shape[0]
            piece = min(length, 256)
            for t in range(length // piece):
                at = pl.ds(t * piece, piece)
                to = pl.ds(offset + t * piece, piece)
                kv = kv_refs[s][at, :]
                feat = feat_refs[s][at, :]
                lane = lane_index(piece)
                tail = jnp.where(lane == HEAD_DIM, 1.0, jnp.where((lane >= 96) & (lane < 99), -1.0, 0.0)).astype(bf16)
                for h in range(heads):
                    k = kv[:, h * HEAD_DIM : (h + 1) * HEAD_DIM]
                    v = kv[:, width + h * HEAD_DIM : width + (h + 1) * HEAD_DIM]
                    k_aug[h, to, :] = jnp.concatenate([k, feat[:, HEAD_DIM:]], axis=1)
                    v_aug[h, to, :] = jnp.concatenate([v, tail[:, HEAD_DIM:]], axis=1)
            offset += length

    m_scr[...] = jnp.full(m_scr.shape, floor_max, f32)
    acc_scr[...] = jnp.zeros(acc_scr.shape, f32)

    def visit(j, carry):
        @pl.when(flag_ref[step * count + j] > 0)
        def go():
            at = pl.ds(pl.multiple_of(j * block, block), block)
            for h in range(heads):
                s = mm(q_ref[h], k_aug[h, at, :], NT)
                old = m_scr[h]
                cuts = [s[:, c : c + LANES] for c in range(0, block, LANES)]
                top = functools.reduce(jnp.maximum, cuts)
                new = jnp.maximum(old, jnp.max(top, axis=1, keepdims=True))
                p = jnp.concatenate([jnp.exp2(cut - new) for cut in cuts], axis=1)
                m_scr[h] = new
                acc_scr[h] = acc_scr[h] * jnp.exp2(old - new) + mm(p.astype(bf16), v_aug[h, at, :])

        return carry

    lax.fori_loop(0, count, visit, 0)
    lane = lane_index(rows)
    outs = []
    for h in range(heads):
        acc = acc_scr[h]
        total = acc[:, HEAD_DIM : HEAD_DIM + 1]
        alive = total > 0.0
        safe = jnp.where(alive, total, 1.0)
        outs.append((acc / safe)[:, :HEAD_DIM].astype(bf16))
        level = jnp.where(alive, m_scr[h][:, 0:1] + jnp.log2(safe), 0.0)
        q_out[h] = place_three(q_ref[h].astype(f32), level, lane).astype(bf16)
    o = jnp.concatenate(outs, axis=1)
    o_ref[...] = o
    store_halves(p_first, p_last, mm(o, w_ref[...], NT).astype(bf16))


def attend_forward(flags, q_aug, w, kvs, feats, heads, block):
    rows = q_aug.shape[1]
    tall = min(256, rows // 2)
    steps = rows // tall
    width = w.shape[0]
    keys = sum(kv.shape[0] for kv in kvs)
    segments = len(kvs)
    whole = lambda a: pl.BlockSpec(a.shape, lambda i, f: (0,) * a.ndim)
    q_spec = pl.BlockSpec((heads, tall, LANES), lambda i, f: (0, i, 0))
    k_spec = pl.BlockSpec((heads, keys, LANES), lambda i, f: (0, 0, 0))
    local = heads * HEAD_DIM
    return pl.pallas_call(
        functools.partial(forward_kernel, heads, segments, block),
        grid_spec=pltpu.PrefetchScalarGridSpec(
            num_scalar_prefetch=1,
            grid=(rows // tall,),
            in_specs=[q_spec, whole(w)] + [whole(kv) for kv in kvs] + [whole(f) for f in feats],
            out_specs=[
                pl.BlockSpec((tall, local), lambda i, f: (i, 0)),
                q_spec,
                k_spec,
                k_spec,
                pl.BlockSpec((tall, width), first_blocks(steps)),
                pl.BlockSpec((tall, width), last_blocks(steps)),
            ],
            scratch_shapes=[
                pltpu.VMEM((heads, tall, LANES), f32),
                pltpu.VMEM((heads, tall, LANES), f32),
            ],
        ),
        out_shape=[
            jax.ShapeDtypeStruct((rows, local), bf16),
            jax.ShapeDtypeStruct((heads, rows, LANES), bf16),
            jax.ShapeDtypeStruct((heads, keys, LANES), bf16),
            jax.ShapeDtypeStruct((heads, keys, LANES), bf16),
            jax.ShapeDtypeStruct((rows // 2, width), bf16),
            jax.ShapeDtypeStruct((rows // 2, width), bf16),
        ],
        cost_estimate=pl.CostEstimate(
            flops=2 * rows * keys * heads * LANES, bytes_accessed=8 * keys * local, transcendentals=rows * keys * heads // 2
        ),
        name="attend_forward",
    )(flags, q_aug, w, *kvs, *feats)


def backward_kernel(
    heads, segments, block, flag_ref, q_ref, ga_first, ga_last, w_ref, o_ref, k_aug, v_aug, cosq_ref, sinq_ref, *refs
):
    cosk_refs = refs[:segments]
    sink_refs = refs[segments : 2 * segments]
    dq_ref = refs[2 * segments]
    dkv_refs = refs[2 * segments + 1 : 3 * segments + 1]
    k_turn, dk_acc, dv_acc, dq_acc, go_scr = refs[3 * segments + 1 :]
    step = pl.program_id(0)
    keys = k_aug.shape[1]
    count = keys // block
    rows = q_ref.shape[1]
    scale = HEAD_DIM**-0.5

    @pl.when(step == 0)
    def build():
        dk_acc[...] = jnp.zeros(dk_acc.shape, f32)
        dv_acc[...] = jnp.zeros(dv_acc.shape, f32)
        for h in range(heads):
            for t in range(count):
                at = pl.ds(t * block, block)
                k_turn[h, :, at] = k_aug[h, at, :].T

    lane = lane_index(rows)
    ga = jnp.where(step < pl.num_programs(0) // 2, ga_first[...], ga_last[...])
    go_all = mm(ga, w_ref[...]).astype(bf16).astype(f32)
    for h in range(heads):
        cut = slice(h * HEAD_DIM, (h + 1) * HEAD_DIM)
        go = go_all[:, cut]
        delta = jnp.sum(go * o_ref[:, cut].astype(f32), axis=1, keepdims=True)
        go_scr[h] = place_three(widen(go), delta, lane).astype(bf16)
    dq_acc[...] = jnp.zeros(dq_acc.shape, f32)

    def visit(j, carry):
        @pl.when(flag_ref[step * count + j] > 0)
        def run():
            at = pl.ds(pl.multiple_of(j * block, block), block)
            for h in range(heads):
                q, go = q_ref[h], go_scr[h]
                p = jnp.exp2(mm(k_aug[h, at, :], q, NT))
                ds = (p * mm(v_aug[h, at, :], go, NT)).astype(bf16)
                dv_acc[h, at, :] += mm(p.astype(bf16), go)
                dk_acc[h, at, :] += mm(ds, q)
                dq_acc[h] += mm(k_turn[h, :, at], ds)

        return carry

    lax.fori_loop(0, count, visit, 0)

    def turn_back(w, cos, sin, index):
        return w * cos - swap_halves(w, index) * sin

    outs = []
    for h in range(heads):
        w = dq_acc[h].T
        back = turn_back(w, cosq_ref[...], sinq_ref[...], lane) * scale
        outs.append(back[:, :HEAD_DIM].astype(bf16))
    dq_ref[...] = jnp.concatenate(outs, axis=1)

    @pl.when(step == pl.num_programs(0) - 1)
    def finish():
        offset = 0
        for s in range(segments):
            length = dkv_refs[s].shape[0]
            piece = min(length, 256)
            index = lane_index(piece)
            for t in range(length // piece):
                at = pl.ds(t * piece, piece)
                of = pl.ds(offset + t * piece, piece)
                parts = []
                for h in range(heads):
                    w = dk_acc[h, of, :]
                    back = turn_back(w, cosk_refs[s][at, :], sink_refs[s][at, :], index) * (1.0 / log2e)
                    parts.append(back[:, :HEAD_DIM].astype(bf16))
                for h in range(heads):
                    parts.append(dv_acc[h, of, :][:, :HEAD_DIM].astype(bf16))
                dkv_refs[s][at, :] = jnp.concatenate(parts, axis=1)
            offset += length


def attend_backward(flags, q_aug, ga, w, o, k_aug, v_aug, cos_q, sin_q, cos_k, sin_k, heads, block):
    rows = q_aug.shape[1]
    tall = min(256, rows // 2)
    steps = rows // tall
    width = w.shape[0]
    keys = k_aug.shape[1]
    segments = len(cos_k)
    local = heads * HEAD_DIM
    whole = lambda a: pl.BlockSpec(a.shape, lambda i, f: (0,) * a.ndim)
    by_rows = lambda n: pl.BlockSpec((tall, n), lambda i, f: (i, 0))
    q_spec = pl.BlockSpec((heads, tall, LANES), lambda i, f: (0, i, 0))
    return pl.pallas_call(
        functools.partial(backward_kernel, heads, segments, block),
        grid_spec=pltpu.PrefetchScalarGridSpec(
            num_scalar_prefetch=1,
            grid=(rows // tall,),
            in_specs=[
                q_spec,
                pl.BlockSpec((tall, width), first_blocks(steps)),
                pl.BlockSpec((tall, width), last_blocks(steps)),
                whole(w),
                by_rows(local),
                whole(k_aug),
                whole(v_aug),
                by_rows(LANES),
                by_rows(LANES),
            ]
            + [whole(t) for t in cos_k]
            + [whole(t) for t in sin_k],
            out_specs=[by_rows(local)]
            + [pl.BlockSpec((t.shape[0], 2 * local), lambda i, f: (0, 0)) for t in cos_k],
            scratch_shapes=[
                pltpu.VMEM((heads, LANES, keys), bf16),
                pltpu.VMEM((heads, keys, LANES), f32),
                pltpu.VMEM((heads, keys, LANES), f32),
                pltpu.VMEM((heads, LANES, tall), f32),
                pltpu.VMEM((heads, tall, LANES), bf16),
            ],
        ),
        out_shape=[jax.ShapeDtypeStruct((rows, local), bf16)]
        + [jax.ShapeDtypeStruct((t.shape[0], 2 * local), bf16) for t in cos_k],
        cost_estimate=pl.CostEstimate(
            flops=5 * rows * keys * heads * LANES, bytes_accessed=16 * keys * local, transcendentals=rows * keys * heads // 2
        ),
        name="attend_backward",
    )(flags, q_aug, *ga, w, o, k_aug, v_aug, cos_q, sin_q, *cos_k, *sin_k)


def feed_kernel(chunk, c_first, c_last, g_ref, up_ref, down_ref, shift_ref, z_ref, gu_ref, gc_first, gc_last, feed_first, feed_last, sum_ref):
    step = pl.program_id(0)
    c = jnp.where(step < pl.num_programs(0) // 2, c_first[...], c_last[...])
    g = g_ref[...]
    sums = []
    for begin in range(0, up_ref.shape[1], chunk):
        cut = slice(begin, begin + chunk)
        u = mm(c, up_ref[:, cut]) + shift_ref[0:1, cut]
        sg = 0.5 + 0.5 * jnp.tanh(0.851 * u)
        z = (u * sg).astype(bf16)
        gu = (mm(g, down_ref[:, cut]) * (sg + 1.702 * u * sg * (1.0 - sg))).astype(bf16)
        z_ref[:, cut] = z
        gu_ref[:, cut] = gu
        sums.append(jnp.sum(gu.astype(f32), axis=0, keepdims=True))
    store_halves(gc_first, gc_last, mm(gu_ref[...], up_ref[...], NT).astype(bf16))
    store_halves(feed_first, feed_last, mm(z_ref[...], down_ref[...], NT).astype(bf16))

    @pl.when(step == 0)
    def clear():
        sum_ref[...] = jnp.zeros(sum_ref.shape, f32)

    sum_ref[0:1, :] += jnp.concatenate(sums, axis=1)
    sum_ref[1:2, : g.shape[1]] += jnp.sum(g.astype(f32), axis=0, keepdims=True)


def feed_forward(c, g, w_up, w_down, shift):
    rows, width = g.shape
    hidden = w_up.shape[1]
    tall = min(256, rows // 2)
    steps = rows // tall
    chunk = 256 if hidden % 256 == 0 else hidden
    by_rows = lambda n: pl.BlockSpec((tall, n), lambda i: (i, 0))
    whole = lambda a: pl.BlockSpec(a.shape, lambda i: (0,) * a.ndim)
    first = pl.BlockSpec((tall, width), first_blocks(steps))
    last = pl.BlockSpec((tall, width), last_blocks(steps))
    part = jax.ShapeDtypeStruct((rows // 2, width), bf16)
    longest = max(width, hidden)
    return pl.pallas_call(
        functools.partial(feed_kernel, chunk),
        grid=(steps,),
        in_specs=[first, last, by_rows(width), whole(w_up), whole(w_down), whole(shift)],
        out_specs=[by_rows(hidden), by_rows(hidden), first, last, first, last, pl.BlockSpec((8, longest), lambda i: (0, 0))],
        out_shape=[
            jax.ShapeDtypeStruct((rows, hidden), bf16),
            jax.ShapeDtypeStruct((rows, hidden), bf16),
            part,
            part,
            part,
            part,
            jax.ShapeDtypeStruct((8, longest), f32),
        ],
        cost_estimate=pl.CostEstimate(
            flops=8 * rows * width * hidden, bytes_accessed=4 * width * hidden + 12 * rows * width, transcendentals=rows * hidden
        ),
        name="feed_forward",
    )(*c, g, w_up, w_down, shift)


def back_kernel(pieces, x_ref, w_ref, gq_ref, *refs):
    kv_refs = refs[:pieces]
    p_first, p_last, dkv_ref, sum_ref = refs[pieces:]
    gq = gq_ref[...]
    if pieces == 1:
        dkv = kv_refs[0][...]
    else:
        other = jnp.where(pl.program_id(0) < pl.num_programs(0) // 2, kv_refs[1][...], kv_refs[2][...])
        dkv = (kv_refs[0][...].astype(f32) + other.astype(f32)).astype(bf16)
    dkv_ref[...] = dkv
    tail = jnp.zeros((gq.shape[0], w_ref.shape[1] - gq.shape[1] - dkv.shape[1]), bf16)
    e = mm(jnp.concatenate([gq, dkv, tail], axis=1), w_ref[...], NT)
    store_halves(p_first, p_last, e.astype(bf16))
    x = x_ref[...].astype(f32)
    center = x - jnp.mean(x, axis=1, keepdims=True)
    unit = center * lax.rsqrt(jnp.mean(center * center, axis=1, keepdims=True) + norm_eps)

    @pl.when(pl.program_id(0) == 0)
    def clear():
        sum_ref[...] = jnp.zeros(sum_ref.shape, f32)

    local = gq.shape[1]
    sum_ref[0:1, :] += jnp.sum(e * unit, axis=0, keepdims=True)
    sum_ref[1:2, :] += jnp.sum(e, axis=0, keepdims=True)
    sum_ref[2:3, :local] += jnp.sum(gq.astype(f32), axis=0, keepdims=True)
    sum_ref[3:4, : 2 * local] += jnp.sum(dkv.astype(f32), axis=0, keepdims=True)


def project_back(x, w, gq, dkvs):
    rows, width = x.shape
    local = gq.shape[1]
    tall = min(512, rows // 2)
    steps = rows // tall
    by_rows = lambda n: pl.BlockSpec((tall, n), lambda i: (i, 0))
    whole = lambda a: pl.BlockSpec(a.shape, lambda i: (0,) * a.ndim)
    part = jax.ShapeDtypeStruct((rows // 2, width), bf16)
    kv_specs = [
        by_rows(2 * local),
        pl.BlockSpec((tall, 2 * local), first_blocks(steps)),
        pl.BlockSpec((tall, 2 * local), last_blocks(steps)),
    ]
    return pl.pallas_call(
        functools.partial(back_kernel, len(dkvs)),
        grid=(steps,),
        in_specs=[by_rows(width), whole(w), by_rows(local)] + kv_specs[: len(dkvs)],
        out_specs=[
            pl.BlockSpec((tall, width), first_blocks(steps)),
            pl.BlockSpec((tall, width), last_blocks(steps)),
            by_rows(2 * local),
            pl.BlockSpec((8, width), lambda i: (0, 0)),
        ],
        out_shape=[part, part, jax.ShapeDtypeStruct((rows, 2 * local), bf16), jax.ShapeDtypeStruct((8, width), f32)],
        cost_estimate=pl.CostEstimate(
            flops=6 * rows * width * local, bytes_accessed=6 * width * local + 6 * rows * width, transcendentals=rows
        ),
        name="project_back",
    )(x, w, gq, *dkvs)


def norm_stats(rows_in):
    center = rows_in - jnp.mean(rows_in, axis=1, keepdims=True)
    inverse = lax.rsqrt(jnp.mean(center * center, axis=1, keepdims=True) + norm_eps)
    return center * inverse, inverse


def norm_backward(grad_rows, unit_rows, inverse, gain):
    scaled = grad_rows * gain
    return inverse * (
        scaled
        - jnp.mean(scaled, axis=1, keepdims=True)
        - unit_rows * jnp.mean(scaled * unit_rows, axis=1, keepdims=True)
    )


def norm_two_kernel(x_ref, near_ref, far_ref, vec_ref, h_ref, c_ref):
    h = x_ref[...].astype(f32) + (near_ref[...].astype(f32) + far_ref[...].astype(f32)) + vec_ref[0:1, :]
    h_ref[...] = h
    c_ref[...] = (norm_stats(h)[0] * vec_ref[1:2, :] + vec_ref[2:3, :]).astype(bf16)


def norm_two_back_kernel(h_ref, near_ref, far_ref, g_ref, vec_ref, gh_ref, ga_ref, sum_ref):
    unit, inverse = norm_stats(h_ref[...])
    gc = near_ref[...].astype(f32) + far_ref[...].astype(f32)
    gh = g_ref[...].astype(f32) + norm_backward(gc, unit, inverse, vec_ref[1:2, :])
    ga = gh.astype(bf16)
    gh_ref[...] = gh
    ga_ref[...] = ga

    @pl.when(pl.program_id(0) == 0)
    def clear():
        sum_ref[...] = jnp.zeros(sum_ref.shape, f32)

    sum_ref[0:1, :] += jnp.sum(gc * unit, axis=0, keepdims=True)
    sum_ref[1:2, :] += jnp.sum(gc, axis=0, keepdims=True)
    sum_ref[2:3, :] += jnp.sum(ga.astype(f32), axis=0, keepdims=True)


def norm_one_back_kernel(x_ref, near_ref, far_ref, gh_ref, vec_ref, out_ref):
    unit, inverse = norm_stats(x_ref[...].astype(f32))
    ga1 = near_ref[...].astype(f32) + far_ref[...].astype(f32)
    out_ref[...] = (gh_ref[...] + norm_backward(ga1, unit, inverse, vec_ref[0:1, :])).astype(bf16)


def close_kernel(h_ref, near_ref, far_ref, live_ref, vec_ref, out_ref):
    feed = near_ref[...].astype(f32) + far_ref[...].astype(f32)
    out_ref[...] = ((h_ref[...] + feed + vec_ref[0:1, :]) * live_ref[...]).astype(bf16)


def by_tokens(body, arrays, vectors, kinds, name, sums=False):
    count, width = arrays[1].shape
    tall = min(256, count)
    in_specs = [pl.BlockSpec((tall, a.shape[1]), lambda i: (i, 0)) for a in arrays]
    out_specs = [pl.BlockSpec((tall, width), lambda i: (i, 0)) for _ in kinds]
    out_shape = [jax.ShapeDtypeStruct((count, width), kind) for kind in kinds]
    if sums:
        out_specs.append(pl.BlockSpec((8, width), lambda i: (0, 0)))
        out_shape.append(jax.ShapeDtypeStruct((8, width), f32))
    return pl.pallas_call(
        body,
        grid=(count // tall,),
        in_specs=in_specs + [pl.BlockSpec(vectors.shape, lambda i: (0, 0))],
        out_specs=out_specs,
        out_shape=out_shape,
        cost_estimate=pl.CostEstimate(flops=20 * count * width, bytes_accessed=14 * count * width, transcendentals=count),
        name=name,
    )(*arrays, vectors)


def gather_rows_kernel(side_ref, *refs):
    step = pl.program_id(0)
    for index, piece in enumerate(refs[:-1]):

        @pl.when(step == index)
        def copy(piece=piece):
            refs[-1][0] = piece[...]


def gather_rows(side, pieces):
    half, width = pieces[0].shape
    count = len(pieces)
    return pl.pallas_call(
        gather_rows_kernel,
        grid_spec=pltpu.PrefetchScalarGridSpec(
            num_scalar_prefetch=1,
            grid=(count,),
            in_specs=[pl.BlockSpec((half, width), lambda t, s: (0, 0)) for _ in pieces],
            out_specs=pl.BlockSpec((1, half, width), lambda t, s: (t // 2, jnp.where(t % 2 == 0, s[0], 1 - s[0]), 0)),
        ),
        out_shape=jax.ShapeDtypeStruct((count // 2, 2 * half, width), bf16),
        cost_estimate=pl.CostEstimate(flops=0, bytes_accessed=4 * count * half * width, transcendentals=0),
        name="gather_rows",
    )(side, *pieces)


def tables(grid_pos):
    lane = jnp.arange(LANES)
    quarter = HEAD_DIM // 4
    frequency = jnp.power(10000.0, -4.0 * (lane % quarter).astype(f32) / HEAD_DIM)
    place = jnp.where((lane // quarter) % 2 == 0, grid_pos[0][:, None], grid_pos[1][:, None])
    angle = jnp.where(lane < HEAD_DIM, place.astype(f32) * frequency, 0.0)
    return jnp.cos(angle), jnp.where(lane < HEAD_DIM // 2, -1.0, 1.0) * jnp.sin(angle)


def query_features(ids):
    lane = jnp.arange(LANES)
    return (lane == HEAD_DIM + 1 + ids[:, None]).astype(bf16)


def key_features(ids):
    lane = jnp.arange(LANES)
    slot = lane - HEAD_DIM
    same = (slot >= 1) & (slot == ids[:, None] + 1)
    wall = jnp.where((slot >= 0) & (slot < 16) & ~same, -hide, 0.0)
    return jnp.where((lane >= 96) & (lane < 99), -1.0, wall).astype(bf16)


def visit_flags(query_ids, key_ids, tall, block):
    q = query_ids.reshape(-1, tall)
    k = key_ids.reshape(-1, block)
    q_top, k_top = jnp.max(q, axis=1), jnp.max(k, axis=1)
    q_low = jnp.min(jnp.where(q >= 0, q, 1 << 20), axis=1)
    k_low = jnp.min(jnp.where(k >= 0, k, 1 << 20), axis=1)
    meet = (q_low[:, None] <= k_top[None, :]) & (k_low[None, :] <= q_top[:, None])
    return meet.astype(jnp.int32).reshape(-1)


def on_device(
    patches,
    cotangent,
    picture_ids,
    positions,
    ln1_gain,
    ln1_bias,
    qkv_weight,
    qkv_bias,
    proj_weight,
    proj_bias,
    ln2_gain,
    ln2_bias,
    fc1_weight,
    fc1_bias,
    fc2_weight,
    fc2_bias,
):
    row_count, row_share, width = patches.shape
    owners = lax.axis_size("shard")
    contexts = lax.axis_size("ctx")
    ways = lax.axis_size("tp")
    part = qkv_weight.shape[0]
    local = qkv_weight.shape[2]
    heads = local // HEAD_DIM
    half = row_share // 2
    side = lax.axis_index("tp") % 2
    context = lax.axis_index("ctx")
    pairs_near = [(i, i ^ 1) for i in range(ways)]
    pairs_far = [(i, i ^ 2) for i in range(ways)]
    pad = -3 * local % 256
    wide = 3 * local + pad

    def near(v):
        return lax.ppermute(v, "tp", pairs_near)

    def far(v):
        return lax.ppermute(v, "tp", pairs_far)

    def over_ctx(v):
        return lax.ppermute(v, "ctx", [(0, 1), (1, 0)])

    def mine_first(v, axis=0):
        return jnp.where(side == 0, v, jnp.roll(v, half, axis=axis))

    def column(v):
        flat = v.reshape(-1)
        return jnp.pad(flat, (0, part - flat.shape[0]))

    vectors = [ln1_gain, ln1_bias, ln2_gain, ln2_bias, proj_bias, fc2_bias, qkv_bias, fc1_bias]
    place = lax.axis_index("shard")
    context_first = context == 0

    def rotate_gather(piece):
        whole = lax.dynamic_update_index_in_dim(jnp.zeros((owners,) + piece.shape, piece.dtype), piece, place, 0)
        for step in range(1, owners):
            got = lax.ppermute(piece, "shard", [(i, (i + step) % owners) for i in range(owners)])
            whole = lax.dynamic_update_index_in_dim(whole, got, (place - step) % owners, 0)
        return whole

    tail = rotate_gather(jnp.stack([column(v) for v in vectors]).astype(bf16))
    packed = jnp.transpose(tail, (1, 0, 2)).reshape(len(vectors), width).astype(f32)
    qkv_piece = jnp.pad(qkv_weight.reshape(part, 3 * local), ((0, 0), (0, pad))).astype(bf16)
    gather = lambda v: lax.all_gather(v, "shard", axis=0, tiled=True)
    up_piece = fc1_weight.astype(bf16)
    down_piece = fc2_weight.T.astype(bf16)
    w_qkv = gather(qkv_piece)
    w_proj = rotate_gather(tie(proj_weight.T.astype(bf16), w_qkv)).reshape(owners * part, local)
    gain_one, bias_one, gain_two, bias_two, proj_shift, down_shift = [packed[i] for i in range(6)]
    qb_size = qkv_bias.size
    qkv_shift = packed[6].reshape(owners, part)[:, :qb_size].reshape((owners,) + qkv_bias.shape)
    qkv_shift = jnp.transpose(qkv_shift, (1, 2, 0, 3)).reshape(-1)
    qkv_shift = jnp.pad(qkv_shift, (0, pad)).reshape(1, wide)
    up_shift = packed[7].reshape(owners, part)[:, : fc1_bias.size].reshape((owners,) + fc1_bias.shape)
    up_shift = jnp.transpose(up_shift, (1, 0, 2)).reshape(1, -1)
    ln_one = tie(packed[0:2], up_piece, down_piece)

    ids_by_ctx = mine_first(picture_ids.reshape(row_count, contexts, row_share), axis=2)
    places = mine_first(positions, axis=2)
    block = min(256, half)

    def cut_last(spots):
        return [spots[0], spots[1][:half], spots[1][half:]] if contexts == 2 else spots

    key_block = 256
    rows = []
    for r in range(row_count):
        x = mine_first(patches[r])
        g = mine_first(cotangent[r])
        ids = lax.dynamic_index_in_dim(ids_by_ctx[r], context, 0, keepdims=False)
        if contexts == 2:
            other = lax.dynamic_index_in_dim(ids_by_ctx[r], 1 - context, 0, keepdims=False)
            key_ids = [ids, other]
            spots = [places[:, r], over_ctx(places[:, r])]
        else:
            key_ids = [ids_by_ctx[r].reshape(-1)]
            spots = [lax.all_gather(places[:, r], "ctx", axis=1, tiled=True)]
        live = (ids >= 0).astype(f32)[:, None]
        turns = [tables(spot) for spot in spots]
        own_turn = turns[0] if contexts == 2 else tables(places[:, r])
        rows.append(
            dict(
                x=x,
                g=(g.astype(f32) * live).astype(bf16),
                live=live,
                ids=ids,
                cos=own_turn[0],
                sin=own_turn[1],
                cos_k=cut_last([t[0] for t in turns]),
                sin_k=cut_last([t[1] for t in turns]),
                q_feat=query_features(ids),
                k_feat=[key_features(k) for k in key_ids],
                flags=visit_flags(ids, jnp.concatenate(key_ids), block, key_block),
            )
        )

    ln_one = tie(ln_one, qkv_shift, up_shift, *[row["g"] for row in rows])

    for row in rows:
        row["a"], row["q"], row["kv"] = project_row(
            row["x"], w_qkv, ln_one, qkv_shift, row["cos"], row["sin"], row["q_feat"], heads
        )
        if row is rows[0]:
            row["kv"], w_proj = lax.optimization_barrier((row["kv"], w_proj))
        if contexts == 2:
            row["kvs"] = [row["kv"], over_ctx(row["kv"])]
        else:
            row["kvs"] = [lax.all_gather(row["kv"], "ctx", axis=0, tiled=True)]

    down_piece, up_piece = lax.optimization_barrier((down_piece, up_piece, w_proj))[:2]
    if contexts == 2:
        down_cut = down_piece.reshape(2, part // 2, -1)
        down_near = gather(lax.dynamic_index_in_dim(down_cut, context, 0, keepdims=False))
        down_near = down_near.reshape(owners, part // 2, -1)
    else:
        w_down = gather(down_piece)
    w_up = gather(up_piece)

    def sum_near(first, last):
        return (first.astype(f32) + near(last).astype(f32)).astype(bf16)

    norm_vectors = jnp.pad(jnp.stack([proj_shift, gain_two, bias_two]), ((0, 5), (0, 0)))

    def norm_two(row, vectors):
        row["h"], mine = by_tokens(
            norm_two_kernel, [row["x"], row["branch"], row["branch_far"]], vectors, [f32, bf16], "norm_two"
        )
        row["c"] = (mine, near(mine))

    hold = lax.optimization_barrier
    before = rows[-1]["kv"]
    for index, row in enumerate(rows):
        row["o"], row["q"], row["k_aug"], row["v_aug"], first, last = attend_forward(
            tie(row["flags"], before), row["q"], w_proj, row["kvs"], row["k_feat"], heads, key_block
        )
        if index:
            prior = rows[index - 1]
            first, last, prior["branch_far"] = hold((first, last, prior["branch_far"]))
        if index + 1 < row_count:
            follow = rows[index + 1]
            first, last, follow["kvs"] = hold((first, last, follow["kvs"]))
            if contexts == 2:
                first, last, down_near = hold((first, last, down_near))
                down_far = over_ctx(down_near)
        elif contexts == 2:
            first, last, down_far, w_up = hold((first, last, down_far, w_up))
        before = row["branch"] = sum_near(first, last)
        row["branch_far"] = far(before)
    if contexts == 2:
        low = jnp.where(context_first, down_near, down_far)
        high = jnp.where(context_first, down_far, down_near)
        w_down = jnp.concatenate([low, high], axis=1).reshape(owners * part, -1)

    norm_two(rows[0], tie(norm_vectors, before))
    for index, row in enumerate(rows):
        shift = tie(up_shift, before)
        row["z"], row["gu"], gc_first, gc_last, feed_first, feed_last, row["feed_sums"] = feed_forward(
            row["c"], row["g"], w_up, w_down, shift
        )
        other, key = (rows[-1], "branch_far") if index == 0 else (rows[index - 1], "gc_far")
        gc_first, gc_last, other[key] = hold((gc_first, gc_last, other[key]))
        before = row["gc"] = sum_near(gc_first, gc_last)
        row["gc_far"] = far(before)
        row["feed"] = (feed_first, feed_last)
        if index + 1 < row_count:
            norm_two(rows[index + 1], norm_vectors)
    for row in rows:
        row["feed"] = sum_near(*row["feed"])

    join = lambda key: jnp.concatenate([row[key] for row in rows], axis=0)
    join_two = lambda key: jnp.concatenate([piece for row in rows for piece in row[key]], axis=0)
    scatter = lambda v: lax.psum_scatter(v, "shard", scatter_dimension=0, tiled=True)
    if contexts == 2:
        finish = lambda v: v.astype(f32) + over_ctx(v).astype(f32)
    else:
        finish = lambda v: lax.psum(v, "ctx").astype(f32)
    last_row = rows[-1]

    def norm_two_back(row):
        row["gh"], ga, norm_sums = by_tokens(
            norm_two_back_kernel,
            [row["h"], row["gc"], row["gc_far"], row["g"]],
            norm_vectors,
            [f32, bf16],
            "norm_two_back",
            sums=True,
        )
        row["ga"] = (ga, near(ga))
        return norm_sums[0:3]

    pair = sum(norm_two_back(row) for row in rows[:-1])
    last_row["gu"], last_row["z"] = hold((last_row["gu"], last_row["z"], before, *[row["ga"][0] for row in rows[:-1]]))[:2]
    grad_up = mm(join_two("c"), join("gu"), TN).astype(bf16)
    grad_down = mm(join("g"), join("z"), TN).astype(bf16)
    grad_up, grad_down, last_row["gc_far"] = hold((grad_up, grad_down, last_row["gc_far"]))
    pair = pair + norm_two_back(last_row)
    grad_proj = mm(join_two("ga"), join("o"), TN).astype(bf16)
    before = (grad_up, grad_down)
    y_free = last_row["gc_far"]
    grad_up = scatter(grad_up)
    if contexts == 2:
        cut = grad_down.reshape(owners, 2, part // 2, -1)
        keep = lax.dynamic_index_in_dim(cut, context, 1, keepdims=False)
        came = over_ctx(lax.dynamic_index_in_dim(cut, 1 - context, 1, keepdims=False))
    else:
        grad_down = scatter(grad_down)

    for index, row in enumerate(rows):
        feed_far = far(tie(row["feed"], y_free))
        out = attend_backward(
            tie(row["flags"], *before),
            row["q"],
            row["ga"],
            w_proj,
            row["o"],
            row["k_aug"],
            row["v_aug"],
            row["cos"],
            row["sin"],
            row["cos_k"],
            row["sin_k"],
            heads,
            key_block,
        )
        if index:
            prior = rows[index - 1]
            *out, feed_far, prior["dkvs"], grad_up = hold((*out, feed_far, prior["dkvs"], grad_up))
            if contexts == 2:
                *out, grad_down = hold((*out, grad_down))
        elif contexts == 2:
            *out, feed_far, came = hold((*out, feed_far, came))
            grad_down = scatter((keep.astype(f32) + came.astype(f32)).astype(bf16).reshape(owners * part // 2, -1))
        else:
            *out, feed_far = hold((*out, feed_far))
        y_free = feed_far
        before = (out[0], grad_proj)
        row["gq"] = out[0]
        row["feed_far"] = feed_far
        if contexts == 2:
            row["dkvs"] = [out[1], over_ctx(out[2]), over_ctx(out[3])]
        else:
            row["dkvs"] = [lax.psum_scatter(out[1], "ctx", scatter_dimension=0, tiled=True)]

    side_list = side.reshape(1).astype(jnp.int32)
    grad_proj = scatter(grad_proj)
    sums = 0.0
    for index, row in enumerate(rows):
        first, last, row["dkv"], back_sums = project_back(row["x"], w_qkv, tie(row["gq"], *before), row["dkvs"])
        sums = sums + back_sums
        if index == 0:
            kvs = last_row["dkvs"]
            first, last, row["dkv"], kvs[:-1] = hold((first, last, row["dkv"], kvs[:-1]))
            last_row["gq"] = tie(last_row["gq"], row["dkv"])
            grad_q = mm(join("a"), join("gq"), TN).astype(bf16)
            kvs[-1] = tie(kvs[-1], grad_q)
            grad_q = scatter(grad_q)
            outs = []
            for done in rows:
                mine = by_tokens(
                    close_kernel,
                    [done["h"], done["feed"], done["feed_far"], done["live"]],
                    tie(jnp.broadcast_to(down_shift, (8, width)), row["dkv"]),
                    [bf16],
                    "close",
                )[0]
                outs += [mine, near(mine)]
            outs = gather_rows(side_list, outs)
            before = (row["dkv"], kvs[-1], outs)
        else:
            prior = rows[index - 1]
            down_came = over_ctx(tie(grad_down, kvs[-1])) if contexts == 2 else grad_down
            first, last, prior["ga1_far"], down_came = hold((first, last, prior["ga1_far"], down_came))
            before = (row["dkv"],)
        row["ga1"] = sum_near(first, last)
        row["ga1_far"] = far(row["ga1"])
    grad_kv = mm(join("a"), join("dkv"), TN).astype(bf16)
    def sum_over(v, axis):
        size, step = lax.axis_size(axis), 1
        while step < size:
            v = v + lax.ppermute(v, axis, [(i, i ^ step) for i in range(size)])
            step *= 2
        return v

    def owned(v):
        v = v.reshape(owners, -1)
        return jnp.pad(v, ((0, 0), (0, part - v.shape[1]))).reshape(-1)

    feed_sums = sum(row["feed_sums"] for row in rows)
    d_qb = jnp.concatenate([sums[2, :local], sums[3, : 2 * local]]).reshape(3, heads, owners, -1)
    d_qb = owned(jnp.transpose(d_qb, (2, 0, 1, 3)))
    d_ub = feed_sums[0, : fc1_bias.size * owners].reshape(fc1_bias.shape[0], owners, fc1_bias.shape[1])
    d_ub = owned(jnp.transpose(d_ub, (1, 0, 2)))
    vector = jnp.concatenate([pair, feed_sums[1:2, :width], d_qb[None], d_ub[None], sums[0:2]], axis=0)
    vector_one = sum_over(vector, "ctx")
    up_came = over_ctx(tie(grad_up, vector_one)) if contexts == 2 else grad_up
    last_row["ga1_far"], up_came, grad_q, grad_proj = hold((last_row["ga1_far"], up_came, grad_q, grad_proj))
    grad_kv = scatter(grad_kv)
    if contexts == 2:
        grad_up = grad_up.astype(f32) + up_came.astype(f32)
        low = jnp.where(context_first, grad_down, down_came)
        high = jnp.where(context_first, down_came, grad_down)
        grad_down = jnp.concatenate([low, high], axis=0).astype(f32)
    else:
        grad_up, grad_down = finish(up_came), finish(down_came)
    grad_q, grad_proj = finish(grad_q), finish(grad_proj)

    ins = []
    for row in rows:
        mine = by_tokens(
            norm_one_back_kernel,
            [row["x"], row["ga1"], row["ga1_far"], row["gh"]],
            jnp.broadcast_to(gain_one, (8, width)),
            [bf16],
            "norm_one_back",
        )[0]
        ins += [mine, near(mine)]

    vector = sum_over(tie(vector_one, ins[0]), "shard")
    vector = lax.dynamic_slice_in_dim(vector, place * part, part, axis=1)
    both = vector + near(vector)
    norm_one = both[6:8] + far(both[6:8])

    ins = gather_rows(side_list, ins)
    grad_kv = finish(tie(grad_kv, ins, grad_q, grad_proj))
    return (
        outs,
        ins,
        norm_one[0],
        norm_one[1],
        jnp.concatenate([grad_q, grad_kv], axis=1).reshape(qkv_weight.shape),
        vector[4, :qb_size].reshape(qkv_bias.shape),
        grad_proj.T,
        both[2],
        both[0],
        both[1],
        grad_up,
        vector[5, : fc1_bias.size].reshape(fc1_bias.shape),
        grad_down.T,
        vector[3],
    )


def solution(mesh):
    in_specs = (
        P("shard", "ctx", None),
        P("shard", "ctx", None),
        P("shard", None),
        P(None, "shard", "ctx"),
        P("shard"),
        P("shard"),
        P("shard", None, "tp"),
        P(None, "tp", "shard"),
        P("tp", "shard"),
        P("shard"),
        P("shard"),
        P("shard"),
        P("shard", "tp"),
        P("tp", "shard"),
        P("tp", "shard"),
        P("shard"),
    )
    out_specs = (
        P("shard", "ctx", None),
        P("shard", "ctx", None),
        P("shard"),
        P("shard"),
        P("shard", None, "tp"),
        P(None, "tp", "shard"),
        P("tp", "shard"),
        P("shard"),
        P("shard"),
        P("shard"),
        P("shard", "tp"),
        P("tp", "shard"),
        P("tp", "shard"),
        P("shard"),
    )
    return jax.shard_map(
        on_device, mesh=mesh, in_specs=in_specs, out_specs=out_specs, check_vma=False
    )
```

```python
import functools
import math

import jax
import jax.numpy as jnp
from jax import lax
from jax.experimental import pallas as pl
from jax.experimental.pallas import tpu as pltpu
from jax.sharding import PartitionSpec as P

HEAD_DIM = 80
LANES = 128
norm_eps = 1e-06
hide = 1e30
floor_max = -1e29
log2e = math.log2(math.e)
bf16 = jnp.bfloat16
f32 = jnp.float32
NT = (((1,), (1,)), ((), ()))
NN = (((1,), (0,)), ((), ()))
TN = (((0,), (0,)), ((), ()))


def mm(a, b, dims=NN):
    return lax.dot_general(a, b, dims, preferred_element_type=f32)


def tie(value, *others):
    return lax.optimization_barrier((value,) + others)[0]


def first_blocks(steps):
    return lambda i, *_: (jnp.minimum(i, steps // 2 - 1), 0)


def last_blocks(steps):
    return lambda i, *_: (jnp.maximum(i - steps // 2, 0), 0)


def store_halves(first_ref, last_ref, value):
    step, split = pl.program_id(0), pl.num_programs(0) // 2

    @pl.when(step < split)
    def first():
        first_ref[...] = value

    @pl.when(step >= split)
    def last():
        last_ref[...] = value


def lane_index(rows):
    return lax.broadcasted_iota(jnp.int32, (rows, LANES), 1)


def swap_halves(w, lane):
    half = HEAD_DIM // 2
    up = pltpu.roll(w, LANES - half, 1)
    down = pltpu.roll(w, half, 1)
    return jnp.where(lane < half, up, down)


def widen(piece):
    rows = piece.shape[0]
    tail = jnp.zeros((rows, LANES - piece.shape[1]), piece.dtype)
    return jnp.concatenate([piece, tail], axis=1)


def split_three(column):
    high = column.astype(bf16).astype(f32)
    rest = column - high
    mid = rest.astype(bf16).astype(f32)
    return high, mid, rest - mid


def place_three(base, column, lane):
    high, mid, low = split_three(column)
    base = jnp.where(lane == 96, high, base)
    base = jnp.where(lane == 97, mid, base)
    return jnp.where(lane == 98, low, base)


def qkv_kernel(heads, x_ref, w_ref, ln_ref, b_ref, cos_ref, sin_ref, feat_ref, a_ref, q_ref, kv_ref):
    width = heads * HEAD_DIM
    x = x_ref[...].astype(f32)
    rows = x.shape[0]
    center = x - jnp.mean(x, axis=1, keepdims=True)
    inverse = lax.rsqrt(jnp.mean(center * center, axis=1, keepdims=True) + norm_eps)
    a = (center * inverse * ln_ref[0:1, :] + ln_ref[1:2, :]).astype(bf16)
    a_ref[...] = a
    y = mm(a, w_ref[...]) + b_ref[0:1, :]
    cos, sin = cos_ref[...], sin_ref[...]
    lane = lane_index(rows)
    kv = []
    for h in range(heads):
        w = widen(y[:, h * HEAD_DIM : (h + 1) * HEAD_DIM])
        q = (w * cos + swap_halves(w, lane) * sin) * (HEAD_DIM**-0.5 * log2e)
        q_ref[h] = jnp.where(lane < HEAD_DIM, q.astype(bf16), feat_ref[...])
    for h in range(heads):
        begin = width + h * HEAD_DIM
        w = widen(y[:, begin : begin + HEAD_DIM])
        kv.append((w * cos + swap_halves(w, lane) * sin)[:, :HEAD_DIM].astype(bf16))
    kv.append(y[:, 2 * width : 3 * width].astype(bf16))
    kv_ref[...] = jnp.concatenate(kv, axis=1)


def project_row(x, w, ln, bias, cos, sin, feat, heads):
    rows, width = x.shape
    block = min(256, rows)
    wide = w.shape[1]
    local = heads * HEAD_DIM
    by_rows = lambda n: pl.BlockSpec((block, n), lambda i: (i, 0))
    whole = lambda a: pl.BlockSpec(a.shape, lambda i: (0,) * a.ndim)
    return pl.pallas_call(
        functools.partial(qkv_kernel, heads),
        grid=(rows // block,),
        in_specs=[
            by_rows(width),
            whole(w),
            whole(ln),
            whole(bias),
            by_rows(LANES),
            by_rows(LANES),
            by_rows(LANES),
        ],
        out_specs=[
            by_rows(width),
            pl.BlockSpec((heads, block, LANES), lambda i: (0, i, 0)),
            by_rows(2 * local),
        ],
        out_shape=[
            jax.ShapeDtypeStruct((rows, width), bf16),
            jax.ShapeDtypeStruct((heads, rows, LANES), bf16),
            jax.ShapeDtypeStruct((rows, 2 * local), bf16),
        ],
        cost_estimate=pl.CostEstimate(
            flops=2 * rows * width * wide, bytes_accessed=rows * width * 4 + width * wide * 2, transcendentals=0
        ),
        name="project_row",
    )(x, w, ln, bias, cos, sin, feat)


def forward_kernel(heads, segments, block, flag_ref, q_ref, w_ref, *refs):
    kv_refs = refs[:segments]
    feat_refs = refs[segments : 2 * segments]
    o_ref, q_out, k_aug, v_aug, p_first, p_last, m_scr, acc_scr = refs[2 * segments :]
    width = heads * HEAD_DIM
    step = pl.program_id(0)
    keys = k_aug.shape[1]
    count = keys // block
    rows = q_ref.shape[1]

    @pl.when(step == 0)
    def build():
        offset = 0
        for s in range(segments):
            length = kv_refs[s].shape[0]
            piece = min(length, 256)
            for t in range(length // piece):
                at = pl.ds(t * piece, piece)
                to = pl.ds(offset + t * piece, piece)
                kv = kv_refs[s][at, :]
                feat = feat_refs[s][at, :]
                lane = lane_index(piece)
                tail = jnp.where(lane == HEAD_DIM, 1.0, jnp.where((lane >= 96) & (lane < 99), -1.0, 0.0)).astype(bf16)
                for h in range(heads):
                    k = kv[:, h * HEAD_DIM : (h + 1) * HEAD_DIM]
                    v = kv[:, width + h * HEAD_DIM : width + (h + 1) * HEAD_DIM]
                    k_aug[h, to, :] = jnp.concatenate([k, feat[:, HEAD_DIM:]], axis=1)
                    v_aug[h, to, :] = jnp.concatenate([v, tail[:, HEAD_DIM:]], axis=1)
            offset += length

    m_scr[...] = jnp.full(m_scr.shape, floor_max, f32)
    acc_scr[...] = jnp.zeros(acc_scr.shape, f32)

    def visit(j, carry):
        @pl.when(flag_ref[step * count + j] > 0)
        def go():
            at = pl.ds(pl.multiple_of(j * block, block), block)
            for h in range(heads):
                s = mm(q_ref[h], k_aug[h, at, :], NT)
                old = m_scr[h]
                cuts = [s[:, c : c + LANES] for c in range(0, block, LANES)]
                top = functools.reduce(jnp.maximum, cuts)
                new = jnp.maximum(old, jnp.max(top, axis=1, keepdims=True))
                p = jnp.concatenate([jnp.exp2(cut - new) for cut in cuts], axis=1)
                m_scr[h] = new
                acc_scr[h] = acc_scr[h] * jnp.exp2(old - new) + mm(p.astype(bf16), v_aug[h, at, :])

        return carry

    lax.fori_loop(0, count, visit, 0)
    lane = lane_index(rows)
    outs = []
    for h in range(heads):
        acc = acc_scr[h]
        total = acc[:, HEAD_DIM : HEAD_DIM + 1]
        alive = total > 0.0
        safe = jnp.where(alive, total, 1.0)
        outs.append((acc / safe)[:, :HEAD_DIM].astype(bf16))
        level = jnp.where(alive, m_scr[h][:, 0:1] + jnp.log2(safe), 0.0)
        q_out[h] = place_three(q_ref[h].astype(f32), level, lane).astype(bf16)
    o = jnp.concatenate(outs, axis=1)
    o_ref[...] = o
    store_halves(p_first, p_last, mm(o, w_ref[...], NT).astype(bf16))


def attend_forward(flags, q_aug, w, kvs, feats, heads, block):
    rows = q_aug.shape[1]
    tall = min(256, rows // 2)
    steps = rows // tall
    width = w.shape[0]
    keys = sum(kv.shape[0] for kv in kvs)
    segments = len(kvs)
    whole = lambda a: pl.BlockSpec(a.shape, lambda i, f: (0,) * a.ndim)
    q_spec = pl.BlockSpec((heads, tall, LANES), lambda i, f: (0, i, 0))
    k_spec = pl.BlockSpec((heads, keys, LANES), lambda i, f: (0, 0, 0))
    local = heads * HEAD_DIM
    return pl.pallas_call(
        functools.partial(forward_kernel, heads, segments, block),
        grid_spec=pltpu.PrefetchScalarGridSpec(
            num_scalar_prefetch=1,
            grid=(rows // tall,),
            in_specs=[q_spec, whole(w)] + [whole(kv) for kv in kvs] + [whole(f) for f in feats],
            out_specs=[
                pl.BlockSpec((tall, local), lambda i, f: (i, 0)),
                q_spec,
                k_spec,
                k_spec,
                pl.BlockSpec((tall, width), first_blocks(steps)),
                pl.BlockSpec((tall, width), last_blocks(steps)),
            ],
            scratch_shapes=[
                pltpu.VMEM((heads, tall, LANES), f32),
                pltpu.VMEM((heads, tall, LANES), f32),
            ],
        ),
        out_shape=[
            jax.ShapeDtypeStruct((rows, local), bf16),
            jax.ShapeDtypeStruct((heads, rows, LANES), bf16),
            jax.ShapeDtypeStruct((heads, keys, LANES), bf16),
            jax.ShapeDtypeStruct((heads, keys, LANES), bf16),
            jax.ShapeDtypeStruct((rows // 2, width), bf16),
            jax.ShapeDtypeStruct((rows // 2, width), bf16),
        ],
        cost_estimate=pl.CostEstimate(
            flops=2 * rows * keys * heads * LANES, bytes_accessed=8 * keys * local, transcendentals=rows * keys * heads // 2
        ),
        name="attend_forward",
    )(flags, q_aug, w, *kvs, *feats)


def backward_kernel(
    heads, segments, block, flag_ref, q_ref, ga_first, ga_last, w_ref, o_ref, k_aug, v_aug, cosq_ref, sinq_ref, *refs
):
    cosk_refs = refs[:segments]
    sink_refs = refs[segments : 2 * segments]
    dq_ref = refs[2 * segments]
    dkv_refs = refs[2 * segments + 1 : 3 * segments + 1]
    k_turn, dk_acc, dv_acc, dq_acc, go_scr = refs[3 * segments + 1 :]
    step = pl.program_id(0)
    keys = k_aug.shape[1]
    count = keys // block
    rows = q_ref.shape[1]
    scale = HEAD_DIM**-0.5

    @pl.when(step == 0)
    def build():
        dk_acc[...] = jnp.zeros(dk_acc.shape, f32)
        dv_acc[...] = jnp.zeros(dv_acc.shape, f32)
        for h in range(heads):
            for t in range(count):
                at = pl.ds(t * block, block)
                k_turn[h, :, at] = k_aug[h, at, :].T

    lane = lane_index(rows)
    ga = jnp.where(step < pl.num_programs(0) // 2, ga_first[...], ga_last[...])
    go_all = mm(ga, w_ref[...]).astype(bf16).astype(f32)
    for h in range(heads):
        cut = slice(h * HEAD_DIM, (h + 1) * HEAD_DIM)
        go = go_all[:, cut]
        delta = jnp.sum(go * o_ref[:, cut].astype(f32), axis=1, keepdims=True)
        go_scr[h] = place_three(widen(go), delta, lane).astype(bf16)
    dq_acc[...] = jnp.zeros(dq_acc.shape, f32)

    def visit(j, carry):
        @pl.when(flag_ref[step * count + j] > 0)
        def run():
            at = pl.ds(pl.multiple_of(j * block, block), block)
            for h in range(heads):
                q, go = q_ref[h], go_scr[h]
                p = jnp.exp2(mm(k_aug[h, at, :], q, NT))
                ds = (p * mm(v_aug[h, at, :], go, NT)).astype(bf16)
                dv_acc[h, at, :] += mm(p.astype(bf16), go)
                dk_acc[h, at, :] += mm(ds, q)
                dq_acc[h] += mm(k_turn[h, :, at], ds)

        return carry

    lax.fori_loop(0, count, visit, 0)

    def turn_back(w, cos, sin, index):
        return w * cos - swap_halves(w, index) * sin

    outs = []
    for h in range(heads):
        w = dq_acc[h].T
        back = turn_back(w, cosq_ref[...], sinq_ref[...], lane) * scale
        outs.append(back[:, :HEAD_DIM].astype(bf16))
    dq_ref[...] = jnp.concatenate(outs, axis=1)

    @pl.when(step == pl.num_programs(0) - 1)
    def finish():
        offset = 0
        for s in range(segments):
            length = dkv_refs[s].shape[0]
            piece = min(length, 256)
            index = lane_index(piece)
            for t in range(length // piece):
                at = pl.ds(t * piece, piece)
                of = pl.ds(offset + t * piece, piece)
                parts = []
                for h in range(heads):
                    w = dk_acc[h, of, :]
                    back = turn_back(w, cosk_refs[s][at, :], sink_refs[s][at, :], index) * (1.0 / log2e)
                    parts.append(back[:, :HEAD_DIM].astype(bf16))
                for h in range(heads):
                    parts.append(dv_acc[h, of, :][:, :HEAD_DIM].astype(bf16))
                dkv_refs[s][at, :] = jnp.concatenate(parts, axis=1)
            offset += length


def attend_backward(flags, q_aug, ga, w, o, k_aug, v_aug, cos_q, sin_q, cos_k, sin_k, heads, block):
    rows = q_aug.shape[1]
    tall = min(256, rows // 2)
    steps = rows // tall
    width = w.shape[0]
    keys = k_aug.shape[1]
    segments = len(cos_k)
    local = heads * HEAD_DIM
    whole = lambda a: pl.BlockSpec(a.shape, lambda i, f: (0,) * a.ndim)
    by_rows = lambda n: pl.BlockSpec((tall, n), lambda i, f: (i, 0))
    q_spec = pl.BlockSpec((heads, tall, LANES), lambda i, f: (0, i, 0))
    return pl.pallas_call(
        functools.partial(backward_kernel, heads, segments, block),
        grid_spec=pltpu.PrefetchScalarGridSpec(
            num_scalar_prefetch=1,
            grid=(rows // tall,),
            in_specs=[
                q_spec,
                pl.BlockSpec((tall, width), first_blocks(steps)),
                pl.BlockSpec((tall, width), last_blocks(steps)),
                whole(w),
                by_rows(local),
                whole(k_aug),
                whole(v_aug),
                by_rows(LANES),
                by_rows(LANES),
            ]
            + [whole(t) for t in cos_k]
            + [whole(t) for t in sin_k],
            out_specs=[by_rows(local)]
            + [pl.BlockSpec((t.shape[0], 2 * local), lambda i, f: (0, 0)) for t in cos_k],
            scratch_shapes=[
                pltpu.VMEM((heads, LANES, keys), bf16),
                pltpu.VMEM((heads, keys, LANES), f32),
                pltpu.VMEM((heads, keys, LANES), f32),
                pltpu.VMEM((heads, LANES, tall), f32),
                pltpu.VMEM((heads, tall, LANES), bf16),
            ],
        ),
        out_shape=[jax.ShapeDtypeStruct((rows, local), bf16)]
        + [jax.ShapeDtypeStruct((t.shape[0], 2 * local), bf16) for t in cos_k],
        cost_estimate=pl.CostEstimate(
            flops=5 * rows * keys * heads * LANES, bytes_accessed=16 * keys * local, transcendentals=rows * keys * heads // 2
        ),
        name="attend_backward",
    )(flags, q_aug, *ga, w, o, k_aug, v_aug, cos_q, sin_q, *cos_k, *sin_k)


def feed_kernel(chunk, c_first, c_last, g_ref, up_ref, down_ref, shift_ref, z_ref, gu_ref, gc_first, gc_last, feed_first, feed_last, sum_ref):
    step = pl.program_id(0)
    c = jnp.where(step < pl.num_programs(0) // 2, c_first[...], c_last[...])
    g = g_ref[...]
    sums = []
    for begin in range(0, up_ref.shape[1], chunk):
        cut = slice(begin, begin + chunk)
        u = mm(c, up_ref[:, cut]) + shift_ref[0:1, cut]
        sg = 0.5 + 0.5 * jnp.tanh(0.851 * u)
        z = (u * sg).astype(bf16)
        gu = (mm(g, down_ref[:, cut]) * (sg + 1.702 * u * sg * (1.0 - sg))).astype(bf16)
        z_ref[:, cut] = z
        gu_ref[:, cut] = gu
        sums.append(jnp.sum(gu.astype(f32), axis=0, keepdims=True))
    store_halves(gc_first, gc_last, mm(gu_ref[...], up_ref[...], NT).astype(bf16))
    store_halves(feed_first, feed_last, mm(z_ref[...], down_ref[...], NT).astype(bf16))

    @pl.when(step == 0)
    def clear():
        sum_ref[...] = jnp.zeros(sum_ref.shape, f32)

    sum_ref[0:1, :] += jnp.concatenate(sums, axis=1)
    sum_ref[1:2, : g.shape[1]] += jnp.sum(g.astype(f32), axis=0, keepdims=True)


def feed_forward(c, g, w_up, w_down, shift):
    rows, width = g.shape
    hidden = w_up.shape[1]
    tall = min(256, rows // 2)
    steps = rows // tall
    chunk = 256 if hidden % 256 == 0 else hidden
    by_rows = lambda n: pl.BlockSpec((tall, n), lambda i: (i, 0))
    whole = lambda a: pl.BlockSpec(a.shape, lambda i: (0,) * a.ndim)
    first = pl.BlockSpec((tall, width), first_blocks(steps))
    last = pl.BlockSpec((tall, width), last_blocks(steps))
    part = jax.ShapeDtypeStruct((rows // 2, width), bf16)
    longest = max(width, hidden)
    return pl.pallas_call(
        functools.partial(feed_kernel, chunk),
        grid=(steps,),
        in_specs=[first, last, by_rows(width), whole(w_up), whole(w_down), whole(shift)],
        out_specs=[by_rows(hidden), by_rows(hidden), first, last, first, last, pl.BlockSpec((8, longest), lambda i: (0, 0))],
        out_shape=[
            jax.ShapeDtypeStruct((rows, hidden), bf16),
            jax.ShapeDtypeStruct((rows, hidden), bf16),
            part,
            part,
            part,
            part,
            jax.ShapeDtypeStruct((8, longest), f32),
        ],
        cost_estimate=pl.CostEstimate(
            flops=8 * rows * width * hidden, bytes_accessed=4 * width * hidden + 12 * rows * width, transcendentals=rows * hidden
        ),
        name="feed_forward",
    )(*c, g, w_up, w_down, shift)


def back_kernel(pieces, x_ref, w_ref, gq_ref, *refs):
    kv_refs = refs[:pieces]
    p_first, p_last, dkv_ref, sum_ref = refs[pieces:]
    gq = gq_ref[...]
    if pieces == 1:
        dkv = kv_refs[0][...]
    else:
        other = jnp.where(pl.program_id(0) < pl.num_programs(0) // 2, kv_refs[1][...], kv_refs[2][...])
        dkv = (kv_refs[0][...].astype(f32) + other.astype(f32)).astype(bf16)
    dkv_ref[...] = dkv
    tail = jnp.zeros((gq.shape[0], w_ref.shape[1] - gq.shape[1] - dkv.shape[1]), bf16)
    e = mm(jnp.concatenate([gq, dkv, tail], axis=1), w_ref[...], NT)
    store_halves(p_first, p_last, e.astype(bf16))
    x = x_ref[...].astype(f32)
    center = x - jnp.mean(x, axis=1, keepdims=True)
    unit = center * lax.rsqrt(jnp.mean(center * center, axis=1, keepdims=True) + norm_eps)

    @pl.when(pl.program_id(0) == 0)
    def clear():
        sum_ref[...] = jnp.zeros(sum_ref.shape, f32)

    local = gq.shape[1]
    sum_ref[0:1, :] += jnp.sum(e * unit, axis=0, keepdims=True)
    sum_ref[1:2, :] += jnp.sum(e, axis=0, keepdims=True)
    sum_ref[2:3, :local] += jnp.sum(gq.astype(f32), axis=0, keepdims=True)
    sum_ref[3:4, : 2 * local] += jnp.sum(dkv.astype(f32), axis=0, keepdims=True)


def project_back(x, w, gq, dkvs):
    rows, width = x.shape
    local = gq.shape[1]
    tall = min(512, rows // 2)
    steps = rows // tall
    by_rows = lambda n: pl.BlockSpec((tall, n), lambda i: (i, 0))
    whole = lambda a: pl.BlockSpec(a.shape, lambda i: (0,) * a.ndim)
    part = jax.ShapeDtypeStruct((rows // 2, width), bf16)
    kv_specs = [
        by_rows(2 * local),
        pl.BlockSpec((tall, 2 * local), first_blocks(steps)),
        pl.BlockSpec((tall, 2 * local), last_blocks(steps)),
    ]
    return pl.pallas_call(
        functools.partial(back_kernel, len(dkvs)),
        grid=(steps,),
        in_specs=[by_rows(width), whole(w), by_rows(local)] + kv_specs[: len(dkvs)],
        out_specs=[
            pl.BlockSpec((tall, width), first_blocks(steps)),
            pl.BlockSpec((tall, width), last_blocks(steps)),
            by_rows(2 * local),
            pl.BlockSpec((8, width), lambda i: (0, 0)),
        ],
        out_shape=[part, part, jax.ShapeDtypeStruct((rows, 2 * local), bf16), jax.ShapeDtypeStruct((8, width), f32)],
        cost_estimate=pl.CostEstimate(
            flops=6 * rows * width * local, bytes_accessed=6 * width * local + 6 * rows * width, transcendentals=rows
        ),
        name="project_back",
    )(x, w, gq, *dkvs)


def norm_stats(rows_in):
    center = rows_in - jnp.mean(rows_in, axis=1, keepdims=True)
    inverse = lax.rsqrt(jnp.mean(center * center, axis=1, keepdims=True) + norm_eps)
    return center * inverse, inverse


def norm_backward(grad_rows, unit_rows, inverse, gain):
    scaled = grad_rows * gain
    return inverse * (
        scaled
        - jnp.mean(scaled, axis=1, keepdims=True)
        - unit_rows * jnp.mean(scaled * unit_rows, axis=1, keepdims=True)
    )


def norm_two_kernel(x_ref, near_ref, far_ref, vec_ref, h_ref, c_ref):
    h = x_ref[...].astype(f32) + (near_ref[...].astype(f32) + far_ref[...].astype(f32)) + vec_ref[0:1, :]
    h_ref[...] = h
    c_ref[...] = (norm_stats(h)[0] * vec_ref[1:2, :] + vec_ref[2:3, :]).astype(bf16)


def norm_two_back_kernel(h_ref, near_ref, far_ref, g_ref, vec_ref, gh_ref, ga_ref, sum_ref):
    unit, inverse = norm_stats(h_ref[...])
    gc = near_ref[...].astype(f32) + far_ref[...].astype(f32)
    gh = g_ref[...].astype(f32) + norm_backward(gc, unit, inverse, vec_ref[1:2, :])
    ga = gh.astype(bf16)
    gh_ref[...] = gh
    ga_ref[...] = ga

    @pl.when(pl.program_id(0) == 0)
    def clear():
        sum_ref[...] = jnp.zeros(sum_ref.shape, f32)

    sum_ref[0:1, :] += jnp.sum(gc * unit, axis=0, keepdims=True)
    sum_ref[1:2, :] += jnp.sum(gc, axis=0, keepdims=True)
    sum_ref[2:3, :] += jnp.sum(ga.astype(f32), axis=0, keepdims=True)


def norm_one_back_kernel(x_ref, near_ref, far_ref, gh_ref, vec_ref, out_ref):
    unit, inverse = norm_stats(x_ref[...].astype(f32))
    ga1 = near_ref[...].astype(f32) + far_ref[...].astype(f32)
    out_ref[...] = (gh_ref[...] + norm_backward(ga1, unit, inverse, vec_ref[0:1, :])).astype(bf16)


def close_kernel(h_ref, near_ref, far_ref, live_ref, vec_ref, out_ref):
    feed = near_ref[...].astype(f32) + far_ref[...].astype(f32)
    out_ref[...] = ((h_ref[...] + feed + vec_ref[0:1, :]) * live_ref[...]).astype(bf16)


def by_tokens(body, arrays, vectors, kinds, name, sums=False):
    count, width = arrays[1].shape
    tall = min(128, count)
    in_specs = [pl.BlockSpec((tall, a.shape[1]), lambda i: (i, 0)) for a in arrays]
    out_specs = [pl.BlockSpec((tall, width), lambda i: (i, 0)) for _ in kinds]
    out_shape = [jax.ShapeDtypeStruct((count, width), kind) for kind in kinds]
    if sums:
        out_specs.append(pl.BlockSpec((8, width), lambda i: (0, 0)))
        out_shape.append(jax.ShapeDtypeStruct((8, width), f32))
    return pl.pallas_call(
        body,
        grid=(count // tall,),
        in_specs=in_specs + [pl.BlockSpec(vectors.shape, lambda i: (0, 0))],
        out_specs=out_specs,
        out_shape=out_shape,
        cost_estimate=pl.CostEstimate(flops=20 * count * width, bytes_accessed=14 * count * width, transcendentals=count),
        name=name,
    )(*arrays, vectors)


def gather_rows_kernel(side_ref, *refs):
    step = pl.program_id(0)
    for index, piece in enumerate(refs[:-1]):

        @pl.when(step == index)
        def copy(piece=piece):
            refs[-1][0] = piece[...]


def gather_rows(side, pieces):
    half, width = pieces[0].shape
    count = len(pieces)
    return pl.pallas_call(
        gather_rows_kernel,
        grid_spec=pltpu.PrefetchScalarGridSpec(
            num_scalar_prefetch=1,
            grid=(count,),
            in_specs=[pl.BlockSpec((half, width), lambda t, s: (0, 0)) for _ in pieces],
            out_specs=pl.BlockSpec((1, half, width), lambda t, s: (t // 2, jnp.where(t % 2 == 0, s[0], 1 - s[0]), 0)),
        ),
        out_shape=jax.ShapeDtypeStruct((count // 2, 2 * half, width), bf16),
        cost_estimate=pl.CostEstimate(flops=0, bytes_accessed=4 * count * half * width, transcendentals=0),
        name="gather_rows",
    )(side, *pieces)


def tables(grid_pos):
    lane = jnp.arange(LANES)
    quarter = HEAD_DIM // 4
    frequency = jnp.power(10000.0, -4.0 * (lane % quarter).astype(f32) / HEAD_DIM)
    place = jnp.where((lane // quarter) % 2 == 0, grid_pos[0][:, None], grid_pos[1][:, None])
    angle = jnp.where(lane < HEAD_DIM, place.astype(f32) * frequency, 0.0)
    return jnp.cos(angle), jnp.where(lane < HEAD_DIM // 2, -1.0, 1.0) * jnp.sin(angle)


def query_features(ids):
    lane = jnp.arange(LANES)
    return (lane == HEAD_DIM + 1 + ids[:, None]).astype(bf16)


def key_features(ids):
    lane = jnp.arange(LANES)
    slot = lane - HEAD_DIM
    same = (slot >= 1) & (slot == ids[:, None] + 1)
    wall = jnp.where((slot >= 0) & (slot < 16) & ~same, -hide, 0.0)
    return jnp.where((lane >= 96) & (lane < 99), -1.0, wall).astype(bf16)


def visit_flags(query_ids, key_ids, tall, block):
    q = query_ids.reshape(-1, tall)
    k = key_ids.reshape(-1, block)
    q_top, k_top = jnp.max(q, axis=1), jnp.max(k, axis=1)
    q_low = jnp.min(jnp.where(q >= 0, q, 1 << 20), axis=1)
    k_low = jnp.min(jnp.where(k >= 0, k, 1 << 20), axis=1)
    meet = (q_low[:, None] <= k_top[None, :]) & (k_low[None, :] <= q_top[:, None])
    return meet.astype(jnp.int32).reshape(-1)


def on_device(
    patches,
    cotangent,
    picture_ids,
    positions,
    ln1_gain,
    ln1_bias,
    qkv_weight,
    qkv_bias,
    proj_weight,
    proj_bias,
    ln2_gain,
    ln2_bias,
    fc1_weight,
    fc1_bias,
    fc2_weight,
    fc2_bias,
):
    row_count, row_share, width = patches.shape
    owners = lax.axis_size("shard")
    contexts = lax.axis_size("ctx")
    ways = lax.axis_size("tp")
    part = qkv_weight.shape[0]
    local = qkv_weight.shape[2]
    heads = local // HEAD_DIM
    half = row_share // 2
    side = lax.axis_index("tp") % 2
    context = lax.axis_index("ctx")
    pairs_near = [(i, i ^ 1) for i in range(ways)]
    pairs_far = [(i, i ^ 2) for i in range(ways)]
    pad = -3 * local % 256
    wide = 3 * local + pad

    def near(v):
        return lax.ppermute(v, "tp", pairs_near)

    def far(v):
        return lax.ppermute(v, "tp", pairs_far)

    def over_ctx(v):
        return lax.ppermute(v, "ctx", [(0, 1), (1, 0)])

    def mine_first(v, axis=0):
        return jnp.where(side == 0, v, jnp.roll(v, half, axis=axis))

    def column(v):
        flat = v.reshape(-1)
        return jnp.pad(flat, (0, part - flat.shape[0]))

    vectors = [ln1_gain, ln1_bias, ln2_gain, ln2_bias, proj_bias, fc2_bias, qkv_bias, fc1_bias]
    place = lax.axis_index("shard")
    context_first = context == 0

    def rotate_gather(piece):
        whole = lax.dynamic_update_index_in_dim(jnp.zeros((owners,) + piece.shape, piece.dtype), piece, place, 0)
        for step in range(1, owners):
            got = lax.ppermute(piece, "shard", [(i, (i + step) % owners) for i in range(owners)])
            whole = lax.dynamic_update_index_in_dim(whole, got, (place - step) % owners, 0)
        return whole

    tail = rotate_gather(jnp.stack([column(v) for v in vectors]).astype(bf16))
    packed = jnp.transpose(tail, (1, 0, 2)).reshape(len(vectors), width).astype(f32)
    qkv_piece = jnp.pad(qkv_weight.reshape(part, 3 * local), ((0, 0), (0, pad))).astype(bf16)
    gather = lambda v: lax.all_gather(v, "shard", axis=0, tiled=True)
    up_piece = fc1_weight.astype(bf16)
    down_piece = fc2_weight.T.astype(bf16)
    w_qkv = gather(qkv_piece)
    w_proj = rotate_gather(tie(proj_weight.T.astype(bf16), w_qkv)).reshape(owners * part, local)
    gain_one, bias_one, gain_two, bias_two, proj_shift, down_shift = [packed[i] for i in range(6)]
    qb_size = qkv_bias.size
    qkv_shift = packed[6].reshape(owners, part)[:, :qb_size].reshape((owners,) + qkv_bias.shape)
    qkv_shift = jnp.transpose(qkv_shift, (1, 2, 0, 3)).reshape(-1)
    qkv_shift = jnp.pad(qkv_shift, (0, pad)).reshape(1, wide)
    up_shift = packed[7].reshape(owners, part)[:, : fc1_bias.size].reshape((owners,) + fc1_bias.shape)
    up_shift = jnp.transpose(up_shift, (1, 0, 2)).reshape(1, -1)
    ln_one = tie(packed[0:2], up_piece, down_piece)

    ids_by_ctx = mine_first(picture_ids.reshape(row_count, contexts, row_share), axis=2)
    places = mine_first(positions, axis=2)
    block = min(256, half)

    def cut_last(spots):
        return [spots[0], spots[1][:half], spots[1][half:]] if contexts == 2 else spots

    key_block = 256
    rows = []
    for r in range(row_count):
        x = mine_first(patches[r])
        g = mine_first(cotangent[r])
        ids = lax.dynamic_index_in_dim(ids_by_ctx[r], context, 0, keepdims=False)
        if contexts == 2:
            other = lax.dynamic_index_in_dim(ids_by_ctx[r], 1 - context, 0, keepdims=False)
            key_ids = [ids, other]
            spots = [places[:, r], over_ctx(places[:, r])]
        else:
            key_ids = [ids_by_ctx[r].reshape(-1)]
            spots = [lax.all_gather(places[:, r], "ctx", axis=1, tiled=True)]
        live = (ids >= 0).astype(f32)[:, None]
        turns = [tables(spot) for spot in spots]
        own_turn = turns[0] if contexts == 2 else tables(places[:, r])
        rows.append(
            dict(
                x=x,
                g=(g.astype(f32) * live).astype(bf16),
                live=live,
                ids=ids,
                cos=own_turn[0],
                sin=own_turn[1],
                cos_k=cut_last([t[0] for t in turns]),
                sin_k=cut_last([t[1] for t in turns]),
                q_feat=query_features(ids),
                k_feat=[key_features(k) for k in key_ids],
                flags=visit_flags(ids, jnp.concatenate(key_ids), block, key_block),
            )
        )

    ln_one = tie(ln_one, qkv_shift, up_shift, *[row["g"] for row in rows])

    for row in rows:
        row["a"], row["q"], row["kv"] = project_row(
            row["x"], w_qkv, ln_one, qkv_shift, row["cos"], row["sin"], row["q_feat"], heads
        )
        if row is rows[0]:
            row["kv"], w_proj = lax.optimization_barrier((row["kv"], w_proj))
        if contexts == 2:
            row["kvs"] = [row["kv"], over_ctx(row["kv"])]
        else:
            row["kvs"] = [lax.all_gather(row["kv"], "ctx", axis=0, tiled=True)]

    down_piece, up_piece = lax.optimization_barrier((down_piece, up_piece, w_proj))[:2]
    if contexts == 2:
        down_cut = down_piece.reshape(2, part // 2, -1)
        down_near = gather(lax.dynamic_index_in_dim(down_cut, context, 0, keepdims=False))
        down_near = down_near.reshape(owners, part // 2, -1)
    else:
        w_down = gather(down_piece)
    w_up = gather(up_piece)

    def sum_near(first, last):
        return (first.astype(f32) + near(last).astype(f32)).astype(bf16)

    norm_vectors = jnp.pad(jnp.stack([proj_shift, gain_two, bias_two]), ((0, 5), (0, 0)))

    def norm_two(row, vectors):
        row["h"], mine = by_tokens(
            norm_two_kernel, [row["x"], row["branch"], row["branch_far"]], vectors, [f32, bf16], "norm_two"
        )
        row["c"] = (mine, near(mine))

    hold = lax.optimization_barrier
    before = rows[-1]["kv"]
    for index, row in enumerate(rows):
        row["o"], row["q"], row["k_aug"], row["v_aug"], first, last = attend_forward(
            tie(row["flags"], before), row["q"], w_proj, row["kvs"], row["k_feat"], heads, key_block
        )
        if index:
            prior = rows[index - 1]
            first, last, prior["branch_far"] = hold((first, last, prior["branch_far"]))
        if index + 1 < row_count:
            follow = rows[index + 1]
            first, last, follow["kvs"] = hold((first, last, follow["kvs"]))
            if contexts == 2:
                first, last, down_near = hold((first, last, down_near))
                down_far = over_ctx(down_near)
        elif contexts == 2:
            first, last, down_far, w_up = hold((first, last, down_far, w_up))
        before = row["branch"] = sum_near(first, last)
        row["branch_far"] = far(before)
    if contexts == 2:
        low = jnp.where(context_first, down_near, down_far)
        high = jnp.where(context_first, down_far, down_near)
        w_down = jnp.concatenate([low, high], axis=1).reshape(owners * part, -1)

    norm_two(rows[0], tie(norm_vectors, before))
    for index, row in enumerate(rows):
        shift = tie(up_shift, before)
        row["z"], row["gu"], gc_first, gc_last, feed_first, feed_last, row["feed_sums"] = feed_forward(
            row["c"], row["g"], w_up, w_down, shift
        )
        other, key = (rows[-1], "branch_far") if index == 0 else (rows[index - 1], "gc_far")
        gc_first, gc_last, other[key] = hold((gc_first, gc_last, other[key]))
        before = row["gc"] = sum_near(gc_first, gc_last)
        row["gc_far"] = far(before)
        row["feed"] = (feed_first, feed_last)
        if index + 1 < row_count:
            norm_two(rows[index + 1], norm_vectors)
    for row in rows:
        row["feed"] = sum_near(*row["feed"])

    join = lambda key: jnp.concatenate([row[key] for row in rows], axis=0)
    join_two = lambda key: jnp.concatenate([piece for row in rows for piece in row[key]], axis=0)
    scatter = lambda v: lax.psum_scatter(v, "shard", scatter_dimension=0, tiled=True)
    if contexts == 2:
        finish = lambda v: v.astype(f32) + over_ctx(v).astype(f32)
    else:
        finish = lambda v: lax.psum(v, "ctx").astype(f32)
    last_row = rows[-1]

    def norm_two_back(row):
        row["gh"], ga, norm_sums = by_tokens(
            norm_two_back_kernel,
            [row["h"], row["gc"], row["gc_far"], row["g"]],
            norm_vectors,
            [f32, bf16],
            "norm_two_back",
            sums=True,
        )
        row["ga"] = (ga, near(ga))
        return norm_sums[0:3]

    pair = sum(norm_two_back(row) for row in rows[:-1])
    last_row["gu"], last_row["z"] = hold((last_row["gu"], last_row["z"], before, *[row["ga"][0] for row in rows[:-1]]))[:2]
    grad_up = mm(join_two("c"), join("gu"), TN).astype(bf16)
    grad_down = mm(join("g"), join("z"), TN).astype(bf16)
    grad_up, grad_down, last_row["gc_far"] = hold((grad_up, grad_down, last_row["gc_far"]))
    pair = pair + norm_two_back(last_row)
    grad_proj = mm(join_two("ga"), join("o"), TN).astype(bf16)
    before = (grad_up, grad_down)
    y_free = last_row["gc_far"]
    grad_up = scatter(grad_up)
    if contexts == 2:
        cut = grad_down.reshape(owners, 2, part // 2, -1)
        keep = lax.dynamic_index_in_dim(cut, context, 1, keepdims=False)
        came = over_ctx(lax.dynamic_index_in_dim(cut, 1 - context, 1, keepdims=False))
    else:
        grad_down = scatter(grad_down)

    for index, row in enumerate(rows):
        feed_far = far(tie(row["feed"], y_free))
        out = attend_backward(
            tie(row["flags"], *before),
            row["q"],
            row["ga"],
            w_proj,
            row["o"],
            row["k_aug"],
            row["v_aug"],
            row["cos"],
            row["sin"],
            row["cos_k"],
            row["sin_k"],
            heads,
            key_block,
        )
        if index:
            prior = rows[index - 1]
            *out, feed_far, prior["dkvs"], grad_up = hold((*out, feed_far, prior["dkvs"], grad_up))
            if contexts == 2:
                *out, grad_down = hold((*out, grad_down))
        elif contexts == 2:
            *out, feed_far, came = hold((*out, feed_far, came))
            grad_down = scatter((keep.astype(f32) + came.astype(f32)).astype(bf16).reshape(owners * part // 2, -1))
        else:
            *out, feed_far = hold((*out, feed_far))
        y_free = feed_far
        before = (out[0], grad_proj)
        row["gq"] = out[0]
        row["feed_far"] = feed_far
        if contexts == 2:
            row["dkvs"] = [out[1], over_ctx(out[2]), over_ctx(out[3])]
        else:
            row["dkvs"] = [lax.psum_scatter(out[1], "ctx", scatter_dimension=0, tiled=True)]

    side_list = side.reshape(1).astype(jnp.int32)
    grad_proj = scatter(grad_proj)
    sums = 0.0
    for index, row in enumerate(rows):
        first, last, row["dkv"], back_sums = project_back(row["x"], w_qkv, tie(row["gq"], *before), row["dkvs"])
        sums = sums + back_sums
        if index == 0:
            kvs = last_row["dkvs"]
            first, last, row["dkv"], kvs[:-1] = hold((first, last, row["dkv"], kvs[:-1]))
            last_row["gq"] = tie(last_row["gq"], row["dkv"])
            grad_q = mm(join("a"), join("gq"), TN).astype(bf16)
            kvs[-1] = tie(kvs[-1], grad_q)
            grad_q = scatter(grad_q)
            outs = []
            for done in rows:
                mine = by_tokens(
                    close_kernel,
                    [done["h"], done["feed"], done["feed_far"], done["live"]],
                    tie(jnp.broadcast_to(down_shift, (8, width)), row["dkv"]),
                    [bf16],
                    "close",
                )[0]
                outs += [mine, near(mine)]
            outs = gather_rows(side_list, outs)
            before = (row["dkv"], kvs[-1], outs)
        else:
            prior = rows[index - 1]
            down_came = over_ctx(tie(grad_down, kvs[-1])) if contexts == 2 else grad_down
            first, last, prior["ga1_far"], down_came = hold((first, last, prior["ga1_far"], down_came))
            before = (row["dkv"],)
        row["ga1"] = sum_near(first, last)
        row["ga1_far"] = far(row["ga1"])
    grad_kv = mm(join("a"), join("dkv"), TN).astype(bf16)
    def sum_over(v, axis):
        size, step = lax.axis_size(axis), 1
        while step < size:
            v = v + lax.ppermute(v, axis, [(i, i ^ step) for i in range(size)])
            step *= 2
        return v

    def owned(v):
        v = v.reshape(owners, -1)
        return jnp.pad(v, ((0, 0), (0, part - v.shape[1]))).reshape(-1)

    feed_sums = sum(row["feed_sums"] for row in rows)
    d_qb = jnp.concatenate([sums[2, :local], sums[3, : 2 * local]]).reshape(3, heads, owners, -1)
    d_qb = owned(jnp.transpose(d_qb, (2, 0, 1, 3)))
    d_ub = feed_sums[0, : fc1_bias.size * owners].reshape(fc1_bias.shape[0], owners, fc1_bias.shape[1])
    d_ub = owned(jnp.transpose(d_ub, (1, 0, 2)))
    vector = jnp.concatenate([pair, feed_sums[1:2, :width], d_qb[None], d_ub[None], sums[0:2]], axis=0)
    vector_one = sum_over(vector, "ctx")
    up_came = over_ctx(tie(grad_up, vector_one)) if contexts == 2 else grad_up
    last_row["ga1_far"], up_came, grad_q, grad_proj = hold((last_row["ga1_far"], up_came, grad_q, grad_proj))
    grad_kv = scatter(grad_kv)
    if contexts == 2:
        grad_up = grad_up.astype(f32) + up_came.astype(f32)
        low = jnp.where(context_first, grad_down, down_came)
        high = jnp.where(context_first, down_came, grad_down)
        grad_down = jnp.concatenate([low, high], axis=0).astype(f32)
    else:
        grad_up, grad_down = finish(up_came), finish(down_came)
    come = over_ctx if contexts == 2 else lambda v: v
    add = (lambda v, w: v.astype(f32) + w.astype(f32)) if contexts == 2 else lambda v, w: finish(v)
    q_came, proj_came, kv_came = come(grad_q), come(grad_proj), come(grad_kv)

    ins = []
    for row in rows:
        mine = by_tokens(
            norm_one_back_kernel,
            [row["x"], row["ga1"], row["ga1_far"], row["gh"]],
            jnp.broadcast_to(gain_one, (8, width)),
            [bf16],
            "norm_one_back",
        )[0]
        if row is last_row:
            mine, q_came, proj_came = hold((mine, q_came, proj_came))
        ins += [mine, near(mine)]

    vector = sum_over(tie(vector_one, ins[0]), "shard")
    vector = lax.dynamic_slice_in_dim(vector, place * part, part, axis=1)
    both = vector + near(vector)
    norm_one = both[6:8] + far(both[6:8])

    ins, kv_came = hold((gather_rows(side_list, ins), kv_came))
    grad_q, grad_proj, grad_kv = add(grad_q, q_came), add(grad_proj, proj_came), add(grad_kv, kv_came)
    return (
        outs,
        ins,
        norm_one[0],
        norm_one[1],
        jnp.concatenate([grad_q, grad_kv], axis=1).reshape(qkv_weight.shape),
        vector[4, :qb_size].reshape(qkv_bias.shape),
        grad_proj.T,
        both[2],
        both[0],
        both[1],
        grad_up,
        vector[5, : fc1_bias.size].reshape(fc1_bias.shape),
        grad_down.T,
        vector[3],
    )


def solution(mesh):
    in_specs = (
        P("shard", "ctx", None),
        P("shard", "ctx", None),
        P("shard", None),
        P(None, "shard", "ctx"),
        P("shard"),
        P("shard"),
        P("shard", None, "tp"),
        P(None, "tp", "shard"),
        P("tp", "shard"),
        P("shard"),
        P("shard"),
        P("shard"),
        P("shard", "tp"),
        P("tp", "shard"),
        P("tp", "shard"),
        P("shard"),
    )
    out_specs = (
        P("shard", "ctx", None),
        P("shard", "ctx", None),
        P("shard"),
        P("shard"),
        P("shard", None, "tp"),
        P(None, "tp", "shard"),
        P("tp", "shard"),
        P("shard"),
        P("shard"),
        P("shard"),
        P("shard", "tp"),
        P("tp", "shard"),
        P("tp", "shard"),
        P("shard"),
    )
    return jax.shard_map(
        on_device, mesh=mesh, in_specs=in_specs, out_specs=out_specs, check_vma=False
    )
```

```python
import functools
import math

import jax
import jax.numpy as jnp
from jax import lax
from jax.experimental import pallas as pl
from jax.experimental.pallas import tpu as pltpu
from jax.sharding import PartitionSpec as P

HEAD_DIM = 80
LANES = 128
norm_eps = 1e-06
hide = 1e30
floor_max = -1e29
log2e = math.log2(math.e)
bf16 = jnp.bfloat16
f32 = jnp.float32
NT = (((1,), (1,)), ((), ()))
NN = (((1,), (0,)), ((), ()))
TN = (((0,), (0,)), ((), ()))


def mm(a, b, dims=NN):
    return lax.dot_general(a, b, dims, preferred_element_type=f32)


def tie(value, *others):
    return lax.optimization_barrier((value,) + others)[0]


def first_blocks(steps):
    return lambda i, *_: (jnp.minimum(i, steps // 2 - 1), 0)


def last_blocks(steps):
    return lambda i, *_: (jnp.maximum(i - steps // 2, 0), 0)


def store_halves(first_ref, last_ref, value):
    step, split = pl.program_id(0), pl.num_programs(0) // 2

    @pl.when(step < split)
    def first():
        first_ref[...] = value

    @pl.when(step >= split)
    def last():
        last_ref[...] = value


def lane_index(rows):
    return lax.broadcasted_iota(jnp.int32, (rows, LANES), 1)


def swap_halves(w, lane):
    half = HEAD_DIM // 2
    up = pltpu.roll(w, LANES - half, 1)
    down = pltpu.roll(w, half, 1)
    return jnp.where(lane < half, up, down)


def widen(piece):
    rows = piece.shape[0]
    tail = jnp.zeros((rows, LANES - piece.shape[1]), piece.dtype)
    return jnp.concatenate([piece, tail], axis=1)


def split_three(column):
    high = column.astype(bf16).astype(f32)
    rest = column - high
    mid = rest.astype(bf16).astype(f32)
    return high, mid, rest - mid


def place_three(base, column, lane):
    high, mid, low = split_three(column)
    base = jnp.where(lane == 96, high, base)
    base = jnp.where(lane == 97, mid, base)
    return jnp.where(lane == 98, low, base)


def qkv_kernel(heads, x_ref, w_ref, ln_ref, b_ref, cos_ref, sin_ref, feat_ref, a_ref, q_ref, kv_ref):
    width = heads * HEAD_DIM
    x = x_ref[...].astype(f32)
    rows = x.shape[0]
    center = x - jnp.mean(x, axis=1, keepdims=True)
    inverse = lax.rsqrt(jnp.mean(center * center, axis=1, keepdims=True) + norm_eps)
    a = (center * inverse * ln_ref[0:1, :] + ln_ref[1:2, :]).astype(bf16)
    a_ref[...] = a
    y = mm(a, w_ref[...]) + b_ref[0:1, :]
    cos, sin = cos_ref[...], sin_ref[...]
    lane = lane_index(rows)
    kv = []
    for h in range(heads):
        w = widen(y[:, h * HEAD_DIM : (h + 1) * HEAD_DIM])
        q = (w * cos + swap_halves(w, lane) * sin) * (HEAD_DIM**-0.5 * log2e)
        q_ref[h] = jnp.where(lane < HEAD_DIM, q.astype(bf16), feat_ref[...])
    for h in range(heads):
        begin = width + h * HEAD_DIM
        w = widen(y[:, begin : begin + HEAD_DIM])
        kv.append((w * cos + swap_halves(w, lane) * sin)[:, :HEAD_DIM].astype(bf16))
    kv.append(y[:, 2 * width : 3 * width].astype(bf16))
    kv_ref[...] = jnp.concatenate(kv, axis=1)


def project_row(x, w, ln, bias, cos, sin, feat, heads):
    rows, width = x.shape
    block = min(256, rows)
    wide = w.shape[1]
    local = heads * HEAD_DIM
    by_rows = lambda n: pl.BlockSpec((block, n), lambda i: (i, 0))
    whole = lambda a: pl.BlockSpec(a.shape, lambda i: (0,) * a.ndim)
    return pl.pallas_call(
        functools.partial(qkv_kernel, heads),
        grid=(rows // block,),
        in_specs=[
            by_rows(width),
            whole(w),
            whole(ln),
            whole(bias),
            by_rows(LANES),
            by_rows(LANES),
            by_rows(LANES),
        ],
        out_specs=[
            by_rows(width),
            pl.BlockSpec((heads, block, LANES), lambda i: (0, i, 0)),
            by_rows(2 * local),
        ],
        out_shape=[
            jax.ShapeDtypeStruct((rows, width), bf16),
            jax.ShapeDtypeStruct((heads, rows, LANES), bf16),
            jax.ShapeDtypeStruct((rows, 2 * local), bf16),
        ],
        cost_estimate=pl.CostEstimate(
            flops=2 * rows * width * wide, bytes_accessed=rows * width * 4 + width * wide * 2, transcendentals=0
        ),
        name="project_row",
    )(x, w, ln, bias, cos, sin, feat)


def forward_kernel(heads, segments, block, flag_ref, q_ref, w_ref, *refs):
    kv_refs = refs[:segments]
    feat_refs = refs[segments : 2 * segments]
    o_ref, q_out, k_aug, v_aug, p_first, p_last, m_scr, acc_scr = refs[2 * segments :]
    width = heads * HEAD_DIM
    step = pl.program_id(0)
    keys = k_aug.shape[1]
    count = keys // block
    rows = q_ref.shape[1]

    @pl.when(step == 0)
    def build():
        offset = 0
        for s in range(segments):
            length = kv_refs[s].shape[0]
            piece = min(length, 256)
            for t in range(length // piece):
                at = pl.ds(t * piece, piece)
                to = pl.ds(offset + t * piece, piece)
                kv = kv_refs[s][at, :]
                feat = feat_refs[s][at, :]
                lane = lane_index(piece)
                tail = jnp.where(lane == HEAD_DIM, 1.0, jnp.where((lane >= 96) & (lane < 99), -1.0, 0.0)).astype(bf16)
                for h in range(heads):
                    k = kv[:, h * HEAD_DIM : (h + 1) * HEAD_DIM]
                    v = kv[:, width + h * HEAD_DIM : width + (h + 1) * HEAD_DIM]
                    k_aug[h, to, :] = jnp.concatenate([k, feat[:, HEAD_DIM:]], axis=1)
                    v_aug[h, to, :] = jnp.concatenate([v, tail[:, HEAD_DIM:]], axis=1)
            offset += length

    m_scr[...] = jnp.full(m_scr.shape, floor_max, f32)
    acc_scr[...] = jnp.zeros(acc_scr.shape, f32)

    def visit(j, carry):
        @pl.when(flag_ref[step * count + j] > 0)
        def go():
            at = pl.ds(pl.multiple_of(j * block, block), block)
            for h in range(heads):
                s = mm(q_ref[h], k_aug[h, at, :], NT)
                old = m_scr[h]
                cuts = [s[:, c : c + LANES] for c in range(0, block, LANES)]
                top = functools.reduce(jnp.maximum, cuts)
                new = jnp.maximum(old, jnp.max(top, axis=1, keepdims=True))
                p = jnp.concatenate([jnp.exp2(cut - new) for cut in cuts], axis=1)
                m_scr[h] = new
                acc_scr[h] = acc_scr[h] * jnp.exp2(old - new) + mm(p.astype(bf16), v_aug[h, at, :])

        return carry

    lax.fori_loop(0, count, visit, 0)
    lane = lane_index(rows)
    outs = []
    for h in range(heads):
        acc = acc_scr[h]
        total = acc[:, HEAD_DIM : HEAD_DIM + 1]
        alive = total > 0.0
        safe = jnp.where(alive, total, 1.0)
        outs.append((acc / safe)[:, :HEAD_DIM].astype(bf16))
        level = jnp.where(alive, m_scr[h][:, 0:1] + jnp.log2(safe), 0.0)
        q_out[h] = place_three(q_ref[h].astype(f32), level, lane).astype(bf16)
    o = jnp.concatenate(outs, axis=1)
    o_ref[...] = o
    store_halves(p_first, p_last, mm(o, w_ref[...], NT).astype(bf16))


def attend_forward(flags, q_aug, w, kvs, feats, heads, block):
    rows = q_aug.shape[1]
    tall = min(256, rows // 2)
    steps = rows // tall
    width = w.shape[0]
    keys = sum(kv.shape[0] for kv in kvs)
    segments = len(kvs)
    whole = lambda a: pl.BlockSpec(a.shape, lambda i, f: (0,) * a.ndim)
    q_spec = pl.BlockSpec((heads, tall, LANES), lambda i, f: (0, i, 0))
    k_spec = pl.BlockSpec((heads, keys, LANES), lambda i, f: (0, 0, 0))
    local = heads * HEAD_DIM
    return pl.pallas_call(
        functools.partial(forward_kernel, heads, segments, block),
        grid_spec=pltpu.PrefetchScalarGridSpec(
            num_scalar_prefetch=1,
            grid=(rows // tall,),
            in_specs=[q_spec, whole(w)] + [whole(kv) for kv in kvs] + [whole(f) for f in feats],
            out_specs=[
                pl.BlockSpec((tall, local), lambda i, f: (i, 0)),
                q_spec,
                k_spec,
                k_spec,
                pl.BlockSpec((tall, width), first_blocks(steps)),
                pl.BlockSpec((tall, width), last_blocks(steps)),
            ],
            scratch_shapes=[
                pltpu.VMEM((heads, tall, LANES), f32),
                pltpu.VMEM((heads, tall, LANES), f32),
            ],
        ),
        out_shape=[
            jax.ShapeDtypeStruct((rows, local), bf16),
            jax.ShapeDtypeStruct((heads, rows, LANES), bf16),
            jax.ShapeDtypeStruct((heads, keys, LANES), bf16),
            jax.ShapeDtypeStruct((heads, keys, LANES), bf16),
            jax.ShapeDtypeStruct((rows // 2, width), bf16),
            jax.ShapeDtypeStruct((rows // 2, width), bf16),
        ],
        cost_estimate=pl.CostEstimate(
            flops=2 * rows * keys * heads * LANES, bytes_accessed=8 * keys * local, transcendentals=rows * keys * heads // 2
        ),
        name="attend_forward",
    )(flags, q_aug, w, *kvs, *feats)


def backward_kernel(
    heads, segments, block, flag_ref, q_ref, ga_first, ga_last, w_ref, o_ref, k_aug, v_aug, cosq_ref, sinq_ref, *refs
):
    cosk_refs = refs[:segments]
    sink_refs = refs[segments : 2 * segments]
    dq_ref = refs[2 * segments]
    dkv_refs = refs[2 * segments + 1 : 3 * segments + 1]
    k_turn, dk_acc, dv_acc, dq_acc, go_scr = refs[3 * segments + 1 :]
    step = pl.program_id(0)
    keys = k_aug.shape[1]
    count = keys // block
    rows = q_ref.shape[1]
    scale = HEAD_DIM**-0.5

    @pl.when(step == 0)
    def build():
        dk_acc[...] = jnp.zeros(dk_acc.shape, f32)
        dv_acc[...] = jnp.zeros(dv_acc.shape, f32)
        for h in range(heads):
            for t in range(count):
                at = pl.ds(t * block, block)
                k_turn[h, :, at] = k_aug[h, at, :].T

    lane = lane_index(rows)
    ga = jnp.where(step < pl.num_programs(0) // 2, ga_first[...], ga_last[...])
    go_all = mm(ga, w_ref[...]).astype(bf16).astype(f32)
    for h in range(heads):
        cut = slice(h * HEAD_DIM, (h + 1) * HEAD_DIM)
        go = go_all[:, cut]
        delta = jnp.sum(go * o_ref[:, cut].astype(f32), axis=1, keepdims=True)
        go_scr[h] = place_three(widen(go), delta, lane).astype(bf16)
    dq_acc[...] = jnp.zeros(dq_acc.shape, f32)

    def visit(j, carry):
        @pl.when(flag_ref[step * count + j] > 0)
        def run():
            at = pl.ds(pl.multiple_of(j * block, block), block)
            for h in range(heads):
                q, go = q_ref[h], go_scr[h]
                p = jnp.exp2(mm(k_aug[h, at, :], q, NT))
                ds = (p * mm(v_aug[h, at, :], go, NT)).astype(bf16)
                dv_acc[h, at, :] += mm(p.astype(bf16), go)
                dk_acc[h, at, :] += mm(ds, q)
                dq_acc[h] += mm(k_turn[h, :, at], ds)

        return carry

    lax.fori_loop(0, count, visit, 0)

    def turn_back(w, cos, sin, index):
        return w * cos - swap_halves(w, index) * sin

    outs = []
    for h in range(heads):
        w = dq_acc[h].T
        back = turn_back(w, cosq_ref[...], sinq_ref[...], lane) * scale
        outs.append(back[:, :HEAD_DIM].astype(bf16))
    dq_ref[...] = jnp.concatenate(outs, axis=1)

    @pl.when(step == pl.num_programs(0) - 1)
    def finish():
        offset = 0
        for s in range(segments):
            length = dkv_refs[s].shape[0]
            piece = min(length, 256)
            index = lane_index(piece)
            for t in range(length // piece):
                at = pl.ds(t * piece, piece)
                of = pl.ds(offset + t * piece, piece)
                parts = []
                for h in range(heads):
                    w = dk_acc[h, of, :]
                    back = turn_back(w, cosk_refs[s][at, :], sink_refs[s][at, :], index) * (1.0 / log2e)
                    parts.append(back[:, :HEAD_DIM].astype(bf16))
                for h in range(heads):
                    parts.append(dv_acc[h, of, :][:, :HEAD_DIM].astype(bf16))
                dkv_refs[s][at, :] = jnp.concatenate(parts, axis=1)
            offset += length


def attend_backward(flags, q_aug, ga, w, o, k_aug, v_aug, cos_q, sin_q, cos_k, sin_k, heads, block):
    rows = q_aug.shape[1]
    tall = min(256, rows // 2)
    steps = rows // tall
    width = w.shape[0]
    keys = k_aug.shape[1]
    segments = len(cos_k)
    local = heads * HEAD_DIM
    whole = lambda a: pl.BlockSpec(a.shape, lambda i, f: (0,) * a.ndim)
    by_rows = lambda n: pl.BlockSpec((tall, n), lambda i, f: (i, 0))
    q_spec = pl.BlockSpec((heads, tall, LANES), lambda i, f: (0, i, 0))
    return pl.pallas_call(
        functools.partial(backward_kernel, heads, segments, block),
        grid_spec=pltpu.PrefetchScalarGridSpec(
            num_scalar_prefetch=1,
            grid=(rows // tall,),
            in_specs=[
                q_spec,
                pl.BlockSpec((tall, width), first_blocks(steps)),
                pl.BlockSpec((tall, width), last_blocks(steps)),
                whole(w),
                by_rows(local),
                whole(k_aug),
                whole(v_aug),
                by_rows(LANES),
                by_rows(LANES),
            ]
            + [whole(t) for t in cos_k]
            + [whole(t) for t in sin_k],
            out_specs=[by_rows(local)]
            + [pl.BlockSpec((t.shape[0], 2 * local), lambda i, f: (0, 0)) for t in cos_k],
            scratch_shapes=[
                pltpu.VMEM((heads, LANES, keys), bf16),
                pltpu.VMEM((heads, keys, LANES), f32),
                pltpu.VMEM((heads, keys, LANES), f32),
                pltpu.VMEM((heads, LANES, tall), f32),
                pltpu.VMEM((heads, tall, LANES), bf16),
            ],
        ),
        out_shape=[jax.ShapeDtypeStruct((rows, local), bf16)]
        + [jax.ShapeDtypeStruct((t.shape[0], 2 * local), bf16) for t in cos_k],
        cost_estimate=pl.CostEstimate(
            flops=5 * rows * keys * heads * LANES, bytes_accessed=16 * keys * local, transcendentals=rows * keys * heads // 2
        ),
        name="attend_backward",
    )(flags, q_aug, *ga, w, o, k_aug, v_aug, cos_q, sin_q, *cos_k, *sin_k)


def feed_kernel(chunk, c_first, c_last, g_ref, up_ref, down_ref, shift_ref, z_ref, gu_ref, gc_first, gc_last, feed_first, feed_last, sum_ref):
    step = pl.program_id(0)
    c = jnp.where(step < pl.num_programs(0) // 2, c_first[...], c_last[...])
    g = g_ref[...]
    sums = []
    for begin in range(0, up_ref.shape[1], chunk):
        cut = slice(begin, begin + chunk)
        u = mm(c, up_ref[:, cut]) + shift_ref[0:1, cut]
        sg = 0.5 + 0.5 * jnp.tanh(0.851 * u)
        z = (u * sg).astype(bf16)
        gu = (mm(g, down_ref[:, cut]) * (sg + 1.702 * u * sg * (1.0 - sg))).astype(bf16)
        z_ref[:, cut] = z
        gu_ref[:, cut] = gu
        sums.append(jnp.sum(gu.astype(f32), axis=0, keepdims=True))
    store_halves(gc_first, gc_last, mm(gu_ref[...], up_ref[...], NT).astype(bf16))
    store_halves(feed_first, feed_last, mm(z_ref[...], down_ref[...], NT).astype(bf16))

    @pl.when(step == 0)
    def clear():
        sum_ref[...] = jnp.zeros(sum_ref.shape, f32)

    sum_ref[0:1, :] += jnp.concatenate(sums, axis=1)
    sum_ref[1:2, : g.shape[1]] += jnp.sum(g.astype(f32), axis=0, keepdims=True)


def feed_forward(c, g, w_up, w_down, shift):
    rows, width = g.shape
    hidden = w_up.shape[1]
    tall = min(256, rows // 2)
    steps = rows // tall
    chunk = 256 if hidden % 256 == 0 else hidden
    by_rows = lambda n: pl.BlockSpec((tall, n), lambda i: (i, 0))
    whole = lambda a: pl.BlockSpec(a.shape, lambda i: (0,) * a.ndim)
    first = pl.BlockSpec((tall, width), first_blocks(steps))
    last = pl.BlockSpec((tall, width), last_blocks(steps))
    part = jax.ShapeDtypeStruct((rows // 2, width), bf16)
    longest = max(width, hidden)
    return pl.pallas_call(
        functools.partial(feed_kernel, chunk),
        grid=(steps,),
        in_specs=[first, last, by_rows(width), whole(w_up), whole(w_down), whole(shift)],
        out_specs=[by_rows(hidden), by_rows(hidden), first, last, first, last, pl.BlockSpec((8, longest), lambda i: (0, 0))],
        out_shape=[
            jax.ShapeDtypeStruct((rows, hidden), bf16),
            jax.ShapeDtypeStruct((rows, hidden), bf16),
            part,
            part,
            part,
            part,
            jax.ShapeDtypeStruct((8, longest), f32),
        ],
        cost_estimate=pl.CostEstimate(
            flops=8 * rows * width * hidden, bytes_accessed=4 * width * hidden + 12 * rows * width, transcendentals=rows * hidden
        ),
        name="feed_forward",
    )(*c, g, w_up, w_down, shift)


def back_kernel(pieces, x_ref, w_ref, gq_ref, *refs):
    kv_refs = refs[:pieces]
    p_first, p_last, dkv_ref, sum_ref = refs[pieces:]
    gq = gq_ref[...]
    if pieces == 1:
        dkv = kv_refs[0][...]
    else:
        other = jnp.where(pl.program_id(0) < pl.num_programs(0) // 2, kv_refs[1][...], kv_refs[2][...])
        dkv = (kv_refs[0][...].astype(f32) + other.astype(f32)).astype(bf16)
    dkv_ref[...] = dkv
    tail = jnp.zeros((gq.shape[0], w_ref.shape[1] - gq.shape[1] - dkv.shape[1]), bf16)
    e = mm(jnp.concatenate([gq, dkv, tail], axis=1), w_ref[...], NT)
    store_halves(p_first, p_last, e.astype(bf16))
    x = x_ref[...].astype(f32)
    center = x - jnp.mean(x, axis=1, keepdims=True)
    unit = center * lax.rsqrt(jnp.mean(center * center, axis=1, keepdims=True) + norm_eps)

    @pl.when(pl.program_id(0) == 0)
    def clear():
        sum_ref[...] = jnp.zeros(sum_ref.shape, f32)

    local = gq.shape[1]
    sum_ref[0:1, :] += jnp.sum(e * unit, axis=0, keepdims=True)
    sum_ref[1:2, :] += jnp.sum(e, axis=0, keepdims=True)
    sum_ref[2:3, :local] += jnp.sum(gq.astype(f32), axis=0, keepdims=True)
    sum_ref[3:4, : 2 * local] += jnp.sum(dkv.astype(f32), axis=0, keepdims=True)


def project_back(x, w, gq, dkvs):
    rows, width = x.shape
    local = gq.shape[1]
    tall = min(512, rows // 2)
    steps = rows // tall
    by_rows = lambda n: pl.BlockSpec((tall, n), lambda i: (i, 0))
    whole = lambda a: pl.BlockSpec(a.shape, lambda i: (0,) * a.ndim)
    part = jax.ShapeDtypeStruct((rows // 2, width), bf16)
    kv_specs = [
        by_rows(2 * local),
        pl.BlockSpec((tall, 2 * local), first_blocks(steps)),
        pl.BlockSpec((tall, 2 * local), last_blocks(steps)),
    ]
    return pl.pallas_call(
        functools.partial(back_kernel, len(dkvs)),
        grid=(steps,),
        in_specs=[by_rows(width), whole(w), by_rows(local)] + kv_specs[: len(dkvs)],
        out_specs=[
            pl.BlockSpec((tall, width), first_blocks(steps)),
            pl.BlockSpec((tall, width), last_blocks(steps)),
            by_rows(2 * local),
            pl.BlockSpec((8, width), lambda i: (0, 0)),
        ],
        out_shape=[part, part, jax.ShapeDtypeStruct((rows, 2 * local), bf16), jax.ShapeDtypeStruct((8, width), f32)],
        cost_estimate=pl.CostEstimate(
            flops=6 * rows * width * local, bytes_accessed=6 * width * local + 6 * rows * width, transcendentals=rows
        ),
        name="project_back",
    )(x, w, gq, *dkvs)


def norm_stats(rows_in):
    center = rows_in - jnp.mean(rows_in, axis=1, keepdims=True)
    inverse = lax.rsqrt(jnp.mean(center * center, axis=1, keepdims=True) + norm_eps)
    return center * inverse, inverse


def norm_backward(grad_rows, unit_rows, inverse, gain):
    scaled = grad_rows * gain
    return inverse * (
        scaled
        - jnp.mean(scaled, axis=1, keepdims=True)
        - unit_rows * jnp.mean(scaled * unit_rows, axis=1, keepdims=True)
    )


def norm_two_kernel(x_ref, near_ref, far_ref, vec_ref, h_ref, c_ref):
    h = x_ref[...].astype(f32) + (near_ref[...].astype(f32) + far_ref[...].astype(f32)) + vec_ref[0:1, :]
    h_ref[...] = h
    c_ref[...] = (norm_stats(h)[0] * vec_ref[1:2, :] + vec_ref[2:3, :]).astype(bf16)


def norm_two_back_kernel(h_ref, near_ref, far_ref, g_ref, vec_ref, gh_ref, ga_ref, sum_ref):
    unit, inverse = norm_stats(h_ref[...])
    gc = near_ref[...].astype(f32) + far_ref[...].astype(f32)
    gh = g_ref[...].astype(f32) + norm_backward(gc, unit, inverse, vec_ref[1:2, :])
    ga = gh.astype(bf16)
    gh_ref[...] = gh
    ga_ref[...] = ga

    @pl.when(pl.program_id(0) == 0)
    def clear():
        sum_ref[...] = jnp.zeros(sum_ref.shape, f32)

    sum_ref[0:1, :] += jnp.sum(gc * unit, axis=0, keepdims=True)
    sum_ref[1:2, :] += jnp.sum(gc, axis=0, keepdims=True)
    sum_ref[2:3, :] += jnp.sum(ga.astype(f32), axis=0, keepdims=True)


def norm_one_back_kernel(x_ref, near_ref, far_ref, gh_ref, vec_ref, out_ref):
    unit, inverse = norm_stats(x_ref[...].astype(f32))
    ga1 = near_ref[...].astype(f32) + far_ref[...].astype(f32)
    out_ref[...] = (gh_ref[...] + norm_backward(ga1, unit, inverse, vec_ref[0:1, :])).astype(bf16)


def close_kernel(h_ref, near_ref, far_ref, live_ref, vec_ref, out_ref):
    feed = near_ref[...].astype(f32) + far_ref[...].astype(f32)
    out_ref[...] = ((h_ref[...] + feed + vec_ref[0:1, :]) * live_ref[...]).astype(bf16)


def by_tokens(body, arrays, vectors, kinds, name, sums=False):
    count, width = arrays[1].shape
    tall = min(256, count)
    in_specs = [pl.BlockSpec((tall, a.shape[1]), lambda i: (i, 0)) for a in arrays]
    out_specs = [pl.BlockSpec((tall, width), lambda i: (i, 0)) for _ in kinds]
    out_shape = [jax.ShapeDtypeStruct((count, width), kind) for kind in kinds]
    if sums:
        out_specs.append(pl.BlockSpec((8, width), lambda i: (0, 0)))
        out_shape.append(jax.ShapeDtypeStruct((8, width), f32))
    return pl.pallas_call(
        body,
        grid=(count // tall,),
        in_specs=in_specs + [pl.BlockSpec(vectors.shape, lambda i: (0, 0))],
        out_specs=out_specs,
        out_shape=out_shape,
        cost_estimate=pl.CostEstimate(flops=20 * count * width, bytes_accessed=14 * count * width, transcendentals=count),
        name=name,
    )(*arrays, vectors)


def gather_rows_kernel(side_ref, *refs):
    step = pl.program_id(0)
    for index, piece in enumerate(refs[:-1]):

        @pl.when(step == index)
        def copy(piece=piece):
            refs[-1][0] = piece[...]


def gather_rows(side, pieces):
    half, width = pieces[0].shape
    count = len(pieces)
    return pl.pallas_call(
        gather_rows_kernel,
        grid_spec=pltpu.PrefetchScalarGridSpec(
            num_scalar_prefetch=1,
            grid=(count,),
            in_specs=[pl.BlockSpec((half, width), lambda t, s: (0, 0)) for _ in pieces],
            out_specs=pl.BlockSpec((1, half, width), lambda t, s: (t // 2, jnp.where(t % 2 == 0, s[0], 1 - s[0]), 0)),
        ),
        out_shape=jax.ShapeDtypeStruct((count // 2, 2 * half, width), bf16),
        cost_estimate=pl.CostEstimate(flops=0, bytes_accessed=4 * count * half * width, transcendentals=0),
        name="gather_rows",
    )(side, *pieces)


def tables(grid_pos):
    lane = jnp.arange(LANES)
    quarter = HEAD_DIM // 4
    frequency = jnp.power(10000.0, -4.0 * (lane % quarter).astype(f32) / HEAD_DIM)
    place = jnp.where((lane // quarter) % 2 == 0, grid_pos[0][:, None], grid_pos[1][:, None])
    angle = jnp.where(lane < HEAD_DIM, place.astype(f32) * frequency, 0.0)
    return jnp.cos(angle), jnp.where(lane < HEAD_DIM // 2, -1.0, 1.0) * jnp.sin(angle)


def query_features(ids):
    lane = jnp.arange(LANES)
    return (lane == HEAD_DIM + 1 + ids[:, None]).astype(bf16)


def key_features(ids):
    lane = jnp.arange(LANES)
    slot = lane - HEAD_DIM
    same = (slot >= 1) & (slot == ids[:, None] + 1)
    wall = jnp.where((slot >= 0) & (slot < 16) & ~same, -hide, 0.0)
    return jnp.where((lane >= 96) & (lane < 99), -1.0, wall).astype(bf16)


def visit_flags(query_ids, key_ids, tall, block):
    q = query_ids.reshape(-1, tall)
    k = key_ids.reshape(-1, block)
    q_top, k_top = jnp.max(q, axis=1), jnp.max(k, axis=1)
    q_low = jnp.min(jnp.where(q >= 0, q, 1 << 20), axis=1)
    k_low = jnp.min(jnp.where(k >= 0, k, 1 << 20), axis=1)
    meet = (q_low[:, None] <= k_top[None, :]) & (k_low[None, :] <= q_top[:, None])
    return meet.astype(jnp.int32).reshape(-1)


def on_device(
    patches,
    cotangent,
    picture_ids,
    positions,
    ln1_gain,
    ln1_bias,
    qkv_weight,
    qkv_bias,
    proj_weight,
    proj_bias,
    ln2_gain,
    ln2_bias,
    fc1_weight,
    fc1_bias,
    fc2_weight,
    fc2_bias,
):
    row_count, row_share, width = patches.shape
    owners = lax.axis_size("shard")
    contexts = lax.axis_size("ctx")
    ways = lax.axis_size("tp")
    part = qkv_weight.shape[0]
    local = qkv_weight.shape[2]
    heads = local // HEAD_DIM
    half = row_share // 2
    side = lax.axis_index("tp") % 2
    context = lax.axis_index("ctx")
    pairs_near = [(i, i ^ 1) for i in range(ways)]
    pairs_far = [(i, i ^ 2) for i in range(ways)]
    pad = -3 * local % 256
    wide = 3 * local + pad

    def near(v):
        return lax.ppermute(v, "tp", pairs_near)

    def far(v):
        return lax.ppermute(v, "tp", pairs_far)

    def over_ctx(v):
        return lax.ppermute(v, "ctx", [(0, 1), (1, 0)])

    def mine_first(v, axis=0):
        return jnp.where(side == 0, v, jnp.roll(v, half, axis=axis))

    def column(v):
        flat = v.reshape(-1)
        return jnp.pad(flat, (0, part - flat.shape[0]))

    vectors = [ln1_gain, ln1_bias, ln2_gain, ln2_bias, proj_bias, fc2_bias, qkv_bias, fc1_bias]
    place = lax.axis_index("shard")
    context_first = context == 0

    def rotate_gather(piece):
        whole = lax.dynamic_update_index_in_dim(jnp.zeros((owners,) + piece.shape, piece.dtype), piece, place, 0)
        for step in range(1, owners):
            got = lax.ppermute(piece, "shard", [(i, (i + step) % owners) for i in range(owners)])
            whole = lax.dynamic_update_index_in_dim(whole, got, (place - step) % owners, 0)
        return whole

    tail = rotate_gather(jnp.stack([column(v) for v in vectors]).astype(bf16))
    packed = jnp.transpose(tail, (1, 0, 2)).reshape(len(vectors), width).astype(f32)
    qkv_piece = jnp.pad(qkv_weight.reshape(part, 3 * local), ((0, 0), (0, pad))).astype(bf16)
    gather = lambda v: lax.all_gather(v, "shard", axis=0, tiled=True)
    up_piece = fc1_weight.astype(bf16)
    down_piece = fc2_weight.T.astype(bf16)
    w_qkv = gather(qkv_piece)
    w_proj = rotate_gather(tie(proj_weight.T.astype(bf16), w_qkv)).reshape(owners * part, local)
    gain_one, bias_one, gain_two, bias_two, proj_shift, down_shift = [packed[i] for i in range(6)]
    qb_size = qkv_bias.size
    qkv_shift = packed[6].reshape(owners, part)[:, :qb_size].reshape((owners,) + qkv_bias.shape)
    qkv_shift = jnp.transpose(qkv_shift, (1, 2, 0, 3)).reshape(-1)
    qkv_shift = jnp.pad(qkv_shift, (0, pad)).reshape(1, wide)
    up_shift = packed[7].reshape(owners, part)[:, : fc1_bias.size].reshape((owners,) + fc1_bias.shape)
    up_shift = jnp.transpose(up_shift, (1, 0, 2)).reshape(1, -1)
    ln_one = tie(packed[0:2], up_piece, down_piece)

    ids_by_ctx = mine_first(picture_ids.reshape(row_count, contexts, row_share), axis=2)
    places = mine_first(positions, axis=2)
    block = min(256, half)

    def cut_last(spots):
        return [spots[0], spots[1][:half], spots[1][half:]] if contexts == 2 else spots

    key_block = 256
    rows = []
    for r in range(row_count):
        x = mine_first(patches[r])
        g = mine_first(cotangent[r])
        ids = lax.dynamic_index_in_dim(ids_by_ctx[r], context, 0, keepdims=False)
        if contexts == 2:
            other = lax.dynamic_index_in_dim(ids_by_ctx[r], 1 - context, 0, keepdims=False)
            key_ids = [ids, other]
            spots = [places[:, r], over_ctx(places[:, r])]
        else:
            key_ids = [ids_by_ctx[r].reshape(-1)]
            spots = [lax.all_gather(places[:, r], "ctx", axis=1, tiled=True)]
        live = (ids >= 0).astype(f32)[:, None]
        turns = [tables(spot) for spot in spots]
        own_turn = turns[0] if contexts == 2 else tables(places[:, r])
        rows.append(
            dict(
                x=x,
                g=(g.astype(f32) * live).astype(bf16),
                live=live,
                ids=ids,
                cos=own_turn[0],
                sin=own_turn[1],
                cos_k=cut_last([t[0] for t in turns]),
                sin_k=cut_last([t[1] for t in turns]),
                q_feat=query_features(ids),
                k_feat=[key_features(k) for k in key_ids],
                flags=visit_flags(ids, jnp.concatenate(key_ids), block, key_block),
            )
        )

    ln_one = tie(ln_one, qkv_shift, up_shift, *[row["g"] for row in rows])

    for index, row in enumerate(rows):
        row["a"], row["q"], row["kv"] = project_row(
            row["x"], w_qkv, ln_one, qkv_shift, row["cos"], row["sin"], row["q_feat"], heads
        )
        if index == 1:
            row["kv"], w_proj = lax.optimization_barrier((row["kv"], w_proj))
        if contexts == 2:
            row["kvs"] = [row["kv"], over_ctx(row["kv"])]
        else:
            row["kvs"] = [lax.all_gather(row["kv"], "ctx", axis=0, tiled=True)]

    down_piece, up_piece = lax.optimization_barrier((down_piece, up_piece, rows[0]["q"]))[:2]
    if contexts == 2:
        down_cut = down_piece.reshape(2, part // 2, -1)
        down_near = gather(lax.dynamic_index_in_dim(down_cut, context, 0, keepdims=False))
        down_near = down_near.reshape(owners, part // 2, -1)
    else:
        w_down = gather(down_piece)
    w_up = gather(up_piece)

    def sum_near(first, last):
        return (first.astype(f32) + near(last).astype(f32)).astype(bf16)

    norm_vectors = jnp.pad(jnp.stack([proj_shift, gain_two, bias_two]), ((0, 5), (0, 0)))

    def norm_two(row, vectors):
        row["h"], mine = by_tokens(
            norm_two_kernel, [row["x"], row["branch"], row["branch_far"]], vectors, [f32, bf16], "norm_two"
        )
        row["c"] = (mine, near(mine))

    hold = lax.optimization_barrier
    before = rows[-1]["kv"]
    for index, row in enumerate(rows):
        row["o"], row["q"], row["k_aug"], row["v_aug"], first, last = attend_forward(
            tie(row["flags"], before), row["q"], w_proj, row["kvs"], row["k_feat"], heads, key_block
        )
        if index:
            prior = rows[index - 1]
            first, last, prior["branch_far"] = hold((first, last, prior["branch_far"]))
        if index + 1 < row_count:
            follow = rows[index + 1]
            first, last, follow["kvs"] = hold((first, last, follow["kvs"]))
            if contexts == 2:
                first, last, down_near = hold((first, last, down_near))
                down_far = over_ctx(down_near)
        elif contexts == 2:
            first, last, down_far, w_up = hold((first, last, down_far, w_up))
        before = row["branch"] = sum_near(first, last)
        row["branch_far"] = far(before)
    if contexts == 2:
        low = jnp.where(context_first, down_near, down_far)
        high = jnp.where(context_first, down_far, down_near)
        w_down = jnp.concatenate([low, high], axis=1).reshape(owners * part, -1)

    norm_two(rows[0], tie(norm_vectors, before))
    for index, row in enumerate(rows):
        shift = tie(up_shift, before)
        row["z"], row["gu"], gc_first, gc_last, feed_first, feed_last, row["feed_sums"] = feed_forward(
            row["c"], row["g"], w_up, w_down, shift
        )
        other, key = (rows[-1], "branch_far") if index == 0 else (rows[index - 1], "gc_far")
        gc_first, gc_last, other[key] = hold((gc_first, gc_last, other[key]))
        before = row["gc"] = sum_near(gc_first, gc_last)
        row["gc_far"] = far(before)
        row["feed"] = (feed_first, feed_last)
        if index + 1 < row_count:
            norm_two(rows[index + 1], norm_vectors)
    for row in rows:
        row["feed"] = sum_near(*row["feed"])

    join = lambda key: jnp.concatenate([row[key] for row in rows], axis=0)
    join_two = lambda key: jnp.concatenate([piece for row in rows for piece in row[key]], axis=0)
    scatter = lambda v: lax.psum_scatter(v, "shard", scatter_dimension=0, tiled=True)
    if contexts == 2:
        finish = lambda v: v.astype(f32) + over_ctx(v).astype(f32)
    else:
        finish = lambda v: lax.psum(v, "ctx").astype(f32)
    last_row = rows[-1]

    def norm_two_back(row):
        row["gh"], ga, norm_sums = by_tokens(
            norm_two_back_kernel,
            [row["h"], row["gc"], row["gc_far"], row["g"]],
            norm_vectors,
            [f32, bf16],
            "norm_two_back",
            sums=True,
        )
        row["ga"] = (ga, near(ga))
        return norm_sums[0:3]

    pair = sum(norm_two_back(row) for row in rows[:-1])
    last_row["gu"], last_row["z"] = hold((last_row["gu"], last_row["z"], before, *[row["ga"][0] for row in rows[:-1]]))[:2]
    grad_up = mm(join_two("c"), join("gu"), TN).astype(bf16)
    grad_down = mm(join("g"), join("z"), TN).astype(bf16)
    grad_up, grad_down, last_row["gc_far"] = hold((grad_up, grad_down, last_row["gc_far"]))
    pair = pair + norm_two_back(last_row)
    grad_proj = mm(join_two("ga"), join("o"), TN).astype(bf16)
    before = (grad_up, grad_down)
    y_free = last_row["gc_far"]
    grad_up = scatter(grad_up)
    if contexts == 2:
        cut = grad_down.reshape(owners, 2, part // 2, -1)
        keep = lax.dynamic_index_in_dim(cut, context, 1, keepdims=False)
        came = over_ctx(lax.dynamic_index_in_dim(cut, 1 - context, 1, keepdims=False))
    else:
        grad_down = scatter(grad_down)

    for index, row in enumerate(rows):
        feed_far = far(tie(row["feed"], y_free))
        out = attend_backward(
            tie(row["flags"], *before),
            row["q"],
            row["ga"],
            w_proj,
            row["o"],
            row["k_aug"],
            row["v_aug"],
            row["cos"],
            row["sin"],
            row["cos_k"],
            row["sin_k"],
            heads,
            key_block,
        )
        if index:
            prior = rows[index - 1]
            *out, feed_far, prior["dkvs"], grad_up = hold((*out, feed_far, prior["dkvs"], grad_up))
            if contexts == 2:
                *out, grad_down = hold((*out, grad_down))
        elif contexts == 2:
            *out, feed_far, came = hold((*out, feed_far, came))
            grad_down = scatter((keep.astype(f32) + came.astype(f32)).astype(bf16).reshape(owners * part // 2, -1))
        else:
            *out, feed_far = hold((*out, feed_far))
        y_free = feed_far
        before = (out[0], grad_proj)
        row["gq"] = out[0]
        row["feed_far"] = feed_far
        if contexts == 2:
            row["dkvs"] = [out[1], over_ctx(out[2]), over_ctx(out[3])]
        else:
            row["dkvs"] = [lax.psum_scatter(out[1], "ctx", scatter_dimension=0, tiled=True)]

    side_list = side.reshape(1).astype(jnp.int32)
    grad_proj = scatter(grad_proj)
    sums = 0.0
    for index, row in enumerate(rows):
        first, last, row["dkv"], back_sums = project_back(row["x"], w_qkv, tie(row["gq"], *before), row["dkvs"])
        sums = sums + back_sums
        if index == 0:
            kvs = last_row["dkvs"]
            first, last, row["dkv"], kvs[:-1] = hold((first, last, row["dkv"], kvs[:-1]))
            last_row["gq"] = tie(last_row["gq"], row["dkv"])
            grad_q = mm(join("a"), join("gq"), TN).astype(bf16)
            kvs[-1] = tie(kvs[-1], grad_q)
            grad_q = scatter(grad_q)
            outs = []
            for done in rows:
                mine = by_tokens(
                    close_kernel,
                    [done["h"], done["feed"], done["feed_far"], done["live"]],
                    tie(jnp.broadcast_to(down_shift, (8, width)), row["dkv"]),
                    [bf16],
                    "close",
                )[0]
                outs += [mine, near(mine)]
            outs = gather_rows(side_list, outs)
            before = (row["dkv"], kvs[-1], outs)
        else:
            prior = rows[index - 1]
            down_came = over_ctx(tie(grad_down, kvs[-1])) if contexts == 2 else grad_down
            first, last, prior["ga1_far"], down_came = hold((first, last, prior["ga1_far"], down_came))
            before = (row["dkv"],)
        row["ga1"] = sum_near(first, last)
        row["ga1_far"] = far(row["ga1"])
    grad_kv = mm(join("a"), join("dkv"), TN).astype(bf16)
    def sum_over(v, axis):
        size, step = lax.axis_size(axis), 1
        while step < size:
            v = v + lax.ppermute(v, axis, [(i, i ^ step) for i in range(size)])
            step *= 2
        return v

    def owned(v):
        v = v.reshape(owners, -1)
        return jnp.pad(v, ((0, 0), (0, part - v.shape[1]))).reshape(-1)

    feed_sums = sum(row["feed_sums"] for row in rows)
    d_qb = jnp.concatenate([sums[2, :local], sums[3, : 2 * local]]).reshape(3, heads, owners, -1)
    d_qb = owned(jnp.transpose(d_qb, (2, 0, 1, 3)))
    d_ub = feed_sums[0, : fc1_bias.size * owners].reshape(fc1_bias.shape[0], owners, fc1_bias.shape[1])
    d_ub = owned(jnp.transpose(d_ub, (1, 0, 2)))
    vector = jnp.concatenate([pair, feed_sums[1:2, :width], d_qb[None], d_ub[None], sums[0:2]], axis=0)
    vector_one = sum_over(vector, "ctx")
    up_came = over_ctx(tie(grad_up, vector_one)) if contexts == 2 else grad_up
    last_row["ga1_far"], up_came, grad_q, grad_proj = hold((last_row["ga1_far"], up_came, grad_q, grad_proj))
    grad_kv = scatter(grad_kv)
    if contexts == 2:
        grad_up = grad_up.astype(f32) + up_came.astype(f32)
        low = jnp.where(context_first, grad_down, down_came)
        high = jnp.where(context_first, down_came, grad_down)
        grad_down = jnp.concatenate([low, high], axis=0).astype(f32)
    else:
        grad_up, grad_down = finish(up_came), finish(down_came)
    come = over_ctx if contexts == 2 else lambda v: v
    add = (lambda v, w: v.astype(f32) + w.astype(f32)) if contexts == 2 else lambda v, w: finish(v)
    q_came, proj_came, kv_came = come(grad_q), come(grad_proj), come(grad_kv)

    ins = []
    for row in rows:
        mine = by_tokens(
            norm_one_back_kernel,
            [row["x"], row["ga1"], row["ga1_far"], row["gh"]],
            jnp.broadcast_to(gain_one, (8, width)),
            [bf16],
            "norm_one_back",
        )[0]
        if row is last_row:
            mine, q_came, proj_came = hold((mine, q_came, proj_came))
        ins += [mine, near(mine)]

    vector = sum_over(tie(vector_one, ins[0]), "shard")
    vector = lax.dynamic_slice_in_dim(vector, place * part, part, axis=1)
    both = vector + near(vector)
    norm_one = both[6:8] + far(both[6:8])

    ins, kv_came = hold((gather_rows(side_list, ins), kv_came))
    grad_q, grad_proj, grad_kv = add(grad_q, q_came), add(grad_proj, proj_came), add(grad_kv, kv_came)
    return (
        outs,
        ins,
        norm_one[0],
        norm_one[1],
        jnp.concatenate([grad_q, grad_kv], axis=1).reshape(qkv_weight.shape),
        vector[4, :qb_size].reshape(qkv_bias.shape),
        grad_proj.T,
        both[2],
        both[0],
        both[1],
        grad_up,
        vector[5, : fc1_bias.size].reshape(fc1_bias.shape),
        grad_down.T,
        vector[3],
    )


def solution(mesh):
    in_specs = (
        P("shard", "ctx", None),
        P("shard", "ctx", None),
        P("shard", None),
        P(None, "shard", "ctx"),
        P("shard"),
        P("shard"),
        P("shard", None, "tp"),
        P(None, "tp", "shard"),
        P("tp", "shard"),
        P("shard"),
        P("shard"),
        P("shard"),
        P("shard", "tp"),
        P("tp", "shard"),
        P("tp", "shard"),
        P("shard"),
    )
    out_specs = (
        P("shard", "ctx", None),
        P("shard", "ctx", None),
        P("shard"),
        P("shard"),
        P("shard", None, "tp"),
        P(None, "tp", "shard"),
        P("tp", "shard"),
        P("shard"),
        P("shard"),
        P("shard"),
        P("shard", "tp"),
        P("tp", "shard"),
        P("tp", "shard"),
        P("shard"),
    )
    return jax.shard_map(
        on_device, mesh=mesh, in_specs=in_specs, out_specs=out_specs, check_vma=False
    )
```

```python
import functools
import math

import jax
import jax.numpy as jnp
from jax import lax
from jax.experimental import pallas as pl
from jax.experimental.pallas import tpu as pltpu
from jax.sharding import PartitionSpec as P

HEAD_DIM = 80
LANES = 128
norm_eps = 1e-06
hide = 1e30
floor_max = -1e29
log2e = math.log2(math.e)
bf16 = jnp.bfloat16
f32 = jnp.float32
NT = (((1,), (1,)), ((), ()))
NN = (((1,), (0,)), ((), ()))
TN = (((0,), (0,)), ((), ()))


def mm(a, b, dims=NN):
    return lax.dot_general(a, b, dims, preferred_element_type=f32)


def tie(value, *others):
    return lax.optimization_barrier((value,) + others)[0]


def first_blocks(steps):
    return lambda i, *_: (jnp.minimum(i, steps // 2 - 1), 0)


def last_blocks(steps):
    return lambda i, *_: (jnp.maximum(i - steps // 2, 0), 0)


def store_halves(first_ref, last_ref, value):
    step, split = pl.program_id(0), pl.num_programs(0) // 2

    @pl.when(step < split)
    def first():
        first_ref[...] = value

    @pl.when(step >= split)
    def last():
        last_ref[...] = value


def lane_index(rows):
    return lax.broadcasted_iota(jnp.int32, (rows, LANES), 1)


def swap_halves(w, lane):
    half = HEAD_DIM // 2
    up = pltpu.roll(w, LANES - half, 1)
    down = pltpu.roll(w, half, 1)
    return jnp.where(lane < half, up, down)


def widen(piece):
    rows = piece.shape[0]
    tail = jnp.zeros((rows, LANES - piece.shape[1]), piece.dtype)
    return jnp.concatenate([piece, tail], axis=1)


def split_three(column):
    high = column.astype(bf16).astype(f32)
    rest = column - high
    mid = rest.astype(bf16).astype(f32)
    return high, mid, rest - mid


def place_three(base, column, lane):
    high, mid, low = split_three(column)
    base = jnp.where(lane == 96, high, base)
    base = jnp.where(lane == 97, mid, base)
    return jnp.where(lane == 98, low, base)


def qkv_kernel(heads, x_ref, w_ref, ln_ref, b_ref, cos_ref, sin_ref, feat_ref, a_ref, q_ref, kv_ref):
    width = heads * HEAD_DIM
    x = x_ref[...].astype(f32)
    rows = x.shape[0]
    center = x - jnp.mean(x, axis=1, keepdims=True)
    inverse = lax.rsqrt(jnp.mean(center * center, axis=1, keepdims=True) + norm_eps)
    a = (center * inverse * ln_ref[0:1, :] + ln_ref[1:2, :]).astype(bf16)
    a_ref[...] = a
    y = mm(a, w_ref[...]) + b_ref[0:1, :]
    cos, sin = cos_ref[...], sin_ref[...]
    lane = lane_index(rows)
    kv = []
    for h in range(heads):
        w = widen(y[:, h * HEAD_DIM : (h + 1) * HEAD_DIM])
        q = (w * cos + swap_halves(w, lane) * sin) * (HEAD_DIM**-0.5 * log2e)
        q_ref[h] = jnp.where(lane < HEAD_DIM, q.astype(bf16), feat_ref[...])
    for h in range(heads):
        begin = width + h * HEAD_DIM
        w = widen(y[:, begin : begin + HEAD_DIM])
        kv.append((w * cos + swap_halves(w, lane) * sin)[:, :HEAD_DIM].astype(bf16))
    kv.append(y[:, 2 * width : 3 * width].astype(bf16))
    kv_ref[...] = jnp.concatenate(kv, axis=1)


def project_row(x, w, ln, bias, cos, sin, feat, heads):
    rows, width = x.shape
    block = min(256, rows)
    wide = w.shape[1]
    local = heads * HEAD_DIM
    by_rows = lambda n: pl.BlockSpec((block, n), lambda i: (i, 0))
    whole = lambda a: pl.BlockSpec(a.shape, lambda i: (0,) * a.ndim)
    return pl.pallas_call(
        functools.partial(qkv_kernel, heads),
        grid=(rows // block,),
        in_specs=[
            by_rows(width),
            whole(w),
            whole(ln),
            whole(bias),
            by_rows(LANES),
            by_rows(LANES),
            by_rows(LANES),
        ],
        out_specs=[
            by_rows(width),
            pl.BlockSpec((heads, block, LANES), lambda i: (0, i, 0)),
            by_rows(2 * local),
        ],
        out_shape=[
            jax.ShapeDtypeStruct((rows, width), bf16),
            jax.ShapeDtypeStruct((heads, rows, LANES), bf16),
            jax.ShapeDtypeStruct((rows, 2 * local), bf16),
        ],
        cost_estimate=pl.CostEstimate(
            flops=2 * rows * width * wide, bytes_accessed=rows * width * 4 + width * wide * 2, transcendentals=0
        ),
        name="project_row",
    )(x, w, ln, bias, cos, sin, feat)


def forward_kernel(heads, segments, block, flag_ref, q_ref, w_ref, *refs):
    kv_refs = refs[:segments]
    feat_refs = refs[segments : 2 * segments]
    o_ref, q_out, k_aug, v_aug, p_first, p_last, m_scr, acc_scr = refs[2 * segments :]
    width = heads * HEAD_DIM
    step = pl.program_id(0)
    keys = k_aug.shape[1]
    count = keys // block
    rows = q_ref.shape[1]

    @pl.when(step == 0)
    def build():
        offset = 0
        for s in range(segments):
            length = kv_refs[s].shape[0]
            piece = min(length, 256)
            for t in range(length // piece):
                at = pl.ds(t * piece, piece)
                to = pl.ds(offset + t * piece, piece)
                kv = kv_refs[s][at, :]
                feat = feat_refs[s][at, :]
                lane = lane_index(piece)
                tail = jnp.where(lane == HEAD_DIM, 1.0, jnp.where((lane >= 96) & (lane < 99), -1.0, 0.0)).astype(bf16)
                for h in range(heads):
                    k = kv[:, h * HEAD_DIM : (h + 1) * HEAD_DIM]
                    v = kv[:, width + h * HEAD_DIM : width + (h + 1) * HEAD_DIM]
                    k_aug[h, to, :] = jnp.concatenate([k, feat[:, HEAD_DIM:]], axis=1)
                    v_aug[h, to, :] = jnp.concatenate([v, tail[:, HEAD_DIM:]], axis=1)
            offset += length

    m_scr[...] = jnp.full(m_scr.shape, floor_max, f32)
    acc_scr[...] = jnp.zeros(acc_scr.shape, f32)

    def visit(j, carry):
        @pl.when(flag_ref[step * count + j] > 0)
        def go():
            at = pl.ds(pl.multiple_of(j * block, block), block)
            for h in range(heads):
                s = mm(q_ref[h], k_aug[h, at, :], NT)
                old = m_scr[h]
                cuts = [s[:, c : c + LANES] for c in range(0, block, LANES)]
                top = functools.reduce(jnp.maximum, cuts)
                new = jnp.maximum(old, jnp.max(top, axis=1, keepdims=True))
                p = jnp.concatenate([jnp.exp2(cut - new) for cut in cuts], axis=1)
                m_scr[h] = new
                acc_scr[h] = acc_scr[h] * jnp.exp2(old - new) + mm(p.astype(bf16), v_aug[h, at, :])

        return carry

    lax.fori_loop(0, count, visit, 0)
    lane = lane_index(rows)
    outs = []
    for h in range(heads):
        acc = acc_scr[h]
        total = acc[:, HEAD_DIM : HEAD_DIM + 1]
        alive = total > 0.0
        safe = jnp.where(alive, total, 1.0)
        outs.append((acc / safe)[:, :HEAD_DIM].astype(bf16))
        level = jnp.where(alive, m_scr[h][:, 0:1] + jnp.log2(safe), 0.0)
        q_out[h] = place_three(q_ref[h].astype(f32), level, lane).astype(bf16)
    o = jnp.concatenate(outs, axis=1)
    o_ref[...] = o
    store_halves(p_first, p_last, mm(o, w_ref[...], NT).astype(bf16))


def attend_forward(flags, q_aug, w, kvs, feats, heads, block):
    rows = q_aug.shape[1]
    tall = min(256, rows // 2)
    steps = rows // tall
    width = w.shape[0]
    keys = sum(kv.shape[0] for kv in kvs)
    segments = len(kvs)
    whole = lambda a: pl.BlockSpec(a.shape, lambda i, f: (0,) * a.ndim)
    q_spec = pl.BlockSpec((heads, tall, LANES), lambda i, f: (0, i, 0))
    k_spec = pl.BlockSpec((heads, keys, LANES), lambda i, f: (0, 0, 0))
    local = heads * HEAD_DIM
    return pl.pallas_call(
        functools.partial(forward_kernel, heads, segments, block),
        grid_spec=pltpu.PrefetchScalarGridSpec(
            num_scalar_prefetch=1,
            grid=(rows // tall,),
            in_specs=[q_spec, whole(w)] + [whole(kv) for kv in kvs] + [whole(f) for f in feats],
            out_specs=[
                pl.BlockSpec((tall, local), lambda i, f: (i, 0)),
                q_spec,
                k_spec,
                k_spec,
                pl.BlockSpec((tall, width), first_blocks(steps)),
                pl.BlockSpec((tall, width), last_blocks(steps)),
            ],
            scratch_shapes=[
                pltpu.VMEM((heads, tall, LANES), f32),
                pltpu.VMEM((heads, tall, LANES), f32),
            ],
        ),
        out_shape=[
            jax.ShapeDtypeStruct((rows, local), bf16),
            jax.ShapeDtypeStruct((heads, rows, LANES), bf16),
            jax.ShapeDtypeStruct((heads, keys, LANES), bf16),
            jax.ShapeDtypeStruct((heads, keys, LANES), bf16),
            jax.ShapeDtypeStruct((rows // 2, width), bf16),
            jax.ShapeDtypeStruct((rows // 2, width), bf16),
        ],
        cost_estimate=pl.CostEstimate(
            flops=2 * rows * keys * heads * LANES, bytes_accessed=8 * keys * local, transcendentals=rows * keys * heads // 2
        ),
        name="attend_forward",
    )(flags, q_aug, w, *kvs, *feats)


def backward_kernel(
    heads, segments, block, flag_ref, q_ref, ga_first, ga_last, w_ref, o_ref, k_aug, v_aug, cosq_ref, sinq_ref, *refs
):
    cosk_refs = refs[:segments]
    sink_refs = refs[segments : 2 * segments]
    dq_ref = refs[2 * segments]
    dkv_refs = refs[2 * segments + 1 : 3 * segments + 1]
    k_turn, dk_acc, dv_acc, dq_acc, go_scr = refs[3 * segments + 1 :]
    step = pl.program_id(0)
    keys = k_aug.shape[1]
    count = keys // block
    rows = q_ref.shape[1]
    scale = HEAD_DIM**-0.5

    @pl.when(step == 0)
    def build():
        dk_acc[...] = jnp.zeros(dk_acc.shape, f32)
        dv_acc[...] = jnp.zeros(dv_acc.shape, f32)
        for h in range(heads):
            for t in range(count):
                at = pl.ds(t * block, block)
                k_turn[h, :, at] = k_aug[h, at, :].T

    lane = lane_index(rows)
    ga = jnp.where(step < pl.num_programs(0) // 2, ga_first[...], ga_last[...])
    go_all = mm(ga, w_ref[...]).astype(bf16).astype(f32)
    for h in range(heads):
        cut = slice(h * HEAD_DIM, (h + 1) * HEAD_DIM)
        go = go_all[:, cut]
        delta = jnp.sum(go * o_ref[:, cut].astype(f32), axis=1, keepdims=True)
        go_scr[h] = place_three(widen(go), delta, lane).astype(bf16)
    dq_acc[...] = jnp.zeros(dq_acc.shape, f32)

    def visit(j, carry):
        @pl.when(flag_ref[step * count + j] > 0)
        def run():
            at = pl.ds(pl.multiple_of(j * block, block), block)
            for h in range(heads):
                q, go = q_ref[h], go_scr[h]
                p = jnp.exp2(mm(k_aug[h, at, :], q, NT))
                ds = (p * mm(v_aug[h, at, :], go, NT)).astype(bf16)
                dv_acc[h, at, :] += mm(p.astype(bf16), go)
                dk_acc[h, at, :] += mm(ds, q)
                dq_acc[h] += mm(k_turn[h, :, at], ds)

        return carry

    lax.fori_loop(0, count, visit, 0)

    def turn_back(w, cos, sin, index):
        return w * cos - swap_halves(w, index) * sin

    outs = []
    for h in range(heads):
        w = dq_acc[h].T
        back = turn_back(w, cosq_ref[...], sinq_ref[...], lane) * scale
        outs.append(back[:, :HEAD_DIM].astype(bf16))
    dq_ref[...] = jnp.concatenate(outs, axis=1)

    @pl.when(step == pl.num_programs(0) - 1)
    def finish():
        offset = 0
        for s in range(segments):
            length = dkv_refs[s].shape[0]
            piece = min(length, 256)
            index = lane_index(piece)
            for t in range(length // piece):
                at = pl.ds(t * piece, piece)
                of = pl.ds(offset + t * piece, piece)
                parts = []
                for h in range(heads):
                    w = dk_acc[h, of, :]
                    back = turn_back(w, cosk_refs[s][at, :], sink_refs[s][at, :], index) * (1.0 / log2e)
                    parts.append(back[:, :HEAD_DIM].astype(bf16))
                for h in range(heads):
                    parts.append(dv_acc[h, of, :][:, :HEAD_DIM].astype(bf16))
                dkv_refs[s][at, :] = jnp.concatenate(parts, axis=1)
            offset += length


def attend_backward(flags, q_aug, ga, w, o, k_aug, v_aug, cos_q, sin_q, cos_k, sin_k, heads, block):
    rows = q_aug.shape[1]
    tall = min(256, rows // 2)
    steps = rows // tall
    width = w.shape[0]
    keys = k_aug.shape[1]
    segments = len(cos_k)
    local = heads * HEAD_DIM
    whole = lambda a: pl.BlockSpec(a.shape, lambda i, f: (0,) * a.ndim)
    by_rows = lambda n: pl.BlockSpec((tall, n), lambda i, f: (i, 0))
    q_spec = pl.BlockSpec((heads, tall, LANES), lambda i, f: (0, i, 0))
    return pl.pallas_call(
        functools.partial(backward_kernel, heads, segments, block),
        grid_spec=pltpu.PrefetchScalarGridSpec(
            num_scalar_prefetch=1,
            grid=(rows // tall,),
            in_specs=[
                q_spec,
                pl.BlockSpec((tall, width), first_blocks(steps)),
                pl.BlockSpec((tall, width), last_blocks(steps)),
                whole(w),
                by_rows(local),
                whole(k_aug),
                whole(v_aug),
                by_rows(LANES),
                by_rows(LANES),
            ]
            + [whole(t) for t in cos_k]
            + [whole(t) for t in sin_k],
            out_specs=[by_rows(local)]
            + [pl.BlockSpec((t.shape[0], 2 * local), lambda i, f: (0, 0)) for t in cos_k],
            scratch_shapes=[
                pltpu.VMEM((heads, LANES, keys), bf16),
                pltpu.VMEM((heads, keys, LANES), f32),
                pltpu.VMEM((heads, keys, LANES), f32),
                pltpu.VMEM((heads, LANES, tall), f32),
                pltpu.VMEM((heads, tall, LANES), bf16),
            ],
        ),
        out_shape=[jax.ShapeDtypeStruct((rows, local), bf16)]
        + [jax.ShapeDtypeStruct((t.shape[0], 2 * local), bf16) for t in cos_k],
        cost_estimate=pl.CostEstimate(
            flops=5 * rows * keys * heads * LANES, bytes_accessed=16 * keys * local, transcendentals=rows * keys * heads // 2
        ),
        name="attend_backward",
    )(flags, q_aug, *ga, w, o, k_aug, v_aug, cos_q, sin_q, *cos_k, *sin_k)


def feed_kernel(chunk, c_first, c_last, g_ref, up_ref, down_ref, shift_ref, z_ref, gu_ref, gc_first, gc_last, feed_first, feed_last, sum_ref):
    step = pl.program_id(0)
    c = jnp.where(step < pl.num_programs(0) // 2, c_first[...], c_last[...])
    g = g_ref[...]
    sums = []
    for begin in range(0, up_ref.shape[1], chunk):
        cut = slice(begin, begin + chunk)
        u = mm(c, up_ref[:, cut]) + shift_ref[0:1, cut]
        sg = 0.5 + 0.5 * jnp.tanh(0.851 * u)
        z = (u * sg).astype(bf16)
        gu = (mm(g, down_ref[:, cut]) * (sg + 1.702 * u * sg * (1.0 - sg))).astype(bf16)
        z_ref[:, cut] = z
        gu_ref[:, cut] = gu
        sums.append(jnp.sum(gu.astype(f32), axis=0, keepdims=True))
    store_halves(gc_first, gc_last, mm(gu_ref[...], up_ref[...], NT).astype(bf16))
    store_halves(feed_first, feed_last, mm(z_ref[...], down_ref[...], NT).astype(bf16))

    @pl.when(step == 0)
    def clear():
        sum_ref[...] = jnp.zeros(sum_ref.shape, f32)

    sum_ref[0:1, :] += jnp.concatenate(sums, axis=1)
    sum_ref[1:2, : g.shape[1]] += jnp.sum(g.astype(f32), axis=0, keepdims=True)


def feed_forward(c, g, w_up, w_down, shift):
    rows, width = g.shape
    hidden = w_up.shape[1]
    tall = min(256, rows // 2)
    steps = rows // tall
    chunk = 256 if hidden % 256 == 0 else hidden
    by_rows = lambda n: pl.BlockSpec((tall, n), lambda i: (i, 0))
    whole = lambda a: pl.BlockSpec(a.shape, lambda i: (0,) * a.ndim)
    first = pl.BlockSpec((tall, width), first_blocks(steps))
    last = pl.BlockSpec((tall, width), last_blocks(steps))
    part = jax.ShapeDtypeStruct((rows // 2, width), bf16)
    longest = max(width, hidden)
    return pl.pallas_call(
        functools.partial(feed_kernel, chunk),
        grid=(steps,),
        in_specs=[first, last, by_rows(width), whole(w_up), whole(w_down), whole(shift)],
        out_specs=[by_rows(hidden), by_rows(hidden), first, last, first, last, pl.BlockSpec((8, longest), lambda i: (0, 0))],
        out_shape=[
            jax.ShapeDtypeStruct((rows, hidden), bf16),
            jax.ShapeDtypeStruct((rows, hidden), bf16),
            part,
            part,
            part,
            part,
            jax.ShapeDtypeStruct((8, longest), f32),
        ],
        cost_estimate=pl.CostEstimate(
            flops=8 * rows * width * hidden, bytes_accessed=4 * width * hidden + 12 * rows * width, transcendentals=rows * hidden
        ),
        name="feed_forward",
    )(*c, g, w_up, w_down, shift)


def back_kernel(pieces, x_ref, w_ref, gq_ref, *refs):
    kv_refs = refs[:pieces]
    p_first, p_last, dkv_ref, sum_ref = refs[pieces:]
    gq = gq_ref[...]
    if pieces == 1:
        dkv = kv_refs[0][...]
    else:
        other = jnp.where(pl.program_id(0) < pl.num_programs(0) // 2, kv_refs[1][...], kv_refs[2][...])
        dkv = (kv_refs[0][...].astype(f32) + other.astype(f32)).astype(bf16)
    dkv_ref[...] = dkv
    tail = jnp.zeros((gq.shape[0], w_ref.shape[1] - gq.shape[1] - dkv.shape[1]), bf16)
    e = mm(jnp.concatenate([gq, dkv, tail], axis=1), w_ref[...], NT)
    store_halves(p_first, p_last, e.astype(bf16))
    x = x_ref[...].astype(f32)
    center = x - jnp.mean(x, axis=1, keepdims=True)
    unit = center * lax.rsqrt(jnp.mean(center * center, axis=1, keepdims=True) + norm_eps)

    @pl.when(pl.program_id(0) == 0)
    def clear():
        sum_ref[...] = jnp.zeros(sum_ref.shape, f32)

    local = gq.shape[1]
    sum_ref[0:1, :] += jnp.sum(e * unit, axis=0, keepdims=True)
    sum_ref[1:2, :] += jnp.sum(e, axis=0, keepdims=True)
    sum_ref[2:3, :local] += jnp.sum(gq.astype(f32), axis=0, keepdims=True)
    sum_ref[3:4, : 2 * local] += jnp.sum(dkv.astype(f32), axis=0, keepdims=True)


def project_back(x, w, gq, dkvs):
    rows, width = x.shape
    local = gq.shape[1]
    tall = min(512, rows // 2)
    steps = rows // tall
    by_rows = lambda n: pl.BlockSpec((tall, n), lambda i: (i, 0))
    whole = lambda a: pl.BlockSpec(a.shape, lambda i: (0,) * a.ndim)
    part = jax.ShapeDtypeStruct((rows // 2, width), bf16)
    kv_specs = [
        by_rows(2 * local),
        pl.BlockSpec((tall, 2 * local), first_blocks(steps)),
        pl.BlockSpec((tall, 2 * local), last_blocks(steps)),
    ]
    return pl.pallas_call(
        functools.partial(back_kernel, len(dkvs)),
        grid=(steps,),
        in_specs=[by_rows(width), whole(w), by_rows(local)] + kv_specs[: len(dkvs)],
        out_specs=[
            pl.BlockSpec((tall, width), first_blocks(steps)),
            pl.BlockSpec((tall, width), last_blocks(steps)),
            by_rows(2 * local),
            pl.BlockSpec((8, width), lambda i: (0, 0)),
        ],
        out_shape=[part, part, jax.ShapeDtypeStruct((rows, 2 * local), bf16), jax.ShapeDtypeStruct((8, width), f32)],
        cost_estimate=pl.CostEstimate(
            flops=6 * rows * width * local, bytes_accessed=6 * width * local + 6 * rows * width, transcendentals=rows
        ),
        name="project_back",
    )(x, w, gq, *dkvs)


def norm_stats(rows_in):
    center = rows_in - jnp.mean(rows_in, axis=1, keepdims=True)
    inverse = lax.rsqrt(jnp.mean(center * center, axis=1, keepdims=True) + norm_eps)
    return center * inverse, inverse


def norm_backward(grad_rows, unit_rows, inverse, gain):
    scaled = grad_rows * gain
    return inverse * (
        scaled
        - jnp.mean(scaled, axis=1, keepdims=True)
        - unit_rows * jnp.mean(scaled * unit_rows, axis=1, keepdims=True)
    )


def norm_two_kernel(x_ref, near_ref, far_ref, vec_ref, h_ref, c_ref):
    h = x_ref[...].astype(f32) + (near_ref[...].astype(f32) + far_ref[...].astype(f32)) + vec_ref[0:1, :]
    h_ref[...] = h
    c_ref[...] = (norm_stats(h)[0] * vec_ref[1:2, :] + vec_ref[2:3, :]).astype(bf16)


def norm_two_back_kernel(h_ref, near_ref, far_ref, g_ref, vec_ref, gh_ref, ga_ref, sum_ref):
    unit, inverse = norm_stats(h_ref[...])
    gc = near_ref[...].astype(f32) + far_ref[...].astype(f32)
    gh = g_ref[...].astype(f32) + norm_backward(gc, unit, inverse, vec_ref[1:2, :])
    ga = gh.astype(bf16)
    gh_ref[...] = gh
    ga_ref[...] = ga

    @pl.when(pl.program_id(0) == 0)
    def clear():
        sum_ref[...] = jnp.zeros(sum_ref.shape, f32)

    sum_ref[0:1, :] += jnp.sum(gc * unit, axis=0, keepdims=True)
    sum_ref[1:2, :] += jnp.sum(gc, axis=0, keepdims=True)
    sum_ref[2:3, :] += jnp.sum(ga.astype(f32), axis=0, keepdims=True)


def norm_one_back_kernel(x_ref, near_ref, far_ref, gh_ref, vec_ref, out_ref):
    unit, inverse = norm_stats(x_ref[...].astype(f32))
    ga1 = near_ref[...].astype(f32) + far_ref[...].astype(f32)
    out_ref[...] = (gh_ref[...] + norm_backward(ga1, unit, inverse, vec_ref[0:1, :])).astype(bf16)


def close_kernel(h_ref, near_ref, far_ref, live_ref, vec_ref, out_ref):
    feed = near_ref[...].astype(f32) + far_ref[...].astype(f32)
    out_ref[...] = ((h_ref[...] + feed + vec_ref[0:1, :]) * live_ref[...]).astype(bf16)


def by_tokens(body, arrays, vectors, kinds, name, sums=False):
    count, width = arrays[1].shape
    tall = min(256, count)
    in_specs = [pl.BlockSpec((tall, a.shape[1]), lambda i: (i, 0)) for a in arrays]
    out_specs = [pl.BlockSpec((tall, width), lambda i: (i, 0)) for _ in kinds]
    out_shape = [jax.ShapeDtypeStruct((count, width), kind) for kind in kinds]
    if sums:
        out_specs.append(pl.BlockSpec((8, width), lambda i: (0, 0)))
        out_shape.append(jax.ShapeDtypeStruct((8, width), f32))
    return pl.pallas_call(
        body,
        grid=(count // tall,),
        in_specs=in_specs + [pl.BlockSpec(vectors.shape, lambda i: (0, 0))],
        out_specs=out_specs,
        out_shape=out_shape,
        cost_estimate=pl.CostEstimate(flops=20 * count * width, bytes_accessed=14 * count * width, transcendentals=count),
        name=name,
    )(*arrays, vectors)


def gather_rows_kernel(side_ref, *refs):
    step = pl.program_id(0)
    for index, piece in enumerate(refs[:-1]):

        @pl.when(step == index)
        def copy(piece=piece):
            refs[-1][0] = piece[...]


def gather_rows(side, pieces):
    half, width = pieces[0].shape
    count = len(pieces)
    return pl.pallas_call(
        gather_rows_kernel,
        grid_spec=pltpu.PrefetchScalarGridSpec(
            num_scalar_prefetch=1,
            grid=(count,),
            in_specs=[pl.BlockSpec((half, width), lambda t, s: (0, 0)) for _ in pieces],
            out_specs=pl.BlockSpec((1, half, width), lambda t, s: (t // 2, jnp.where(t % 2 == 0, s[0], 1 - s[0]), 0)),
        ),
        out_shape=jax.ShapeDtypeStruct((count // 2, 2 * half, width), bf16),
        cost_estimate=pl.CostEstimate(flops=0, bytes_accessed=4 * count * half * width, transcendentals=0),
        name="gather_rows",
    )(side, *pieces)


def tables(grid_pos):
    lane = jnp.arange(LANES)
    quarter = HEAD_DIM // 4
    frequency = jnp.power(10000.0, -4.0 * (lane % quarter).astype(f32) / HEAD_DIM)
    place = jnp.where((lane // quarter) % 2 == 0, grid_pos[0][:, None], grid_pos[1][:, None])
    angle = jnp.where(lane < HEAD_DIM, place.astype(f32) * frequency, 0.0)
    return jnp.cos(angle), jnp.where(lane < HEAD_DIM // 2, -1.0, 1.0) * jnp.sin(angle)


def query_features(ids):
    lane = jnp.arange(LANES)
    return (lane == HEAD_DIM + 1 + ids[:, None]).astype(bf16)


def key_features(ids):
    lane = jnp.arange(LANES)
    slot = lane - HEAD_DIM
    same = (slot >= 1) & (slot == ids[:, None] + 1)
    wall = jnp.where((slot >= 0) & (slot < 16) & ~same, -hide, 0.0)
    return jnp.where((lane >= 96) & (lane < 99), -1.0, wall).astype(bf16)


def visit_flags(query_ids, key_ids, tall, block):
    q = query_ids.reshape(-1, tall)
    k = key_ids.reshape(-1, block)
    q_top, k_top = jnp.max(q, axis=1), jnp.max(k, axis=1)
    q_low = jnp.min(jnp.where(q >= 0, q, 1 << 20), axis=1)
    k_low = jnp.min(jnp.where(k >= 0, k, 1 << 20), axis=1)
    meet = (q_low[:, None] <= k_top[None, :]) & (k_low[None, :] <= q_top[:, None])
    return meet.astype(jnp.int32).reshape(-1)


def on_device(
    patches,
    cotangent,
    picture_ids,
    positions,
    ln1_gain,
    ln1_bias,
    qkv_weight,
    qkv_bias,
    proj_weight,
    proj_bias,
    ln2_gain,
    ln2_bias,
    fc1_weight,
    fc1_bias,
    fc2_weight,
    fc2_bias,
):
    row_count, row_share, width = patches.shape
    owners = lax.axis_size("shard")
    contexts = lax.axis_size("ctx")
    ways = lax.axis_size("tp")
    part = qkv_weight.shape[0]
    local = qkv_weight.shape[2]
    heads = local // HEAD_DIM
    half = row_share // 2
    side = lax.axis_index("tp") % 2
    context = lax.axis_index("ctx")
    pairs_near = [(i, i ^ 1) for i in range(ways)]
    pairs_far = [(i, i ^ 2) for i in range(ways)]
    pad = -3 * local % 256
    wide = 3 * local + pad

    def near(v):
        return lax.ppermute(v, "tp", pairs_near)

    def far(v):
        return lax.ppermute(v, "tp", pairs_far)

    def over_ctx(v):
        return lax.ppermute(v, "ctx", [(0, 1), (1, 0)])

    def mine_first(v, axis=0):
        return jnp.where(side == 0, v, jnp.roll(v, half, axis=axis))

    def column(v):
        flat = v.reshape(-1)
        return jnp.pad(flat, (0, part - flat.shape[0]))

    vectors = [ln1_gain, ln1_bias, ln2_gain, ln2_bias, proj_bias, fc2_bias, qkv_bias, fc1_bias]
    place = lax.axis_index("shard")
    context_first = context == 0

    def rotate_gather(piece):
        whole = lax.dynamic_update_index_in_dim(jnp.zeros((owners,) + piece.shape, piece.dtype), piece, place, 0)
        for step in range(1, owners):
            got = lax.ppermute(piece, "shard", [(i, (i + step) % owners) for i in range(owners)])
            whole = lax.dynamic_update_index_in_dim(whole, got, (place - step) % owners, 0)
        return whole

    tail = rotate_gather(jnp.stack([column(v) for v in vectors]).astype(bf16))
    packed = jnp.transpose(tail, (1, 0, 2)).reshape(len(vectors), width).astype(f32)
    qkv_piece = jnp.pad(qkv_weight.reshape(part, 3 * local), ((0, 0), (0, pad))).astype(bf16)
    gather = lambda v: lax.all_gather(v, "shard", axis=0, tiled=True)
    up_piece = fc1_weight.astype(bf16)
    down_piece = fc2_weight.T.astype(bf16)
    w_qkv = gather(qkv_piece)
    w_proj = rotate_gather(tie(proj_weight.T.astype(bf16), w_qkv)).reshape(owners * part, local)
    gain_one, bias_one, gain_two, bias_two, proj_shift, down_shift = [packed[i] for i in range(6)]
    qb_size = qkv_bias.size
    qkv_shift = packed[6].reshape(owners, part)[:, :qb_size].reshape((owners,) + qkv_bias.shape)
    qkv_shift = jnp.transpose(qkv_shift, (1, 2, 0, 3)).reshape(-1)
    qkv_shift = jnp.pad(qkv_shift, (0, pad)).reshape(1, wide)
    up_shift = packed[7].reshape(owners, part)[:, : fc1_bias.size].reshape((owners,) + fc1_bias.shape)
    up_shift = jnp.transpose(up_shift, (1, 0, 2)).reshape(1, -1)
    ln_one = tie(packed[0:2], up_piece, down_piece)

    ids_by_ctx = mine_first(picture_ids.reshape(row_count, contexts, row_share), axis=2)
    places = mine_first(positions, axis=2)
    block = min(256, half)

    def cut_last(spots):
        return [spots[0], spots[1][:half], spots[1][half:]] if contexts == 2 else spots

    key_block = 256
    rows = []
    for r in range(row_count):
        x = mine_first(patches[r])
        g = mine_first(cotangent[r])
        ids = lax.dynamic_index_in_dim(ids_by_ctx[r], context, 0, keepdims=False)
        if contexts == 2:
            other = lax.dynamic_index_in_dim(ids_by_ctx[r], 1 - context, 0, keepdims=False)
            key_ids = [ids, other]
            spots = [places[:, r], over_ctx(places[:, r])]
        else:
            key_ids = [ids_by_ctx[r].reshape(-1)]
            spots = [lax.all_gather(places[:, r], "ctx", axis=1, tiled=True)]
        live = (ids >= 0).astype(f32)[:, None]
        turns = [tables(spot) for spot in spots]
        own_turn = turns[0] if contexts == 2 else tables(places[:, r])
        rows.append(
            dict(
                x=x,
                g=(g.astype(f32) * live).astype(bf16),
                live=live,
                ids=ids,
                cos=own_turn[0],
                sin=own_turn[1],
                cos_k=cut_last([t[0] for t in turns]),
                sin_k=cut_last([t[1] for t in turns]),
                q_feat=query_features(ids),
                k_feat=[key_features(k) for k in key_ids],
                flags=visit_flags(ids, jnp.concatenate(key_ids), block, key_block),
            )
        )

    ln_one = tie(ln_one, qkv_shift, up_shift, *[row["g"] for row in rows])

    for index, row in enumerate(rows):
        row["a"], row["q"], row["kv"] = project_row(
            row["x"], w_qkv, ln_one, qkv_shift, row["cos"], row["sin"], row["q_feat"], heads
        )
        if index == 1:
            row["kv"], w_proj = lax.optimization_barrier((row["kv"], w_proj))
        if contexts == 2:
            row["kvs"] = [row["kv"], over_ctx(row["kv"])]
        else:
            row["kvs"] = [lax.all_gather(row["kv"], "ctx", axis=0, tiled=True)]

    down_piece, up_piece = lax.optimization_barrier(
        (down_piece, up_piece, w_qkv, ln_one, [(row["x"], row["cos"], row["sin"], row["cos_k"], row["sin_k"]) for row in rows])
    )[:2]
    if contexts == 2:
        down_cut = down_piece.reshape(2, part // 2, -1)
        down_near = gather(lax.dynamic_index_in_dim(down_cut, context, 0, keepdims=False))
        down_near = down_near.reshape(owners, part // 2, -1)
    else:
        w_down = gather(down_piece)
    w_up = gather(up_piece)

    def sum_near(first, last):
        return (first.astype(f32) + near(last).astype(f32)).astype(bf16)

    norm_vectors = jnp.pad(jnp.stack([proj_shift, gain_two, bias_two]), ((0, 5), (0, 0)))

    def norm_two(row, vectors):
        row["h"], mine = by_tokens(
            norm_two_kernel, [row["x"], row["branch"], row["branch_far"]], vectors, [f32, bf16], "norm_two"
        )
        row["c"] = (mine, near(mine))

    hold = lax.optimization_barrier
    before = rows[-1]["kv"]
    for index, row in enumerate(rows):
        row["o"], row["q"], row["k_aug"], row["v_aug"], first, last = attend_forward(
            tie(row["flags"], before), row["q"], w_proj, row["kvs"], row["k_feat"], heads, key_block
        )
        if index:
            prior = rows[index - 1]
            first, last, prior["branch_far"] = hold((first, last, prior["branch_far"]))
        if index + 1 < row_count:
            follow = rows[index + 1]
            first, last, follow["kvs"] = hold((first, last, follow["kvs"]))
            if contexts == 2:
                first, last, down_near = hold((first, last, down_near))
                down_far = over_ctx(down_near)
        elif contexts == 2:
            first, last, down_far, w_up = hold((first, last, down_far, w_up))
        before = row["branch"] = sum_near(first, last)
        row["branch_far"] = far(before)
    if contexts == 2:
        low = jnp.where(context_first, down_near, down_far)
        high = jnp.where(context_first, down_far, down_near)
        w_down = jnp.concatenate([low, high], axis=1).reshape(owners * part, -1)

    norm_two(rows[0], tie(norm_vectors, before))
    for index, row in enumerate(rows):
        shift = tie(up_shift, before)
        row["z"], row["gu"], gc_first, gc_last, feed_first, feed_last, row["feed_sums"] = feed_forward(
            row["c"], row["g"], w_up, w_down, shift
        )
        other, key = (rows[-1], "branch_far") if index == 0 else (rows[index - 1], "gc_far")
        gc_first, gc_last, other[key] = hold((gc_first, gc_last, other[key]))
        before = row["gc"] = sum_near(gc_first, gc_last)
        row["gc_far"] = far(before)
        row["feed"] = (feed_first, feed_last)
        if index + 1 < row_count:
            norm_two(rows[index + 1], norm_vectors)
    for row in rows:
        row["feed"] = sum_near(*row["feed"])

    join = lambda key: jnp.concatenate([row[key] for row in rows], axis=0)
    join_two = lambda key: jnp.concatenate([piece for row in rows for piece in row[key]], axis=0)
    scatter = lambda v: lax.psum_scatter(v, "shard", scatter_dimension=0, tiled=True)
    if contexts == 2:
        finish = lambda v: v.astype(f32) + over_ctx(v).astype(f32)
    else:
        finish = lambda v: lax.psum(v, "ctx").astype(f32)
    last_row = rows[-1]

    def norm_two_back(row):
        row["gh"], ga, norm_sums = by_tokens(
            norm_two_back_kernel,
            [row["h"], row["gc"], row["gc_far"], row["g"]],
            norm_vectors,
            [f32, bf16],
            "norm_two_back",
            sums=True,
        )
        row["ga"] = (ga, near(ga))
        return norm_sums[0:3]

    pair = sum(norm_two_back(row) for row in rows[:-1])
    last_row["gu"], last_row["z"] = hold((last_row["gu"], last_row["z"], before, *[row["ga"][0] for row in rows[:-1]]))[:2]
    grad_up = mm(join_two("c"), join("gu"), TN).astype(bf16)
    grad_down = mm(join("g"), join("z"), TN).astype(bf16)
    grad_up, grad_down, last_row["gc_far"] = hold((grad_up, grad_down, last_row["gc_far"]))
    pair = pair + norm_two_back(last_row)
    grad_proj = mm(join_two("ga"), join("o"), TN).astype(bf16)
    before = (grad_up, grad_down)
    y_free = last_row["gc_far"]
    grad_up = scatter(grad_up)
    if contexts == 2:
        cut = grad_down.reshape(owners, 2, part // 2, -1)
        keep = lax.dynamic_index_in_dim(cut, context, 1, keepdims=False)
        came = over_ctx(lax.dynamic_index_in_dim(cut, 1 - context, 1, keepdims=False))
    else:
        grad_down = scatter(grad_down)

    for index, row in enumerate(rows):
        feed_far = far(tie(row["feed"], y_free))
        out = attend_backward(
            tie(row["flags"], *before),
            row["q"],
            row["ga"],
            w_proj,
            row["o"],
            row["k_aug"],
            row["v_aug"],
            row["cos"],
            row["sin"],
            row["cos_k"],
            row["sin_k"],
            heads,
            key_block,
        )
        if index:
            prior = rows[index - 1]
            *out, feed_far, prior["dkvs"], grad_up = hold((*out, feed_far, prior["dkvs"], grad_up))
            if contexts == 2:
                *out, grad_down = hold((*out, grad_down))
        elif contexts == 2:
            *out, feed_far, came = hold((*out, feed_far, came))
            grad_down = scatter((keep.astype(f32) + came.astype(f32)).astype(bf16).reshape(owners * part // 2, -1))
        else:
            *out, feed_far = hold((*out, feed_far))
        y_free = feed_far
        before = (out[0], grad_proj)
        row["gq"] = out[0]
        row["feed_far"] = feed_far
        if contexts == 2:
            row["dkvs"] = [out[1], over_ctx(out[2]), over_ctx(out[3])]
        else:
            row["dkvs"] = [lax.psum_scatter(out[1], "ctx", scatter_dimension=0, tiled=True)]

    side_list = side.reshape(1).astype(jnp.int32)
    grad_proj = scatter(grad_proj)
    sums = 0.0
    for index, row in enumerate(rows):
        first, last, row["dkv"], back_sums = project_back(row["x"], w_qkv, tie(row["gq"], *before), row["dkvs"])
        sums = sums + back_sums
        if index == 0:
            kvs = last_row["dkvs"]
            first, last, row["dkv"], kvs[:-1] = hold((first, last, row["dkv"], kvs[:-1]))
            last_row["gq"] = tie(last_row["gq"], row["dkv"])
            grad_q = mm(join("a"), join("gq"), TN).astype(bf16)
            kvs[-1] = tie(kvs[-1], grad_q)
            grad_q = scatter(grad_q)
            outs = []
            for done in rows:
                mine = by_tokens(
                    close_kernel,
                    [done["h"], done["feed"], done["feed_far"], done["live"]],
                    tie(jnp.broadcast_to(down_shift, (8, width)), row["dkv"]),
                    [bf16],
                    "close",
                )[0]
                outs += [mine, near(mine)]
            outs = gather_rows(side_list, outs)
            before = (row["dkv"], kvs[-1], outs)
        else:
            prior = rows[index - 1]
            down_came = over_ctx(tie(grad_down, kvs[-1])) if contexts == 2 else grad_down
            first, last, prior["ga1_far"], down_came = hold((first, last, prior["ga1_far"], down_came))
            before = (row["dkv"],)
        row["ga1"] = sum_near(first, last)
        row["ga1_far"] = far(row["ga1"])
    grad_kv = mm(join("a"), join("dkv"), TN).astype(bf16)
    def sum_over(v, axis):
        size, step = lax.axis_size(axis), 1
        while step < size:
            v = v + lax.ppermute(v, axis, [(i, i ^ step) for i in range(size)])
            step *= 2
        return v

    def owned(v):
        v = v.reshape(owners, -1)
        return jnp.pad(v, ((0, 0), (0, part - v.shape[1]))).reshape(-1)

    feed_sums = sum(row["feed_sums"] for row in rows)
    d_qb = jnp.concatenate([sums[2, :local], sums[3, : 2 * local]]).reshape(3, heads, owners, -1)
    d_qb = owned(jnp.transpose(d_qb, (2, 0, 1, 3)))
    d_ub = feed_sums[0, : fc1_bias.size * owners].reshape(fc1_bias.shape[0], owners, fc1_bias.shape[1])
    d_ub = owned(jnp.transpose(d_ub, (1, 0, 2)))
    vector = jnp.concatenate([pair, feed_sums[1:2, :width], d_qb[None], d_ub[None], sums[0:2]], axis=0)
    vector_one = sum_over(vector, "ctx")
    up_came = over_ctx(tie(grad_up, vector_one)) if contexts == 2 else grad_up
    last_row["ga1_far"], up_came, grad_q, grad_proj = hold((last_row["ga1_far"], up_came, grad_q, grad_proj))
    grad_kv = scatter(grad_kv)
    if contexts == 2:
        grad_up = grad_up.astype(f32) + up_came.astype(f32)
        low = jnp.where(context_first, grad_down, down_came)
        high = jnp.where(context_first, down_came, grad_down)
        grad_down = jnp.concatenate([low, high], axis=0).astype(f32)
    else:
        grad_up, grad_down = finish(up_came), finish(down_came)
    come = over_ctx if contexts == 2 else lambda v: v
    add = (lambda v, w: v.astype(f32) + w.astype(f32)) if contexts == 2 else lambda v, w: finish(v)
    q_came, proj_came, kv_came = come(grad_q), come(grad_proj), come(grad_kv)

    ins = []
    for row in rows:
        mine = by_tokens(
            norm_one_back_kernel,
            [row["x"], row["ga1"], row["ga1_far"], row["gh"]],
            jnp.broadcast_to(gain_one, (8, width)),
            [bf16],
            "norm_one_back",
        )[0]
        if row is last_row:
            mine, q_came, proj_came = hold((mine, q_came, proj_came))
        ins += [mine, near(mine)]

    vector = sum_over(tie(vector_one, ins[0]), "shard")
    vector = lax.dynamic_slice_in_dim(vector, place * part, part, axis=1)
    both = vector + near(vector)
    norm_one = both[6:8] + far(both[6:8])

    ins, kv_came = hold((gather_rows(side_list, ins), kv_came))
    grad_q, grad_proj, grad_kv = add(grad_q, q_came), add(grad_proj, proj_came), add(grad_kv, kv_came)
    return (
        outs,
        ins,
        norm_one[0],
        norm_one[1],
        jnp.concatenate([grad_q, grad_kv], axis=1).reshape(qkv_weight.shape),
        vector[4, :qb_size].reshape(qkv_bias.shape),
        grad_proj.T,
        both[2],
        both[0],
        both[1],
        grad_up,
        vector[5, : fc1_bias.size].reshape(fc1_bias.shape),
        grad_down.T,
        vector[3],
    )


def solution(mesh):
    in_specs = (
        P("shard", "ctx", None),
        P("shard", "ctx", None),
        P("shard", None),
        P(None, "shard", "ctx"),
        P("shard"),
        P("shard"),
        P("shard", None, "tp"),
        P(None, "tp", "shard"),
        P("tp", "shard"),
        P("shard"),
        P("shard"),
        P("shard"),
        P("shard", "tp"),
        P("tp", "shard"),
        P("tp", "shard"),
        P("shard"),
    )
    out_specs = (
        P("shard", "ctx", None),
        P("shard", "ctx", None),
        P("shard"),
        P("shard"),
        P("shard", None, "tp"),
        P(None, "tp", "shard"),
        P("tp", "shard"),
        P("shard"),
        P("shard"),
        P("shard"),
        P("shard", "tp"),
        P("tp", "shard"),
        P("tp", "shard"),
        P("shard"),
    )
    return jax.shard_map(
        on_device, mesh=mesh, in_specs=in_specs, out_specs=out_specs, check_vma=False
    )
```

```python
import functools
import math

import jax
import jax.numpy as jnp
from jax import lax
from jax.experimental import pallas as pl
from jax.experimental.pallas import tpu as pltpu
from jax.sharding import PartitionSpec as P

HEAD_DIM = 80
LANES = 128
norm_eps = 1e-06
hide = 1e30
floor_max = -1e29
log2e = math.log2(math.e)
bf16 = jnp.bfloat16
f32 = jnp.float32
NT = (((1,), (1,)), ((), ()))
NN = (((1,), (0,)), ((), ()))
TN = (((0,), (0,)), ((), ()))


def mm(a, b, dims=NN):
    return lax.dot_general(a, b, dims, preferred_element_type=f32)


def tie(value, *others):
    return lax.optimization_barrier((value,) + others)[0]


def first_blocks(steps):
    return lambda i, *_: (jnp.minimum(i, steps // 2 - 1), 0)


def last_blocks(steps):
    return lambda i, *_: (jnp.maximum(i - steps // 2, 0), 0)


def store_halves(first_ref, last_ref, value):
    step, split = pl.program_id(0), pl.num_programs(0) // 2

    @pl.when(step < split)
    def first():
        first_ref[...] = value

    @pl.when(step >= split)
    def last():
        last_ref[...] = value


def lane_index(rows):
    return lax.broadcasted_iota(jnp.int32, (rows, LANES), 1)


def swap_halves(w, lane):
    half = HEAD_DIM // 2
    up = pltpu.roll(w, LANES - half, 1)
    down = pltpu.roll(w, half, 1)
    return jnp.where(lane < half, up, down)


def widen(piece):
    rows = piece.shape[0]
    tail = jnp.zeros((rows, LANES - piece.shape[1]), piece.dtype)
    return jnp.concatenate([piece, tail], axis=1)


def split_three(column):
    high = column.astype(bf16).astype(f32)
    rest = column - high
    mid = rest.astype(bf16).astype(f32)
    return high, mid, rest - mid


def place_three(base, column, lane):
    high, mid, low = split_three(column)
    base = jnp.where(lane == 96, high, base)
    base = jnp.where(lane == 97, mid, base)
    return jnp.where(lane == 98, low, base)


def qkv_kernel(heads, x_ref, w_ref, ln_ref, b_ref, cos_ref, sin_ref, feat_ref, a_ref, q_ref, kv_ref):
    width = heads * HEAD_DIM
    x = x_ref[...].astype(f32)
    rows = x.shape[0]
    center = x - jnp.mean(x, axis=1, keepdims=True)
    inverse = lax.rsqrt(jnp.mean(center * center, axis=1, keepdims=True) + norm_eps)
    a = (center * inverse * ln_ref[0:1, :] + ln_ref[1:2, :]).astype(bf16)
    a_ref[...] = a
    y = mm(a, w_ref[...]) + b_ref[0:1, :]
    cos, sin = cos_ref[...], sin_ref[...]
    lane = lane_index(rows)
    kv = []
    for h in range(heads):
        w = widen(y[:, h * HEAD_DIM : (h + 1) * HEAD_DIM])
        q = (w * cos + swap_halves(w, lane) * sin) * (HEAD_DIM**-0.5 * log2e)
        q_ref[h] = jnp.where(lane < HEAD_DIM, q.astype(bf16), feat_ref[...])
    for h in range(heads):
        begin = width + h * HEAD_DIM
        w = widen(y[:, begin : begin + HEAD_DIM])
        kv.append((w * cos + swap_halves(w, lane) * sin)[:, :HEAD_DIM].astype(bf16))
    kv.append(y[:, 2 * width : 3 * width].astype(bf16))
    kv_ref[...] = jnp.concatenate(kv, axis=1)


def project_row(x, w, ln, bias, cos, sin, feat, heads):
    rows, width = x.shape
    block = min(256, rows)
    wide = w.shape[1]
    local = heads * HEAD_DIM
    by_rows = lambda n: pl.BlockSpec((block, n), lambda i: (i, 0))
    whole = lambda a: pl.BlockSpec(a.shape, lambda i: (0,) * a.ndim)
    return pl.pallas_call(
        functools.partial(qkv_kernel, heads),
        grid=(rows // block,),
        in_specs=[
            by_rows(width),
            whole(w),
            whole(ln),
            whole(bias),
            by_rows(LANES),
            by_rows(LANES),
            by_rows(LANES),
        ],
        out_specs=[
            by_rows(width),
            pl.BlockSpec((heads, block, LANES), lambda i: (0, i, 0)),
            by_rows(2 * local),
        ],
        out_shape=[
            jax.ShapeDtypeStruct((rows, width), bf16),
            jax.ShapeDtypeStruct((heads, rows, LANES), bf16),
            jax.ShapeDtypeStruct((rows, 2 * local), bf16),
        ],
        cost_estimate=pl.CostEstimate(
            flops=2 * rows * width * wide, bytes_accessed=rows * width * 4 + width * wide * 2, transcendentals=0
        ),
        name="project_row",
    )(x, w, ln, bias, cos, sin, feat)


def forward_kernel(heads, segments, block, flag_ref, q_ref, w_ref, *refs):
    kv_refs = refs[:segments]
    feat_refs = refs[segments : 2 * segments]
    o_ref, q_out, k_aug, v_aug, p_first, p_last, m_scr, acc_scr = refs[2 * segments :]
    width = heads * HEAD_DIM
    step = pl.program_id(0)
    keys = k_aug.shape[1]
    count = keys // block
    rows = q_ref.shape[1]

    @pl.when(step == 0)
    def build():
        offset = 0
        for s in range(segments):
            length = kv_refs[s].shape[0]
            piece = min(length, 256)
            for t in range(length // piece):
                at = pl.ds(t * piece, piece)
                to = pl.ds(offset + t * piece, piece)
                kv = kv_refs[s][at, :]
                feat = feat_refs[s][at, :]
                lane = lane_index(piece)
                tail = jnp.where(lane == HEAD_DIM, 1.0, jnp.where((lane >= 96) & (lane < 99), -1.0, 0.0)).astype(bf16)
                for h in range(heads):
                    k = kv[:, h * HEAD_DIM : (h + 1) * HEAD_DIM]
                    v = kv[:, width + h * HEAD_DIM : width + (h + 1) * HEAD_DIM]
                    k_aug[h, to, :] = jnp.concatenate([k, feat[:, HEAD_DIM:]], axis=1)
                    v_aug[h, to, :] = jnp.concatenate([v, tail[:, HEAD_DIM:]], axis=1)
            offset += length

    m_scr[...] = jnp.full(m_scr.shape, floor_max, f32)
    acc_scr[...] = jnp.zeros(acc_scr.shape, f32)

    def visit(j, carry):
        @pl.when(flag_ref[step * count + j] > 0)
        def go():
            at = pl.ds(pl.multiple_of(j * block, block), block)
            for h in range(heads):
                s = mm(q_ref[h], k_aug[h, at, :], NT)
                old = m_scr[h]
                cuts = [s[:, c : c + LANES] for c in range(0, block, LANES)]
                top = functools.reduce(jnp.maximum, cuts)
                new = jnp.maximum(old, jnp.max(top, axis=1, keepdims=True))
                p = jnp.concatenate([jnp.exp2(cut - new) for cut in cuts], axis=1)
                m_scr[h] = new
                acc_scr[h] = acc_scr[h] * jnp.exp2(old - new) + mm(p.astype(bf16), v_aug[h, at, :])

        return carry

    lax.fori_loop(0, count, visit, 0)
    lane = lane_index(rows)
    outs = []
    for h in range(heads):
        acc = acc_scr[h]
        total = acc[:, HEAD_DIM : HEAD_DIM + 1]
        alive = total > 0.0
        safe = jnp.where(alive, total, 1.0)
        outs.append((acc / safe)[:, :HEAD_DIM].astype(bf16))
        level = jnp.where(alive, m_scr[h][:, 0:1] + jnp.log2(safe), 0.0)
        q_out[h] = place_three(q_ref[h].astype(f32), level, lane).astype(bf16)
    o = jnp.concatenate(outs, axis=1)
    o_ref[...] = o
    store_halves(p_first, p_last, mm(o, w_ref[...], NT).astype(bf16))


def attend_forward(flags, q_aug, w, kvs, feats, heads, block):
    rows = q_aug.shape[1]
    tall = min(256, rows // 2)
    steps = rows // tall
    width = w.shape[0]
    keys = sum(kv.shape[0] for kv in kvs)
    segments = len(kvs)
    whole = lambda a: pl.BlockSpec(a.shape, lambda i, f: (0,) * a.ndim)
    q_spec = pl.BlockSpec((heads, tall, LANES), lambda i, f: (0, i, 0))
    k_spec = pl.BlockSpec((heads, keys, LANES), lambda i, f: (0, 0, 0))
    local = heads * HEAD_DIM
    return pl.pallas_call(
        functools.partial(forward_kernel, heads, segments, block),
        grid_spec=pltpu.PrefetchScalarGridSpec(
            num_scalar_prefetch=1,
            grid=(rows // tall,),
            in_specs=[q_spec, whole(w)] + [whole(kv) for kv in kvs] + [whole(f) for f in feats],
            out_specs=[
                pl.BlockSpec((tall, local), lambda i, f: (i, 0)),
                q_spec,
                k_spec,
                k_spec,
                pl.BlockSpec((tall, width), first_blocks(steps)),
                pl.BlockSpec((tall, width), last_blocks(steps)),
            ],
            scratch_shapes=[
                pltpu.VMEM((heads, tall, LANES), f32),
                pltpu.VMEM((heads, tall, LANES), f32),
            ],
        ),
        out_shape=[
            jax.ShapeDtypeStruct((rows, local), bf16),
            jax.ShapeDtypeStruct((heads, rows, LANES), bf16),
            jax.ShapeDtypeStruct((heads, keys, LANES), bf16),
            jax.ShapeDtypeStruct((heads, keys, LANES), bf16),
            jax.ShapeDtypeStruct((rows // 2, width), bf16),
            jax.ShapeDtypeStruct((rows // 2, width), bf16),
        ],
        cost_estimate=pl.CostEstimate(
            flops=2 * rows * keys * heads * LANES, bytes_accessed=8 * keys * local, transcendentals=rows * keys * heads // 2
        ),
        name="attend_forward",
    )(flags, q_aug, w, *kvs, *feats)


def backward_kernel(
    heads, segments, block, flag_ref, q_ref, ga_first, ga_last, w_ref, o_ref, k_aug, v_aug, cosq_ref, sinq_ref, *refs
):
    cosk_refs = refs[:segments]
    sink_refs = refs[segments : 2 * segments]
    dq_ref = refs[2 * segments]
    dkv_refs = refs[2 * segments + 1 : 3 * segments + 1]
    k_turn, dk_acc, dv_acc, dq_acc, go_scr = refs[3 * segments + 1 :]
    step = pl.program_id(0)
    keys = k_aug.shape[1]
    count = keys // block
    rows = q_ref.shape[1]
    scale = HEAD_DIM**-0.5

    @pl.when(step == 0)
    def build():
        dk_acc[...] = jnp.zeros(dk_acc.shape, f32)
        dv_acc[...] = jnp.zeros(dv_acc.shape, f32)
        for h in range(heads):
            for t in range(count):
                at = pl.ds(t * block, block)
                k_turn[h, :, at] = k_aug[h, at, :].T

    lane = lane_index(rows)
    ga = jnp.where(step < pl.num_programs(0) // 2, ga_first[...], ga_last[...])
    go_all = mm(ga, w_ref[...]).astype(bf16).astype(f32)
    for h in range(heads):
        cut = slice(h * HEAD_DIM, (h + 1) * HEAD_DIM)
        go = go_all[:, cut]
        delta = jnp.sum(go * o_ref[:, cut].astype(f32), axis=1, keepdims=True)
        go_scr[h] = place_three(widen(go), delta, lane).astype(bf16)
    dq_acc[...] = jnp.zeros(dq_acc.shape, f32)

    def visit(j, carry):
        @pl.when(flag_ref[step * count + j] > 0)
        def run():
            at = pl.ds(pl.multiple_of(j * block, block), block)
            for h in range(heads):
                q, go = q_ref[h], go_scr[h]
                p = jnp.exp2(mm(k_aug[h, at, :], q, NT))
                ds = (p * mm(v_aug[h, at, :], go, NT)).astype(bf16)
                dv_acc[h, at, :] += mm(p.astype(bf16), go)
                dk_acc[h, at, :] += mm(ds, q)
                dq_acc[h] += mm(k_turn[h, :, at], ds)

        return carry

    lax.fori_loop(0, count, visit, 0)

    def turn_back(w, cos, sin, index):
        return w * cos - swap_halves(w, index) * sin

    outs = []
    for h in range(heads):
        w = dq_acc[h].T
        back = turn_back(w, cosq_ref[...], sinq_ref[...], lane) * scale
        outs.append(back[:, :HEAD_DIM].astype(bf16))
    dq_ref[...] = jnp.concatenate(outs, axis=1)

    @pl.when(step == pl.num_programs(0) - 1)
    def finish():
        offset = 0
        for s in range(segments):
            length = dkv_refs[s].shape[0]
            piece = min(length, 256)
            index = lane_index(piece)
            for t in range(length // piece):
                at = pl.ds(t * piece, piece)
                of = pl.ds(offset + t * piece, piece)
                parts = []
                for h in range(heads):
                    w = dk_acc[h, of, :]
                    back = turn_back(w, cosk_refs[s][at, :], sink_refs[s][at, :], index) * (1.0 / log2e)
                    parts.append(back[:, :HEAD_DIM].astype(bf16))
                for h in range(heads):
                    parts.append(dv_acc[h, of, :][:, :HEAD_DIM].astype(bf16))
                dkv_refs[s][at, :] = jnp.concatenate(parts, axis=1)
            offset += length


def attend_backward(flags, q_aug, ga, w, o, k_aug, v_aug, cos_q, sin_q, cos_k, sin_k, heads, block):
    rows = q_aug.shape[1]
    tall = min(256, rows // 2)
    steps = rows // tall
    width = w.shape[0]
    keys = k_aug.shape[1]
    segments = len(cos_k)
    local = heads * HEAD_DIM
    whole = lambda a: pl.BlockSpec(a.shape, lambda i, f: (0,) * a.ndim)
    by_rows = lambda n: pl.BlockSpec((tall, n), lambda i, f: (i, 0))
    q_spec = pl.BlockSpec((heads, tall, LANES), lambda i, f: (0, i, 0))
    return pl.pallas_call(
        functools.partial(backward_kernel, heads, segments, block),
        grid_spec=pltpu.PrefetchScalarGridSpec(
            num_scalar_prefetch=1,
            grid=(rows // tall,),
            in_specs=[
                q_spec,
                pl.BlockSpec((tall, width), first_blocks(steps)),
                pl.BlockSpec((tall, width), last_blocks(steps)),
                whole(w),
                by_rows(local),
                whole(k_aug),
                whole(v_aug),
                by_rows(LANES),
                by_rows(LANES),
            ]
            + [whole(t) for t in cos_k]
            + [whole(t) for t in sin_k],
            out_specs=[by_rows(local)]
            + [pl.BlockSpec((t.shape[0], 2 * local), lambda i, f: (0, 0)) for t in cos_k],
            scratch_shapes=[
                pltpu.VMEM((heads, LANES, keys), bf16),
                pltpu.VMEM((heads, keys, LANES), f32),
                pltpu.VMEM((heads, keys, LANES), f32),
                pltpu.VMEM((heads, LANES, tall), f32),
                pltpu.VMEM((heads, tall, LANES), bf16),
            ],
        ),
        out_shape=[jax.ShapeDtypeStruct((rows, local), bf16)]
        + [jax.ShapeDtypeStruct((t.shape[0], 2 * local), bf16) for t in cos_k],
        cost_estimate=pl.CostEstimate(
            flops=5 * rows * keys * heads * LANES, bytes_accessed=16 * keys * local, transcendentals=rows * keys * heads // 2
        ),
        name="attend_backward",
    )(flags, q_aug, *ga, w, o, k_aug, v_aug, cos_q, sin_q, *cos_k, *sin_k)


def feed_kernel(chunk, c_first, c_last, g_ref, up_ref, down_ref, shift_ref, z_ref, gu_ref, gc_first, gc_last, feed_first, feed_last, sum_ref):
    step = pl.program_id(0)
    c = jnp.where(step < pl.num_programs(0) // 2, c_first[...], c_last[...])
    g = g_ref[...]
    sums = []
    for begin in range(0, up_ref.shape[1], chunk):
        cut = slice(begin, begin + chunk)
        u = mm(c, up_ref[:, cut]) + shift_ref[0:1, cut]
        sg = 0.5 + 0.5 * jnp.tanh(0.851 * u)
        z = (u * sg).astype(bf16)
        gu = (mm(g, down_ref[:, cut]) * (sg + 1.702 * u * sg * (1.0 - sg))).astype(bf16)
        z_ref[:, cut] = z
        gu_ref[:, cut] = gu
        sums.append(jnp.sum(gu.astype(f32), axis=0, keepdims=True))
    store_halves(gc_first, gc_last, mm(gu_ref[...], up_ref[...], NT).astype(bf16))
    store_halves(feed_first, feed_last, mm(z_ref[...], down_ref[...], NT).astype(bf16))

    @pl.when(step == 0)
    def clear():
        sum_ref[...] = jnp.zeros(sum_ref.shape, f32)

    sum_ref[0:1, :] += jnp.concatenate(sums, axis=1)
    sum_ref[1:2, : g.shape[1]] += jnp.sum(g.astype(f32), axis=0, keepdims=True)


def feed_forward(c, g, w_up, w_down, shift):
    rows, width = g.shape
    hidden = w_up.shape[1]
    tall = min(256, rows // 2)
    steps = rows // tall
    chunk = 256 if hidden % 256 == 0 else hidden
    by_rows = lambda n: pl.BlockSpec((tall, n), lambda i: (i, 0))
    whole = lambda a: pl.BlockSpec(a.shape, lambda i: (0,) * a.ndim)
    first = pl.BlockSpec((tall, width), first_blocks(steps))
    last = pl.BlockSpec((tall, width), last_blocks(steps))
    part = jax.ShapeDtypeStruct((rows // 2, width), bf16)
    longest = max(width, hidden)
    return pl.pallas_call(
        functools.partial(feed_kernel, chunk),
        grid=(steps,),
        in_specs=[first, last, by_rows(width), whole(w_up), whole(w_down), whole(shift)],
        out_specs=[by_rows(hidden), by_rows(hidden), first, last, first, last, pl.BlockSpec((8, longest), lambda i: (0, 0))],
        out_shape=[
            jax.ShapeDtypeStruct((rows, hidden), bf16),
            jax.ShapeDtypeStruct((rows, hidden), bf16),
            part,
            part,
            part,
            part,
            jax.ShapeDtypeStruct((8, longest), f32),
        ],
        cost_estimate=pl.CostEstimate(
            flops=8 * rows * width * hidden, bytes_accessed=4 * width * hidden + 12 * rows * width, transcendentals=rows * hidden
        ),
        name="feed_forward",
    )(*c, g, w_up, w_down, shift)


def back_kernel(pieces, x_ref, w_ref, gq_ref, *refs):
    kv_refs = refs[:pieces]
    p_first, p_last, dkv_ref, sum_ref = refs[pieces:]
    gq = gq_ref[...]
    if pieces == 1:
        dkv = kv_refs[0][...]
    else:
        other = jnp.where(pl.program_id(0) < pl.num_programs(0) // 2, kv_refs[1][...], kv_refs[2][...])
        dkv = (kv_refs[0][...].astype(f32) + other.astype(f32)).astype(bf16)
    dkv_ref[...] = dkv
    tail = jnp.zeros((gq.shape[0], w_ref.shape[1] - gq.shape[1] - dkv.shape[1]), bf16)
    e = mm(jnp.concatenate([gq, dkv, tail], axis=1), w_ref[...], NT)
    store_halves(p_first, p_last, e.astype(bf16))
    x = x_ref[...].astype(f32)
    center = x - jnp.mean(x, axis=1, keepdims=True)
    unit = center * lax.rsqrt(jnp.mean(center * center, axis=1, keepdims=True) + norm_eps)

    @pl.when(pl.program_id(0) == 0)
    def clear():
        sum_ref[...] = jnp.zeros(sum_ref.shape, f32)

    local = gq.shape[1]
    sum_ref[0:1, :] += jnp.sum(e * unit, axis=0, keepdims=True)
    sum_ref[1:2, :] += jnp.sum(e, axis=0, keepdims=True)
    sum_ref[2:3, :local] += jnp.sum(gq.astype(f32), axis=0, keepdims=True)
    sum_ref[3:4, : 2 * local] += jnp.sum(dkv.astype(f32), axis=0, keepdims=True)


def project_back(x, w, gq, dkvs):
    rows, width = x.shape
    local = gq.shape[1]
    tall = min(512, rows // 2)
    steps = rows // tall
    by_rows = lambda n: pl.BlockSpec((tall, n), lambda i: (i, 0))
    whole = lambda a: pl.BlockSpec(a.shape, lambda i: (0,) * a.ndim)
    part = jax.ShapeDtypeStruct((rows // 2, width), bf16)
    kv_specs = [
        by_rows(2 * local),
        pl.BlockSpec((tall, 2 * local), first_blocks(steps)),
        pl.BlockSpec((tall, 2 * local), last_blocks(steps)),
    ]
    return pl.pallas_call(
        functools.partial(back_kernel, len(dkvs)),
        grid=(steps,),
        in_specs=[by_rows(width), whole(w), by_rows(local)] + kv_specs[: len(dkvs)],
        out_specs=[
            pl.BlockSpec((tall, width), first_blocks(steps)),
            pl.BlockSpec((tall, width), last_blocks(steps)),
            by_rows(2 * local),
            pl.BlockSpec((8, width), lambda i: (0, 0)),
        ],
        out_shape=[part, part, jax.ShapeDtypeStruct((rows, 2 * local), bf16), jax.ShapeDtypeStruct((8, width), f32)],
        cost_estimate=pl.CostEstimate(
            flops=6 * rows * width * local, bytes_accessed=6 * width * local + 6 * rows * width, transcendentals=rows
        ),
        name="project_back",
    )(x, w, gq, *dkvs)


def norm_stats(rows_in):
    center = rows_in - jnp.mean(rows_in, axis=1, keepdims=True)
    inverse = lax.rsqrt(jnp.mean(center * center, axis=1, keepdims=True) + norm_eps)
    return center * inverse, inverse


def norm_backward(grad_rows, unit_rows, inverse, gain):
    scaled = grad_rows * gain
    return inverse * (
        scaled
        - jnp.mean(scaled, axis=1, keepdims=True)
        - unit_rows * jnp.mean(scaled * unit_rows, axis=1, keepdims=True)
    )


def norm_two_kernel(x_ref, near_ref, far_ref, vec_ref, h_ref, c_ref):
    h = x_ref[...].astype(f32) + (near_ref[...].astype(f32) + far_ref[...].astype(f32)) + vec_ref[0:1, :]
    h_ref[...] = h
    c_ref[...] = (norm_stats(h)[0] * vec_ref[1:2, :] + vec_ref[2:3, :]).astype(bf16)


def norm_two_back_kernel(h_ref, near_ref, far_ref, g_ref, vec_ref, gh_ref, ga_ref, sum_ref):
    unit, inverse = norm_stats(h_ref[...])
    gc = near_ref[...].astype(f32) + far_ref[...].astype(f32)
    gh = g_ref[...].astype(f32) + norm_backward(gc, unit, inverse, vec_ref[1:2, :])
    ga = gh.astype(bf16)
    gh_ref[...] = gh
    ga_ref[...] = ga

    @pl.when(pl.program_id(0) == 0)
    def clear():
        sum_ref[...] = jnp.zeros(sum_ref.shape, f32)

    sum_ref[0:1, :] += jnp.sum(gc * unit, axis=0, keepdims=True)
    sum_ref[1:2, :] += jnp.sum(gc, axis=0, keepdims=True)
    sum_ref[2:3, :] += jnp.sum(ga.astype(f32), axis=0, keepdims=True)


def norm_one_back_kernel(x_ref, near_ref, far_ref, gh_ref, vec_ref, out_ref):
    unit, inverse = norm_stats(x_ref[...].astype(f32))
    ga1 = near_ref[...].astype(f32) + far_ref[...].astype(f32)
    out_ref[...] = (gh_ref[...] + norm_backward(ga1, unit, inverse, vec_ref[0:1, :])).astype(bf16)


def close_kernel(h_ref, near_ref, far_ref, live_ref, vec_ref, out_ref):
    feed = near_ref[...].astype(f32) + far_ref[...].astype(f32)
    out_ref[...] = ((h_ref[...] + feed + vec_ref[0:1, :]) * live_ref[...]).astype(bf16)


def by_tokens(body, arrays, vectors, kinds, name, sums=False):
    count, width = arrays[1].shape
    tall = min(256, count)
    in_specs = [pl.BlockSpec((tall, a.shape[1]), lambda i: (i, 0)) for a in arrays]
    out_specs = [pl.BlockSpec((tall, width), lambda i: (i, 0)) for _ in kinds]
    out_shape = [jax.ShapeDtypeStruct((count, width), kind) for kind in kinds]
    if sums:
        out_specs.append(pl.BlockSpec((8, width), lambda i: (0, 0)))
        out_shape.append(jax.ShapeDtypeStruct((8, width), f32))
    return pl.pallas_call(
        body,
        grid=(count // tall,),
        in_specs=in_specs + [pl.BlockSpec(vectors.shape, lambda i: (0, 0))],
        out_specs=out_specs,
        out_shape=out_shape,
        cost_estimate=pl.CostEstimate(flops=20 * count * width, bytes_accessed=14 * count * width, transcendentals=count),
        name=name,
    )(*arrays, vectors)


def gather_rows_kernel(side_ref, *refs):
    step = pl.program_id(0)
    for index, piece in enumerate(refs[:-1]):

        @pl.when(step == index)
        def copy(piece=piece):
            refs[-1][0] = piece[...]


def gather_rows(side, pieces):
    half, width = pieces[0].shape
    count = len(pieces)
    return pl.pallas_call(
        gather_rows_kernel,
        grid_spec=pltpu.PrefetchScalarGridSpec(
            num_scalar_prefetch=1,
            grid=(count,),
            in_specs=[pl.BlockSpec((half, width), lambda t, s: (0, 0)) for _ in pieces],
            out_specs=pl.BlockSpec((1, half, width), lambda t, s: (t // 2, jnp.where(t % 2 == 0, s[0], 1 - s[0]), 0)),
        ),
        out_shape=jax.ShapeDtypeStruct((count // 2, 2 * half, width), bf16),
        cost_estimate=pl.CostEstimate(flops=0, bytes_accessed=4 * count * half * width, transcendentals=0),
        name="gather_rows",
    )(side, *pieces)


def tables(grid_pos):
    lane = jnp.arange(LANES)
    quarter = HEAD_DIM // 4
    frequency = jnp.power(10000.0, -4.0 * (lane % quarter).astype(f32) / HEAD_DIM)
    place = jnp.where((lane // quarter) % 2 == 0, grid_pos[0][:, None], grid_pos[1][:, None])
    angle = jnp.where(lane < HEAD_DIM, place.astype(f32) * frequency, 0.0)
    return jnp.cos(angle), jnp.where(lane < HEAD_DIM // 2, -1.0, 1.0) * jnp.sin(angle)


def query_features(ids):
    lane = jnp.arange(LANES)
    return (lane == HEAD_DIM + 1 + ids[:, None]).astype(bf16)


def key_features(ids):
    lane = jnp.arange(LANES)
    slot = lane - HEAD_DIM
    same = (slot >= 1) & (slot == ids[:, None] + 1)
    wall = jnp.where((slot >= 0) & (slot < 16) & ~same, -hide, 0.0)
    return jnp.where((lane >= 96) & (lane < 99), -1.0, wall).astype(bf16)


def visit_flags(query_ids, key_ids, tall, block):
    q = query_ids.reshape(-1, tall)
    k = key_ids.reshape(-1, block)
    q_top, k_top = jnp.max(q, axis=1), jnp.max(k, axis=1)
    q_low = jnp.min(jnp.where(q >= 0, q, 1 << 20), axis=1)
    k_low = jnp.min(jnp.where(k >= 0, k, 1 << 20), axis=1)
    meet = (q_low[:, None] <= k_top[None, :]) & (k_low[None, :] <= q_top[:, None])
    return meet.astype(jnp.int32).reshape(-1)


def on_device(
    patches,
    cotangent,
    picture_ids,
    positions,
    ln1_gain,
    ln1_bias,
    qkv_weight,
    qkv_bias,
    proj_weight,
    proj_bias,
    ln2_gain,
    ln2_bias,
    fc1_weight,
    fc1_bias,
    fc2_weight,
    fc2_bias,
):
    row_count, row_share, width = patches.shape
    owners = lax.axis_size("shard")
    contexts = lax.axis_size("ctx")
    ways = lax.axis_size("tp")
    part = qkv_weight.shape[0]
    local = qkv_weight.shape[2]
    heads = local // HEAD_DIM
    half = row_share // 2
    side = lax.axis_index("tp") % 2
    context = lax.axis_index("ctx")
    pairs_near = [(i, i ^ 1) for i in range(ways)]
    pairs_far = [(i, i ^ 2) for i in range(ways)]
    pad = -3 * local % 256
    wide = 3 * local + pad

    def near(v):
        return lax.ppermute(v, "tp", pairs_near)

    def far(v):
        return lax.ppermute(v, "tp", pairs_far)

    def over_ctx(v):
        return lax.ppermute(v, "ctx", [(0, 1), (1, 0)])

    def mine_first(v, axis=0):
        return jnp.where(side == 0, v, jnp.roll(v, half, axis=axis))

    def column(v):
        flat = v.reshape(-1)
        return jnp.pad(flat, (0, part - flat.shape[0]))

    vectors = [ln1_gain, ln1_bias, ln2_gain, ln2_bias, proj_bias, fc2_bias, qkv_bias, fc1_bias]
    place = lax.axis_index("shard")
    context_first = context == 0

    def rotate_gather(piece):
        whole = lax.dynamic_update_index_in_dim(jnp.zeros((owners,) + piece.shape, piece.dtype), piece, place, 0)
        for step in range(1, owners):
            got = lax.ppermute(piece, "shard", [(i, (i + step) % owners) for i in range(owners)])
            whole = lax.dynamic_update_index_in_dim(whole, got, (place - step) % owners, 0)
        return whole

    tail = rotate_gather(jnp.stack([column(v) for v in vectors]).astype(bf16))
    packed = jnp.transpose(tail, (1, 0, 2)).reshape(len(vectors), width).astype(f32)
    qkv_piece = jnp.pad(qkv_weight.reshape(part, 3 * local), ((0, 0), (0, pad))).astype(bf16)
    gather = lambda v: lax.all_gather(v, "shard", axis=0, tiled=True)
    up_piece = fc1_weight.astype(bf16)
    down_piece = fc2_weight.T.astype(bf16)
    w_qkv = gather(qkv_piece)
    w_proj = rotate_gather(tie(proj_weight.T.astype(bf16), w_qkv)).reshape(owners * part, local)
    gain_one, bias_one, gain_two, bias_two, proj_shift, down_shift = [packed[i] for i in range(6)]
    qb_size = qkv_bias.size
    qkv_shift = packed[6].reshape(owners, part)[:, :qb_size].reshape((owners,) + qkv_bias.shape)
    qkv_shift = jnp.transpose(qkv_shift, (1, 2, 0, 3)).reshape(-1)
    qkv_shift = jnp.pad(qkv_shift, (0, pad)).reshape(1, wide)
    up_shift = packed[7].reshape(owners, part)[:, : fc1_bias.size].reshape((owners,) + fc1_bias.shape)
    up_shift = jnp.transpose(up_shift, (1, 0, 2)).reshape(1, -1)
    ln_one = tie(packed[0:2], up_piece, down_piece)

    ids_by_ctx = mine_first(picture_ids.reshape(row_count, contexts, row_share), axis=2)
    places = mine_first(positions, axis=2)
    block = min(256, half)

    def cut_last(spots):
        return [spots[0], spots[1][:half], spots[1][half:]] if contexts == 2 else spots

    key_block = 256
    rows = []
    for r in range(row_count):
        x = mine_first(patches[r])
        g = mine_first(cotangent[r])
        ids = lax.dynamic_index_in_dim(ids_by_ctx[r], context, 0, keepdims=False)
        if contexts == 2:
            other = lax.dynamic_index_in_dim(ids_by_ctx[r], 1 - context, 0, keepdims=False)
            key_ids = [ids, other]
            spots = [places[:, r], over_ctx(places[:, r])]
        else:
            key_ids = [ids_by_ctx[r].reshape(-1)]
            spots = [lax.all_gather(places[:, r], "ctx", axis=1, tiled=True)]
        live = (ids >= 0).astype(f32)[:, None]
        turns = [tables(spot) for spot in spots]
        own_turn = turns[0] if contexts == 2 else tables(places[:, r])
        rows.append(
            dict(
                x=x,
                g=(g.astype(f32) * live).astype(bf16),
                live=live,
                ids=ids,
                cos=own_turn[0],
                sin=own_turn[1],
                cos_k=cut_last([t[0] for t in turns]),
                sin_k=cut_last([t[1] for t in turns]),
                q_feat=query_features(ids),
                k_feat=[key_features(k) for k in key_ids],
                flags=visit_flags(ids, jnp.concatenate(key_ids), block, key_block),
            )
        )

    ln_one = tie(ln_one, qkv_shift, up_shift, *[row["g"] for row in rows])

    for index, row in enumerate(rows):
        row["a"], row["q"], row["kv"] = project_row(
            row["x"], w_qkv, ln_one, qkv_shift, row["cos"], row["sin"], row["q_feat"], heads
        )
        if index == 1:
            row["kv"], w_proj = lax.optimization_barrier((row["kv"], w_proj))
        if contexts == 2:
            row["kvs"] = [row["kv"], over_ctx(tie(row["kv"], *[(r["kvs"][1], r["k_feat"], r["flags"]) for r in rows[:index]]))]
        else:
            row["kvs"] = [lax.all_gather(row["kv"], "ctx", axis=0, tiled=True)]

    down_piece, up_piece = lax.optimization_barrier(
        (down_piece, up_piece, w_qkv, ln_one, [(row["x"], row["cos"], row["sin"], row["cos_k"], row["sin_k"]) for row in rows])
    )[:2]
    if contexts == 2:
        down_cut = down_piece.reshape(2, part // 2, -1)
        down_near = gather(lax.dynamic_index_in_dim(down_cut, context, 0, keepdims=False))
        down_near = down_near.reshape(owners, part // 2, -1)
    else:
        w_down = gather(down_piece)
    w_up = gather(up_piece)

    def sum_near(first, last):
        return (first.astype(f32) + near(last).astype(f32)).astype(bf16)

    norm_vectors = jnp.pad(jnp.stack([proj_shift, gain_two, bias_two]), ((0, 5), (0, 0)))

    def norm_two(row, vectors):
        row["h"], mine = by_tokens(
            norm_two_kernel, [row["x"], row["branch"], row["branch_far"]], vectors, [f32, bf16], "norm_two"
        )
        row["c"] = (mine, near(mine))

    hold = lax.optimization_barrier
    before = rows[-1]["kv"]
    for index, row in enumerate(rows):
        row["o"], row["q"], row["k_aug"], row["v_aug"], first, last = attend_forward(
            tie(row["flags"], before), row["q"], w_proj, row["kvs"], row["k_feat"], heads, key_block
        )
        if index:
            prior = rows[index - 1]
            first, last, prior["branch_far"] = hold((first, last, prior["branch_far"]))
        if index + 1 < row_count:
            follow = rows[index + 1]
            first, last, follow["kvs"] = hold((first, last, follow["kvs"]))
            if contexts == 2:
                first, last, down_near = hold((first, last, down_near))
                down_far = over_ctx(down_near)
        elif contexts == 2:
            first, last, down_far, w_up = hold((first, last, down_far, w_up))
        before = row["branch"] = sum_near(first, last)
        row["branch_far"] = far(before)
    if contexts == 2:
        low = jnp.where(context_first, down_near, down_far)
        high = jnp.where(context_first, down_far, down_near)
        w_down = jnp.concatenate([low, high], axis=1).reshape(owners * part, -1)

    norm_two(rows[0], tie(norm_vectors, before))
    for index, row in enumerate(rows):
        shift = tie(up_shift, before)
        row["z"], row["gu"], gc_first, gc_last, feed_first, feed_last, row["feed_sums"] = feed_forward(
            row["c"], row["g"], w_up, w_down, shift
        )
        other, key = (rows[-1], "branch_far") if index == 0 else (rows[index - 1], "gc_far")
        gc_first, gc_last, other[key] = hold((gc_first, gc_last, other[key]))
        before = row["gc"] = sum_near(gc_first, gc_last)
        row["gc_far"] = far(before)
        row["feed"] = (feed_first, feed_last)
        if index + 1 < row_count:
            norm_two(rows[index + 1], norm_vectors)
    for row in rows:
        row["feed"] = sum_near(*row["feed"])

    join = lambda key: jnp.concatenate([row[key] for row in rows], axis=0)
    join_two = lambda key: jnp.concatenate([piece for row in rows for piece in row[key]], axis=0)
    scatter = lambda v: lax.psum_scatter(v, "shard", scatter_dimension=0, tiled=True)
    if contexts == 2:
        finish = lambda v: v.astype(f32) + over_ctx(v).astype(f32)
    else:
        finish = lambda v: lax.psum(v, "ctx").astype(f32)
    last_row = rows[-1]

    def norm_two_back(row):
        row["gh"], ga, norm_sums = by_tokens(
            norm_two_back_kernel,
            [row["h"], row["gc"], row["gc_far"], row["g"]],
            norm_vectors,
            [f32, bf16],
            "norm_two_back",
            sums=True,
        )
        row["ga"] = (ga, near(ga))
        return norm_sums[0:3]

    pair = sum(norm_two_back(row) for row in rows[:-1])
    last_row["gu"], last_row["z"] = hold((last_row["gu"], last_row["z"], before, *[row["ga"][0] for row in rows[:-1]]))[:2]
    grad_up = mm(join_two("c"), join("gu"), TN).astype(bf16)
    grad_down = mm(join("g"), join("z"), TN).astype(bf16)
    grad_up, grad_down, last_row["gc_far"] = hold((grad_up, grad_down, last_row["gc_far"]))
    pair = pair + norm_two_back(last_row)
    grad_proj = mm(join_two("ga"), join("o"), TN).astype(bf16)
    before = (grad_up, grad_down)
    y_free = last_row["gc_far"]
    grad_up = scatter(grad_up)
    if contexts == 2:
        cut = grad_down.reshape(owners, 2, part // 2, -1)
        keep = lax.dynamic_index_in_dim(cut, context, 1, keepdims=False)
        came = over_ctx(lax.dynamic_index_in_dim(cut, 1 - context, 1, keepdims=False))
    else:
        grad_down = scatter(grad_down)

    for index, row in enumerate(rows):
        feed_far = far(tie(row["feed"], y_free))
        out = attend_backward(
            tie(row["flags"], *before),
            row["q"],
            row["ga"],
            w_proj,
            row["o"],
            row["k_aug"],
            row["v_aug"],
            row["cos"],
            row["sin"],
            row["cos_k"],
            row["sin_k"],
            heads,
            key_block,
        )
        if index:
            prior = rows[index - 1]
            *out, feed_far, prior["dkvs"], grad_up = hold((*out, feed_far, prior["dkvs"], grad_up))
            if contexts == 2:
                *out, grad_down = hold((*out, grad_down))
        elif contexts == 2:
            *out, feed_far, came = hold((*out, feed_far, came))
            grad_down = scatter((keep.astype(f32) + came.astype(f32)).astype(bf16).reshape(owners * part // 2, -1))
        else:
            *out, feed_far = hold((*out, feed_far))
        y_free = feed_far
        before = (out[0], grad_proj)
        row["gq"] = out[0]
        row["feed_far"] = feed_far
        if contexts == 2:
            row["dkvs"] = [out[1], over_ctx(out[2]), over_ctx(out[3])]
        else:
            row["dkvs"] = [lax.psum_scatter(out[1], "ctx", scatter_dimension=0, tiled=True)]

    side_list = side.reshape(1).astype(jnp.int32)
    grad_proj = scatter(grad_proj)
    sums = 0.0
    for index, row in enumerate(rows):
        first, last, row["dkv"], back_sums = project_back(row["x"], w_qkv, tie(row["gq"], *before), row["dkvs"])
        sums = sums + back_sums
        if index == 0:
            kvs = last_row["dkvs"]
            first, last, row["dkv"], kvs[:-1] = hold((first, last, row["dkv"], kvs[:-1]))
            last_row["gq"] = tie(last_row["gq"], row["dkv"])
            grad_q = mm(join("a"), join("gq"), TN).astype(bf16)
            kvs[-1] = tie(kvs[-1], grad_q)
            grad_q = scatter(grad_q)
            outs = []
            for done in rows:
                mine = by_tokens(
                    close_kernel,
                    [done["h"], done["feed"], done["feed_far"], done["live"]],
                    tie(jnp.broadcast_to(down_shift, (8, width)), row["dkv"]),
                    [bf16],
                    "close",
                )[0]
                outs += [mine, near(mine)]
            outs = gather_rows(side_list, outs)
            before = (row["dkv"], kvs[-1], outs)
        else:
            prior = rows[index - 1]
            down_came = over_ctx(tie(grad_down, kvs[-1])) if contexts == 2 else grad_down
            first, last, prior["ga1_far"], down_came = hold((first, last, prior["ga1_far"], down_came))
            before = (row["dkv"],)
        row["ga1"] = sum_near(first, last)
        row["ga1_far"] = far(row["ga1"])
    grad_kv = mm(join("a"), join("dkv"), TN).astype(bf16)
    def sum_over(v, axis):
        size, step = lax.axis_size(axis), 1
        while step < size:
            v = v + lax.ppermute(v, axis, [(i, i ^ step) for i in range(size)])
            step *= 2
        return v

    def owned(v):
        v = v.reshape(owners, -1)
        return jnp.pad(v, ((0, 0), (0, part - v.shape[1]))).reshape(-1)

    feed_sums = sum(row["feed_sums"] for row in rows)
    d_qb = jnp.concatenate([sums[2, :local], sums[3, : 2 * local]]).reshape(3, heads, owners, -1)
    d_qb = owned(jnp.transpose(d_qb, (2, 0, 1, 3)))
    d_ub = feed_sums[0, : fc1_bias.size * owners].reshape(fc1_bias.shape[0], owners, fc1_bias.shape[1])
    d_ub = owned(jnp.transpose(d_ub, (1, 0, 2)))
    vector = jnp.concatenate([pair, feed_sums[1:2, :width], d_qb[None], d_ub[None], sums[0:2]], axis=0)
    vector_one = sum_over(vector, "ctx")
    up_came = over_ctx(tie(grad_up, vector_one)) if contexts == 2 else grad_up
    last_row["ga1_far"], up_came, grad_q, grad_proj = hold((last_row["ga1_far"], up_came, grad_q, grad_proj))
    grad_kv = scatter(grad_kv)
    if contexts == 2:
        grad_up = grad_up.astype(f32) + up_came.astype(f32)
        low = jnp.where(context_first, grad_down, down_came)
        high = jnp.where(context_first, down_came, grad_down)
        grad_down = jnp.concatenate([low, high], axis=0).astype(f32)
    else:
        grad_up, grad_down = finish(up_came), finish(down_came)
    come = over_ctx if contexts == 2 else lambda v: v
    add = (lambda v, w: v.astype(f32) + w.astype(f32)) if contexts == 2 else lambda v, w: finish(v)
    q_came, proj_came, kv_came = come(grad_q), come(grad_proj), come(grad_kv)

    ins = []
    for row in rows:
        mine = by_tokens(
            norm_one_back_kernel,
            [row["x"], row["ga1"], row["ga1_far"], row["gh"]],
            jnp.broadcast_to(gain_one, (8, width)),
            [bf16],
            "norm_one_back",
        )[0]
        if row is last_row:
            mine, q_came, proj_came = hold((mine, q_came, proj_came))
        ins += [mine, near(mine)]

    vector = sum_over(tie(vector_one, ins[0]), "shard")
    vector = lax.dynamic_slice_in_dim(vector, place * part, part, axis=1)
    both = vector + near(vector)
    norm_one = both[6:8] + far(both[6:8])

    ins, kv_came = hold((gather_rows(side_list, ins), kv_came))
    grad_q, grad_proj, grad_kv = add(grad_q, q_came), add(grad_proj, proj_came), add(grad_kv, kv_came)
    return (
        outs,
        ins,
        norm_one[0],
        norm_one[1],
        jnp.concatenate([grad_q, grad_kv], axis=1).reshape(qkv_weight.shape),
        vector[4, :qb_size].reshape(qkv_bias.shape),
        grad_proj.T,
        both[2],
        both[0],
        both[1],
        grad_up,
        vector[5, : fc1_bias.size].reshape(fc1_bias.shape),
        grad_down.T,
        vector[3],
    )


def solution(mesh):
    in_specs = (
        P("shard", "ctx", None),
        P("shard", "ctx", None),
        P("shard", None),
        P(None, "shard", "ctx"),
        P("shard"),
        P("shard"),
        P("shard", None, "tp"),
        P(None, "tp", "shard"),
        P("tp", "shard"),
        P("shard"),
        P("shard"),
        P("shard"),
        P("shard", "tp"),
        P("tp", "shard"),
        P("tp", "shard"),
        P("shard"),
    )
    out_specs = (
        P("shard", "ctx", None),
        P("shard", "ctx", None),
        P("shard"),
        P("shard"),
        P("shard", None, "tp"),
        P(None, "tp", "shard"),
        P("tp", "shard"),
        P("shard"),
        P("shard"),
        P("shard"),
        P("shard", "tp"),
        P("tp", "shard"),
        P("tp", "shard"),
        P("shard"),
    )
    return jax.shard_map(
        on_device, mesh=mesh, in_specs=in_specs, out_specs=out_specs, check_vma=False
    )
```
